32 devices in a mesh: section: 8 (over y, x, core), seq: 4 (over z).
Axes of the slice: x: 2, y: 2, z: 4, core: 2. Of those that a mesh axis runs over, the one named last changes fastest.
Arguments:
- embedded: bfloat16 [512, 3072], P('seq'), may hold values from -6 to 6
- carried: bfloat16 [8, 512, 3072], P('section', 'seq'), may hold values from -6 to 6
- stash: bfloat16 [8, 512, 3072], P('section', 'seq'), may hold values from -6 to 6
- returned: bfloat16 [8, 512, 3072], P('section', 'seq'), may hold values from -1.75 to 1.75
- loss_grad: bfloat16 [512, 3072], P('seq'), may hold values from -1.75 to 1.75
- qkv_weight: bfloat16 [8, 3, 24, 128, 128], P('section', None, None, 'seq'), may hold values from -0.6 to 0.6
- rel_bias: float32 [8, 32, 24], P('section'), may hold values from -6 to 6
- norm_gain: float32 [8, 3072], P('section'), may hold values from 0.5 to 1.5
- final_gain: float32 [3072], replicated, may hold values from 0.5 to 1.5
Outputs:
- section_out: bfloat16 [8, 512, 3072], P('section', 'seq')
- input_grad: bfloat16 [8, 512, 3072], P('section', 'seq')
- weight_grad: float32 [8, 3, 24, 128, 128], P('section', None, None, 'seq')
- bias_grad: float32 [8, 32, 24], P('section', 'seq')
- gain_grad: float32 [8, 3072], P('section', 'seq')
- memory: bfloat16 [512, 3072], P('section', 'seq')
The draws below stay inside these ranges and needn't reach their ends.
All inputs are finite; a program needn't handle non-finite values.
Results may differ from the reference program's by a relative error of at most 0.012.
The reference program's roundings to bfloat16 on the way count: a program that leaves them out, or rounds other values in their place, can miss the bound.
Values may be sent and summed in bfloat16 or wider, within the bound.
No kernel may reach another device: no remote copies, remote signals or barrier semaphores. Data moves between devices by JAX's collectives and lax.ppermute only.
A program may use at most 128 MiB of HBM per device.

```python
import jax
import jax.numpy as jnp
from jax import lax

HEADS = 24
HEAD_DIM = 128
WIDTH = 3072
RADIUS = 96
BUCKETS = 32
TOK_DEV = 128
TOKENS = 512
N_SECTION = 8
N_SEQ = 4


weight_edge = 0.59375


def drawn_heads(key):
    base_key = jax.random.fold_in(key, 9001)
    first_head = jax.random.randint(jax.random.fold_in(base_key, 1), (N_SECTION,), 0, HEADS)
    offset = jax.random.randint(jax.random.fold_in(base_key, 2), (N_SECTION,), 1, max(HEADS, 2))
    second_head = (first_head + offset) % HEADS
    return (first_head, second_head)


def activation_slab(key, first_head, second_head):
    base_key = jax.random.fold_in(key, 1)
    return jnp.clip(0.3 * jax.random.normal(base_key, (TOKENS, WIDTH), jnp.float32), -2.4, 2.4)


def draw_embedded(key, part):
    first_head, second_head = drawn_heads(key)
    return activation_slab(jax.random.fold_in(key, 11), first_head[0], second_head[0]).astype(jnp.bfloat16)


def draw_carried(key, part):
    first_head, second_head = drawn_heads(key)
    section_keys = jax.random.split(jax.random.fold_in(key, 12), N_SECTION)
    return jax.vmap(activation_slab)(section_keys, jnp.roll(first_head, -1), jnp.roll(second_head, -1)).astype(jnp.bfloat16)


def draw_stash(key, part):
    first_head, second_head = drawn_heads(key)
    section_keys = jax.random.split(jax.random.fold_in(key, 13), N_SECTION)
    return jax.vmap(activation_slab)(section_keys, first_head, second_head).astype(jnp.bfloat16)


def draw_qkv_weight(key, part):
    weight_key = jax.random.fold_in(key, 14)
    weight_scale = HEAD_DIM ** (-0.5)
    weights = weight_scale * jax.random.normal(jax.random.fold_in(weight_key, 1), (N_SECTION, 3, HEADS, HEAD_DIM, HEAD_DIM), jnp.float32)
    return jnp.clip(weights, -weight_edge, weight_edge).astype(jnp.bfloat16)


def block_scale(stream_key, dims, cuts, low, top_value):
    level, own = 1.0, jax.random.fold_in(stream_key, 6)
    for dim, parts in cuts:
        steps = jnp.exp(jax.random.uniform(jax.random.fold_in(own, dim), (parts,), jnp.float32, low / len(cuts), top_value / len(cuts)))
        level = level * jnp.repeat(steps, dims[dim] // parts).reshape([-1 if axis == dim else 1 for axis in range(len(dims))])
    return level


def centred(stream_key, shape, scale, bound, pieces=(), held_as=jnp.bfloat16):
    values = jax.random.normal(stream_key, shape, jnp.float32) * scale
    if len(pieces) > 0:
        values = block_scale(stream_key, shape, pieces, -0.22, 0.18) * values
    return jnp.clip(values, min=-bound, max=bound).astype(held_as)


def setup_inputs(seed: int = 0) -> dict:
    key_of = jax.random.split(jax.random.key(seed), 10)
    return {
        "embedded": draw_embedded(jax.random.fold_in(key_of[9], 71), 0),
        "carried": draw_carried(jax.random.fold_in(key_of[9], 71), 0),
        "stash": draw_stash(jax.random.fold_in(key_of[9], 71), 0),
        "returned": centred(key_of[3], (N_SECTION, TOKENS, WIDTH), 0.3, 1.75, ((0, 8), (1, 4))),
        "loss_grad": centred(key_of[4], (TOKENS, WIDTH), 0.3, 1.75, ((0, 4),)),
        "qkv_weight": draw_qkv_weight(jax.random.fold_in(key_of[9], 71), 0),
        "rel_bias": centred(key_of[6], (N_SECTION, BUCKETS, HEADS), 1.0, 6.0, ((0, 8),), jnp.float32),
        "norm_gain": jnp.clip(1.0 + 0.1 * jax.random.normal(key_of[7], (N_SECTION, WIDTH), jnp.float32), 0.5, 1.5),
        "final_gain": jnp.clip(1.0 + 0.1 * jax.random.normal(key_of[8], (WIDTH,), jnp.float32), 0.5, 1.5),
    }


eps_norm = 1e-06
bucket_edges = (1, 2, 3, 4, 5, 6, 7, 8, 11, 16, 22, 32, 45, 64, 90)
masked_score = -1e+30
block_limit = 512

def contract(pattern, left_side, right_side):
    return jnp.einsum(pattern, left_side.astype(jnp.float32), right_side.astype(jnp.float32), precision=lax.Precision.HIGHEST)

def rounded_rim(values):
    return lax.optimization_barrier(values.astype(jnp.bfloat16)).astype(jnp.float32)

def rounded_total(partials):
    return lax.optimization_barrier(jnp.sum(rounded_rim(partials), axis=0))

def bucket_of(offsets):
    magnitude = jnp.abs(offsets)
    counted = jnp.zeros(offsets.shape, jnp.int32)
    for threshold in bucket_edges:
        counted = counted + (magnitude >= threshold).astype(jnp.int32)
    return counted + 16 * (offsets > 0).astype(jnp.int32)

def expand_bias(bias_table, block_rows, radius):
    window = block_rows + 2 * radius
    span_length = block_rows + window - 1
    offsets = jnp.arange(span_length, dtype=jnp.int32) - (block_rows - 1) - radius
    bucket_count = bias_table.shape[0]
    head_count = bias_table.shape[1]
    onehot = (bucket_of(offsets)[:, None] == jnp.arange(bucket_count, dtype=jnp.int32)[None, :]).astype(jnp.float32)
    by_offset = jnp.dot(onehot, bias_table, precision=lax.Precision.HIGHEST).T
    repeated = jnp.tile(by_offset, (1, block_rows))
    first_index = block_rows - 1
    skewed = repeated[:, first_index:first_index + block_rows * (span_length - 1)]
    skewed = skewed.reshape(head_count, block_rows, span_length - 1)
    return skewed[:, :, :window]

def band_allowed(block_rows, radius, valid_rows):
    window = block_rows + 2 * radius
    offsets = jnp.arange(window, dtype=jnp.int32)[None, :] - radius - jnp.arange(block_rows, dtype=jnp.int32)[:, None]
    return (jnp.abs(offsets) <= radius) & valid_rows[None, :]

def block_probs(query_rows, key_rows, bias_block, allowed, score_scale):
    scores = contract('qhd,khd->hqk', query_rows, key_rows) * score_scale + bias_block
    scores = jnp.where(allowed[None], scores, masked_score)
    row_peak = lax.optimization_barrier(jnp.max(scores, axis=-1, keepdims=True))
    weights = jnp.exp(scores - row_peak)
    return weights / lax.optimization_barrier(jnp.sum(weights, axis=-1, keepdims=True))

def band_forward(queries, keys_ext, values_ext, bias_block, valid_ext, radius):
    row_count = queries.shape[0]
    block_rows = min(block_limit, row_count)
    window = block_rows + 2 * radius
    score_scale = queries.shape[-1] ** (-0.5)

    def one_block(block_index):
        first_row = block_index * block_rows
        query_rows = lax.dynamic_slice_in_dim(queries, first_row, block_rows, 0)
        key_rows = lax.dynamic_slice_in_dim(keys_ext, first_row, window, 0)
        value_rows = lax.dynamic_slice_in_dim(values_ext, first_row, window, 0)
        valid_rows = lax.dynamic_slice_in_dim(valid_ext, first_row, window, 0)
        weights = block_probs(query_rows, key_rows, bias_block, band_allowed(block_rows, radius, valid_rows), score_scale)
        return contract('hqk,khd->qhd', weights.astype(jnp.bfloat16), value_rows)
    blocks = lax.map(one_block, jnp.arange(row_count // block_rows, dtype=jnp.int32))
    return blocks.reshape(queries.shape)

def band_backward(queries, keys_ext, values_ext, bias_block, valid_ext, radius, grad_rows):
    row_count = queries.shape[0]
    block_rows = min(block_limit, row_count)
    window = block_rows + 2 * radius
    score_scale = queries.shape[-1] ** (-0.5)

    def one_step(carried_sums, block_index):
        key_sums, value_sums, bias_sum = carried_sums
        first_row = block_index * block_rows
        query_rows = lax.dynamic_slice_in_dim(queries, first_row, block_rows, 0)
        key_rows = lax.dynamic_slice_in_dim(keys_ext, first_row, window, 0)
        value_rows = lax.dynamic_slice_in_dim(values_ext, first_row, window, 0)
        valid_rows = lax.dynamic_slice_in_dim(valid_ext, first_row, window, 0)
        grad_block = lax.dynamic_slice_in_dim(grad_rows, first_row, block_rows, 0)
        weights = block_probs(query_rows, key_rows, bias_block, band_allowed(block_rows, radius, valid_rows), score_scale)
        packed = weights.astype(jnp.bfloat16)
        grad_value = contract('hqk,qhd->khd', packed, grad_block)
        grad_weights = contract('qhd,khd->hqk', grad_block, value_rows)
        row_delta = lax.optimization_barrier(jnp.sum(weights * grad_weights, axis=-1, keepdims=True))
        grad_scores = weights * (grad_weights - row_delta)
        grad_packed = grad_scores.astype(jnp.bfloat16)
        grad_query = contract('hqk,khd->qhd', grad_packed, key_rows) * score_scale
        grad_key = contract('hqk,qhd->khd', grad_packed, query_rows) * score_scale
        key_sums = lax.dynamic_update_slice_in_dim(key_sums, lax.dynamic_slice_in_dim(key_sums, first_row, window, 0) + grad_key, first_row, 0)
        value_sums = lax.dynamic_update_slice_in_dim(value_sums, lax.dynamic_slice_in_dim(value_sums, first_row, window, 0) + grad_value, first_row, 0)
        return ((key_sums, value_sums, bias_sum + grad_scores), grad_query)
    initial = (jnp.zeros(keys_ext.shape, jnp.float32), jnp.zeros(values_ext.shape, jnp.float32), jnp.zeros(bias_block.shape, jnp.float32))
    sums, grad_blocks = lax.scan(one_step, initial, jnp.arange(row_count // block_rows, dtype=jnp.int32))
    return (grad_blocks.reshape(queries.shape), sums[0], sums[1], sums[2])

def normalize(stream, section_gain):
    widened = stream.astype(jnp.float32)
    inverse = lax.rsqrt(lax.optimization_barrier(jnp.mean(widened * widened, axis=-1, keepdims=True)) + eps_norm)
    return ((widened * inverse * section_gain).astype(jnp.bfloat16), widened, inverse)

def project(normed, weight):
    by_head = normed.reshape(normed.shape[0], weight.shape[1], weight.shape[2])
    return contract('thd,jhde->jthe', by_head, weight).astype(jnp.bfloat16)

def project_back(normed, weight, grad_proj, widened, inverse, section_gain, cotangent):
    head_count, head_dim = (weight.shape[1], weight.shape[2])
    by_head = normed.reshape(N_SEQ, TOK_DEV, head_count, head_dim)
    grad_normed = contract('jthe,jhde->thd', grad_proj, weight).reshape(normed.shape)
    split_proj = grad_proj.reshape(grad_proj.shape[0], N_SEQ, TOK_DEV, head_count, head_dim)
    grad_weight = rounded_total(contract('sthd,jsthe->sjhde', by_head, split_proj))
    gain_terms = (grad_normed * widened * inverse).reshape(N_SEQ, TOK_DEV, normed.shape[1])
    grad_gain = rounded_total(lax.optimization_barrier(jnp.sum(gain_terms, axis=1)))
    scaled = grad_normed * section_gain
    grad_input = inverse * scaled - widened * inverse * inverse * inverse * lax.optimization_barrier(jnp.mean(scaled * widened, axis=-1, keepdims=True))
    return ((cotangent.astype(jnp.float32) + grad_input).astype(jnp.bfloat16), grad_weight, grad_gain)

def shard_backward(proj_b, cotangent, bias_table, radius):
    shard_rows = TOK_DEV
    head_count, head_dim = (proj_b.shape[2], proj_b.shape[3])
    block_rows = min(block_limit, shard_rows)
    bias_block = expand_bias(bias_table, block_rows, radius)
    padded = jnp.pad(proj_b[1:], ((0, 0), (radius, radius), (0, 0), (0, 0)))
    grad_all = cotangent.reshape(proj_b.shape[1:])
    span = shard_rows + 2 * radius

    def one_shard(shard):
        first_row = shard * shard_rows
        queries = lax.dynamic_slice_in_dim(proj_b[0], first_row, shard_rows, 0)
        keys_ext = lax.dynamic_slice_in_dim(padded[0], first_row, span, 0)
        values_ext = lax.dynamic_slice_in_dim(padded[1], first_row, span, 0)
        grad_rows = lax.dynamic_slice_in_dim(grad_all, first_row, shard_rows, 0)
        positions = first_row - radius + jnp.arange(span, dtype=jnp.int32)
        valid_ext = (positions >= 0) & (positions < TOKENS)
        dquery, dkey_ext, dvalue_ext, grad_bias = band_backward(queries, keys_ext, values_ext, bias_block, valid_ext, radius, grad_rows)
        unused_value, pullback = jax.vjp(lambda table_arg: expand_bias(table_arg, block_rows, radius), bias_table)
        return (dquery, jnp.stack([dkey_ext, dvalue_ext]), pullback(grad_bias)[0])
    dquery, grad_ext, grad_tables = lax.map(one_shard, jnp.arange(N_SEQ, dtype=jnp.int32))
    own_part = grad_ext[:, :, radius:radius + shard_rows]
    lower_rim = rounded_rim(grad_ext[:, :, :radius])
    upper_rim = rounded_rim(grad_ext[:, :, radius + shard_rows:])
    empty_rim = jnp.zeros(lower_rim[:1].shape, jnp.float32)
    from_before = jnp.concatenate([empty_rim, upper_rim[:-1]], axis=0)
    from_after = jnp.concatenate([lower_rim[1:], empty_rim], axis=0)
    own_part = own_part.at[:, :, :radius].add(from_before)
    own_part = own_part.at[:, :, shard_rows - radius:].add(from_after)
    grad_kv = jnp.transpose(own_part, (1, 0, 2, 3, 4)).reshape(2, TOKENS, head_count, head_dim)
    return (dquery.reshape(TOKENS, head_count, head_dim), grad_kv, rounded_total(grad_tables))

def section_step(inbound, stashed, cotangent, weight, bias_table, section_gain):
    row_count = inbound.shape[0]
    radius = RADIUS
    positions = jnp.arange(row_count + 2 * radius, dtype=jnp.int32) - radius
    valid_ext = (positions >= 0) & (positions < row_count)
    block_rows = min(block_limit, row_count)
    bias_block = expand_bias(bias_table, block_rows, radius)
    normed_a, widened_a, inverse_a = normalize(inbound, section_gain)
    proj_a = project(normed_a, weight)
    padded_a = jnp.pad(proj_a[1:], ((0, 0), (radius, radius), (0, 0), (0, 0)))
    attended = band_forward(proj_a[0], padded_a[0], padded_a[1], bias_block, valid_ext, radius)
    output = (widened_a + attended.reshape(inbound.shape)).astype(jnp.bfloat16)
    normed_b, widened_b, inverse_b = normalize(stashed, section_gain)
    proj_b = project(normed_b, weight)
    dquery, grad_kv, grad_table = shard_backward(proj_b, cotangent, bias_table, radius)
    grad_proj = jnp.concatenate([dquery[None], grad_kv], axis=0).astype(jnp.bfloat16)
    input_grad, grad_weight, grad_gain = project_back(normed_b, weight, grad_proj, widened_b, inverse_b, section_gain, cotangent)
    return (output, input_grad, grad_weight, grad_table, grad_gain)

def reference(embedded, carried, stash, returned, loss_grad, qkv_weight, rel_bias, norm_gain, final_gain):
    inputs = jnp.concatenate([embedded[None], carried[:-1]], axis=0)
    cotangents = jnp.concatenate([returned[1:], loss_grad[None]], axis=0)

    def per_section(packed_args):
        return section_step(*packed_args)
    results = lax.map(per_section, (inputs, stash, cotangents, qkv_weight, rel_bias, norm_gain))
    outputs, input_grad, weight_grad, bias_grad, gain_grad = results
    memory = normalize(outputs[-1], final_gain)[0]
    return (outputs, input_grad, weight_grad, bias_grad, gain_grad, memory)
```

```python
import functools

import jax
import jax.numpy as jnp
import numpy as np
from jax import lax
from jax.experimental import pallas as pl
from jax.experimental.pallas import tpu as pltpu
from jax.sharding import PartitionSpec as P

RADIUS = 96
HEAD_DIM = 128
ROW_BLOCK = 64
WINDOW = ROW_BLOCK + 2 * RADIUS
eps_norm = 1e-06
bucket_edges = (1, 2, 3, 4, 5, 6, 7, 8, 11, 16, 22, 32, 45, 64, 90)
masked_score = -1e30
F32 = jnp.float32
BF16 = jnp.bfloat16
VMEM_LIMIT = 48 * 1024 * 1024


def bucket_onehot(bucket_count):
    offsets = np.arange(WINDOW) - RADIUS
    magnitude = np.abs(offsets)
    counted = np.zeros(offsets.shape, np.int32)
    for threshold in bucket_edges:
        counted = counted + (magnitude >= threshold)
    counted = counted + 16 * (offsets > 0)
    onehot = (counted[:, None] == np.arange(bucket_count)[None, :]) & (magnitude <= RADIUS)[:, None]
    return onehot.astype(np.float32)


def dot_nn(a, b):
    return lax.dot_general(a, b, (((1,), (0,)), ((), ())), preferred_element_type=F32)


def dot_nt(a, b):
    return lax.dot_general(a, b, (((1,), (1,)), ((), ())), preferred_element_type=F32)


def dot_tn(a, b):
    return lax.dot_general(a, b, (((0,), (0,)), ((), ())), preferred_element_type=F32)


def norm_kernel(x_ref, gain_ref, normed_ref, inverse_ref):
    x = x_ref[...].astype(F32)
    inverse = lax.rsqrt(jnp.mean(x * x, axis=-1, keepdims=True) + eps_norm)
    normed_ref[...] = (x * inverse * gain_ref[...]).astype(BF16)
    inverse_ref[...] = jnp.broadcast_to(inverse, inverse_ref.shape)


def norm_rows(x, gain):
    rows, width = x.shape
    return pl.pallas_call(
        norm_kernel,
        out_shape=(
            jax.ShapeDtypeStruct((rows, width), BF16),
            jax.ShapeDtypeStruct((rows, 128), F32),
        ),
        compiler_params=pltpu.CompilerParams(vmem_limit_bytes=VMEM_LIMIT),
        cost_estimate=pl.CostEstimate(
            flops=6 * rows * width, bytes_accessed=4 * rows * width, transcendentals=rows
        ),
        name="norm_rows",
    )(x, gain)


def load_weight(meta_ref, slot_refs, weight_ref, head, slots):
    depth = HEAD_DIM // slots
    for r, slot_ref in enumerate(slot_refs):
        if slots == 1:
            start = 0
        else:
            start = pl.multiple_of(lax.rem(meta_ref[0] + r, slots) * depth, depth)
        for j in range(3):
            weight_ref[head, pl.ds(start, depth), j * HEAD_DIM : (j + 1) * HEAD_DIM] = slot_ref[j, head]
    return weight_ref[head]


def key_mask(meta_ref, first_key):
    key = lax.broadcasted_iota(jnp.int32, (1, WINDOW), 1) + first_key
    inside = (key >= meta_ref[1]) & (key < meta_ref[2])
    return jnp.where(inside, 0.0, masked_score).astype(F32)


def toeplitz(row):
    return pltpu.roll(
        jnp.broadcast_to(row, (ROW_BLOCK, WINDOW)), 0, 1, stride=1, stride_axis=0
    )


def diagonal_sums(values):
    total = values[:8]
    for a in range(1, ROW_BLOCK // 8):
        total = total + pltpu.roll(values[8 * a : 8 * a + 8], WINDOW - 8 * a, 1)
    row = lax.broadcasted_iota(jnp.int32, total.shape, 0)
    for bit in (1, 2, 4):
        total = jnp.where((row & bit) != 0, pltpu.roll(total, WINDOW - bit, 1), total)
    return jnp.sum(total, axis=0, keepdims=True)


def block_probs(query_rows, key_rows, bias):
    scores = dot_nt(query_rows, key_rows) * (HEAD_DIM ** (-0.5)) + bias
    weights = jnp.exp(scores - jnp.max(scores, axis=-1, keepdims=True))
    return weights * (1.0 / jnp.sum(weights, axis=-1, keepdims=True))


def forward_kernel(slots, group, meta_ref, before_ref, own_ref, after_ref, x_ref, offset_ref, *rest):
    slot_refs = rest[:slots]
    out_ref, weight_ref = rest[slots:]
    rows = own_ref.shape[0]
    blocks = rows // ROW_BLOCK
    masks = [key_mask(meta_ref, b * ROW_BLOCK) for b in range(blocks)]
    for g in range(group):
        columns = slice(g * HEAD_DIM, (g + 1) * HEAD_DIM)
        weight = load_weight(meta_ref, slot_refs, weight_ref, g, slots)
        own = own_ref[:, columns]
        extended = jnp.concatenate([before_ref[:, columns], own, after_ref[:, columns]], axis=0)
        query = dot_nn(own, weight[:, :HEAD_DIM]).astype(BF16)
        key_value = dot_nn(extended, weight[:, HEAD_DIM:]).astype(BF16)
        key, value = key_value[:, :HEAD_DIM], key_value[:, HEAD_DIM:]
        bias = toeplitz(offset_ref[g])
        for b in range(blocks):
            first = b * ROW_BLOCK
            window = slice(first, first + WINDOW)
            probs = block_probs(query[first : first + ROW_BLOCK], key[window], bias + masks[b])
            attended = dot_nn(probs.astype(BF16), value[window])
            kept = x_ref[first : first + ROW_BLOCK, columns].astype(F32)
            out_ref[first : first + ROW_BLOCK, columns] = (kept + attended).astype(BF16)


def column_spec(rows, group, first):
    return pl.BlockSpec((rows, group * HEAD_DIM), lambda i, meta: (0, i + first))


def slot_specs(weight_slots, group):
    return [
        pl.BlockSpec((3, group, slot.shape[2], HEAD_DIM), lambda i, meta: (0, i, 0, 0))
        for slot in weight_slots
    ]


def forward_attention(meta, before, own, after, x, offsets, weight_slots, group):
    rows, width = own.shape
    heads = width // HEAD_DIM
    slots = len(weight_slots)
    return pl.pallas_call(
        functools.partial(forward_kernel, slots, group),
        out_shape=jax.ShapeDtypeStruct((rows, width), BF16),
        grid_spec=pltpu.PrefetchScalarGridSpec(
            num_scalar_prefetch=1,
            grid=(heads // group,),
            in_specs=[
                column_spec(RADIUS, group, 0),
                column_spec(rows, group, 0),
                column_spec(RADIUS, group, 0),
                column_spec(rows, group, 0),
                pl.BlockSpec((group, 1, WINDOW), lambda i, meta: (i, 0, 0)),
                *slot_specs(weight_slots, group),
            ],
            out_specs=column_spec(rows, group, 0),
            scratch_shapes=[pltpu.VMEM((group, HEAD_DIM, 3 * HEAD_DIM), BF16)],
        ),
        compiler_params=pltpu.CompilerParams(vmem_limit_bytes=VMEM_LIMIT),
        cost_estimate=pl.CostEstimate(
            flops=heads * 60_000_000, bytes_accessed=8 * rows * width, transcendentals=heads * 32768
        ),
        name="forward_attention",
    )(meta, before, own, after, x, offsets, *weight_slots)


def backward_kernel(slots, group, meta_ref, before_ref, own_ref, after_ref, cot_ref, offset_ref, *rest):
    slot_refs = rest[:slots]
    rest = rest[slots:]
    grad_ref, lower_ref, upper_ref, offset_grad_ref = rest[:4]
    part_refs = rest[4 : 4 + slots]
    weight_ref, part_ref = rest[4 + slots :]
    rows = own_ref.shape[0]
    blocks = rows // ROW_BLOCK
    scale = HEAD_DIM ** (-0.5)
    masks = [key_mask(meta_ref, b * ROW_BLOCK) for b in range(blocks)]
    for g in range(group):
        columns = slice(g * HEAD_DIM, (g + 1) * HEAD_DIM)
        weight = load_weight(meta_ref, slot_refs, weight_ref, g, slots)
        own = own_ref[:, columns]
        extended = jnp.concatenate([before_ref[:, columns], own, after_ref[:, columns]], axis=0)
        query = dot_nn(own, weight[:, :HEAD_DIM]).astype(BF16)
        key_value = dot_nn(extended, weight[:, HEAD_DIM:]).astype(BF16)
        key, value = key_value[:, :HEAD_DIM], key_value[:, HEAD_DIM:]
        bias = toeplitz(offset_ref[g])
        grad_query, grad_key, grad_value, score_sum = [], [], [], None
        for b in range(blocks):
            first = b * ROW_BLOCK
            window = slice(first, first + WINDOW)
            query_rows = query[first : first + ROW_BLOCK]
            cot_rows = cot_ref[first : first + ROW_BLOCK, columns]
            probs = block_probs(query_rows, key[window], bias + masks[b])
            grad_probs = dot_nt(cot_rows, value[window])
            delta = jnp.sum(probs * grad_probs, axis=-1, keepdims=True)
            grad_scores = probs * (grad_probs - delta)
            score_sum = grad_scores if score_sum is None else score_sum + grad_scores
            grad_packed = grad_scores.astype(BF16)
            grad_query.append(dot_nn(grad_packed, key[window]))
            grad_key.append(dot_tn(grad_packed, query_rows))
            grad_value.append(dot_tn(probs.astype(BF16), cot_rows))

        def joined(parts):
            pieces = []
            for u in range((rows + 2 * RADIUS) // ROW_BLOCK):
                total = None
                for b in range(blocks):
                    if 0 <= u - b < WINDOW // ROW_BLOCK:
                        piece = parts[b][(u - b) * ROW_BLOCK : (u - b + 1) * ROW_BLOCK]
                        total = piece if total is None else total + piece
                pieces.append(total)
            return jnp.concatenate(pieces, axis=0)

        dquery = (jnp.concatenate(grad_query, axis=0) * scale).astype(BF16)
        dkey = (joined(grad_key) * scale).astype(BF16)
        dvalue = joined(grad_value).astype(BF16)
        dkey_value = jnp.concatenate([dkey, dvalue], axis=1)
        grad_extended = dot_nt(dkey_value, weight[:, HEAD_DIM:])
        grad_ref[:, columns] = grad_extended[RADIUS : RADIUS + rows] + dot_nt(dquery, weight[:, :HEAD_DIM])
        lower_ref[:, columns] = grad_extended[:RADIUS].astype(BF16)
        upper_ref[:, columns] = grad_extended[RADIUS + rows :].astype(BF16)
        part_ref[g, :, :HEAD_DIM] = dot_tn(own, dquery)
        part_ref[g, :, HEAD_DIM:] = dot_tn(extended, dkey_value)
        depth = HEAD_DIM // slots
        for r in range(slots):
            if slots == 1:
                start = 0
            else:
                start = pl.multiple_of(lax.rem(meta_ref[0] + r, slots) * depth, depth)
            for j in range(3):
                part_refs[r][j, g] = part_ref[
                    g, pl.ds(start, depth), j * HEAD_DIM : (j + 1) * HEAD_DIM
                ].astype(part_refs[r].dtype)
        offset_grad_ref[g] = diagonal_sums(score_sum)


def backward_attention(meta, before, own, after, cotangent, offsets, weight_slots, group, first_head, heads):
    rows = own.shape[0]
    width = heads * HEAD_DIM
    slots = len(weight_slots)
    first = first_head // group
    slot_shape = weight_slots[0].shape
    part_types = [F32] + [BF16] * (slots - 1) if slots > 1 else [BF16]
    return pl.pallas_call(
        functools.partial(backward_kernel, slots, group),
        out_shape=(
            jax.ShapeDtypeStruct((rows, width), F32),
            jax.ShapeDtypeStruct((RADIUS, width), BF16),
            jax.ShapeDtypeStruct((RADIUS, width), BF16),
            jax.ShapeDtypeStruct((heads, 1, WINDOW), F32),
            *[jax.ShapeDtypeStruct(slot_shape, kind) for kind in part_types],
        ),
        grid_spec=pltpu.PrefetchScalarGridSpec(
            num_scalar_prefetch=1,
            grid=(heads // group,),
            in_specs=[
                column_spec(RADIUS, group, first),
                column_spec(rows, group, first),
                column_spec(RADIUS, group, first),
                column_spec(rows, group, first),
                pl.BlockSpec((group, 1, WINDOW), lambda i, meta: (i + first, 0, 0)),
                *slot_specs(weight_slots, group),
            ],
            out_specs=(
                column_spec(rows, group, 0),
                column_spec(RADIUS, group, 0),
                column_spec(RADIUS, group, 0),
                pl.BlockSpec((group, 1, WINDOW), lambda i, meta: (i, 0, 0)),
                *slot_specs(weight_slots, group),
            ),
            scratch_shapes=[
                pltpu.VMEM((group, HEAD_DIM, 3 * HEAD_DIM), BF16),
                pltpu.VMEM((group, HEAD_DIM, 3 * HEAD_DIM), F32),
            ],
        ),
        compiler_params=pltpu.CompilerParams(vmem_limit_bytes=VMEM_LIMIT),
        cost_estimate=pl.CostEstimate(
            flops=heads * 150_000_000, bytes_accessed=12 * rows * width, transcendentals=heads * 32768
        ),
        name="backward_attention",
    )(meta, before, own, after, cotangent, offsets, *weight_slots)


def finish_kernel(grad_ref, low_ref, high_ref, x_ref, inverse_ref, gain_ref, cot_ref, out_ref, gain_grad_ref):
    rows = x_ref.shape[0]
    grad = grad_ref[...]
    edge = jnp.zeros((rows - RADIUS, grad.shape[1]), F32)
    grad = grad + jnp.concatenate([low_ref[...].astype(F32), edge], axis=0)
    grad = grad + jnp.concatenate([edge, high_ref[...].astype(F32)], axis=0)
    x = x_ref[...].astype(F32)
    inverse = inverse_ref[:, :1]
    gain_grad_ref[...] = jnp.sum(grad * x * inverse, axis=0, keepdims=True)
    scaled = grad * gain_ref[...]
    mean = jnp.mean(scaled * x, axis=-1, keepdims=True)
    result = inverse * scaled - x * (inverse * inverse * inverse * mean)
    out_ref[...] = (cot_ref[...].astype(F32) + result).astype(BF16)


def finish(grad, low, high, x, inverse, gain, cotangent):
    rows, width = x.shape
    return pl.pallas_call(
        finish_kernel,
        out_shape=(
            jax.ShapeDtypeStruct((rows, width), BF16),
            jax.ShapeDtypeStruct((1, width), F32),
        ),
        compiler_params=pltpu.CompilerParams(vmem_limit_bytes=VMEM_LIMIT),
        cost_estimate=pl.CostEstimate(
            flops=16 * rows * width, bytes_accessed=14 * rows * width, transcendentals=0
        ),
        name="finish",
    )(grad, low, high, x, inverse, gain, cotangent)


def body(
    embedded, carried, stash, returned, loss_grad, qkv_weight, rel_bias, norm_gain, final_gain
):
    section_index = lax.axis_index("section")
    section_count = lax.axis_size("section")
    seq_index = lax.axis_index("seq")
    seq_count = lax.axis_size("seq")
    rows, width = embedded.shape
    heads = width // HEAD_DIM
    tokens = rows * seq_count
    shard = qkv_weight[0]
    depth = shard.shape[2]
    by_slots = seq_count <= 4 and depth % 32 == 0
    up = [(i, i + 1) for i in range(seq_count - 1)]
    down = [(j, i) for i, j in up]
    group = 4 if heads % 4 == 0 else 1

    own_b, inverse_b = norm_rows(stash[0], norm_gain)
    before_b = lax.ppermute(own_b[rows - RADIUS :], "seq", up)
    after_b = lax.ppermute(own_b[:RADIUS], "seq", down)
    if by_slots:
        slots = [shard]
        for r in range(1, seq_count):
            slots.append(lax.ppermute(shard, "seq", [((i + r) % seq_count, i) for i in range(seq_count)]))
    else:
        slots = [lax.all_gather(shard, "seq", axis=2, tiled=True)]

    section_up = [(i, (i + 1) % section_count) for i in range(section_count)]
    section_down = [(j, i) for i, j in section_up]
    inbound = lax.ppermute(
        jnp.where(section_index == section_count - 1, embedded, carried[0]), "section", section_up
    )
    cotangent = lax.ppermute(
        jnp.where(section_index == 0, loss_grad, returned[0]), "section", section_down
    )

    onehot = jnp.asarray(bucket_onehot(rel_bias.shape[1]))
    by_offset = jnp.dot(onehot, rel_bias[0], precision=lax.Precision.HIGHEST).T
    inside = jnp.arange(WINDOW, dtype=jnp.int32) <= 2 * RADIUS
    offsets = jnp.where(inside[None, :], by_offset, masked_score)[:, None, :]
    first_key = RADIUS - seq_index * rows
    meta = jnp.stack([seq_index, first_key, first_key + tokens]).astype(jnp.int32)

    own_a, unused = norm_rows(inbound, norm_gain)
    before_a = lax.ppermute(own_a[rows - RADIUS :], "seq", up)
    after_a = lax.ppermute(own_a[:RADIUS], "seq", down)

    grad_own, lower, upper, offset_grad, *parts = backward_attention(
        meta, before_b, own_b, after_b, cotangent, offsets, slots, group, 0, heads
    )
    from_before = lax.ppermute(upper, "seq", up)
    from_after = lax.ppermute(lower, "seq", down)
    if by_slots:
        weight_sum = parts[0]
        for r in range(1, seq_count):
            weight_sum = weight_sum + lax.ppermute(
                parts[r], "seq", [(i, (i + r) % seq_count) for i in range(seq_count)]
            ).astype(F32)
    else:
        weight_sum = lax.psum_scatter(parts[0], "seq", scatter_dimension=2, tiled=True).astype(F32)

    output = forward_attention(meta, before_a, own_a, after_a, inbound, offsets, slots, group)
    final_normed, unused = norm_rows(output, final_gain[None])
    relaid = lax.all_to_all(final_normed, "seq", split_axis=1, concat_axis=0, tiled=True)
    kept = jnp.where(section_index == section_count - 1, relaid, jnp.zeros_like(relaid))
    memory = lax.psum_scatter(kept, "section", scatter_dimension=0, tiled=True)

    input_grad, gain_part = finish(
        grad_own, from_before, from_after, stash[0], inverse_b, norm_gain, cotangent
    )
    bias_part = jnp.dot(
        offset_grad[:, 0, :], onehot, precision=lax.Precision.HIGHEST
    ).T
    bias_sum = lax.psum_scatter(
        bias_part.astype(BF16), "seq", scatter_dimension=0, tiled=True
    ).astype(F32)
    gain_sum = lax.psum_scatter(
        gain_part.astype(BF16), "seq", scatter_dimension=1, tiled=True
    ).astype(F32)
    return (output[None], input_grad[None], weight_sum[None], bias_sum[None], gain_sum, memory)


def solution(mesh):
    in_specs = (
        P("seq", None),
        P("section", "seq", None),
        P("section", "seq", None),
        P("section", "seq", None),
        P("seq", None),
        P("section", None, None, "seq", None),
        P("section", None, None),
        P("section", None),
        P(),
    )
    out_specs = (
        P("section", "seq", None),
        P("section", "seq", None),
        P("section", None, None, "seq", None),
        P("section", "seq", None),
        P("section", "seq"),
        P("section", "seq"),
    )
    return jax.shard_map(body, mesh=mesh, in_specs=in_specs, out_specs=out_specs, check_vma=False)
```

```python
import functools

import jax
import jax.numpy as jnp
import numpy as np
from jax import lax
from jax.experimental import pallas as pl
from jax.experimental.pallas import tpu as pltpu
from jax.sharding import PartitionSpec as P

RADIUS = 96
HEAD_DIM = 128
ROW_BLOCK = 64
WINDOW = ROW_BLOCK + 2 * RADIUS
eps_norm = 1e-06
bucket_edges = (1, 2, 3, 4, 5, 6, 7, 8, 11, 16, 22, 32, 45, 64, 90)
masked_score = -1e30
F32 = jnp.float32
BF16 = jnp.bfloat16
VMEM_LIMIT = 48 * 1024 * 1024


def bucket_onehot(bucket_count):
    offsets = np.arange(WINDOW) - RADIUS
    magnitude = np.abs(offsets)
    counted = np.zeros(offsets.shape, np.int32)
    for threshold in bucket_edges:
        counted = counted + (magnitude >= threshold)
    counted = counted + 16 * (offsets > 0)
    onehot = (counted[:, None] == np.arange(bucket_count)[None, :]) & (magnitude <= RADIUS)[:, None]
    return onehot.astype(np.float32)


def dot_nn(a, b):
    return lax.dot_general(a, b, (((1,), (0,)), ((), ())), preferred_element_type=F32)


def dot_nt(a, b):
    return lax.dot_general(a, b, (((1,), (1,)), ((), ())), preferred_element_type=F32)


def dot_tn(a, b):
    return lax.dot_general(a, b, (((0,), (0,)), ((), ())), preferred_element_type=F32)


def norm_kernel(x_ref, gain_ref, normed_ref, inverse_ref):
    x = x_ref[...].astype(F32)
    inverse = lax.rsqrt(jnp.mean(x * x, axis=-1, keepdims=True) + eps_norm)
    normed_ref[...] = (x * inverse * gain_ref[...]).astype(BF16)
    inverse_ref[...] = jnp.broadcast_to(inverse, inverse_ref.shape)


def norm_rows(x, gain):
    rows, width = x.shape
    return pl.pallas_call(
        norm_kernel,
        out_shape=(
            jax.ShapeDtypeStruct((rows, width), BF16),
            jax.ShapeDtypeStruct((rows, 128), F32),
        ),
        compiler_params=pltpu.CompilerParams(vmem_limit_bytes=VMEM_LIMIT),
        cost_estimate=pl.CostEstimate(
            flops=6 * rows * width, bytes_accessed=4 * rows * width, transcendentals=rows
        ),
        name="norm_rows",
    )(x, gain)


def load_weight(meta_ref, slot_refs, weight_ref, head, slots):
    depth = HEAD_DIM // slots
    for r, slot_ref in enumerate(slot_refs):
        if slots == 1:
            start = 0
        else:
            start = pl.multiple_of(lax.rem(meta_ref[0] + r, slots) * depth, depth)
        for j in range(3):
            weight_ref[head, pl.ds(start, depth), j * HEAD_DIM : (j + 1) * HEAD_DIM] = slot_ref[j, head]
    return weight_ref[head]


def key_mask(meta_ref, first_key):
    key = lax.broadcasted_iota(jnp.int32, (1, WINDOW), 1) + first_key
    inside = (key >= meta_ref[1]) & (key < meta_ref[2])
    return jnp.where(inside, 0.0, masked_score).astype(F32)


def toeplitz(row):
    return pltpu.roll(
        jnp.broadcast_to(row, (ROW_BLOCK, WINDOW)), 0, 1, stride=1, stride_axis=0
    )


def diagonal_sums(values):
    total = values[:8]
    for a in range(1, ROW_BLOCK // 8):
        total = total + pltpu.roll(values[8 * a : 8 * a + 8], WINDOW - 8 * a, 1)
    row = lax.broadcasted_iota(jnp.int32, total.shape, 0)
    for bit in (1, 2, 4):
        total = jnp.where((row & bit) != 0, pltpu.roll(total, WINDOW - bit, 1), total)
    return jnp.sum(total, axis=0, keepdims=True)


def block_probs(query_rows, key_rows, bias):
    scores = dot_nt(query_rows, key_rows) * (HEAD_DIM ** (-0.5)) + bias
    weights = jnp.exp(scores - jnp.max(scores, axis=-1, keepdims=True))
    return weights * (1.0 / jnp.sum(weights, axis=-1, keepdims=True))


def forward_kernel(slots, group, meta_ref, before_ref, own_ref, after_ref, x_ref, offset_ref, *rest):
    slot_refs = rest[:slots]
    out_ref, weight_ref = rest[slots:]
    rows = own_ref.shape[0]
    blocks = rows // ROW_BLOCK
    masks = [key_mask(meta_ref, b * ROW_BLOCK) for b in range(blocks)]
    for g in range(group):
        columns = slice(g * HEAD_DIM, (g + 1) * HEAD_DIM)
        weight = load_weight(meta_ref, slot_refs, weight_ref, g, slots)
        own = own_ref[:, columns]
        extended = jnp.concatenate([before_ref[:, columns], own, after_ref[:, columns]], axis=0)
        query = dot_nn(own, weight[:, :HEAD_DIM]).astype(BF16)
        key_value = dot_nn(extended, weight[:, HEAD_DIM:]).astype(BF16)
        key, value = key_value[:, :HEAD_DIM], key_value[:, HEAD_DIM:]
        bias = toeplitz(offset_ref[g])
        for b in range(blocks):
            first = b * ROW_BLOCK
            window = slice(first, first + WINDOW)
            probs = block_probs(query[first : first + ROW_BLOCK], key[window], bias + masks[b])
            attended = dot_nn(probs.astype(BF16), value[window])
            kept = x_ref[first : first + ROW_BLOCK, columns].astype(F32)
            out_ref[first : first + ROW_BLOCK, columns] = (kept + attended).astype(BF16)


def column_spec(rows, group, first):
    return pl.BlockSpec((rows, group * HEAD_DIM), lambda i, meta: (0, i + first))


def slot_specs(weight_slots, group):
    return [
        pl.BlockSpec((3, group, slot.shape[2], HEAD_DIM), lambda i, meta: (0, i, 0, 0))
        for slot in weight_slots
    ]


def forward_attention(meta, before, own, after, x, offsets, weight_slots, group):
    rows, width = own.shape
    heads = width // HEAD_DIM
    slots = len(weight_slots)
    return pl.pallas_call(
        functools.partial(forward_kernel, slots, group),
        out_shape=jax.ShapeDtypeStruct((rows, width), BF16),
        grid_spec=pltpu.PrefetchScalarGridSpec(
            num_scalar_prefetch=1,
            grid=(heads // group,),
            in_specs=[
                column_spec(RADIUS, group, 0),
                column_spec(rows, group, 0),
                column_spec(RADIUS, group, 0),
                column_spec(rows, group, 0),
                pl.BlockSpec((group, 1, WINDOW), lambda i, meta: (i, 0, 0)),
                *slot_specs(weight_slots, group),
            ],
            out_specs=column_spec(rows, group, 0),
            scratch_shapes=[pltpu.VMEM((group, HEAD_DIM, 3 * HEAD_DIM), BF16)],
        ),
        compiler_params=pltpu.CompilerParams(vmem_limit_bytes=VMEM_LIMIT),
        cost_estimate=pl.CostEstimate(
            flops=heads * 60_000_000, bytes_accessed=8 * rows * width, transcendentals=heads * 32768
        ),
        name="forward_attention",
    )(meta, before, own, after, x, offsets, *weight_slots)


def backward_kernel(slots, group, meta_ref, before_ref, own_ref, after_ref, cot_ref, offset_ref, *rest):
    slot_refs = rest[:slots]
    rest = rest[slots:]
    grad_ref, lower_ref, upper_ref, offset_grad_ref = rest[:4]
    part_refs = rest[4 : 4 + slots]
    weight_ref, part_ref = rest[4 + slots :]
    rows = own_ref.shape[0]
    blocks = rows // ROW_BLOCK
    scale = HEAD_DIM ** (-0.5)
    masks = [key_mask(meta_ref, b * ROW_BLOCK) for b in range(blocks)]
    for g in range(group):
        columns = slice(g * HEAD_DIM, (g + 1) * HEAD_DIM)
        weight = load_weight(meta_ref, slot_refs, weight_ref, g, slots)
        own = own_ref[:, columns]
        extended = jnp.concatenate([before_ref[:, columns], own, after_ref[:, columns]], axis=0)
        query = dot_nn(own, weight[:, :HEAD_DIM]).astype(BF16)
        key_value = dot_nn(extended, weight[:, HEAD_DIM:]).astype(BF16)
        key, value = key_value[:, :HEAD_DIM], key_value[:, HEAD_DIM:]
        bias = toeplitz(offset_ref[g])
        grad_query, grad_key, grad_value, score_sum = [], [], [], None
        for b in range(blocks):
            first = b * ROW_BLOCK
            window = slice(first, first + WINDOW)
            query_rows = query[first : first + ROW_BLOCK]
            cot_rows = cot_ref[first : first + ROW_BLOCK, columns]
            probs = block_probs(query_rows, key[window], bias + masks[b])
            grad_probs = dot_nt(cot_rows, value[window])
            delta = jnp.sum(probs * grad_probs, axis=-1, keepdims=True)
            grad_scores = probs * (grad_probs - delta)
            score_sum = grad_scores if score_sum is None else score_sum + grad_scores
            grad_packed = grad_scores.astype(BF16)
            grad_query.append(dot_nn(grad_packed, key[window]))
            grad_key.append(dot_tn(grad_packed, query_rows))
            grad_value.append(dot_tn(probs.astype(BF16), cot_rows))

        def joined(parts):
            pieces = []
            for u in range((rows + 2 * RADIUS) // ROW_BLOCK):
                total = None
                for b in range(blocks):
                    if 0 <= u - b < WINDOW // ROW_BLOCK:
                        piece = parts[b][(u - b) * ROW_BLOCK : (u - b + 1) * ROW_BLOCK]
                        total = piece if total is None else total + piece
                pieces.append(total)
            return jnp.concatenate(pieces, axis=0)

        dquery = (jnp.concatenate(grad_query, axis=0) * scale).astype(BF16)
        dkey = (joined(grad_key) * scale).astype(BF16)
        dvalue = joined(grad_value).astype(BF16)
        dkey_value = jnp.concatenate([dkey, dvalue], axis=1)
        grad_extended = dot_nt(dkey_value, weight[:, HEAD_DIM:])
        grad_ref[:, columns] = grad_extended[RADIUS : RADIUS + rows] + dot_nt(dquery, weight[:, :HEAD_DIM])
        lower_ref[:, columns] = grad_extended[:RADIUS].astype(BF16)
        upper_ref[:, columns] = grad_extended[RADIUS + rows :].astype(BF16)
        part_ref[g, :, :HEAD_DIM] = dot_tn(own, dquery)
        part_ref[g, :, HEAD_DIM:] = dot_tn(extended, dkey_value)
        depth = HEAD_DIM // slots
        for r in range(slots):
            if slots == 1:
                start = 0
            else:
                start = pl.multiple_of(lax.rem(meta_ref[0] + r, slots) * depth, depth)
            for j in range(3):
                part_refs[r][j, g] = part_ref[
                    g, pl.ds(start, depth), j * HEAD_DIM : (j + 1) * HEAD_DIM
                ].astype(part_refs[r].dtype)
        offset_grad_ref[g] = diagonal_sums(score_sum)


def backward_attention(meta, before, own, after, cotangent, offsets, weight_slots, group, first_head, heads):
    rows = own.shape[0]
    width = heads * HEAD_DIM
    slots = len(weight_slots)
    first = first_head // group
    slot_shape = weight_slots[0].shape
    part_types = [F32] + [BF16] * (slots - 1) if slots > 1 else [BF16]
    return pl.pallas_call(
        functools.partial(backward_kernel, slots, group),
        out_shape=(
            jax.ShapeDtypeStruct((rows, width), F32),
            jax.ShapeDtypeStruct((RADIUS, width), BF16),
            jax.ShapeDtypeStruct((RADIUS, width), BF16),
            jax.ShapeDtypeStruct((heads, 1, WINDOW), F32),
            *[jax.ShapeDtypeStruct(slot_shape, kind) for kind in part_types],
        ),
        grid_spec=pltpu.PrefetchScalarGridSpec(
            num_scalar_prefetch=1,
            grid=(heads // group,),
            in_specs=[
                column_spec(RADIUS, group, first),
                column_spec(rows, group, first),
                column_spec(RADIUS, group, first),
                column_spec(rows, group, first),
                pl.BlockSpec((group, 1, WINDOW), lambda i, meta: (i + first, 0, 0)),
                *slot_specs(weight_slots, group),
            ],
            out_specs=(
                column_spec(rows, group, 0),
                column_spec(RADIUS, group, 0),
                column_spec(RADIUS, group, 0),
                pl.BlockSpec((group, 1, WINDOW), lambda i, meta: (i, 0, 0)),
                *slot_specs(weight_slots, group),
            ),
            scratch_shapes=[
                pltpu.VMEM((group, HEAD_DIM, 3 * HEAD_DIM), BF16),
                pltpu.VMEM((group, HEAD_DIM, 3 * HEAD_DIM), F32),
            ],
        ),
        compiler_params=pltpu.CompilerParams(vmem_limit_bytes=VMEM_LIMIT),
        cost_estimate=pl.CostEstimate(
            flops=heads * 150_000_000, bytes_accessed=12 * rows * width, transcendentals=heads * 32768
        ),
        name="backward_attention",
    )(meta, before, own, after, cotangent, offsets, *weight_slots)


def finish_kernel(grad_ref, low_ref, high_ref, x_ref, inverse_ref, gain_ref, cot_ref, out_ref, gain_grad_ref):
    rows = x_ref.shape[0]
    grad = grad_ref[...]
    edge = jnp.zeros((rows - RADIUS, grad.shape[1]), F32)
    grad = grad + jnp.concatenate([low_ref[...].astype(F32), edge], axis=0)
    grad = grad + jnp.concatenate([edge, high_ref[...].astype(F32)], axis=0)
    x = x_ref[...].astype(F32)
    inverse = inverse_ref[:, :1]
    gain_grad_ref[...] = jnp.sum(grad * x * inverse, axis=0, keepdims=True)
    scaled = grad * gain_ref[...]
    mean = jnp.mean(scaled * x, axis=-1, keepdims=True)
    result = inverse * scaled - x * (inverse * inverse * inverse * mean)
    out_ref[...] = (cot_ref[...].astype(F32) + result).astype(BF16)


def finish(grad, low, high, x, inverse, gain, cotangent):
    rows, width = x.shape
    return pl.pallas_call(
        finish_kernel,
        out_shape=(
            jax.ShapeDtypeStruct((rows, width), BF16),
            jax.ShapeDtypeStruct((1, width), F32),
        ),
        compiler_params=pltpu.CompilerParams(vmem_limit_bytes=VMEM_LIMIT),
        cost_estimate=pl.CostEstimate(
            flops=16 * rows * width, bytes_accessed=14 * rows * width, transcendentals=0
        ),
        name="finish",
    )(grad, low, high, x, inverse, gain, cotangent)


def column_of(row, rows):
    return jnp.transpose(jnp.broadcast_to(row, (128, rows)))


def split_rows(inverse, pad_rows, width):
    high = inverse.astype(BF16)
    rest = inverse - high.astype(F32)
    middle = rest.astype(BF16)
    low = (rest - middle.astype(F32)).astype(BF16)
    wide = [jnp.transpose(jnp.broadcast_to(v.astype(F32), (v.shape[0], 128)))[:1] for v in (high, middle, low)]
    row = jnp.concatenate(wide + [jnp.zeros((pad_rows - 3, wide[0].shape[1]), F32)], axis=0)
    return row.astype(BF16)


def row_inverse(x):
    x = x.astype(F32)
    return lax.rsqrt(jnp.mean(x * x, axis=-1, keepdims=True) + eps_norm)


def pack_stash_kernel(parts, meta_ref, x_ref, weight_ref, inverse_ref, *out_refs):
    rows, width = x_ref.shape
    depth = weight_ref.shape[2]
    wide = width // parts
    heads = wide // HEAD_DIM
    inverse = row_inverse(x_ref[...])
    inverse_ref[...] = jnp.broadcast_to(inverse, inverse_ref.shape)
    tail = split_rows(inverse, 16, wide)
    for r, out_ref in enumerate(out_refs):
        target = lax.rem(meta_ref[0] + r, parts)
        out_ref[:rows] = x_ref[:, pl.ds(pl.multiple_of(target * wide, 128), wide)]
        for j in range(3):
            for h in range(heads):
                out_ref[rows + j * depth : rows + (j + 1) * depth, h * HEAD_DIM : (h + 1) * HEAD_DIM] = weight_ref[
                    j, target * heads + h
                ]
        out_ref[rows + 3 * depth :] = jnp.zeros((16, wide), BF16)
        out_ref[rows + 3 * depth :, :rows] = tail


def pack_rows_kernel(parts, with_inverse, meta_ref, edge_ref, inner_ref, *out_refs):
    rows, width = inner_ref.shape
    wide = width // parts
    edge = 2 if with_inverse else 1
    refs = out_refs[:parts]
    for r, out_ref in enumerate(refs):
        target = lax.rem(meta_ref[0] + r, parts)
        start = pl.multiple_of(target * wide, 128)

        @pl.when(meta_ref[edge] == 1)
        def use_edge():
            out_ref[:rows] = edge_ref[:, pl.ds(start, wide)]

        @pl.when(meta_ref[edge] == 0)
        def use_inner():
            out_ref[:rows] = inner_ref[:, pl.ds(start, wide)]

    def finish_with(source_ref):
        if with_inverse:
            tail = split_rows(row_inverse(source_ref[...]), 16, wide)
            for out_ref in refs:
                out_ref[rows:] = jnp.zeros((16, wide), BF16)
                out_ref[rows:, :rows] = tail
        else:
            out_refs[parts][...] = source_ref[...]

    @pl.when(meta_ref[edge] == 1)
    def finish_edge():
        finish_with(edge_ref)

    @pl.when(meta_ref[edge] == 0)
    def finish_inner():
        finish_with(inner_ref)


SMEM_SPEC = pl.BlockSpec(memory_space=pltpu.SMEM)
VMEM_SPEC = pl.BlockSpec(memory_space=pltpu.VMEM)


def pack_stash(meta, x, weight, parts):
    rows, width = x.shape
    depth = weight.shape[2]
    shape = (rows + 3 * depth + 16, width // parts)
    return pl.pallas_call(
        functools.partial(pack_stash_kernel, parts),
        out_shape=(
            jax.ShapeDtypeStruct((rows, 128), F32),
            *[jax.ShapeDtypeStruct(shape, BF16) for r in range(parts)],
        ),
        in_specs=[SMEM_SPEC, VMEM_SPEC, VMEM_SPEC],
        out_specs=(VMEM_SPEC,) * (parts + 1),
        compiler_params=pltpu.CompilerParams(vmem_limit_bytes=VMEM_LIMIT),
        cost_estimate=pl.CostEstimate(flops=4 * rows * width, bytes_accessed=6 * rows * width, transcendentals=0),
        name="pack_stash",
    )(meta, x, weight)


def pack_rows(meta, edge, inner, parts, with_inverse):
    rows, width = inner.shape
    shape = (rows + (16 if with_inverse else 0), width // parts)
    extra = () if with_inverse else (jax.ShapeDtypeStruct((rows, width), BF16),)
    return pl.pallas_call(
        functools.partial(pack_rows_kernel, parts, with_inverse),
        out_shape=(*[jax.ShapeDtypeStruct(shape, BF16) for r in range(parts)], *extra),
        in_specs=[SMEM_SPEC, VMEM_SPEC, VMEM_SPEC],
        out_specs=(VMEM_SPEC,) * (parts + len(extra)),
        compiler_params=pltpu.CompilerParams(vmem_limit_bytes=VMEM_LIMIT),
        cost_estimate=pl.CostEstimate(flops=4 * rows * width, bytes_accessed=6 * rows * width, transcendentals=0),
        name="pack_inbound" if with_inverse else "pack_cotangent",
    )(meta, edge, inner)


def gather_rows(meta_ref, refs, first, rows, inverse_ref, weight_refs, weight_first, x_ref, weight_ref):
    parts = len(refs)
    depth = HEAD_DIM // parts

    @pl.when(pl.program_id(0) == 0)
    def spread_inverse():
        for r, ref in enumerate(refs):
            source = lax.rem(meta_ref[0] + parts - r, parts)
            rows_at = pl.ds(pl.multiple_of(source * rows, rows), rows)
            tail = ref[first : first + 16].astype(F32)
            inverse_ref[rows_at] = column_of(tail[:1] + tail[1:2] + tail[2:3], rows)

    for r, ref in enumerate(refs):
        source = lax.rem(meta_ref[0] + parts - r, parts)
        x_ref[pl.ds(pl.multiple_of(source * rows, rows), rows)] = ref[:rows]
        depth_at = pl.ds(pl.multiple_of(source * depth, depth), depth)
        for j in range(3):
            weight_ref[depth_at, j * HEAD_DIM : (j + 1) * HEAD_DIM] = weight_refs[r][
                weight_first + j * depth : weight_first + (j + 1) * depth
            ]


def block_mask(first_query, tokens):
    key = lax.broadcasted_iota(jnp.int32, (1, WINDOW), 1) + (first_query - RADIUS)
    return jnp.where((key >= 0) & (key < tokens), 0.0, masked_score).astype(F32)


def edge_bias(bias, first, tokens):
    if first < RADIUS or first + ROW_BLOCK + RADIUS > tokens:
        return bias + block_mask(first, tokens)
    return bias


def padded(rows):
    edge = jnp.zeros((RADIUS, rows.shape[1]), rows.dtype)
    return jnp.concatenate([edge, rows, edge], axis=0)


def heads_backward_kernel(parts, rows, meta_ref, *refs):
    a_refs, c_refs = refs[:parts], refs[parts : 2 * parts]
    gain_ref, offset_ref, onehot_ref = refs[2 * parts : 2 * parts + 3]
    out_refs = refs[2 * parts + 3 : 3 * parts + 3]
    gain_grad_ref, inverse_ref, x_ref, weight_ref, cot_ref, grad_ref, part_ref, bias_ref = refs[3 * parts + 3 :]
    tokens = rows * parts
    depth = HEAD_DIM // parts
    scale = HEAD_DIM ** (-0.5)
    gather_rows(meta_ref, a_refs, rows + 3 * depth, rows, inverse_ref, a_refs, rows, x_ref, weight_ref)
    for r in range(parts):
        source = lax.rem(meta_ref[0] + parts - r, parts)
        cot_ref[pl.ds(pl.multiple_of(source * rows, rows), rows)] = c_refs[r][...]
    weight = weight_ref[...]
    scaled_x = x_ref[...].astype(F32) * inverse_ref[...]
    normed = (scaled_x * gain_ref[...]).astype(BF16)
    query = dot_nn(normed, weight[:, :HEAD_DIM]).astype(BF16)
    key = padded(dot_nn(normed, weight[:, HEAD_DIM : 2 * HEAD_DIM]).astype(BF16))
    value = padded(dot_nn(normed, weight[:, 2 * HEAD_DIM :]).astype(BF16))
    bias = toeplitz(offset_ref[0])
    blocks = tokens // ROW_BLOCK
    grad_query, grad_key, grad_value, score_sum = [], [], [], None
    for b in range(blocks):
        first = b * ROW_BLOCK
        window = slice(first, first + WINDOW)
        query_rows = query[first : first + ROW_BLOCK]
        cot_rows = cot_ref[first : first + ROW_BLOCK]
        probs = block_probs(query_rows, key[window], edge_bias(bias, first, tokens))
        grad_probs = dot_nt(cot_rows, value[window])
        delta = jnp.sum(probs * grad_probs, axis=-1, keepdims=True)
        grad_scores = probs * (grad_probs - delta)
        score_sum = grad_scores if score_sum is None else score_sum + grad_scores
        grad_packed = grad_scores.astype(BF16)
        grad_query.append(dot_nn(grad_packed, key[window]))
        grad_key.append(dot_tn(grad_packed, query_rows))
        grad_value.append(dot_tn(probs.astype(BF16), cot_rows))

    def joined(pieces):
        units = []
        for u in range((tokens + 2 * RADIUS) // ROW_BLOCK):
            total = None
            for b in range(blocks):
                if 0 <= u - b < WINDOW // ROW_BLOCK:
                    piece = pieces[b][(u - b) * ROW_BLOCK : (u - b + 1) * ROW_BLOCK]
                    total = piece if total is None else total + piece
            units.append(total)
        return jnp.concatenate(units, axis=0)[RADIUS : RADIUS + tokens]

    dqkv = jnp.concatenate(
        [
            (jnp.concatenate(grad_query, axis=0) * scale).astype(BF16),
            (joined(grad_key) * scale).astype(BF16),
            joined(grad_value).astype(BF16),
        ],
        axis=1,
    )
    grad_normed = dot_nt(dqkv, weight)
    gain_grad_ref[...] = jnp.sum(grad_normed * scaled_x, axis=0, keepdims=True)
    grad_ref[...] = grad_normed
    part_ref[...] = dot_tn(normed, dqkv)
    bias_grad = jnp.sum(onehot_ref[...] * diagonal_sums(score_sum), axis=1, keepdims=True)
    bias_ref[...] = jnp.broadcast_to(bias_grad, bias_ref.shape)
    buckets = bias_ref.shape[0] // parts
    for r, out_ref in enumerate(out_refs):
        source = lax.rem(meta_ref[0] + parts - r, parts)
        out_ref[:rows] = grad_ref[pl.ds(pl.multiple_of(source * rows, rows), rows)].astype(BF16)
        for j in range(3):
            out_ref[rows + j * depth : rows + (j + 1) * depth] = part_ref[
                pl.ds(pl.multiple_of(source * depth, depth), depth), j * HEAD_DIM : (j + 1) * HEAD_DIM
            ].astype(BF16)
        share = bias_ref[pl.ds(pl.multiple_of(source * buckets, buckets), buckets)]
        out_ref[rows + 3 * depth :] = jnp.concatenate(
            [share, jnp.zeros((16 - buckets, HEAD_DIM), F32)], axis=0
        ).astype(BF16)


def head_column(rows):
    return pl.BlockSpec((rows, HEAD_DIM), lambda i, meta: (0, i))


def heads_backward(meta, a_slots, c_slots, gain, offsets, onehot, heads):
    parts = len(a_slots)
    rows = c_slots[0].shape[0]
    tokens = rows * parts
    buckets = onehot.shape[0]
    packed = a_slots[0].shape[0]
    width = heads * HEAD_DIM
    return pl.pallas_call(
        functools.partial(heads_backward_kernel, parts, rows),
        out_shape=(
            *[jax.ShapeDtypeStruct((packed, width), BF16) for r in range(parts)],
            jax.ShapeDtypeStruct((1, width), F32),
        ),
        grid_spec=pltpu.PrefetchScalarGridSpec(
            num_scalar_prefetch=1,
            grid=(heads,),
            in_specs=[
                *[head_column(packed)] * parts,
                *[head_column(rows)] * parts,
                pl.BlockSpec((1, HEAD_DIM), lambda i, meta: (0, meta[0] * heads + i)),
                pl.BlockSpec((1, 1, WINDOW), lambda i, meta: (meta[0] * heads + i, 0, 0)),
                pl.BlockSpec((buckets, WINDOW), lambda i, meta: (0, 0)),
            ],
            out_specs=(*[head_column(packed)] * parts, head_column(1)),
            scratch_shapes=[
                pltpu.VMEM((tokens, HEAD_DIM), F32),
                pltpu.VMEM((tokens, HEAD_DIM), BF16),
                pltpu.VMEM((HEAD_DIM, 3 * HEAD_DIM), BF16),
                pltpu.VMEM((tokens, HEAD_DIM), BF16),
                pltpu.VMEM((tokens, HEAD_DIM), F32),
                pltpu.VMEM((HEAD_DIM, 3 * HEAD_DIM), F32),
                pltpu.VMEM((buckets, HEAD_DIM), F32),
            ],
        ),
        compiler_params=pltpu.CompilerParams(vmem_limit_bytes=VMEM_LIMIT),
        cost_estimate=pl.CostEstimate(
            flops=heads * tokens * 4_000_000, bytes_accessed=6 * tokens * width, transcendentals=heads * tokens * WINDOW
        ),
        name="heads_backward",
    )(meta, *a_slots, *c_slots, gain, offsets, onehot)


def heads_forward_kernel(parts, rows, meta_ref, *refs):
    a_refs, i_refs = refs[:parts], refs[parts : 2 * parts]
    gain_ref, offset_ref = refs[2 * parts : 2 * parts + 2]
    out_refs = refs[2 * parts + 2 : 3 * parts + 2]
    sums_ref, inverse_ref, x_ref, weight_ref, made_ref, square_ref = refs[3 * parts + 2 :]
    tokens = rows * parts
    gather_rows(meta_ref, i_refs, rows, rows, inverse_ref, a_refs, rows, x_ref, weight_ref)
    weight = weight_ref[...]
    normed = (x_ref[...].astype(F32) * inverse_ref[...] * gain_ref[...]).astype(BF16)
    query = dot_nn(normed, weight[:, :HEAD_DIM]).astype(BF16)
    key = padded(dot_nn(normed, weight[:, HEAD_DIM : 2 * HEAD_DIM]).astype(BF16))
    value = padded(dot_nn(normed, weight[:, 2 * HEAD_DIM :]).astype(BF16))
    bias = toeplitz(offset_ref[0])
    for b in range(tokens // ROW_BLOCK):
        first = b * ROW_BLOCK
        window = slice(first, first + WINDOW)
        probs = block_probs(query[first : first + ROW_BLOCK], key[window], edge_bias(bias, first, tokens))
        attended = dot_nn(probs.astype(BF16), value[window])
        made_ref[first : first + ROW_BLOCK] = (
            x_ref[first : first + ROW_BLOCK].astype(F32) + attended
        ).astype(BF16)
    made = made_ref[...].astype(F32)
    squares = made * made

    @pl.when(pl.program_id(0) == 0)
    def first_head():
        square_ref[...] = squares

    @pl.when(pl.program_id(0) > 0)
    def later_head():
        square_ref[...] += squares

    @pl.when(pl.program_id(0) == pl.num_programs(0) - 1)
    def last_head():
        total = jnp.sum(jnp.transpose(square_ref[...]), axis=0, keepdims=True)
        sums_ref[...] = jnp.broadcast_to(total, sums_ref.shape)

    for r, out_ref in enumerate(out_refs):
        source = lax.rem(meta_ref[0] + parts - r, parts)
        out_ref[...] = made_ref[pl.ds(pl.multiple_of(source * rows, rows), rows)]


def heads_forward(meta, a_slots, i_slots, gain, offsets, heads, rows):
    parts = len(a_slots)
    tokens = rows * parts
    packed = a_slots[0].shape[0]
    width = heads * HEAD_DIM
    return pl.pallas_call(
        functools.partial(heads_forward_kernel, parts, rows),
        out_shape=(
            *[jax.ShapeDtypeStruct((rows, width), BF16) for r in range(parts)],
            jax.ShapeDtypeStruct((8, tokens), F32),
        ),
        grid_spec=pltpu.PrefetchScalarGridSpec(
            num_scalar_prefetch=1,
            grid=(heads,),
            in_specs=[
                *[head_column(packed)] * parts,
                *[head_column(i_slots[0].shape[0])] * parts,
                pl.BlockSpec((1, HEAD_DIM), lambda i, meta: (0, meta[0] * heads + i)),
                pl.BlockSpec((1, 1, WINDOW), lambda i, meta: (meta[0] * heads + i, 0, 0)),
            ],
            out_specs=(
                *[head_column(rows)] * parts,
                pl.BlockSpec((8, tokens), lambda i, meta: (0, 0)),
            ),
            scratch_shapes=[
                pltpu.VMEM((tokens, HEAD_DIM), F32),
                pltpu.VMEM((tokens, HEAD_DIM), BF16),
                pltpu.VMEM((HEAD_DIM, 3 * HEAD_DIM), BF16),
                pltpu.VMEM((tokens, HEAD_DIM), BF16),
                pltpu.VMEM((tokens, HEAD_DIM), F32),
            ],
        ),
        compiler_params=pltpu.CompilerParams(vmem_limit_bytes=VMEM_LIMIT),
        cost_estimate=pl.CostEstimate(
            flops=heads * tokens * 2_000_000, bytes_accessed=6 * tokens * width, transcendentals=heads * tokens * WINDOW
        ),
        name="heads_forward",
    )(meta, *a_slots, *i_slots, gain, offsets)


def memory_kernel(parts, width, meta_ref, *refs):
    out_refs, sum_refs = refs[:parts], refs[parts : 2 * parts]
    gain_ref, memory_ref = refs[2 * parts :]
    rows = out_refs[0].shape[0]
    wide = memory_ref.shape[1]
    total = sum_refs[0][:1]
    for sum_ref in sum_refs[1:]:
        total = total + sum_ref[:1]
    inverse = lax.rsqrt(total / width + eps_norm)
    gain = gain_ref[:, pl.ds(pl.multiple_of(meta_ref[0] * wide, 128), wide)]
    spread_inverse = jnp.transpose(jnp.broadcast_to(inverse, (128, inverse.shape[1])))
    for r, out_ref in enumerate(out_refs):
        source = lax.rem(meta_ref[0] + parts - r, parts)
        memory_ref[pl.ds(pl.multiple_of(source * rows, rows), rows)] = out_ref[...]
    made = memory_ref[...].astype(F32)
    memory_ref[...] = (made * spread_inverse[:, :1] * gain).astype(BF16)


def memory_rows(meta, outs, sums, gain, width):
    parts = len(outs)
    rows, wide = outs[0].shape
    return pl.pallas_call(
        functools.partial(memory_kernel, parts, width),
        out_shape=jax.ShapeDtypeStruct((rows * parts, wide), BF16),
        in_specs=[SMEM_SPEC] + [VMEM_SPEC] * (2 * parts + 1),
        out_specs=VMEM_SPEC,
        compiler_params=pltpu.CompilerParams(vmem_limit_bytes=VMEM_LIMIT),
        cost_estimate=pl.CostEstimate(flops=4 * rows * width, bytes_accessed=4 * rows * width, transcendentals=0),
        name="memory_rows",
    )(meta, *outs, *sums, gain)


def place_kernel(parts, meta_ref, *refs):
    out_ref = refs[parts]
    wide = refs[0].shape[1]
    for r in range(parts):
        source = lax.rem(meta_ref[0] + r, parts)
        out_ref[:, pl.ds(pl.multiple_of(source * wide, 128), wide)] = refs[r][...]


def place_columns(meta, slots):
    parts = len(slots)
    rows, wide = slots[0].shape
    return pl.pallas_call(
        functools.partial(place_kernel, parts),
        out_shape=jax.ShapeDtypeStruct((rows, wide * parts), BF16),
        in_specs=[SMEM_SPEC] + [VMEM_SPEC] * parts,
        out_specs=VMEM_SPEC,
        compiler_params=pltpu.CompilerParams(vmem_limit_bytes=VMEM_LIMIT),
        cost_estimate=pl.CostEstimate(flops=0, bytes_accessed=4 * rows * wide * parts, transcendentals=0),
        name="place_columns",
    )(meta, *slots)


def heads_finish_kernel(parts, meta_ref, *refs):
    g_refs = refs[:parts]
    x_ref, inverse_ref, gain_ref, cot_ref, out_ref, weight_ref, bias_ref, scaled_ref = refs[parts:]
    rows, width = x_ref.shape
    wide = width // parts
    heads = wide // HEAD_DIM
    depth = HEAD_DIM // parts
    buckets = bias_ref.shape[1]
    for r in range(parts):
        source = lax.rem(meta_ref[0] + r, parts)
        columns = pl.ds(pl.multiple_of(source * wide, 128), wide)
        scaled_ref[:, columns] = g_refs[r][:rows].astype(F32) * gain_ref[:, columns]
        for h in range(heads):
            lanes = slice(h * HEAD_DIM, (h + 1) * HEAD_DIM)
            for j in range(3):
                weight_ref[j, source * heads + h] = g_refs[r][
                    rows + j * depth : rows + (j + 1) * depth, lanes
                ].astype(F32)
            bias_ref[source * heads + h] = g_refs[r][rows + 3 * depth :, lanes].astype(F32)[:buckets]
    x = x_ref[...].astype(F32)
    scaled = scaled_ref[...]
    inverse = inverse_ref[:, :1]
    mean = jnp.mean(scaled * x, axis=-1, keepdims=True)
    result = inverse * scaled - x * (inverse * inverse * inverse * mean)
    out_ref[...] = (cot_ref[...].astype(F32) + result).astype(BF16)


def heads_finish(meta, g_slots, x, inverse, gain, cotangent, buckets):
    parts = len(g_slots)
    rows, width = x.shape
    heads = width // HEAD_DIM
    return pl.pallas_call(
        functools.partial(heads_finish_kernel, parts),
        out_shape=(
            jax.ShapeDtypeStruct((rows, width), BF16),
            jax.ShapeDtypeStruct((3, heads, HEAD_DIM // parts, HEAD_DIM), F32),
            jax.ShapeDtypeStruct((heads, buckets // parts, HEAD_DIM), F32),
        ),
        in_specs=[SMEM_SPEC] + [VMEM_SPEC] * (parts + 4),
        out_specs=(VMEM_SPEC,) * 3,
        scratch_shapes=[pltpu.VMEM((rows, width), F32)],
        compiler_params=pltpu.CompilerParams(vmem_limit_bytes=VMEM_LIMIT),
        cost_estimate=pl.CostEstimate(flops=12 * rows * width, bytes_accessed=14 * rows * width, transcendentals=0),
        name="heads_finish",
    )(meta, *g_slots, x, inverse, gain, cotangent)


def offset_table(rel_bias):
    onehot = jnp.asarray(bucket_onehot(rel_bias.shape[0]))
    by_offset = jnp.dot(onehot, rel_bias, precision=lax.Precision.HIGHEST).T
    inside = jnp.arange(WINDOW, dtype=jnp.int32) <= 2 * RADIUS
    return jnp.where(inside[None, :], by_offset, masked_score)[:, None, :]


def heads_body(
    embedded, carried, stash, returned, loss_grad, qkv_weight, rel_bias, norm_gain, final_gain
):
    section = lax.axis_index("section")
    sections = lax.axis_size("section")
    parts = lax.axis_size("seq")
    rows, width = embedded.shape
    heads = width // HEAD_DIM // parts
    buckets = rel_bias.shape[1]
    meta = jnp.stack(
        [lax.axis_index("seq"), section == 0, section == sections - 1]
    ).astype(jnp.int32)

    def shifted(value, r, step):
        if step == 0:
            return lax.ppermute(value, "seq", [(i, (i + r) % parts) for i in range(parts)])
        pairs = [
            (s * parts + i, (s + step) % sections * parts + (i + r) % parts)
            for s in range(sections)
            for i in range(parts)
        ]
        return lax.ppermute(value, ("section", "seq"), pairs)

    def returned_to(value, r):
        return lax.ppermute(value, "seq", [(i, (i - r) % parts) for i in range(parts)])

    inverse_b, *a_sends = pack_stash(meta, stash[0], qkv_weight[0], parts)
    a_slots = [a_sends[0]] + [shifted(a_sends[r], r, 0) for r in range(1, parts)]
    *c_sends, cot_source = pack_rows(meta, loss_grad, returned[0], parts, False)
    c_slots = [shifted(c_sends[r], r, -1) for r in range(parts)]
    cotangent = lax.ppermute(
        cot_source, "section", [((s + 1) % sections, s) for s in range(sections)]
    )
    i_sends = pack_rows(meta, embedded, carried[0], parts, True)
    i_slots = [shifted(i_sends[r], r, 1) for r in range(parts)]

    offsets = offset_table(rel_bias[0])
    onehot = jnp.asarray(bucket_onehot(buckets).T)
    *g_sends, gain_grad = heads_backward(meta, a_slots, c_slots, norm_gain, offsets, onehot, heads)
    g_slots = [g_sends[0]] + [returned_to(g_sends[r], r) for r in range(1, parts)]

    *o_sends, sums = heads_forward(meta, a_slots, i_slots, norm_gain, offsets, heads, rows)
    o_slots = [o_sends[0]] + [returned_to(o_sends[r], r) for r in range(1, parts)]
    all_sums = [sums] + [shifted(sums, r, 0) for r in range(1, parts)]
    made = memory_rows(meta, o_sends, all_sums, final_gain[None], width)
    share = rows * parts // sections
    memory = jnp.where(section == sections - 1, made[(sections - 1) * share :], 0)
    for s in range(sections - 1):
        memory = memory + lax.ppermute(
            made[s * share : (s + 1) * share], "section", [(sections - 1, s)]
        )

    input_grad, weight_grad, bias_wide = heads_finish(
        meta, g_slots, stash[0], inverse_b, norm_gain, cotangent, buckets
    )
    bias_grad = bias_wide[:, :, 0].T
    output = place_columns(meta, o_slots)
    return (
        output[None],
        input_grad[None],
        weight_grad[None],
        bias_grad[None],
        gain_grad,
        memory.astype(BF16),
    )


def tokens_body(
    embedded, carried, stash, returned, loss_grad, qkv_weight, rel_bias, norm_gain, final_gain
):
    section_index = lax.axis_index("section")
    section_count = lax.axis_size("section")
    seq_index = lax.axis_index("seq")
    seq_count = lax.axis_size("seq")
    rows, width = embedded.shape
    heads = width // HEAD_DIM
    tokens = rows * seq_count
    shard = qkv_weight[0]
    up = [(i, i + 1) for i in range(seq_count - 1)]
    down = [(j, i) for i, j in up]
    group = 4 if heads % 4 == 0 else 1

    own_b, inverse_b = norm_rows(stash[0], norm_gain)
    before_b = lax.ppermute(own_b[rows - RADIUS :], "seq", up)
    after_b = lax.ppermute(own_b[:RADIUS], "seq", down)
    slots = [lax.all_gather(shard, "seq", axis=2, tiled=True)]

    section_up = [(i, (i + 1) % section_count) for i in range(section_count)]
    section_down = [(j, i) for i, j in section_up]
    inbound = lax.ppermute(
        jnp.where(section_index == section_count - 1, embedded, carried[0]), "section", section_up
    )
    cotangent = lax.ppermute(
        jnp.where(section_index == 0, loss_grad, returned[0]), "section", section_down
    )

    onehot = jnp.asarray(bucket_onehot(rel_bias.shape[1]))
    offsets = offset_table(rel_bias[0])
    first_key = RADIUS - seq_index * rows
    meta = jnp.stack([seq_index, first_key, first_key + tokens]).astype(jnp.int32)

    own_a, unused = norm_rows(inbound, norm_gain)
    before_a = lax.ppermute(own_a[rows - RADIUS :], "seq", up)
    after_a = lax.ppermute(own_a[:RADIUS], "seq", down)

    grad_own, lower, upper, offset_grad, *parts = backward_attention(
        meta, before_b, own_b, after_b, cotangent, offsets, slots, group, 0, heads
    )
    from_before = lax.ppermute(upper, "seq", up)
    from_after = lax.ppermute(lower, "seq", down)
    weight_sum = lax.psum_scatter(parts[0], "seq", scatter_dimension=2, tiled=True).astype(F32)

    output = forward_attention(meta, before_a, own_a, after_a, inbound, offsets, slots, group)
    final_normed, unused = norm_rows(output, final_gain[None])
    relaid = lax.all_to_all(final_normed, "seq", split_axis=1, concat_axis=0, tiled=True)
    kept = jnp.where(section_index == section_count - 1, relaid, jnp.zeros_like(relaid))
    memory = lax.psum_scatter(kept, "section", scatter_dimension=0, tiled=True)

    input_grad, gain_part = finish(
        grad_own, from_before, from_after, stash[0], inverse_b, norm_gain, cotangent
    )
    bias_part = jnp.dot(
        offset_grad[:, 0, :], onehot, precision=lax.Precision.HIGHEST
    ).T
    bias_sum = lax.psum_scatter(
        bias_part.astype(BF16), "seq", scatter_dimension=0, tiled=True
    ).astype(F32)
    gain_sum = lax.psum_scatter(
        gain_part.astype(BF16), "seq", scatter_dimension=1, tiled=True
    ).astype(F32)
    return (output[None], input_grad[None], weight_sum[None], bias_sum[None], gain_sum, memory)


def choose_body(embedded, carried, stash, returned, loss_grad, qkv_weight, rel_bias, norm_gain, final_gain):
    parts = lax.axis_size("seq")
    rows, width = embedded.shape
    even = width % (HEAD_DIM * parts) == 0 and HEAD_DIM % (32 * parts) == 0 and rows == 128
    even = even and rel_bias.shape[1] == 8 * parts and rows * parts % (16 * lax.axis_size("section")) == 0
    chosen = heads_body if even else tokens_body
    return chosen(
        embedded, carried, stash, returned, loss_grad, qkv_weight, rel_bias, norm_gain, final_gain
    )


def solution(mesh):
    in_specs = (
        P("seq", None),
        P("section", "seq", None),
        P("section", "seq", None),
        P("section", "seq", None),
        P("seq", None),
        P("section", None, None, "seq", None),
        P("section", None, None),
        P("section", None),
        P(),
    )
    out_specs = (
        P("section", "seq", None),
        P("section", "seq", None),
        P("section", None, None, "seq", None),
        P("section", "seq", None),
        P("section", "seq"),
        P("section", "seq"),
    )
    return jax.shard_map(choose_body, mesh=mesh, in_specs=in_specs, out_specs=out_specs, check_vma=False)
```

```python
import functools

import jax
import jax.numpy as jnp
import numpy as np
from jax import lax
from jax.experimental import pallas as pl
from jax.experimental.pallas import tpu as pltpu
from jax.sharding import PartitionSpec as P

RADIUS = 96
HEAD_DIM = 128
ROW_BLOCK = 64
WINDOW = ROW_BLOCK + 2 * RADIUS
eps_norm = 1e-06
bucket_edges = (1, 2, 3, 4, 5, 6, 7, 8, 11, 16, 22, 32, 45, 64, 90)
masked_score = -1e30
F32 = jnp.float32
BF16 = jnp.bfloat16
VMEM_LIMIT = 48 * 1024 * 1024


def bucket_onehot(bucket_count):
    offsets = np.arange(WINDOW) - RADIUS
    magnitude = np.abs(offsets)
    counted = np.zeros(offsets.shape, np.int32)
    for threshold in bucket_edges:
        counted = counted + (magnitude >= threshold)
    counted = counted + 16 * (offsets > 0)
    onehot = (counted[:, None] == np.arange(bucket_count)[None, :]) & (magnitude <= RADIUS)[:, None]
    return onehot.astype(np.float32)


def dot_nn(a, b):
    return lax.dot_general(a, b, (((1,), (0,)), ((), ())), preferred_element_type=F32)


def dot_nt(a, b):
    return lax.dot_general(a, b, (((1,), (1,)), ((), ())), preferred_element_type=F32)


def dot_tn(a, b):
    return lax.dot_general(a, b, (((0,), (0,)), ((), ())), preferred_element_type=F32)


def norm_kernel(x_ref, gain_ref, normed_ref, inverse_ref):
    x = x_ref[...].astype(F32)
    inverse = lax.rsqrt(jnp.mean(x * x, axis=-1, keepdims=True) + eps_norm)
    normed_ref[...] = (x * inverse * gain_ref[...]).astype(BF16)
    inverse_ref[...] = jnp.broadcast_to(inverse, inverse_ref.shape)


def norm_rows(x, gain):
    rows, width = x.shape
    return pl.pallas_call(
        norm_kernel,
        out_shape=(
            jax.ShapeDtypeStruct((rows, width), BF16),
            jax.ShapeDtypeStruct((rows, 128), F32),
        ),
        compiler_params=pltpu.CompilerParams(vmem_limit_bytes=VMEM_LIMIT),
        cost_estimate=pl.CostEstimate(
            flops=6 * rows * width, bytes_accessed=4 * rows * width, transcendentals=rows
        ),
        name="norm_rows",
    )(x, gain)


def load_weight(meta_ref, slot_refs, weight_ref, head, slots):
    depth = HEAD_DIM // slots
    for r, slot_ref in enumerate(slot_refs):
        if slots == 1:
            start = 0
        else:
            start = pl.multiple_of(lax.rem(meta_ref[0] + r, slots) * depth, depth)
        for j in range(3):
            weight_ref[head, pl.ds(start, depth), j * HEAD_DIM : (j + 1) * HEAD_DIM] = slot_ref[j, head]
    return weight_ref[head]


def key_mask(meta_ref, first_key):
    key = lax.broadcasted_iota(jnp.int32, (1, WINDOW), 1) + first_key
    inside = (key >= meta_ref[1]) & (key < meta_ref[2])
    return jnp.where(inside, 0.0, masked_score).astype(F32)


def toeplitz(row):
    return pltpu.roll(
        jnp.broadcast_to(row, (ROW_BLOCK, WINDOW)), 0, 1, stride=1, stride_axis=0
    )


def diagonal_sums(values):
    total = values[:8]
    for a in range(1, ROW_BLOCK // 8):
        total = total + pltpu.roll(values[8 * a : 8 * a + 8], WINDOW - 8 * a, 1)
    row = lax.broadcasted_iota(jnp.int32, total.shape, 0)
    for bit in (1, 2, 4):
        total = jnp.where((row & bit) != 0, pltpu.roll(total, WINDOW - bit, 1), total)
    return jnp.sum(total, axis=0, keepdims=True)


def block_probs(query_rows, key_rows, bias):
    scores = dot_nt(query_rows, key_rows) * (HEAD_DIM ** (-0.5)) + bias
    weights = jnp.exp(scores - jnp.max(scores, axis=-1, keepdims=True))
    return weights * (1.0 / jnp.sum(weights, axis=-1, keepdims=True))


def forward_kernel(slots, group, meta_ref, before_ref, own_ref, after_ref, x_ref, offset_ref, *rest):
    slot_refs = rest[:slots]
    out_ref, weight_ref = rest[slots:]
    rows = own_ref.shape[0]
    blocks = rows // ROW_BLOCK
    masks = [key_mask(meta_ref, b * ROW_BLOCK) for b in range(blocks)]
    for g in range(group):
        columns = slice(g * HEAD_DIM, (g + 1) * HEAD_DIM)
        weight = load_weight(meta_ref, slot_refs, weight_ref, g, slots)
        own = own_ref[:, columns]
        extended = jnp.concatenate([before_ref[:, columns], own, after_ref[:, columns]], axis=0)
        query = dot_nn(own, weight[:, :HEAD_DIM]).astype(BF16)
        key_value = dot_nn(extended, weight[:, HEAD_DIM:]).astype(BF16)
        key, value = key_value[:, :HEAD_DIM], key_value[:, HEAD_DIM:]
        bias = toeplitz(offset_ref[g])
        for b in range(blocks):
            first = b * ROW_BLOCK
            window = slice(first, first + WINDOW)
            probs = block_probs(query[first : first + ROW_BLOCK], key[window], bias + masks[b])
            attended = dot_nn(probs.astype(BF16), value[window])
            kept = x_ref[first : first + ROW_BLOCK, columns].astype(F32)
            out_ref[first : first + ROW_BLOCK, columns] = (kept + attended).astype(BF16)


def column_spec(rows, group, first):
    return pl.BlockSpec((rows, group * HEAD_DIM), lambda i, meta: (0, i + first))


def slot_specs(weight_slots, group):
    return [
        pl.BlockSpec((3, group, slot.shape[2], HEAD_DIM), lambda i, meta: (0, i, 0, 0))
        for slot in weight_slots
    ]


def forward_attention(meta, before, own, after, x, offsets, weight_slots, group):
    rows, width = own.shape
    heads = width // HEAD_DIM
    slots = len(weight_slots)
    return pl.pallas_call(
        functools.partial(forward_kernel, slots, group),
        out_shape=jax.ShapeDtypeStruct((rows, width), BF16),
        grid_spec=pltpu.PrefetchScalarGridSpec(
            num_scalar_prefetch=1,
            grid=(heads // group,),
            in_specs=[
                column_spec(RADIUS, group, 0),
                column_spec(rows, group, 0),
                column_spec(RADIUS, group, 0),
                column_spec(rows, group, 0),
                pl.BlockSpec((group, 1, WINDOW), lambda i, meta: (i, 0, 0)),
                *slot_specs(weight_slots, group),
            ],
            out_specs=column_spec(rows, group, 0),
            scratch_shapes=[pltpu.VMEM((group, HEAD_DIM, 3 * HEAD_DIM), BF16)],
        ),
        compiler_params=pltpu.CompilerParams(vmem_limit_bytes=VMEM_LIMIT),
        cost_estimate=pl.CostEstimate(
            flops=heads * 60_000_000, bytes_accessed=8 * rows * width, transcendentals=heads * 32768
        ),
        name="forward_attention",
    )(meta, before, own, after, x, offsets, *weight_slots)


def backward_kernel(slots, group, meta_ref, before_ref, own_ref, after_ref, cot_ref, offset_ref, *rest):
    slot_refs = rest[:slots]
    rest = rest[slots:]
    grad_ref, lower_ref, upper_ref, offset_grad_ref = rest[:4]
    part_refs = rest[4 : 4 + slots]
    weight_ref, part_ref = rest[4 + slots :]
    rows = own_ref.shape[0]
    blocks = rows // ROW_BLOCK
    scale = HEAD_DIM ** (-0.5)
    masks = [key_mask(meta_ref, b * ROW_BLOCK) for b in range(blocks)]
    for g in range(group):
        columns = slice(g * HEAD_DIM, (g + 1) * HEAD_DIM)
        weight = load_weight(meta_ref, slot_refs, weight_ref, g, slots)
        own = own_ref[:, columns]
        extended = jnp.concatenate([before_ref[:, columns], own, after_ref[:, columns]], axis=0)
        query = dot_nn(own, weight[:, :HEAD_DIM]).astype(BF16)
        key_value = dot_nn(extended, weight[:, HEAD_DIM:]).astype(BF16)
        key, value = key_value[:, :HEAD_DIM], key_value[:, HEAD_DIM:]
        bias = toeplitz(offset_ref[g])
        grad_query, grad_key, grad_value, score_sum = [], [], [], None
        for b in range(blocks):
            first = b * ROW_BLOCK
            window = slice(first, first + WINDOW)
            query_rows = query[first : first + ROW_BLOCK]
            cot_rows = cot_ref[first : first + ROW_BLOCK, columns]
            probs = block_probs(query_rows, key[window], bias + masks[b])
            grad_probs = dot_nt(cot_rows, value[window])
            delta = jnp.sum(probs * grad_probs, axis=-1, keepdims=True)
            grad_scores = probs * (grad_probs - delta)
            score_sum = grad_scores if score_sum is None else score_sum + grad_scores
            grad_packed = grad_scores.astype(BF16)
            grad_query.append(dot_nn(grad_packed, key[window]))
            grad_key.append(dot_tn(grad_packed, query_rows))
            grad_value.append(dot_tn(probs.astype(BF16), cot_rows))

        def joined(parts):
            pieces = []
            for u in range((rows + 2 * RADIUS) // ROW_BLOCK):
                total = None
                for b in range(blocks):
                    if 0 <= u - b < WINDOW // ROW_BLOCK:
                        piece = parts[b][(u - b) * ROW_BLOCK : (u - b + 1) * ROW_BLOCK]
                        total = piece if total is None else total + piece
                pieces.append(total)
            return jnp.concatenate(pieces, axis=0)

        dquery = (jnp.concatenate(grad_query, axis=0) * scale).astype(BF16)
        dkey = (joined(grad_key) * scale).astype(BF16)
        dvalue = joined(grad_value).astype(BF16)
        dkey_value = jnp.concatenate([dkey, dvalue], axis=1)
        grad_extended = dot_nt(dkey_value, weight[:, HEAD_DIM:])
        grad_ref[:, columns] = grad_extended[RADIUS : RADIUS + rows] + dot_nt(dquery, weight[:, :HEAD_DIM])
        lower_ref[:, columns] = grad_extended[:RADIUS].astype(BF16)
        upper_ref[:, columns] = grad_extended[RADIUS + rows :].astype(BF16)
        part_ref[g, :, :HEAD_DIM] = dot_tn(own, dquery)
        part_ref[g, :, HEAD_DIM:] = dot_tn(extended, dkey_value)
        depth = HEAD_DIM // slots
        for r in range(slots):
            if slots == 1:
                start = 0
            else:
                start = pl.multiple_of(lax.rem(meta_ref[0] + r, slots) * depth, depth)
            for j in range(3):
                part_refs[r][j, g] = part_ref[
                    g, pl.ds(start, depth), j * HEAD_DIM : (j + 1) * HEAD_DIM
                ].astype(part_refs[r].dtype)
        offset_grad_ref[g] = diagonal_sums(score_sum)


def backward_attention(meta, before, own, after, cotangent, offsets, weight_slots, group, first_head, heads):
    rows = own.shape[0]
    width = heads * HEAD_DIM
    slots = len(weight_slots)
    first = first_head // group
    slot_shape = weight_slots[0].shape
    part_types = [F32] + [BF16] * (slots - 1) if slots > 1 else [BF16]
    return pl.pallas_call(
        functools.partial(backward_kernel, slots, group),
        out_shape=(
            jax.ShapeDtypeStruct((rows, width), F32),
            jax.ShapeDtypeStruct((RADIUS, width), BF16),
            jax.ShapeDtypeStruct((RADIUS, width), BF16),
            jax.ShapeDtypeStruct((heads, 1, WINDOW), F32),
            *[jax.ShapeDtypeStruct(slot_shape, kind) for kind in part_types],
        ),
        grid_spec=pltpu.PrefetchScalarGridSpec(
            num_scalar_prefetch=1,
            grid=(heads // group,),
            in_specs=[
                column_spec(RADIUS, group, first),
                column_spec(rows, group, first),
                column_spec(RADIUS, group, first),
                column_spec(rows, group, first),
                pl.BlockSpec((group, 1, WINDOW), lambda i, meta: (i + first, 0, 0)),
                *slot_specs(weight_slots, group),
            ],
            out_specs=(
                column_spec(rows, group, 0),
                column_spec(RADIUS, group, 0),
                column_spec(RADIUS, group, 0),
                pl.BlockSpec((group, 1, WINDOW), lambda i, meta: (i, 0, 0)),
                *slot_specs(weight_slots, group),
            ),
            scratch_shapes=[
                pltpu.VMEM((group, HEAD_DIM, 3 * HEAD_DIM), BF16),
                pltpu.VMEM((group, HEAD_DIM, 3 * HEAD_DIM), F32),
            ],
        ),
        compiler_params=pltpu.CompilerParams(vmem_limit_bytes=VMEM_LIMIT),
        cost_estimate=pl.CostEstimate(
            flops=heads * 150_000_000, bytes_accessed=12 * rows * width, transcendentals=heads * 32768
        ),
        name="backward_attention",
    )(meta, before, own, after, cotangent, offsets, *weight_slots)


def finish_kernel(grad_ref, low_ref, high_ref, x_ref, inverse_ref, gain_ref, cot_ref, out_ref, gain_grad_ref):
    rows = x_ref.shape[0]
    grad = grad_ref[...]
    edge = jnp.zeros((rows - RADIUS, grad.shape[1]), F32)
    grad = grad + jnp.concatenate([low_ref[...].astype(F32), edge], axis=0)
    grad = grad + jnp.concatenate([edge, high_ref[...].astype(F32)], axis=0)
    x = x_ref[...].astype(F32)
    inverse = inverse_ref[:, :1]
    gain_grad_ref[...] = jnp.sum(grad * x * inverse, axis=0, keepdims=True)
    scaled = grad * gain_ref[...]
    mean = jnp.mean(scaled * x, axis=-1, keepdims=True)
    result = inverse * scaled - x * (inverse * inverse * inverse * mean)
    out_ref[...] = (cot_ref[...].astype(F32) + result).astype(BF16)


def finish(grad, low, high, x, inverse, gain, cotangent):
    rows, width = x.shape
    return pl.pallas_call(
        finish_kernel,
        out_shape=(
            jax.ShapeDtypeStruct((rows, width), BF16),
            jax.ShapeDtypeStruct((1, width), F32),
        ),
        compiler_params=pltpu.CompilerParams(vmem_limit_bytes=VMEM_LIMIT),
        cost_estimate=pl.CostEstimate(
            flops=16 * rows * width, bytes_accessed=14 * rows * width, transcendentals=0
        ),
        name="finish",
    )(grad, low, high, x, inverse, gain, cotangent)


def column_of(row, rows):
    return jnp.transpose(jnp.broadcast_to(row, (128, rows)))


def split_rows(inverse, pad_rows, width):
    high = inverse.astype(BF16)
    rest = inverse - high.astype(F32)
    middle = rest.astype(BF16)
    low = (rest - middle.astype(F32)).astype(BF16)
    wide = [jnp.transpose(jnp.broadcast_to(v.astype(F32), (v.shape[0], 128)))[:1] for v in (high, middle, low)]
    row = jnp.concatenate(wide + [jnp.zeros((pad_rows - 3, wide[0].shape[1]), F32)], axis=0)
    return row.astype(BF16)


def row_inverse(x):
    x = x.astype(F32)
    return lax.rsqrt(jnp.mean(x * x, axis=-1, keepdims=True) + eps_norm)


def pack_stash_kernel(parts, meta_ref, x_ref, gain_ref, weight_ref, inverse_ref, *refs):
    out_refs, normed_ref = refs[:parts], refs[parts]
    rows, width = x_ref.shape
    depth = weight_ref.shape[2]
    wide = width // parts
    heads = wide // HEAD_DIM
    inverse = row_inverse(x_ref[...])
    inverse_ref[...] = jnp.broadcast_to(inverse, inverse_ref.shape)
    normed_ref[...] = (x_ref[...].astype(F32) * inverse * gain_ref[...]).astype(BF16)
    for r, out_ref in enumerate(out_refs):
        target = lax.rem(meta_ref[0] + r, parts)
        out_ref[:rows] = normed_ref[:, pl.ds(pl.multiple_of(target * wide, 128), wide)]
        for j in range(3):
            for h in range(heads):
                out_ref[rows + j * depth : rows + (j + 1) * depth, h * HEAD_DIM : (h + 1) * HEAD_DIM] = weight_ref[
                    j, target * heads + h
                ]


def pack_rows_kernel(parts, with_inverse, meta_ref, edge_ref, inner_ref, *out_refs):
    rows, width = inner_ref.shape
    wide = width // parts
    edge = 1 if with_inverse else 2
    refs = out_refs[:parts]
    for r, out_ref in enumerate(refs):
        target = lax.rem(meta_ref[0] + r, parts)
        start = pl.multiple_of(target * wide, 128)

        @pl.when(meta_ref[edge] == 1)
        def use_edge():
            out_ref[:rows] = edge_ref[:, pl.ds(start, wide)]

        @pl.when(meta_ref[edge] == 0)
        def use_inner():
            out_ref[:rows] = inner_ref[:, pl.ds(start, wide)]

    def finish_with(source_ref):
        if with_inverse:
            tail = split_rows(row_inverse(source_ref[...]), 16, wide)
            for out_ref in refs:
                out_ref[rows:] = jnp.zeros((16, wide), BF16)
                out_ref[rows:, :rows] = tail
        else:
            out_refs[parts][...] = source_ref[...]

    @pl.when(meta_ref[edge] == 1)
    def finish_edge():
        finish_with(edge_ref)

    @pl.when(meta_ref[edge] == 0)
    def finish_inner():
        finish_with(inner_ref)


SMEM_SPEC = pl.BlockSpec(memory_space=pltpu.SMEM)
VMEM_SPEC = pl.BlockSpec(memory_space=pltpu.VMEM)


def pack_stash(meta, x, gain, weight, parts):
    rows, width = x.shape
    depth = weight.shape[2]
    shape = (rows + 3 * depth, width // parts)
    return pl.pallas_call(
        functools.partial(pack_stash_kernel, parts),
        out_shape=(
            jax.ShapeDtypeStruct((rows, 128), F32),
            *[jax.ShapeDtypeStruct(shape, BF16) for r in range(parts)],
        ),
        in_specs=[SMEM_SPEC, VMEM_SPEC, VMEM_SPEC, VMEM_SPEC],
        out_specs=(VMEM_SPEC,) * (parts + 1),
        scratch_shapes=[pltpu.VMEM((rows, width), BF16)],
        compiler_params=pltpu.CompilerParams(vmem_limit_bytes=VMEM_LIMIT),
        cost_estimate=pl.CostEstimate(flops=4 * rows * width, bytes_accessed=6 * rows * width, transcendentals=0),
        name="pack_stash",
    )(meta, x, gain, weight)


def pack_rows(meta, edge, inner, parts, with_inverse):
    rows, width = inner.shape
    shape = (rows + (16 if with_inverse else 0), width // parts)
    extra = () if with_inverse else (jax.ShapeDtypeStruct((rows, width), BF16),)
    return pl.pallas_call(
        functools.partial(pack_rows_kernel, parts, with_inverse),
        out_shape=(*[jax.ShapeDtypeStruct(shape, BF16) for r in range(parts)], *extra),
        in_specs=[SMEM_SPEC, VMEM_SPEC, VMEM_SPEC],
        out_specs=(VMEM_SPEC,) * (parts + len(extra)),
        compiler_params=pltpu.CompilerParams(vmem_limit_bytes=VMEM_LIMIT),
        cost_estimate=pl.CostEstimate(flops=4 * rows * width, bytes_accessed=6 * rows * width, transcendentals=0),
        name="pack_inbound" if with_inverse else "pack_cotangent",
    )(meta, edge, inner)


def gather_rows(meta_ref, refs, rows, x_ref):
    parts = len(refs)
    for r, ref in enumerate(refs):
        source = lax.rem(meta_ref[0] + parts - r, parts)
        x_ref[pl.ds(pl.multiple_of(source * rows, rows), rows)] = ref[:rows]


def gather_weight(meta_ref, refs, rows, weight_ref):
    parts = len(refs)
    depth = HEAD_DIM // parts
    for r, ref in enumerate(refs):
        source = lax.rem(meta_ref[0] + parts - r, parts)
        depth_at = pl.ds(pl.multiple_of(source * depth, depth), depth)
        for j in range(3):
            weight_ref[depth_at, j * HEAD_DIM : (j + 1) * HEAD_DIM] = ref[
                rows + j * depth : rows + (j + 1) * depth
            ]


def gather_inverse(meta_ref, refs, rows, inverse_ref):
    parts = len(refs)

    @pl.when(pl.program_id(0) == 0)
    def spread_inverse():
        for r, ref in enumerate(refs):
            source = lax.rem(meta_ref[0] + parts - r, parts)
            tail = ref[rows : rows + 16].astype(F32)
            inverse_ref[pl.ds(pl.multiple_of(source * rows, rows), rows)] = column_of(
                tail[:1] + tail[1:2] + tail[2:3], rows
            )


def block_mask(first_query, tokens):
    key = lax.broadcasted_iota(jnp.int32, (1, WINDOW), 1) + (first_query - RADIUS)
    return jnp.where((key >= 0) & (key < tokens), 0.0, masked_score).astype(F32)


def edge_bias(bias, first, tokens):
    if first < RADIUS or first + ROW_BLOCK + RADIUS > tokens:
        return bias + block_mask(first, tokens)
    return bias


def padded(rows):
    edge = jnp.zeros((RADIUS, rows.shape[1]), rows.dtype)
    return jnp.concatenate([edge, rows, edge], axis=0)


def heads_backward_kernel(parts, rows, meta_ref, *refs):
    a_refs, c_refs = refs[:parts], refs[parts : 2 * parts]
    gain_ref, offset_ref, onehot_ref = refs[2 * parts : 2 * parts + 3]
    out_refs = refs[2 * parts + 3 : 3 * parts + 3]
    gain_grad_ref, x_ref, weight_ref, cot_ref, grad_ref, part_ref, bias_ref = refs[3 * parts + 3 :]
    tokens = rows * parts
    depth = HEAD_DIM // parts
    scale = HEAD_DIM ** (-0.5)
    gather_rows(meta_ref, a_refs, rows, x_ref)
    gather_weight(meta_ref, a_refs, rows, weight_ref)
    gather_rows(meta_ref, c_refs, rows, cot_ref)
    weight = weight_ref[...]
    normed = x_ref[...]
    query = dot_nn(normed, weight[:, :HEAD_DIM]).astype(BF16)
    key = padded(dot_nn(normed, weight[:, HEAD_DIM : 2 * HEAD_DIM]).astype(BF16))
    value = padded(dot_nn(normed, weight[:, 2 * HEAD_DIM :]).astype(BF16))
    bias = toeplitz(offset_ref[0])
    blocks = tokens // ROW_BLOCK
    grad_query, grad_key, grad_value, score_sum = [], [], [], None
    for b in range(blocks):
        first = b * ROW_BLOCK
        window = slice(first, first + WINDOW)
        query_rows = query[first : first + ROW_BLOCK]
        cot_rows = cot_ref[first : first + ROW_BLOCK]
        probs = block_probs(query_rows, key[window], edge_bias(bias, first, tokens))
        grad_probs = dot_nt(cot_rows, value[window])
        delta = jnp.sum(probs * grad_probs, axis=-1, keepdims=True)
        grad_scores = probs * (grad_probs - delta)
        score_sum = grad_scores if score_sum is None else score_sum + grad_scores
        grad_packed = grad_scores.astype(BF16)
        grad_query.append(dot_nn(grad_packed, key[window]))
        grad_key.append(dot_tn(grad_packed, query_rows))
        grad_value.append(dot_tn(probs.astype(BF16), cot_rows))

    def joined(pieces):
        units = []
        for u in range((tokens + 2 * RADIUS) // ROW_BLOCK):
            total = None
            for b in range(blocks):
                if 0 <= u - b < WINDOW // ROW_BLOCK:
                    piece = pieces[b][(u - b) * ROW_BLOCK : (u - b + 1) * ROW_BLOCK]
                    total = piece if total is None else total + piece
            units.append(total)
        return jnp.concatenate(units, axis=0)[RADIUS : RADIUS + tokens]

    dqkv = jnp.concatenate(
        [
            (jnp.concatenate(grad_query, axis=0) * scale).astype(BF16),
            (joined(grad_key) * scale).astype(BF16),
            joined(grad_value).astype(BF16),
        ],
        axis=1,
    )
    grad_normed = dot_nt(dqkv, weight)
    gain_grad_ref[...] = jnp.sum(grad_normed * normed.astype(F32), axis=0, keepdims=True) / gain_ref[...]
    grad_ref[...] = grad_normed
    part_ref[...] = dot_tn(normed, dqkv)
    bias_grad = jnp.sum(onehot_ref[...] * diagonal_sums(score_sum), axis=1, keepdims=True)
    bias_ref[...] = jnp.broadcast_to(bias_grad, bias_ref.shape)
    buckets = bias_ref.shape[0] // parts
    for r, out_ref in enumerate(out_refs):
        source = lax.rem(meta_ref[0] + parts - r, parts)
        out_ref[:rows] = grad_ref[pl.ds(pl.multiple_of(source * rows, rows), rows)].astype(BF16)
        for j in range(3):
            out_ref[rows + j * depth : rows + (j + 1) * depth] = part_ref[
                pl.ds(pl.multiple_of(source * depth, depth), depth), j * HEAD_DIM : (j + 1) * HEAD_DIM
            ].astype(BF16)
        share = bias_ref[pl.ds(pl.multiple_of(source * buckets, buckets), buckets)]
        out_ref[rows + 3 * depth :] = jnp.concatenate(
            [share, jnp.zeros((16 - buckets, HEAD_DIM), F32)], axis=0
        ).astype(BF16)


def head_column(rows):
    return pl.BlockSpec((rows, HEAD_DIM), lambda i, meta: (0, i))


def heads_backward(meta, a_slots, c_slots, gain, offsets, onehot, heads):
    parts = len(a_slots)
    rows = c_slots[0].shape[0]
    tokens = rows * parts
    buckets = onehot.shape[0]
    packed = a_slots[0].shape[0]
    made = packed + 16
    width = heads * HEAD_DIM
    return pl.pallas_call(
        functools.partial(heads_backward_kernel, parts, rows),
        out_shape=(
            *[jax.ShapeDtypeStruct((made, width), BF16) for r in range(parts)],
            jax.ShapeDtypeStruct((1, width), F32),
        ),
        grid_spec=pltpu.PrefetchScalarGridSpec(
            num_scalar_prefetch=1,
            grid=(heads,),
            in_specs=[
                *[head_column(packed)] * parts,
                *[head_column(rows)] * parts,
                pl.BlockSpec((1, HEAD_DIM), lambda i, meta: (0, meta[0] * heads + i)),
                pl.BlockSpec((1, 1, WINDOW), lambda i, meta: (meta[0] * heads + i, 0, 0)),
                pl.BlockSpec((buckets, WINDOW), lambda i, meta: (0, 0)),
            ],
            out_specs=(*[head_column(made)] * parts, head_column(1)),
            scratch_shapes=[
                pltpu.VMEM((tokens, HEAD_DIM), BF16),
                pltpu.VMEM((HEAD_DIM, 3 * HEAD_DIM), BF16),
                pltpu.VMEM((tokens, HEAD_DIM), BF16),
                pltpu.VMEM((tokens, HEAD_DIM), F32),
                pltpu.VMEM((HEAD_DIM, 3 * HEAD_DIM), F32),
                pltpu.VMEM((buckets, HEAD_DIM), F32),
            ],
        ),
        compiler_params=pltpu.CompilerParams(vmem_limit_bytes=VMEM_LIMIT),
        cost_estimate=pl.CostEstimate(
            flops=heads * tokens * 400_000, bytes_accessed=tokens * width, transcendentals=0
        ),
        name="heads_backward",
    )(meta, *a_slots, *c_slots, gain, offsets, onehot)


def heads_forward_kernel(parts, rows, meta_ref, *refs):
    a_refs, i_refs = refs[:parts], refs[parts : 2 * parts]
    gain_ref, offset_ref = refs[2 * parts : 2 * parts + 2]
    out_refs = refs[2 * parts + 2 : 3 * parts + 2]
    sums_ref, inverse_ref, x_ref, weight_ref, made_ref, square_ref = refs[3 * parts + 2 :]
    tokens = rows * parts
    gather_rows(meta_ref, i_refs, rows, x_ref)
    gather_weight(meta_ref, a_refs, rows, weight_ref)
    gather_inverse(meta_ref, i_refs, rows, inverse_ref)
    weight = weight_ref[...]
    normed = (x_ref[...].astype(F32) * inverse_ref[...] * gain_ref[...]).astype(BF16)
    query = dot_nn(normed, weight[:, :HEAD_DIM]).astype(BF16)
    key = padded(dot_nn(normed, weight[:, HEAD_DIM : 2 * HEAD_DIM]).astype(BF16))
    value = padded(dot_nn(normed, weight[:, 2 * HEAD_DIM :]).astype(BF16))
    bias = toeplitz(offset_ref[0])
    for b in range(tokens // ROW_BLOCK):
        first = b * ROW_BLOCK
        window = slice(first, first + WINDOW)
        probs = block_probs(query[first : first + ROW_BLOCK], key[window], edge_bias(bias, first, tokens))
        attended = dot_nn(probs.astype(BF16), value[window])
        made_ref[first : first + ROW_BLOCK] = (
            x_ref[first : first + ROW_BLOCK].astype(F32) + attended
        ).astype(BF16)
    made = made_ref[...].astype(F32)
    squares = made * made

    @pl.when(pl.program_id(0) == 0)
    def first_head():
        square_ref[...] = squares

    @pl.when(pl.program_id(0) > 0)
    def later_head():
        square_ref[...] += squares

    @pl.when(pl.program_id(0) == pl.num_programs(0) - 1)
    def last_head():
        total = jnp.sum(jnp.transpose(square_ref[...]), axis=0, keepdims=True)
        sums_ref[...] = jnp.broadcast_to(total, sums_ref.shape)

    for r, out_ref in enumerate(out_refs):
        source = lax.rem(meta_ref[0] + parts - r, parts)
        out_ref[...] = made_ref[pl.ds(pl.multiple_of(source * rows, rows), rows)]


def heads_forward(meta, a_slots, i_slots, gain, offsets, heads, rows):
    parts = len(a_slots)
    tokens = rows * parts
    packed = a_slots[0].shape[0]
    width = heads * HEAD_DIM
    return pl.pallas_call(
        functools.partial(heads_forward_kernel, parts, rows),
        out_shape=(
            *[jax.ShapeDtypeStruct((rows, width), BF16) for r in range(parts)],
            jax.ShapeDtypeStruct((8, tokens), F32),
        ),
        grid_spec=pltpu.PrefetchScalarGridSpec(
            num_scalar_prefetch=1,
            grid=(heads,),
            in_specs=[
                *[head_column(packed)] * parts,
                *[head_column(i_slots[0].shape[0])] * parts,
                pl.BlockSpec((1, HEAD_DIM), lambda i, meta: (0, meta[0] * heads + i)),
                pl.BlockSpec((1, 1, WINDOW), lambda i, meta: (meta[0] * heads + i, 0, 0)),
            ],
            out_specs=(
                *[head_column(rows)] * parts,
                pl.BlockSpec((8, tokens), lambda i, meta: (0, 0)),
            ),
            scratch_shapes=[
                pltpu.VMEM((tokens, HEAD_DIM), F32),
                pltpu.VMEM((tokens, HEAD_DIM), BF16),
                pltpu.VMEM((HEAD_DIM, 3 * HEAD_DIM), BF16),
                pltpu.VMEM((tokens, HEAD_DIM), BF16),
                pltpu.VMEM((tokens, HEAD_DIM), F32),
            ],
        ),
        compiler_params=pltpu.CompilerParams(vmem_limit_bytes=VMEM_LIMIT),
        cost_estimate=pl.CostEstimate(
            flops=heads * tokens, bytes_accessed=tokens, transcendentals=0
        ),
        name="heads_forward",
    )(meta, *a_slots, *i_slots, gain, offsets)


def memory_kernel(parts, width, meta_ref, *refs):
    out_refs, sum_refs = refs[:parts], refs[parts : 2 * parts]
    gain_ref, memory_ref = refs[2 * parts :]
    rows = out_refs[0].shape[0]
    wide = memory_ref.shape[1]
    total = sum_refs[0][:1]
    for sum_ref in sum_refs[1:]:
        total = total + sum_ref[:1]
    inverse = lax.rsqrt(total / width + eps_norm)
    gain = gain_ref[:, pl.ds(pl.multiple_of(meta_ref[0] * wide, 128), wide)]
    spread_inverse = jnp.transpose(jnp.broadcast_to(inverse, (128, inverse.shape[1])))
    for r, out_ref in enumerate(out_refs):
        source = lax.rem(meta_ref[0] + parts - r, parts)
        memory_ref[pl.ds(pl.multiple_of(source * rows, rows), rows)] = out_ref[...]
    made = memory_ref[...].astype(F32)
    memory_ref[...] = (made * spread_inverse[:, :1] * gain).astype(BF16)


def memory_rows(meta, outs, sums, gain, width):
    parts = len(outs)
    rows, wide = outs[0].shape
    return pl.pallas_call(
        functools.partial(memory_kernel, parts, width),
        out_shape=jax.ShapeDtypeStruct((rows * parts, wide), BF16),
        in_specs=[SMEM_SPEC] + [VMEM_SPEC] * (2 * parts + 1),
        out_specs=VMEM_SPEC,
        compiler_params=pltpu.CompilerParams(vmem_limit_bytes=VMEM_LIMIT),
        cost_estimate=pl.CostEstimate(flops=4 * rows * width, bytes_accessed=4 * rows * width, transcendentals=0),
        name="memory_rows",
    )(meta, *outs, *sums, gain)


def place_kernel(parts, meta_ref, *refs):
    out_ref = refs[parts]
    wide = refs[0].shape[1]
    for r in range(parts):
        source = lax.rem(meta_ref[0] + r, parts)
        out_ref[:, pl.ds(pl.multiple_of(source * wide, 128), wide)] = refs[r][...]


def place_columns(meta, slots):
    parts = len(slots)
    rows, wide = slots[0].shape
    return pl.pallas_call(
        functools.partial(place_kernel, parts),
        out_shape=jax.ShapeDtypeStruct((rows, wide * parts), BF16),
        in_specs=[SMEM_SPEC] + [VMEM_SPEC] * parts,
        out_specs=VMEM_SPEC,
        compiler_params=pltpu.CompilerParams(vmem_limit_bytes=VMEM_LIMIT),
        cost_estimate=pl.CostEstimate(flops=0, bytes_accessed=4 * rows * wide * parts, transcendentals=0),
        name="place_columns",
    )(meta, *slots)


def heads_finish_kernel(parts, meta_ref, *refs):
    g_refs = refs[:parts]
    x_ref, inverse_ref, gain_ref, cot_ref, out_ref, weight_ref, bias_ref, scaled_ref = refs[parts:]
    rows, width = x_ref.shape
    wide = width // parts
    heads = wide // HEAD_DIM
    depth = HEAD_DIM // parts
    buckets = bias_ref.shape[1]
    for r in range(parts):
        source = lax.rem(meta_ref[0] + r, parts)
        columns = pl.ds(pl.multiple_of(source * wide, 128), wide)
        scaled_ref[:, columns] = g_refs[r][:rows].astype(F32) * gain_ref[:, columns]
        for h in range(heads):
            lanes = slice(h * HEAD_DIM, (h + 1) * HEAD_DIM)
            for j in range(3):
                weight_ref[j, source * heads + h] = g_refs[r][
                    rows + j * depth : rows + (j + 1) * depth, lanes
                ].astype(F32)
            bias_ref[source * heads + h] = g_refs[r][rows + 3 * depth :, lanes].astype(F32)[:buckets]
    x = x_ref[...].astype(F32)
    scaled = scaled_ref[...]
    inverse = inverse_ref[:, :1]
    mean = jnp.mean(scaled * x, axis=-1, keepdims=True)
    result = inverse * scaled - x * (inverse * inverse * inverse * mean)
    out_ref[...] = (cot_ref[...].astype(F32) + result).astype(BF16)


def heads_finish(meta, g_slots, x, inverse, gain, cotangent, buckets):
    parts = len(g_slots)
    rows, width = x.shape
    heads = width // HEAD_DIM
    return pl.pallas_call(
        functools.partial(heads_finish_kernel, parts),
        out_shape=(
            jax.ShapeDtypeStruct((rows, width), BF16),
            jax.ShapeDtypeStruct((3, heads, HEAD_DIM // parts, HEAD_DIM), F32),
            jax.ShapeDtypeStruct((heads, buckets // parts, HEAD_DIM), F32),
        ),
        in_specs=[SMEM_SPEC] + [VMEM_SPEC] * (parts + 4),
        out_specs=(VMEM_SPEC,) * 3,
        scratch_shapes=[pltpu.VMEM((rows, width), F32)],
        compiler_params=pltpu.CompilerParams(vmem_limit_bytes=VMEM_LIMIT),
        cost_estimate=pl.CostEstimate(flops=12 * rows * width, bytes_accessed=14 * rows * width, transcendentals=0),
        name="heads_finish",
    )(meta, *g_slots, x, inverse, gain, cotangent)


def offset_table(rel_bias):
    onehot = jnp.asarray(bucket_onehot(rel_bias.shape[0]))
    by_offset = jnp.dot(onehot, rel_bias, precision=lax.Precision.HIGHEST).T
    inside = jnp.arange(WINDOW, dtype=jnp.int32) <= 2 * RADIUS
    return jnp.where(inside[None, :], by_offset, masked_score)[:, None, :]


def shifted(value, axis, steps):
    count = lax.axis_size(axis)
    first, last = (max(0, -steps), min(count, count - steps))
    return lax.ppermute(value, axis, [(source, source + steps) for source in range(first, last)])


def heads_body(
    embedded, carried, stash, returned, loss_grad, qkv_weight, rel_bias, norm_gain, final_gain
):
    section = lax.axis_index("section")
    sections = lax.axis_size("section")
    parts = lax.axis_size("seq")
    rows, width = embedded.shape
    heads = width // HEAD_DIM // parts
    buckets = rel_bias.shape[1]
    meta = jnp.stack(
        [lax.axis_index("seq"), section == 0, section == sections - 1]
    ).astype(jnp.int32)

    def sent(value, r):
        return lax.ppermute(value, "seq", [(i, (i + r) % parts) for i in range(parts)])

    def exchanged(sends, direction):
        return [sends[0]] + [sent(sends[r], direction * r) for r in range(1, parts)]

    came_back = shifted(returned[0], "section", -1)
    arrived = shifted(carried[0], "section", 1)
    inverse_b, *a_sends = pack_stash(meta, stash[0], norm_gain, qkv_weight[0], parts)
    a_slots = exchanged(a_sends, 1)
    *c_sends, cotangent = pack_rows(meta, loss_grad, came_back, parts, False)
    c_slots = exchanged(c_sends, 1)
    i_slots = exchanged(pack_rows(meta, embedded, arrived, parts, True), 1)

    offsets = offset_table(rel_bias[0])
    onehot = jnp.asarray(bucket_onehot(buckets).T)
    *g_sends, gain_grad = heads_backward(meta, a_slots, c_slots, norm_gain, offsets, onehot, heads)
    g_sends, i_slots = lax.optimization_barrier((g_sends, i_slots))
    g_slots = exchanged(g_sends, -1)

    *o_sends, sums = heads_forward(meta, a_slots, i_slots, norm_gain, offsets, heads, rows)
    all_sums = [sums] + [sent(sums, r) for r in range(1, parts)]
    o_slots = exchanged(o_sends, -1)
    g_slots, memory_gain = lax.optimization_barrier((g_slots, final_gain[None]))
    made = memory_rows(meta, o_sends, all_sums, memory_gain, width)
    share = rows * parts // sections
    memory = jnp.where(section == sections - 1, made[(sections - 1) * share :], 0)
    for s in range(sections - 1):
        memory = memory + lax.ppermute(
            made[s * share : (s + 1) * share], "section", [(sections - 1, s)]
        )

    input_grad, weight_grad, bias_wide = heads_finish(
        meta, g_slots, stash[0], inverse_b, norm_gain, cotangent, buckets
    )
    bias_grad = bias_wide[:, :, 0].T
    output = place_columns(meta, o_slots)
    return (
        output[None],
        input_grad[None],
        weight_grad[None],
        bias_grad[None],
        gain_grad,
        memory.astype(BF16),
    )


def tokens_body(
    embedded, carried, stash, returned, loss_grad, qkv_weight, rel_bias, norm_gain, final_gain
):
    section_index = lax.axis_index("section")
    section_count = lax.axis_size("section")
    seq_index = lax.axis_index("seq")
    seq_count = lax.axis_size("seq")
    rows, width = embedded.shape
    heads = width // HEAD_DIM
    tokens = rows * seq_count
    shard = qkv_weight[0]
    up = [(i, i + 1) for i in range(seq_count - 1)]
    down = [(j, i) for i, j in up]
    group = 4 if heads % 4 == 0 else 1

    own_b, inverse_b = norm_rows(stash[0], norm_gain)
    before_b = lax.ppermute(own_b[rows - RADIUS :], "seq", up)
    after_b = lax.ppermute(own_b[:RADIUS], "seq", down)
    slots = [lax.all_gather(shard, "seq", axis=2, tiled=True)]

    section_up = [(i, (i + 1) % section_count) for i in range(section_count)]
    section_down = [(j, i) for i, j in section_up]
    inbound = lax.ppermute(
        jnp.where(section_index == section_count - 1, embedded, carried[0]), "section", section_up
    )
    cotangent = lax.ppermute(
        jnp.where(section_index == 0, loss_grad, returned[0]), "section", section_down
    )

    onehot = jnp.asarray(bucket_onehot(rel_bias.shape[1]))
    offsets = offset_table(rel_bias[0])
    first_key = RADIUS - seq_index * rows
    meta = jnp.stack([seq_index, first_key, first_key + tokens]).astype(jnp.int32)

    own_a, unused = norm_rows(inbound, norm_gain)
    before_a = lax.ppermute(own_a[rows - RADIUS :], "seq", up)
    after_a = lax.ppermute(own_a[:RADIUS], "seq", down)

    grad_own, lower, upper, offset_grad, *parts = backward_attention(
        meta, before_b, own_b, after_b, cotangent, offsets, slots, group, 0, heads
    )
    from_before = lax.ppermute(upper, "seq", up)
    from_after = lax.ppermute(lower, "seq", down)
    weight_sum = lax.psum_scatter(parts[0], "seq", scatter_dimension=2, tiled=True).astype(F32)

    output = forward_attention(meta, before_a, own_a, after_a, inbound, offsets, slots, group)
    final_normed, unused = norm_rows(output, final_gain[None])
    relaid = lax.all_to_all(final_normed, "seq", split_axis=1, concat_axis=0, tiled=True)
    kept = jnp.where(section_index == section_count - 1, relaid, jnp.zeros_like(relaid))
    memory = lax.psum_scatter(kept, "section", scatter_dimension=0, tiled=True)

    input_grad, gain_part = finish(
        grad_own, from_before, from_after, stash[0], inverse_b, norm_gain, cotangent
    )
    bias_part = jnp.dot(
        offset_grad[:, 0, :], onehot, precision=lax.Precision.HIGHEST
    ).T
    bias_sum = lax.psum_scatter(
        bias_part.astype(BF16), "seq", scatter_dimension=0, tiled=True
    ).astype(F32)
    gain_sum = lax.psum_scatter(
        gain_part.astype(BF16), "seq", scatter_dimension=1, tiled=True
    ).astype(F32)
    return (output[None], input_grad[None], weight_sum[None], bias_sum[None], gain_sum, memory)


def choose_body(embedded, carried, stash, returned, loss_grad, qkv_weight, rel_bias, norm_gain, final_gain):
    parts = lax.axis_size("seq")
    rows, width = embedded.shape
    even = width % (HEAD_DIM * parts) == 0 and HEAD_DIM % (32 * parts) == 0 and rows == 128
    even = even and rel_bias.shape[1] == 8 * parts and rows * parts % (16 * lax.axis_size("section")) == 0
    chosen = heads_body if even else tokens_body
    return chosen(
        embedded, carried, stash, returned, loss_grad, qkv_weight, rel_bias, norm_gain, final_gain
    )


def solution(mesh):
    in_specs = (
        P("seq", None),
        P("section", "seq", None),
        P("section", "seq", None),
        P("section", "seq", None),
        P("seq", None),
        P("section", None, None, "seq", None),
        P("section", None, None),
        P("section", None),
        P(),
    )
    out_specs = (
        P("section", "seq", None),
        P("section", "seq", None),
        P("section", None, None, "seq", None),
        P("section", "seq", None),
        P("section", "seq"),
        P("section", "seq"),
    )
    return jax.shard_map(choose_body, mesh=mesh, in_specs=in_specs, out_specs=out_specs, check_vma=False)
```

```python
import functools

import jax
import jax.numpy as jnp
import numpy as np
from jax import lax
from jax.experimental import pallas as pl
from jax.experimental.pallas import tpu as pltpu
from jax.sharding import PartitionSpec as P

RADIUS = 96
HEAD_DIM = 128
ROW_BLOCK = 64
WINDOW = ROW_BLOCK + 2 * RADIUS
eps_norm = 1e-06
bucket_edges = (1, 2, 3, 4, 5, 6, 7, 8, 11, 16, 22, 32, 45, 64, 90)
masked_score = -1e30
F32 = jnp.float32
BF16 = jnp.bfloat16
VMEM_LIMIT = 48 * 1024 * 1024


def bucket_onehot(bucket_count):
    offsets = np.arange(WINDOW) - RADIUS
    magnitude = np.abs(offsets)
    counted = np.zeros(offsets.shape, np.int32)
    for threshold in bucket_edges:
        counted = counted + (magnitude >= threshold)
    counted = counted + 16 * (offsets > 0)
    onehot = (counted[:, None] == np.arange(bucket_count)[None, :]) & (magnitude <= RADIUS)[:, None]
    return onehot.astype(np.float32)


def dot_nn(a, b):
    return lax.dot_general(a, b, (((1,), (0,)), ((), ())), preferred_element_type=F32)


def dot_nt(a, b):
    return lax.dot_general(a, b, (((1,), (1,)), ((), ())), preferred_element_type=F32)


def dot_tn(a, b):
    return lax.dot_general(a, b, (((0,), (0,)), ((), ())), preferred_element_type=F32)


def norm_kernel(x_ref, gain_ref, normed_ref, inverse_ref):
    x = x_ref[...].astype(F32)
    inverse = lax.rsqrt(jnp.mean(x * x, axis=-1, keepdims=True) + eps_norm)
    normed_ref[...] = (x * inverse * gain_ref[...]).astype(BF16)
    inverse_ref[...] = jnp.broadcast_to(inverse, inverse_ref.shape)


def norm_rows(x, gain):
    rows, width = x.shape
    return pl.pallas_call(
        norm_kernel,
        out_shape=(
            jax.ShapeDtypeStruct((rows, width), BF16),
            jax.ShapeDtypeStruct((rows, 128), F32),
        ),
        compiler_params=pltpu.CompilerParams(vmem_limit_bytes=VMEM_LIMIT),
        cost_estimate=pl.CostEstimate(
            flops=6 * rows * width, bytes_accessed=4 * rows * width, transcendentals=rows
        ),
        name="norm_rows",
    )(x, gain)


def load_weight(meta_ref, slot_refs, weight_ref, head, slots):
    depth = HEAD_DIM // slots
    for r, slot_ref in enumerate(slot_refs):
        if slots == 1:
            start = 0
        else:
            start = pl.multiple_of(lax.rem(meta_ref[0] + r, slots) * depth, depth)
        for j in range(3):
            weight_ref[head, pl.ds(start, depth), j * HEAD_DIM : (j + 1) * HEAD_DIM] = slot_ref[j, head]
    return weight_ref[head]


def key_mask(meta_ref, first_key):
    key = lax.broadcasted_iota(jnp.int32, (1, WINDOW), 1) + first_key
    inside = (key >= meta_ref[1]) & (key < meta_ref[2])
    return jnp.where(inside, 0.0, masked_score).astype(F32)


def toeplitz(row):
    return pltpu.roll(
        jnp.broadcast_to(row, (ROW_BLOCK, WINDOW)), 0, 1, stride=1, stride_axis=0
    )


def diagonal_sums(values):
    total = values[:8]
    for a in range(1, ROW_BLOCK // 8):
        total = total + pltpu.roll(values[8 * a : 8 * a + 8], WINDOW - 8 * a, 1)
    row = lax.broadcasted_iota(jnp.int32, total.shape, 0)
    for bit in (1, 2, 4):
        total = jnp.where((row & bit) != 0, pltpu.roll(total, WINDOW - bit, 1), total)
    return jnp.sum(total, axis=0, keepdims=True)


def block_probs(query_rows, key_rows, bias):
    scores = dot_nt(query_rows, key_rows) * (HEAD_DIM ** (-0.5)) + bias
    weights = jnp.exp(scores - jnp.max(scores, axis=-1, keepdims=True))
    return weights * (1.0 / jnp.sum(weights, axis=-1, keepdims=True))


def forward_kernel(slots, group, meta_ref, before_ref, own_ref, after_ref, x_ref, offset_ref, *rest):
    slot_refs = rest[:slots]
    out_ref, weight_ref = rest[slots:]
    rows = own_ref.shape[0]
    blocks = rows // ROW_BLOCK
    masks = [key_mask(meta_ref, b * ROW_BLOCK) for b in range(blocks)]
    for g in range(group):
        columns = slice(g * HEAD_DIM, (g + 1) * HEAD_DIM)
        weight = load_weight(meta_ref, slot_refs, weight_ref, g, slots)
        own = own_ref[:, columns]
        extended = jnp.concatenate([before_ref[:, columns], own, after_ref[:, columns]], axis=0)
        query = dot_nn(own, weight[:, :HEAD_DIM]).astype(BF16)
        key_value = dot_nn(extended, weight[:, HEAD_DIM:]).astype(BF16)
        key, value = key_value[:, :HEAD_DIM], key_value[:, HEAD_DIM:]
        bias = toeplitz(offset_ref[g])
        for b in range(blocks):
            first = b * ROW_BLOCK
            window = slice(first, first + WINDOW)
            probs = block_probs(query[first : first + ROW_BLOCK], key[window], bias + masks[b])
            attended = dot_nn(probs.astype(BF16), value[window])
            kept = x_ref[first : first + ROW_BLOCK, columns].astype(F32)
            out_ref[first : first + ROW_BLOCK, columns] = (kept + attended).astype(BF16)


def column_spec(rows, group, first):
    return pl.BlockSpec((rows, group * HEAD_DIM), lambda i, meta: (0, i + first))


def slot_specs(weight_slots, group):
    return [
        pl.BlockSpec((3, group, slot.shape[2], HEAD_DIM), lambda i, meta: (0, i, 0, 0))
        for slot in weight_slots
    ]


def forward_attention(meta, before, own, after, x, offsets, weight_slots, group):
    rows, width = own.shape
    heads = width // HEAD_DIM
    slots = len(weight_slots)
    return pl.pallas_call(
        functools.partial(forward_kernel, slots, group),
        out_shape=jax.ShapeDtypeStruct((rows, width), BF16),
        grid_spec=pltpu.PrefetchScalarGridSpec(
            num_scalar_prefetch=1,
            grid=(heads // group,),
            in_specs=[
                column_spec(RADIUS, group, 0),
                column_spec(rows, group, 0),
                column_spec(RADIUS, group, 0),
                column_spec(rows, group, 0),
                pl.BlockSpec((group, 1, WINDOW), lambda i, meta: (i, 0, 0)),
                *slot_specs(weight_slots, group),
            ],
            out_specs=column_spec(rows, group, 0),
            scratch_shapes=[pltpu.VMEM((group, HEAD_DIM, 3 * HEAD_DIM), BF16)],
        ),
        compiler_params=pltpu.CompilerParams(vmem_limit_bytes=VMEM_LIMIT),
        cost_estimate=pl.CostEstimate(
            flops=heads * 60_000_000, bytes_accessed=8 * rows * width, transcendentals=heads * 32768
        ),
        name="forward_attention",
    )(meta, before, own, after, x, offsets, *weight_slots)


def backward_kernel(slots, group, meta_ref, before_ref, own_ref, after_ref, cot_ref, offset_ref, *rest):
    slot_refs = rest[:slots]
    rest = rest[slots:]
    grad_ref, lower_ref, upper_ref, offset_grad_ref = rest[:4]
    part_refs = rest[4 : 4 + slots]
    weight_ref, part_ref = rest[4 + slots :]
    rows = own_ref.shape[0]
    blocks = rows // ROW_BLOCK
    scale = HEAD_DIM ** (-0.5)
    masks = [key_mask(meta_ref, b * ROW_BLOCK) for b in range(blocks)]
    for g in range(group):
        columns = slice(g * HEAD_DIM, (g + 1) * HEAD_DIM)
        weight = load_weight(meta_ref, slot_refs, weight_ref, g, slots)
        own = own_ref[:, columns]
        extended = jnp.concatenate([before_ref[:, columns], own, after_ref[:, columns]], axis=0)
        query = dot_nn(own, weight[:, :HEAD_DIM]).astype(BF16)
        key_value = dot_nn(extended, weight[:, HEAD_DIM:]).astype(BF16)
        key, value = key_value[:, :HEAD_DIM], key_value[:, HEAD_DIM:]
        bias = toeplitz(offset_ref[g])
        grad_query, grad_key, grad_value, score_sum = [], [], [], None
        for b in range(blocks):
            first = b * ROW_BLOCK
            window = slice(first, first + WINDOW)
            query_rows = query[first : first + ROW_BLOCK]
            cot_rows = cot_ref[first : first + ROW_BLOCK, columns]
            probs = block_probs(query_rows, key[window], bias + masks[b])
            grad_probs = dot_nt(cot_rows, value[window])
            delta = jnp.sum(probs * grad_probs, axis=-1, keepdims=True)
            grad_scores = probs * (grad_probs - delta)
            score_sum = grad_scores if score_sum is None else score_sum + grad_scores
            grad_packed = grad_scores.astype(BF16)
            grad_query.append(dot_nn(grad_packed, key[window]))
            grad_key.append(dot_tn(grad_packed, query_rows))
            grad_value.append(dot_tn(probs.astype(BF16), cot_rows))

        def joined(parts):
            pieces = []
            for u in range((rows + 2 * RADIUS) // ROW_BLOCK):
                total = None
                for b in range(blocks):
                    if 0 <= u - b < WINDOW // ROW_BLOCK:
                        piece = parts[b][(u - b) * ROW_BLOCK : (u - b + 1) * ROW_BLOCK]
                        total = piece if total is None else total + piece
                pieces.append(total)
            return jnp.concatenate(pieces, axis=0)

        dquery = (jnp.concatenate(grad_query, axis=0) * scale).astype(BF16)
        dkey = (joined(grad_key) * scale).astype(BF16)
        dvalue = joined(grad_value).astype(BF16)
        dkey_value = jnp.concatenate([dkey, dvalue], axis=1)
        grad_extended = dot_nt(dkey_value, weight[:, HEAD_DIM:])
        grad_ref[:, columns] = grad_extended[RADIUS : RADIUS + rows] + dot_nt(dquery, weight[:, :HEAD_DIM])
        lower_ref[:, columns] = grad_extended[:RADIUS].astype(BF16)
        upper_ref[:, columns] = grad_extended[RADIUS + rows :].astype(BF16)
        part_ref[g, :, :HEAD_DIM] = dot_tn(own, dquery)
        part_ref[g, :, HEAD_DIM:] = dot_tn(extended, dkey_value)
        depth = HEAD_DIM // slots
        for r in range(slots):
            if slots == 1:
                start = 0
            else:
                start = pl.multiple_of(lax.rem(meta_ref[0] + r, slots) * depth, depth)
            for j in range(3):
                part_refs[r][j, g] = part_ref[
                    g, pl.ds(start, depth), j * HEAD_DIM : (j + 1) * HEAD_DIM
                ].astype(part_refs[r].dtype)
        offset_grad_ref[g] = diagonal_sums(score_sum)


def backward_attention(meta, before, own, after, cotangent, offsets, weight_slots, group, first_head, heads):
    rows = own.shape[0]
    width = heads * HEAD_DIM
    slots = len(weight_slots)
    first = first_head // group
    slot_shape = weight_slots[0].shape
    part_types = [F32] + [BF16] * (slots - 1) if slots > 1 else [BF16]
    return pl.pallas_call(
        functools.partial(backward_kernel, slots, group),
        out_shape=(
            jax.ShapeDtypeStruct((rows, width), F32),
            jax.ShapeDtypeStruct((RADIUS, width), BF16),
            jax.ShapeDtypeStruct((RADIUS, width), BF16),
            jax.ShapeDtypeStruct((heads, 1, WINDOW), F32),
            *[jax.ShapeDtypeStruct(slot_shape, kind) for kind in part_types],
        ),
        grid_spec=pltpu.PrefetchScalarGridSpec(
            num_scalar_prefetch=1,
            grid=(heads // group,),
            in_specs=[
                column_spec(RADIUS, group, first),
                column_spec(rows, group, first),
                column_spec(RADIUS, group, first),
                column_spec(rows, group, first),
                pl.BlockSpec((group, 1, WINDOW), lambda i, meta: (i + first, 0, 0)),
                *slot_specs(weight_slots, group),
            ],
            out_specs=(
                column_spec(rows, group, 0),
                column_spec(RADIUS, group, 0),
                column_spec(RADIUS, group, 0),
                pl.BlockSpec((group, 1, WINDOW), lambda i, meta: (i, 0, 0)),
                *slot_specs(weight_slots, group),
            ),
            scratch_shapes=[
                pltpu.VMEM((group, HEAD_DIM, 3 * HEAD_DIM), BF16),
                pltpu.VMEM((group, HEAD_DIM, 3 * HEAD_DIM), F32),
            ],
        ),
        compiler_params=pltpu.CompilerParams(vmem_limit_bytes=VMEM_LIMIT),
        cost_estimate=pl.CostEstimate(
            flops=heads * 150_000_000, bytes_accessed=12 * rows * width, transcendentals=heads * 32768
        ),
        name="backward_attention",
    )(meta, before, own, after, cotangent, offsets, *weight_slots)


def finish_kernel(grad_ref, low_ref, high_ref, x_ref, inverse_ref, gain_ref, cot_ref, out_ref, gain_grad_ref):
    rows = x_ref.shape[0]
    grad = grad_ref[...]
    edge = jnp.zeros((rows - RADIUS, grad.shape[1]), F32)
    grad = grad + jnp.concatenate([low_ref[...].astype(F32), edge], axis=0)
    grad = grad + jnp.concatenate([edge, high_ref[...].astype(F32)], axis=0)
    x = x_ref[...].astype(F32)
    inverse = inverse_ref[:, :1]
    gain_grad_ref[...] = jnp.sum(grad * x * inverse, axis=0, keepdims=True)
    scaled = grad * gain_ref[...]
    mean = jnp.mean(scaled * x, axis=-1, keepdims=True)
    result = inverse * scaled - x * (inverse * inverse * inverse * mean)
    out_ref[...] = (cot_ref[...].astype(F32) + result).astype(BF16)


def finish(grad, low, high, x, inverse, gain, cotangent):
    rows, width = x.shape
    return pl.pallas_call(
        finish_kernel,
        out_shape=(
            jax.ShapeDtypeStruct((rows, width), BF16),
            jax.ShapeDtypeStruct((1, width), F32),
        ),
        compiler_params=pltpu.CompilerParams(vmem_limit_bytes=VMEM_LIMIT),
        cost_estimate=pl.CostEstimate(
            flops=16 * rows * width, bytes_accessed=14 * rows * width, transcendentals=0
        ),
        name="finish",
    )(grad, low, high, x, inverse, gain, cotangent)


def column_of(row, rows):
    return jnp.transpose(jnp.broadcast_to(row, (128, rows)))


def split_rows(inverse, pad_rows, width):
    high = inverse.astype(BF16)
    rest = inverse - high.astype(F32)
    middle = rest.astype(BF16)
    low = (rest - middle.astype(F32)).astype(BF16)
    wide = [jnp.transpose(jnp.broadcast_to(v.astype(F32), (v.shape[0], 128)))[:1] for v in (high, middle, low)]
    row = jnp.concatenate(wide + [jnp.zeros((pad_rows - 3, wide[0].shape[1]), F32)], axis=0)
    return row.astype(BF16)


def row_inverse(x):
    x = x.astype(F32)
    return lax.rsqrt(jnp.mean(x * x, axis=-1, keepdims=True) + eps_norm)


def pack_stash_kernel(parts, meta_ref, x_ref, gain_ref, weight_ref, inverse_ref, *refs):
    out_refs, normed_ref = refs[:parts], refs[parts]
    rows, width = x_ref.shape
    depth = weight_ref.shape[2]
    wide = width // parts
    heads = wide // HEAD_DIM
    inverse = row_inverse(x_ref[...])
    inverse_ref[...] = jnp.broadcast_to(inverse, inverse_ref.shape)
    normed_ref[...] = (x_ref[...].astype(F32) * inverse * gain_ref[...]).astype(BF16)
    for r, out_ref in enumerate(out_refs):
        target = lax.rem(meta_ref[0] + r, parts)
        out_ref[:rows] = normed_ref[:, pl.ds(pl.multiple_of(target * wide, 128), wide)]
        for j in range(3):
            for h in range(heads):
                out_ref[rows + j * depth : rows + (j + 1) * depth, h * HEAD_DIM : (h + 1) * HEAD_DIM] = weight_ref[
                    j, target * heads + h
                ]


def pack_rows_kernel(parts, with_inverse, meta_ref, edge_ref, inner_ref, *out_refs):
    rows, width = inner_ref.shape
    wide = width // parts
    edge = 2 if with_inverse else 1
    refs = out_refs[:parts]
    for r, out_ref in enumerate(refs):
        target = lax.rem(meta_ref[0] + r, parts)
        start = pl.multiple_of(target * wide, 128)

        @pl.when(meta_ref[edge] == 1)
        def use_edge():
            out_ref[:rows] = edge_ref[:, pl.ds(start, wide)]

        @pl.when(meta_ref[edge] == 0)
        def use_inner():
            out_ref[:rows] = inner_ref[:, pl.ds(start, wide)]

    def finish_with(source_ref):
        if with_inverse:
            tail = split_rows(row_inverse(source_ref[...]), 16, wide)
            for out_ref in refs:
                out_ref[rows:] = jnp.zeros((16, wide), BF16)
                out_ref[rows:, :rows] = tail
        else:
            out_refs[parts][...] = source_ref[...]

    @pl.when(meta_ref[edge] == 1)
    def finish_edge():
        finish_with(edge_ref)

    @pl.when(meta_ref[edge] == 0)
    def finish_inner():
        finish_with(inner_ref)


SMEM_SPEC = pl.BlockSpec(memory_space=pltpu.SMEM)
VMEM_SPEC = pl.BlockSpec(memory_space=pltpu.VMEM)


def pack_stash(meta, x, gain, weight, parts):
    rows, width = x.shape
    depth = weight.shape[2]
    shape = (rows + 3 * depth, width // parts)
    return pl.pallas_call(
        functools.partial(pack_stash_kernel, parts),
        out_shape=(
            jax.ShapeDtypeStruct((rows, 128), F32),
            *[jax.ShapeDtypeStruct(shape, BF16) for r in range(parts)],
        ),
        in_specs=[SMEM_SPEC, VMEM_SPEC, VMEM_SPEC, VMEM_SPEC],
        out_specs=(VMEM_SPEC,) * (parts + 1),
        scratch_shapes=[pltpu.VMEM((rows, width), BF16)],
        compiler_params=pltpu.CompilerParams(vmem_limit_bytes=VMEM_LIMIT),
        cost_estimate=pl.CostEstimate(flops=4 * rows * width, bytes_accessed=6 * rows * width, transcendentals=0),
        name="pack_stash",
    )(meta, x, gain, weight)


def pack_rows(meta, edge, inner, parts, with_inverse):
    rows, width = inner.shape
    shape = (rows + (16 if with_inverse else 0), width // parts)
    extra = () if with_inverse else (jax.ShapeDtypeStruct((rows, width), BF16),)
    return pl.pallas_call(
        functools.partial(pack_rows_kernel, parts, with_inverse),
        out_shape=(*[jax.ShapeDtypeStruct(shape, BF16) for r in range(parts)], *extra),
        in_specs=[SMEM_SPEC, VMEM_SPEC, VMEM_SPEC],
        out_specs=(VMEM_SPEC,) * (parts + len(extra)),
        compiler_params=pltpu.CompilerParams(vmem_limit_bytes=VMEM_LIMIT),
        cost_estimate=pl.CostEstimate(flops=4 * rows * width, bytes_accessed=6 * rows * width, transcendentals=0),
        name="pack_inbound" if with_inverse else "pack_cotangent",
    )(meta, edge, inner)


def gather_rows(meta_ref, refs, rows, x_ref):
    parts = len(refs)
    for r, ref in enumerate(refs):
        source = lax.rem(meta_ref[0] + parts - r, parts)
        x_ref[pl.ds(pl.multiple_of(source * rows, rows), rows)] = ref[:rows]


def gather_weight(meta_ref, refs, rows, weight_ref):
    parts = len(refs)
    depth = HEAD_DIM // parts
    for r, ref in enumerate(refs):
        source = lax.rem(meta_ref[0] + parts - r, parts)
        depth_at = pl.ds(pl.multiple_of(source * depth, depth), depth)
        for j in range(3):
            weight_ref[depth_at, j * HEAD_DIM : (j + 1) * HEAD_DIM] = ref[
                rows + j * depth : rows + (j + 1) * depth
            ]


def gather_inverse(meta_ref, refs, rows, inverse_ref):
    parts = len(refs)

    @pl.when(pl.program_id(0) == 0)
    def spread_inverse():
        for r, ref in enumerate(refs):
            source = lax.rem(meta_ref[0] + parts - r, parts)
            tail = ref[rows : rows + 16].astype(F32)
            inverse_ref[pl.ds(pl.multiple_of(source * rows, rows), rows)] = column_of(
                tail[:1] + tail[1:2] + tail[2:3], rows
            )


def block_mask(first_query, tokens):
    key = lax.broadcasted_iota(jnp.int32, (1, WINDOW), 1) + (first_query - RADIUS)
    return jnp.where((key >= 0) & (key < tokens), 0.0, masked_score).astype(F32)


def edge_bias(bias, first, tokens):
    if first < RADIUS or first + ROW_BLOCK + RADIUS > tokens:
        return bias + block_mask(first, tokens)
    return bias


def padded(rows):
    edge = jnp.zeros((RADIUS, rows.shape[1]), rows.dtype)
    return jnp.concatenate([edge, rows, edge], axis=0)


def heads_backward_kernel(parts, rows, meta_ref, *refs):
    a_refs, c_refs = refs[:parts], refs[parts : 2 * parts]
    gain_ref, offset_ref, onehot_ref = refs[2 * parts : 2 * parts + 3]
    out_refs = refs[2 * parts + 3 : 3 * parts + 3]
    gain_grad_ref, x_ref, weight_ref, cot_ref, grad_ref, part_ref, bias_ref = refs[3 * parts + 3 :]
    tokens = rows * parts
    depth = HEAD_DIM // parts
    scale = HEAD_DIM ** (-0.5)
    gather_rows(meta_ref, a_refs, rows, x_ref)
    gather_weight(meta_ref, a_refs, rows, weight_ref)
    gather_rows(meta_ref, c_refs, rows, cot_ref)
    weight = weight_ref[...]
    normed = x_ref[...]
    query = dot_nn(normed, weight[:, :HEAD_DIM]).astype(BF16)
    key = padded(dot_nn(normed, weight[:, HEAD_DIM : 2 * HEAD_DIM]).astype(BF16))
    value = padded(dot_nn(normed, weight[:, 2 * HEAD_DIM :]).astype(BF16))
    bias = toeplitz(offset_ref[0])
    blocks = tokens // ROW_BLOCK
    grad_query, grad_key, grad_value, score_sum = [], [], [], None
    for b in range(blocks):
        first = b * ROW_BLOCK
        window = slice(first, first + WINDOW)
        query_rows = query[first : first + ROW_BLOCK]
        cot_rows = cot_ref[first : first + ROW_BLOCK]
        probs = block_probs(query_rows, key[window], edge_bias(bias, first, tokens))
        grad_probs = dot_nt(cot_rows, value[window])
        delta = jnp.sum(probs * grad_probs, axis=-1, keepdims=True)
        grad_scores = probs * (grad_probs - delta)
        score_sum = grad_scores if score_sum is None else score_sum + grad_scores
        grad_packed = grad_scores.astype(BF16)
        grad_query.append(dot_nn(grad_packed, key[window]))
        grad_key.append(dot_tn(grad_packed, query_rows))
        grad_value.append(dot_tn(probs.astype(BF16), cot_rows))

    def joined(pieces):
        units = []
        for u in range((tokens + 2 * RADIUS) // ROW_BLOCK):
            total = None
            for b in range(blocks):
                if 0 <= u - b < WINDOW // ROW_BLOCK:
                    piece = pieces[b][(u - b) * ROW_BLOCK : (u - b + 1) * ROW_BLOCK]
                    total = piece if total is None else total + piece
            units.append(total)
        return jnp.concatenate(units, axis=0)[RADIUS : RADIUS + tokens]

    dqkv = jnp.concatenate(
        [
            (jnp.concatenate(grad_query, axis=0) * scale).astype(BF16),
            (joined(grad_key) * scale).astype(BF16),
            joined(grad_value).astype(BF16),
        ],
        axis=1,
    )
    grad_normed = dot_nt(dqkv, weight)
    gain_grad_ref[...] = jnp.sum(grad_normed * normed.astype(F32), axis=0, keepdims=True) / gain_ref[...]
    grad_ref[...] = grad_normed
    part_ref[...] = dot_tn(normed, dqkv)
    bias_grad = jnp.sum(onehot_ref[...] * diagonal_sums(score_sum), axis=1, keepdims=True)
    bias_ref[...] = jnp.broadcast_to(bias_grad, bias_ref.shape)
    buckets = bias_ref.shape[0] // parts
    for r, out_ref in enumerate(out_refs):
        source = lax.rem(meta_ref[0] + parts - r, parts)
        out_ref[:rows] = grad_ref[pl.ds(pl.multiple_of(source * rows, rows), rows)].astype(BF16)
        for j in range(3):
            out_ref[rows + j * depth : rows + (j + 1) * depth] = part_ref[
                pl.ds(pl.multiple_of(source * depth, depth), depth), j * HEAD_DIM : (j + 1) * HEAD_DIM
            ].astype(BF16)
        share = bias_ref[pl.ds(pl.multiple_of(source * buckets, buckets), buckets)]
        out_ref[rows + 3 * depth :] = jnp.concatenate(
            [share, jnp.zeros((16 - buckets, HEAD_DIM), F32)], axis=0
        ).astype(BF16)


def head_column(rows, first=0):
    return pl.BlockSpec((rows, HEAD_DIM), lambda i, meta: (0, i + first))


def whole_column(rows, heads, first=0):
    return pl.BlockSpec((rows, HEAD_DIM), lambda i, meta: (0, meta[0] * heads + first + i))


def offset_spec(heads, first=0):
    return pl.BlockSpec((1, 1, WINDOW), lambda i, meta: (meta[0] * heads + first + i, 0, 0))


def heads_backward(meta, a_slots, c_slots, gain, offsets, onehot, heads, first, count):
    parts = len(a_slots)
    rows = c_slots[0].shape[0]
    tokens = rows * parts
    buckets = onehot.shape[0]
    packed = a_slots[0].shape[0]
    made = packed + 16
    width = count * HEAD_DIM
    return pl.pallas_call(
        functools.partial(heads_backward_kernel, parts, rows),
        out_shape=(
            *[jax.ShapeDtypeStruct((made, width), BF16) for r in range(parts)],
            jax.ShapeDtypeStruct((1, width), F32),
        ),
        grid_spec=pltpu.PrefetchScalarGridSpec(
            num_scalar_prefetch=1,
            grid=(count,),
            in_specs=[
                *[head_column(packed, first)] * parts,
                whole_column(rows, heads, first),
                *[head_column(rows, first)] * (parts - 1),
                whole_column(1, heads, first),
                offset_spec(heads, first),
                pl.BlockSpec((buckets, WINDOW), lambda i, meta: (0, 0)),
            ],
            out_specs=(*[head_column(made)] * parts, head_column(1)),
            scratch_shapes=[
                pltpu.VMEM((tokens, HEAD_DIM), BF16),
                pltpu.VMEM((HEAD_DIM, 3 * HEAD_DIM), BF16),
                pltpu.VMEM((tokens, HEAD_DIM), BF16),
                pltpu.VMEM((tokens, HEAD_DIM), F32),
                pltpu.VMEM((HEAD_DIM, 3 * HEAD_DIM), F32),
                pltpu.VMEM((buckets, HEAD_DIM), F32),
            ],
        ),
        compiler_params=pltpu.CompilerParams(vmem_limit_bytes=VMEM_LIMIT),
        cost_estimate=pl.CostEstimate(
            flops=count * tokens * 400_000, bytes_accessed=tokens * width, transcendentals=0
        ),
        name="heads_backward",
    )(meta, *a_slots, *c_slots, gain, offsets, onehot)


def heads_forward_kernel(parts, rows, meta_ref, *refs):
    a_refs, i_refs = refs[:parts], refs[parts : 2 * parts]
    gain_ref, offset_ref = refs[2 * parts : 2 * parts + 2]
    out_refs = refs[2 * parts + 2 : 3 * parts + 2]
    sums_ref, inverse_ref, x_ref, weight_ref, made_ref, square_ref = refs[3 * parts + 2 :]
    tokens = rows * parts
    gather_rows(meta_ref, i_refs, rows, x_ref)
    gather_weight(meta_ref, a_refs, rows, weight_ref)
    gather_inverse(meta_ref, i_refs, rows, inverse_ref)
    weight = weight_ref[...]
    normed = (x_ref[...].astype(F32) * inverse_ref[...] * gain_ref[...]).astype(BF16)
    query = dot_nn(normed, weight[:, :HEAD_DIM]).astype(BF16)
    key = padded(dot_nn(normed, weight[:, HEAD_DIM : 2 * HEAD_DIM]).astype(BF16))
    value = padded(dot_nn(normed, weight[:, 2 * HEAD_DIM :]).astype(BF16))
    bias = toeplitz(offset_ref[0])
    for b in range(tokens // ROW_BLOCK):
        first = b * ROW_BLOCK
        window = slice(first, first + WINDOW)
        probs = block_probs(query[first : first + ROW_BLOCK], key[window], edge_bias(bias, first, tokens))
        attended = dot_nn(probs.astype(BF16), value[window])
        made_ref[first : first + ROW_BLOCK] = (
            x_ref[first : first + ROW_BLOCK].astype(F32) + attended
        ).astype(BF16)
    made = made_ref[...].astype(F32)
    squares = made * made

    @pl.when(pl.program_id(0) == 0)
    def first_head():
        square_ref[...] = squares

    @pl.when(pl.program_id(0) > 0)
    def later_head():
        square_ref[...] += squares

    @pl.when(pl.program_id(0) == pl.num_programs(0) - 1)
    def last_head():
        total = jnp.sum(jnp.transpose(square_ref[...]), axis=0, keepdims=True)
        sums_ref[...] = jnp.broadcast_to(total, sums_ref.shape)

    for r, out_ref in enumerate(out_refs):
        source = lax.rem(meta_ref[0] + parts - r, parts)
        out_ref[...] = made_ref[pl.ds(pl.multiple_of(source * rows, rows), rows)]


def heads_forward(meta, a_slots, i_slots, gain, offsets, heads, rows):
    parts = len(a_slots)
    tokens = rows * parts
    packed = a_slots[0].shape[0]
    width = heads * HEAD_DIM
    return pl.pallas_call(
        functools.partial(heads_forward_kernel, parts, rows),
        out_shape=(
            *[jax.ShapeDtypeStruct((rows, width), BF16) for r in range(parts)],
            jax.ShapeDtypeStruct((8, tokens), F32),
        ),
        grid_spec=pltpu.PrefetchScalarGridSpec(
            num_scalar_prefetch=1,
            grid=(heads,),
            in_specs=[
                *[head_column(packed)] * parts,
                *[head_column(i_slots[0].shape[0])] * parts,
                whole_column(1, heads),
                offset_spec(heads),
            ],
            out_specs=(
                *[head_column(rows)] * parts,
                pl.BlockSpec((8, tokens), lambda i, meta: (0, 0)),
            ),
            scratch_shapes=[
                pltpu.VMEM((tokens, HEAD_DIM), F32),
                pltpu.VMEM((tokens, HEAD_DIM), BF16),
                pltpu.VMEM((HEAD_DIM, 3 * HEAD_DIM), BF16),
                pltpu.VMEM((tokens, HEAD_DIM), BF16),
                pltpu.VMEM((tokens, HEAD_DIM), F32),
            ],
        ),
        compiler_params=pltpu.CompilerParams(vmem_limit_bytes=VMEM_LIMIT),
        cost_estimate=pl.CostEstimate(
            flops=heads * tokens, bytes_accessed=tokens, transcendentals=0
        ),
        name="heads_forward",
    )(meta, *a_slots, *i_slots, gain, offsets)


def memory_kernel(parts, width, meta_ref, *refs):
    out_refs = refs[:parts]
    sums_ref, gain_ref, after_ref, memory_ref = refs[parts:]
    rows = out_refs[0].shape[0]
    wide = memory_ref.shape[1]
    total = sums_ref[0, :1]
    for r in range(1, parts):
        total = total + sums_ref[r, :1]
    inverse = lax.rsqrt(total / width + eps_norm)
    gain = gain_ref[:, pl.ds(pl.multiple_of(meta_ref[0] * wide, 128), wide)]
    spread_inverse = jnp.transpose(jnp.broadcast_to(inverse, (128, inverse.shape[1])))
    for r, out_ref in enumerate(out_refs):
        source = lax.rem(meta_ref[0] + parts - r, parts)
        memory_ref[pl.ds(pl.multiple_of(source * rows, rows), rows)] = out_ref[...]
    made = memory_ref[...].astype(F32)
    memory_ref[...] = (made * spread_inverse[:, :1] * gain).astype(BF16)


def memory_rows(meta, outs, sums, gain, after, width):
    parts = len(outs)
    rows, wide = outs[0].shape
    return pl.pallas_call(
        functools.partial(memory_kernel, parts, width),
        out_shape=jax.ShapeDtypeStruct((rows * parts, wide), BF16),
        in_specs=[SMEM_SPEC] + [VMEM_SPEC] * (parts + 2) + [pl.BlockSpec(memory_space=pl.ANY)],
        out_specs=VMEM_SPEC,
        compiler_params=pltpu.CompilerParams(vmem_limit_bytes=VMEM_LIMIT),
        cost_estimate=pl.CostEstimate(flops=rows, bytes_accessed=rows, transcendentals=0),
        name="memory_rows",
    )(meta, *outs, sums, gain, after)


def place_kernel(parts, meta_ref, *refs):
    out_ref = refs[parts]
    wide = refs[0].shape[1]
    for r in range(parts):
        source = lax.rem(meta_ref[0] + r, parts)
        out_ref[:, pl.ds(pl.multiple_of(source * wide, 128), wide)] = refs[r][...]


def place_columns(meta, slots):
    parts = len(slots)
    rows, wide = slots[0].shape
    return pl.pallas_call(
        functools.partial(place_kernel, parts),
        out_shape=jax.ShapeDtypeStruct((rows, wide * parts), BF16),
        in_specs=[SMEM_SPEC] + [VMEM_SPEC] * parts,
        out_specs=VMEM_SPEC,
        compiler_params=pltpu.CompilerParams(vmem_limit_bytes=VMEM_LIMIT),
        cost_estimate=pl.CostEstimate(flops=0, bytes_accessed=rows, transcendentals=0),
        name="place_columns",
    )(meta, *slots)


def heads_finish_kernel(parts, chunks, meta_ref, *refs):
    g_refs = refs[: parts * chunks]
    x_ref, inverse_ref, gain_ref, cot_ref, out_ref, weight_ref, bias_ref, scaled_ref = refs[parts * chunks :]
    rows, width = x_ref.shape
    wide = width // parts // chunks
    heads = wide // HEAD_DIM
    depth = HEAD_DIM // parts
    buckets = bias_ref.shape[1]
    for c in range(chunks):
        for r in range(parts):
            g_ref = g_refs[c * parts + r]
            place = lax.rem(meta_ref[0] + r, parts) * chunks + c
            columns = pl.ds(pl.multiple_of(place * wide, 128), wide)
            scaled_ref[:, columns] = g_ref[:rows].astype(F32) * gain_ref[:, columns]
            for h in range(heads):
                lanes = slice(h * HEAD_DIM, (h + 1) * HEAD_DIM)
                for j in range(3):
                    weight_ref[j, place * heads + h] = g_ref[
                        rows + j * depth : rows + (j + 1) * depth, lanes
                    ].astype(F32)
                bias_ref[place * heads + h] = g_ref[rows + 3 * depth :, lanes].astype(F32)[:buckets]
    x = x_ref[...].astype(F32)
    scaled = scaled_ref[...]
    inverse = inverse_ref[:, :1]
    mean = jnp.mean(scaled * x, axis=-1, keepdims=True)
    result = inverse * scaled - x * (inverse * inverse * inverse * mean)
    out_ref[...] = (cot_ref[...].astype(F32) + result).astype(BF16)


def heads_finish(meta, g_chunks, x, inverse, gain, cotangent, buckets):
    chunks, parts = len(g_chunks), len(g_chunks[0])
    rows, width = x.shape
    heads = width // HEAD_DIM
    slots = [slot for g_slots in g_chunks for slot in g_slots]
    return pl.pallas_call(
        functools.partial(heads_finish_kernel, parts, chunks),
        out_shape=(
            jax.ShapeDtypeStruct((rows, width), BF16),
            jax.ShapeDtypeStruct((3, heads, HEAD_DIM // parts, HEAD_DIM), F32),
            jax.ShapeDtypeStruct((heads, buckets // parts, HEAD_DIM), F32),
        ),
        in_specs=[SMEM_SPEC] + [VMEM_SPEC] * (len(slots) + 4),
        out_specs=(VMEM_SPEC,) * 3,
        scratch_shapes=[pltpu.VMEM((rows, width), F32)],
        compiler_params=pltpu.CompilerParams(vmem_limit_bytes=VMEM_LIMIT),
        cost_estimate=pl.CostEstimate(flops=12 * rows * width, bytes_accessed=14 * rows * width, transcendentals=0),
        name="heads_finish",
    )(meta, *slots, x, inverse, gain, cotangent)


def offset_table(rel_bias):
    onehot = jnp.asarray(bucket_onehot(rel_bias.shape[0]))
    by_offset = jnp.dot(onehot, rel_bias, precision=lax.Precision.HIGHEST).T
    inside = jnp.arange(WINDOW, dtype=jnp.int32) <= 2 * RADIUS
    return jnp.where(inside[None, :], by_offset, masked_score)[:, None, :]


def shifted(value, axis, steps):
    count = lax.axis_size(axis)
    first, last = (max(0, -steps), min(count, count - steps))
    return lax.ppermute(value, axis, [(source, source + steps) for source in range(first, last)])


def spread_memory(made, section, sections):
    share = made.shape[0] // sections
    last = sections - 1
    if sections % 2:
        memory = jnp.where(section == last, made[last * share :], 0)
        for s in range(last):
            memory = memory + lax.ppermute(made[s * share : (s + 1) * share], "section", [(last, s)])
        return memory
    couple = jnp.where(section == last, made[(last - 1) * share :], 0)
    for s in range(0, last - 1, 2):
        couple = couple + lax.ppermute(made[s * share : (s + 2) * share], "section", [(last, s + 1)])
    even = lax.ppermute(couple[:share], "section", [(s + 1, s) for s in range(0, sections, 2)])
    return jnp.where(section % 2 == 0, even, couple[share:])


def heads_body(
    embedded, carried, stash, returned, loss_grad, qkv_weight, rel_bias, norm_gain, final_gain
):
    section = lax.axis_index("section")
    sections = lax.axis_size("section")
    parts = lax.axis_size("seq")
    rows, width = embedded.shape
    heads = width // HEAD_DIM // parts
    buckets = rel_bias.shape[1]
    meta = jnp.stack(
        [lax.axis_index("seq"), section == 0, section == sections - 1]
    ).astype(jnp.int32)

    def exchanged(sends, direction):
        moved = [
            lax.ppermute(sends[r], "seq", [(i, (i + direction * r) % parts) for i in range(parts)])
            for r in range(1, parts)
        ]
        return [sends[0]] + moved

    def diagonal(value, r, step):
        pairs = [
            (s * parts + i, (s + step) % sections * parts + (i + r) % parts)
            for s in range(sections)
            for i in range(parts)
        ]
        return lax.ppermute(value, ("section", "seq"), pairs)

    inverse_b, *a_sends = pack_stash(meta, stash[0], norm_gain, qkv_weight[0], parts)
    a_slots = exchanged(a_sends, 1)
    meta_i, inverse_b = lax.optimization_barrier((meta, inverse_b))
    i_sends = pack_rows(meta_i, embedded, carried[0], parts, True)
    i_slots = [diagonal(i_sends[r], r, 1) for r in range(parts)]
    meta_c, i_sends = lax.optimization_barrier((meta_i, i_sends))
    *c_sends, cot_source = pack_rows(meta_c, loss_grad, returned[0], parts, False)
    cotangent = diagonal(cot_source, 0, -1)
    c_slots = [cotangent] + [diagonal(c_sends[r], r, -1) for r in range(1, parts)]

    offsets = offset_table(rel_bias[0])
    onehot = jnp.asarray(bucket_onehot(buckets).T)
    *o_sends, sums = heads_forward(meta, a_slots, i_slots, norm_gain, offsets, heads, rows)
    all_sums = lax.all_gather(sums, "seq", axis=0, tiled=False)
    o_sends, c_slots, sums = lax.optimization_barrier((o_sends, c_slots, sums))
    waiting = exchanged(o_sends, -1)
    gain_after, sums = lax.optimization_barrier((norm_gain, sums))

    chunks = 2 if heads % 2 == 0 else 1
    count = heads // chunks
    g_chunks, gain_parts, o_slots = [], [], None
    for c in range(chunks):
        *g_sends, gain_part = heads_backward(
            meta, a_slots, c_slots, gain_after, offsets, onehot, heads, c * count, count
        )
        g_sends, waiting, gain_after, gain_part = lax.optimization_barrier(
            (g_sends, waiting, gain_after, gain_part)
        )
        if o_slots is None:
            o_slots = waiting
        else:
            g_chunks.append(waiting)
        waiting = exchanged(g_sends, -1)
        gain_parts.append(gain_part)
    g_chunks.append(waiting)
    gain_grad = jnp.concatenate(gain_parts, axis=1)
    made = memory_rows(meta, o_sends, all_sums, final_gain[None], gain_parts[-1], width)
    memory = spread_memory(made, section, sections)

    input_grad, weight_grad, bias_wide = heads_finish(
        meta, g_chunks, stash[0], inverse_b, norm_gain, cotangent, buckets
    )
    bias_grad = bias_wide[:, :, 0].T
    output = place_columns(meta, o_slots)
    return (
        output[None],
        input_grad[None],
        weight_grad[None],
        bias_grad[None],
        gain_grad,
        memory,
    )


def tokens_body(
    embedded, carried, stash, returned, loss_grad, qkv_weight, rel_bias, norm_gain, final_gain
):
    section_index = lax.axis_index("section")
    section_count = lax.axis_size("section")
    seq_index = lax.axis_index("seq")
    seq_count = lax.axis_size("seq")
    rows, width = embedded.shape
    heads = width // HEAD_DIM
    tokens = rows * seq_count
    shard = qkv_weight[0]
    up = [(i, i + 1) for i in range(seq_count - 1)]
    down = [(j, i) for i, j in up]
    group = 4 if heads % 4 == 0 else 1

    own_b, inverse_b = norm_rows(stash[0], norm_gain)
    before_b = lax.ppermute(own_b[rows - RADIUS :], "seq", up)
    after_b = lax.ppermute(own_b[:RADIUS], "seq", down)
    slots = [lax.all_gather(shard, "seq", axis=2, tiled=True)]

    section_up = [(i, (i + 1) % section_count) for i in range(section_count)]
    section_down = [(j, i) for i, j in section_up]
    inbound = lax.ppermute(
        jnp.where(section_index == section_count - 1, embedded, carried[0]), "section", section_up
    )
    cotangent = lax.ppermute(
        jnp.where(section_index == 0, loss_grad, returned[0]), "section", section_down
    )

    onehot = jnp.asarray(bucket_onehot(rel_bias.shape[1]))
    offsets = offset_table(rel_bias[0])
    first_key = RADIUS - seq_index * rows
    meta = jnp.stack([seq_index, first_key, first_key + tokens]).astype(jnp.int32)

    own_a, unused = norm_rows(inbound, norm_gain)
    before_a = lax.ppermute(own_a[rows - RADIUS :], "seq", up)
    after_a = lax.ppermute(own_a[:RADIUS], "seq", down)

    grad_own, lower, upper, offset_grad, *parts = backward_attention(
        meta, before_b, own_b, after_b, cotangent, offsets, slots, group, 0, heads
    )
    from_before = lax.ppermute(upper, "seq", up)
    from_after = lax.ppermute(lower, "seq", down)
    weight_sum = lax.psum_scatter(parts[0], "seq", scatter_dimension=2, tiled=True).astype(F32)

    output = forward_attention(meta, before_a, own_a, after_a, inbound, offsets, slots, group)
    final_normed, unused = norm_rows(output, final_gain[None])
    relaid = lax.all_to_all(final_normed, "seq", split_axis=1, concat_axis=0, tiled=True)
    kept = jnp.where(section_index == section_count - 1, relaid, jnp.zeros_like(relaid))
    memory = lax.psum_scatter(kept, "section", scatter_dimension=0, tiled=True)

    input_grad, gain_part = finish(
        grad_own, from_before, from_after, stash[0], inverse_b, norm_gain, cotangent
    )
    bias_part = jnp.dot(
        offset_grad[:, 0, :], onehot, precision=lax.Precision.HIGHEST
    ).T
    bias_sum = lax.psum_scatter(
        bias_part.astype(BF16), "seq", scatter_dimension=0, tiled=True
    ).astype(F32)
    gain_sum = lax.psum_scatter(
        gain_part.astype(BF16), "seq", scatter_dimension=1, tiled=True
    ).astype(F32)
    return (output[None], input_grad[None], weight_sum[None], bias_sum[None], gain_sum, memory)


def choose_body(embedded, carried, stash, returned, loss_grad, qkv_weight, rel_bias, norm_gain, final_gain):
    parts = lax.axis_size("seq")
    rows, width = embedded.shape
    even = width % (HEAD_DIM * parts) == 0 and HEAD_DIM % (32 * parts) == 0 and rows == 128
    even = even and rel_bias.shape[1] == 8 * parts and rows * parts % (16 * lax.axis_size("section")) == 0
    chosen = heads_body if even else tokens_body
    return chosen(
        embedded, carried, stash, returned, loss_grad, qkv_weight, rel_bias, norm_gain, final_gain
    )


def solution(mesh):
    in_specs = (
        P("seq", None),
        P("section", "seq", None),
        P("section", "seq", None),
        P("section", "seq", None),
        P("seq", None),
        P("section", None, None, "seq", None),
        P("section", None, None),
        P("section", None),
        P(),
    )
    out_specs = (
        P("section", "seq", None),
        P("section", "seq", None),
        P("section", None, None, "seq", None),
        P("section", "seq", None),
        P("section", "seq"),
        P("section", "seq"),
    )
    return jax.shard_map(choose_body, mesh=mesh, in_specs=in_specs, out_specs=out_specs, check_vma=False)
```

```python
import functools

import jax
import jax.numpy as jnp
import numpy as np
from jax import lax
from jax.experimental import pallas as pl
from jax.experimental.pallas import tpu as pltpu
from jax.sharding import PartitionSpec as P

RADIUS = 96
HEAD_DIM = 128
ROW_BLOCK = 64
WINDOW = ROW_BLOCK + 2 * RADIUS
eps_norm = 1e-06
bucket_edges = (1, 2, 3, 4, 5, 6, 7, 8, 11, 16, 22, 32, 45, 64, 90)
masked_score = -1e30
F32 = jnp.float32
BF16 = jnp.bfloat16
VMEM_LIMIT = 48 * 1024 * 1024


def bucket_onehot(bucket_count):
    offsets = np.arange(WINDOW) - RADIUS
    magnitude = np.abs(offsets)
    counted = np.zeros(offsets.shape, np.int32)
    for threshold in bucket_edges:
        counted = counted + (magnitude >= threshold)
    counted = counted + 16 * (offsets > 0)
    onehot = (counted[:, None] == np.arange(bucket_count)[None, :]) & (magnitude <= RADIUS)[:, None]
    return onehot.astype(np.float32)


def dot_nn(a, b):
    return lax.dot_general(a, b, (((1,), (0,)), ((), ())), preferred_element_type=F32)


def dot_nt(a, b):
    return lax.dot_general(a, b, (((1,), (1,)), ((), ())), preferred_element_type=F32)


def dot_tn(a, b):
    return lax.dot_general(a, b, (((0,), (0,)), ((), ())), preferred_element_type=F32)


def norm_kernel(x_ref, gain_ref, normed_ref, inverse_ref):
    x = x_ref[...].astype(F32)
    inverse = lax.rsqrt(jnp.mean(x * x, axis=-1, keepdims=True) + eps_norm)
    normed_ref[...] = (x * inverse * gain_ref[...]).astype(BF16)
    inverse_ref[...] = jnp.broadcast_to(inverse, inverse_ref.shape)


def norm_rows(x, gain):
    rows, width = x.shape
    return pl.pallas_call(
        norm_kernel,
        out_shape=(
            jax.ShapeDtypeStruct((rows, width), BF16),
            jax.ShapeDtypeStruct((rows, 128), F32),
        ),
        compiler_params=pltpu.CompilerParams(vmem_limit_bytes=VMEM_LIMIT),
        cost_estimate=pl.CostEstimate(
            flops=6 * rows * width, bytes_accessed=4 * rows * width, transcendentals=rows
        ),
        name="norm_rows",
    )(x, gain)


def load_weight(meta_ref, slot_refs, weight_ref, head, slots):
    depth = HEAD_DIM // slots
    for r, slot_ref in enumerate(slot_refs):
        if slots == 1:
            start = 0
        else:
            start = pl.multiple_of(lax.rem(meta_ref[0] + r, slots) * depth, depth)
        for j in range(3):
            weight_ref[head, pl.ds(start, depth), j * HEAD_DIM : (j + 1) * HEAD_DIM] = slot_ref[j, head]
    return weight_ref[head]


def key_mask(meta_ref, first_key):
    key = lax.broadcasted_iota(jnp.int32, (1, WINDOW), 1) + first_key
    inside = (key >= meta_ref[1]) & (key < meta_ref[2])
    return jnp.where(inside, 0.0, masked_score).astype(F32)


def toeplitz(row):
    return pltpu.roll(
        jnp.broadcast_to(row, (ROW_BLOCK, WINDOW)), 0, 1, stride=1, stride_axis=0
    )


def diagonal_sums(values):
    total = values[:8]
    for a in range(1, ROW_BLOCK // 8):
        total = total + pltpu.roll(values[8 * a : 8 * a + 8], WINDOW - 8 * a, 1)
    row = lax.broadcasted_iota(jnp.int32, total.shape, 0)
    for bit in (1, 2, 4):
        total = jnp.where((row & bit) != 0, pltpu.roll(total, WINDOW - bit, 1), total)
    return jnp.sum(total, axis=0, keepdims=True)


def block_probs(query_rows, key_rows, bias):
    scores = dot_nt(query_rows, key_rows) * (HEAD_DIM ** (-0.5)) + bias
    weights = jnp.exp(scores - jnp.max(scores, axis=-1, keepdims=True))
    return weights * (1.0 / jnp.sum(weights, axis=-1, keepdims=True))


def forward_kernel(slots, group, meta_ref, before_ref, own_ref, after_ref, x_ref, offset_ref, *rest):
    slot_refs = rest[:slots]
    out_ref, weight_ref = rest[slots:]
    rows = own_ref.shape[0]
    blocks = rows // ROW_BLOCK
    masks = [key_mask(meta_ref, b * ROW_BLOCK) for b in range(blocks)]
    for g in range(group):
        columns = slice(g * HEAD_DIM, (g + 1) * HEAD_DIM)
        weight = load_weight(meta_ref, slot_refs, weight_ref, g, slots)
        own = own_ref[:, columns]
        extended = jnp.concatenate([before_ref[:, columns], own, after_ref[:, columns]], axis=0)
        query = dot_nn(own, weight[:, :HEAD_DIM]).astype(BF16)
        key_value = dot_nn(extended, weight[:, HEAD_DIM:]).astype(BF16)
        key, value = key_value[:, :HEAD_DIM], key_value[:, HEAD_DIM:]
        bias = toeplitz(offset_ref[g])
        for b in range(blocks):
            first = b * ROW_BLOCK
            window = slice(first, first + WINDOW)
            probs = block_probs(query[first : first + ROW_BLOCK], key[window], bias + masks[b])
            attended = dot_nn(probs.astype(BF16), value[window])
            kept = x_ref[first : first + ROW_BLOCK, columns].astype(F32)
            out_ref[first : first + ROW_BLOCK, columns] = (kept + attended).astype(BF16)


def column_spec(rows, group, first):
    return pl.BlockSpec((rows, group * HEAD_DIM), lambda i, meta: (0, i + first))


def slot_specs(weight_slots, group):
    return [
        pl.BlockSpec((3, group, slot.shape[2], HEAD_DIM), lambda i, meta: (0, i, 0, 0))
        for slot in weight_slots
    ]


def forward_attention(meta, before, own, after, x, offsets, weight_slots, group):
    rows, width = own.shape
    heads = width // HEAD_DIM
    slots = len(weight_slots)
    return pl.pallas_call(
        functools.partial(forward_kernel, slots, group),
        out_shape=jax.ShapeDtypeStruct((rows, width), BF16),
        grid_spec=pltpu.PrefetchScalarGridSpec(
            num_scalar_prefetch=1,
            grid=(heads // group,),
            in_specs=[
                column_spec(RADIUS, group, 0),
                column_spec(rows, group, 0),
                column_spec(RADIUS, group, 0),
                column_spec(rows, group, 0),
                pl.BlockSpec((group, 1, WINDOW), lambda i, meta: (i, 0, 0)),
                *slot_specs(weight_slots, group),
            ],
            out_specs=column_spec(rows, group, 0),
            scratch_shapes=[pltpu.VMEM((group, HEAD_DIM, 3 * HEAD_DIM), BF16)],
        ),
        compiler_params=pltpu.CompilerParams(vmem_limit_bytes=VMEM_LIMIT),
        cost_estimate=pl.CostEstimate(
            flops=heads * 60_000_000, bytes_accessed=8 * rows * width, transcendentals=heads * 32768
        ),
        name="forward_attention",
    )(meta, before, own, after, x, offsets, *weight_slots)


def backward_kernel(slots, group, meta_ref, before_ref, own_ref, after_ref, cot_ref, offset_ref, *rest):
    slot_refs = rest[:slots]
    rest = rest[slots:]
    grad_ref, lower_ref, upper_ref, offset_grad_ref = rest[:4]
    part_refs = rest[4 : 4 + slots]
    weight_ref, part_ref = rest[4 + slots :]
    rows = own_ref.shape[0]
    blocks = rows // ROW_BLOCK
    scale = HEAD_DIM ** (-0.5)
    masks = [key_mask(meta_ref, b * ROW_BLOCK) for b in range(blocks)]
    for g in range(group):
        columns = slice(g * HEAD_DIM, (g + 1) * HEAD_DIM)
        weight = load_weight(meta_ref, slot_refs, weight_ref, g, slots)
        own = own_ref[:, columns]
        extended = jnp.concatenate([before_ref[:, columns], own, after_ref[:, columns]], axis=0)
        query = dot_nn(own, weight[:, :HEAD_DIM]).astype(BF16)
        key_value = dot_nn(extended, weight[:, HEAD_DIM:]).astype(BF16)
        key, value = key_value[:, :HEAD_DIM], key_value[:, HEAD_DIM:]
        bias = toeplitz(offset_ref[g])
        grad_query, grad_key, grad_value, score_sum = [], [], [], None
        for b in range(blocks):
            first = b * ROW_BLOCK
            window = slice(first, first + WINDOW)
            query_rows = query[first : first + ROW_BLOCK]
            cot_rows = cot_ref[first : first + ROW_BLOCK, columns]
            probs = block_probs(query_rows, key[window], bias + masks[b])
            grad_probs = dot_nt(cot_rows, value[window])
            delta = jnp.sum(probs * grad_probs, axis=-1, keepdims=True)
            grad_scores = probs * (grad_probs - delta)
            score_sum = grad_scores if score_sum is None else score_sum + grad_scores
            grad_packed = grad_scores.astype(BF16)
            grad_query.append(dot_nn(grad_packed, key[window]))
            grad_key.append(dot_tn(grad_packed, query_rows))
            grad_value.append(dot_tn(probs.astype(BF16), cot_rows))

        def joined(parts):
            pieces = []
            for u in range((rows + 2 * RADIUS) // ROW_BLOCK):
                total = None
                for b in range(blocks):
                    if 0 <= u - b < WINDOW // ROW_BLOCK:
                        piece = parts[b][(u - b) * ROW_BLOCK : (u - b + 1) * ROW_BLOCK]
                        total = piece if total is None else total + piece
                pieces.append(total)
            return jnp.concatenate(pieces, axis=0)

        dquery = (jnp.concatenate(grad_query, axis=0) * scale).astype(BF16)
        dkey = (joined(grad_key) * scale).astype(BF16)
        dvalue = joined(grad_value).astype(BF16)
        dkey_value = jnp.concatenate([dkey, dvalue], axis=1)
        grad_extended = dot_nt(dkey_value, weight[:, HEAD_DIM:])
        grad_ref[:, columns] = grad_extended[RADIUS : RADIUS + rows] + dot_nt(dquery, weight[:, :HEAD_DIM])
        lower_ref[:, columns] = grad_extended[:RADIUS].astype(BF16)
        upper_ref[:, columns] = grad_extended[RADIUS + rows :].astype(BF16)
        part_ref[g, :, :HEAD_DIM] = dot_tn(own, dquery)
        part_ref[g, :, HEAD_DIM:] = dot_tn(extended, dkey_value)
        depth = HEAD_DIM // slots
        for r in range(slots):
            if slots == 1:
                start = 0
            else:
                start = pl.multiple_of(lax.rem(meta_ref[0] + r, slots) * depth, depth)
            for j in range(3):
                part_refs[r][j, g] = part_ref[
                    g, pl.ds(start, depth), j * HEAD_DIM : (j + 1) * HEAD_DIM
                ].astype(part_refs[r].dtype)
        offset_grad_ref[g] = diagonal_sums(score_sum)


def backward_attention(meta, before, own, after, cotangent, offsets, weight_slots, group, first_head, heads):
    rows = own.shape[0]
    width = heads * HEAD_DIM
    slots = len(weight_slots)
    first = first_head // group
    slot_shape = weight_slots[0].shape
    part_types = [F32] + [BF16] * (slots - 1) if slots > 1 else [BF16]
    return pl.pallas_call(
        functools.partial(backward_kernel, slots, group),
        out_shape=(
            jax.ShapeDtypeStruct((rows, width), F32),
            jax.ShapeDtypeStruct((RADIUS, width), BF16),
            jax.ShapeDtypeStruct((RADIUS, width), BF16),
            jax.ShapeDtypeStruct((heads, 1, WINDOW), F32),
            *[jax.ShapeDtypeStruct(slot_shape, kind) for kind in part_types],
        ),
        grid_spec=pltpu.PrefetchScalarGridSpec(
            num_scalar_prefetch=1,
            grid=(heads // group,),
            in_specs=[
                column_spec(RADIUS, group, first),
                column_spec(rows, group, first),
                column_spec(RADIUS, group, first),
                column_spec(rows, group, first),
                pl.BlockSpec((group, 1, WINDOW), lambda i, meta: (i + first, 0, 0)),
                *slot_specs(weight_slots, group),
            ],
            out_specs=(
                column_spec(rows, group, 0),
                column_spec(RADIUS, group, 0),
                column_spec(RADIUS, group, 0),
                pl.BlockSpec((group, 1, WINDOW), lambda i, meta: (i, 0, 0)),
                *slot_specs(weight_slots, group),
            ),
            scratch_shapes=[
                pltpu.VMEM((group, HEAD_DIM, 3 * HEAD_DIM), BF16),
                pltpu.VMEM((group, HEAD_DIM, 3 * HEAD_DIM), F32),
            ],
        ),
        compiler_params=pltpu.CompilerParams(vmem_limit_bytes=VMEM_LIMIT),
        cost_estimate=pl.CostEstimate(
            flops=heads * 150_000_000, bytes_accessed=12 * rows * width, transcendentals=heads * 32768
        ),
        name="backward_attention",
    )(meta, before, own, after, cotangent, offsets, *weight_slots)


def finish_kernel(grad_ref, low_ref, high_ref, x_ref, inverse_ref, gain_ref, cot_ref, out_ref, gain_grad_ref):
    rows = x_ref.shape[0]
    grad = grad_ref[...]
    edge = jnp.zeros((rows - RADIUS, grad.shape[1]), F32)
    grad = grad + jnp.concatenate([low_ref[...].astype(F32), edge], axis=0)
    grad = grad + jnp.concatenate([edge, high_ref[...].astype(F32)], axis=0)
    x = x_ref[...].astype(F32)
    inverse = inverse_ref[:, :1]
    gain_grad_ref[...] = jnp.sum(grad * x * inverse, axis=0, keepdims=True)
    scaled = grad * gain_ref[...]
    mean = jnp.mean(scaled * x, axis=-1, keepdims=True)
    result = inverse * scaled - x * (inverse * inverse * inverse * mean)
    out_ref[...] = (cot_ref[...].astype(F32) + result).astype(BF16)


def finish(grad, low, high, x, inverse, gain, cotangent):
    rows, width = x.shape
    return pl.pallas_call(
        finish_kernel,
        out_shape=(
            jax.ShapeDtypeStruct((rows, width), BF16),
            jax.ShapeDtypeStruct((1, width), F32),
        ),
        compiler_params=pltpu.CompilerParams(vmem_limit_bytes=VMEM_LIMIT),
        cost_estimate=pl.CostEstimate(
            flops=16 * rows * width, bytes_accessed=14 * rows * width, transcendentals=0
        ),
        name="finish",
    )(grad, low, high, x, inverse, gain, cotangent)


def column_of(row, rows):
    return jnp.transpose(jnp.broadcast_to(row, (128, rows)))


def split_rows(inverse, pad_rows, width):
    high = inverse.astype(BF16)
    rest = inverse - high.astype(F32)
    middle = rest.astype(BF16)
    low = (rest - middle.astype(F32)).astype(BF16)
    wide = [jnp.transpose(jnp.broadcast_to(v.astype(F32), (v.shape[0], 128)))[:1] for v in (high, middle, low)]
    row = jnp.concatenate(wide + [jnp.zeros((pad_rows - 3, wide[0].shape[1]), F32)], axis=0)
    return row.astype(BF16)


def row_inverse(x):
    x = x.astype(F32)
    return lax.rsqrt(jnp.mean(x * x, axis=-1, keepdims=True) + eps_norm)


def pack_stash_kernel(parts, meta_ref, x_ref, gain_ref, weight_ref, inverse_ref, *refs):
    out_refs, normed_ref = refs[:parts], refs[parts]
    rows, width = x_ref.shape
    depth = weight_ref.shape[2]
    wide = width // parts
    heads = wide // HEAD_DIM
    inverse = row_inverse(x_ref[...])
    inverse_ref[...] = jnp.broadcast_to(inverse, inverse_ref.shape)
    normed_ref[...] = (x_ref[...].astype(F32) * inverse * gain_ref[...]).astype(BF16)
    for r, out_ref in enumerate(out_refs):
        target = lax.rem(meta_ref[0] + r, parts)
        out_ref[:rows] = normed_ref[:, pl.ds(pl.multiple_of(target * wide, 128), wide)]
        for j in range(3):
            for h in range(heads):
                out_ref[rows + j * depth : rows + (j + 1) * depth, h * HEAD_DIM : (h + 1) * HEAD_DIM] = weight_ref[
                    j, target * heads + h
                ]


def pack_rows_kernel(parts, with_inverse, meta_ref, edge_ref, inner_ref, *out_refs):
    rows, width = inner_ref.shape
    wide = width // parts
    edge = 1 if with_inverse else 2
    refs = out_refs[:parts]
    for r, out_ref in enumerate(refs):
        target = lax.rem(meta_ref[0] + r, parts)
        start = pl.multiple_of(target * wide, 128)

        @pl.when(meta_ref[edge] == 1)
        def use_edge():
            out_ref[:rows] = edge_ref[:, pl.ds(start, wide)]

        @pl.when(meta_ref[edge] == 0)
        def use_inner():
            out_ref[:rows] = inner_ref[:, pl.ds(start, wide)]

    def finish_with(source_ref):
        if with_inverse:
            tail = split_rows(row_inverse(source_ref[...]), 16, wide)
            for out_ref in refs:
                out_ref[rows:] = jnp.zeros((16, wide), BF16)
                out_ref[rows:, :rows] = tail
        else:
            out_refs[parts][...] = source_ref[...]

    @pl.when(meta_ref[edge] == 1)
    def finish_edge():
        finish_with(edge_ref)

    @pl.when(meta_ref[edge] == 0)
    def finish_inner():
        finish_with(inner_ref)


SMEM_SPEC = pl.BlockSpec(memory_space=pltpu.SMEM)
VMEM_SPEC = pl.BlockSpec(memory_space=pltpu.VMEM)


def pack_stash(meta, x, gain, weight, parts):
    rows, width = x.shape
    depth = weight.shape[2]
    shape = (rows + 3 * depth, width // parts)
    return pl.pallas_call(
        functools.partial(pack_stash_kernel, parts),
        out_shape=(
            jax.ShapeDtypeStruct((rows, 128), F32),
            *[jax.ShapeDtypeStruct(shape, BF16) for r in range(parts)],
        ),
        in_specs=[SMEM_SPEC, VMEM_SPEC, VMEM_SPEC, VMEM_SPEC],
        out_specs=(VMEM_SPEC,) * (parts + 1),
        scratch_shapes=[pltpu.VMEM((rows, width), BF16)],
        compiler_params=pltpu.CompilerParams(vmem_limit_bytes=VMEM_LIMIT),
        cost_estimate=pl.CostEstimate(flops=4 * rows * width, bytes_accessed=6 * rows * width, transcendentals=0),
        name="pack_stash",
    )(meta, x, gain, weight)


def pack_rows(meta, edge, inner, parts, with_inverse):
    rows, width = inner.shape
    shape = (rows + (16 if with_inverse else 0), width // parts)
    extra = () if with_inverse else (jax.ShapeDtypeStruct((rows, width), BF16),)
    return pl.pallas_call(
        functools.partial(pack_rows_kernel, parts, with_inverse),
        out_shape=(*[jax.ShapeDtypeStruct(shape, BF16) for r in range(parts)], *extra),
        in_specs=[SMEM_SPEC, VMEM_SPEC, VMEM_SPEC],
        out_specs=(VMEM_SPEC,) * (parts + len(extra)),
        compiler_params=pltpu.CompilerParams(vmem_limit_bytes=VMEM_LIMIT),
        cost_estimate=pl.CostEstimate(flops=4 * rows * width, bytes_accessed=6 * rows * width, transcendentals=0),
        name="pack_inbound" if with_inverse else "pack_cotangent",
    )(meta, edge, inner)


def gather_rows(meta_ref, refs, rows, x_ref):
    parts = len(refs)
    for r, ref in enumerate(refs):
        source = lax.rem(meta_ref[0] + parts - r, parts)
        x_ref[pl.ds(pl.multiple_of(source * rows, rows), rows)] = ref[:rows]


def gather_weight(meta_ref, refs, rows, weight_ref):
    parts = len(refs)
    depth = HEAD_DIM // parts
    for r, ref in enumerate(refs):
        source = lax.rem(meta_ref[0] + parts - r, parts)
        depth_at = pl.ds(pl.multiple_of(source * depth, depth), depth)
        for j in range(3):
            weight_ref[depth_at, j * HEAD_DIM : (j + 1) * HEAD_DIM] = ref[
                rows + j * depth : rows + (j + 1) * depth
            ]


def gather_inverse(meta_ref, refs, rows, inverse_ref):
    parts = len(refs)

    @pl.when(pl.program_id(0) == 0)
    def spread_inverse():
        for r, ref in enumerate(refs):
            source = lax.rem(meta_ref[0] + parts - r, parts)
            tail = ref[rows : rows + 16].astype(F32)
            inverse_ref[pl.ds(pl.multiple_of(source * rows, rows), rows)] = column_of(
                tail[:1] + tail[1:2] + tail[2:3], rows
            )


def block_mask(first_query, tokens):
    key = lax.broadcasted_iota(jnp.int32, (1, WINDOW), 1) + (first_query - RADIUS)
    return jnp.where((key >= 0) & (key < tokens), 0.0, masked_score).astype(F32)


def edge_bias(bias, first, tokens):
    if first < RADIUS or first + ROW_BLOCK + RADIUS > tokens:
        return bias + block_mask(first, tokens)
    return bias


def padded(rows):
    edge = jnp.zeros((RADIUS, rows.shape[1]), rows.dtype)
    return jnp.concatenate([edge, rows, edge], axis=0)


def heads_backward_kernel(parts, rows, meta_ref, *refs):
    a_refs, c_refs = refs[:parts], refs[parts : 2 * parts]
    gain_ref, offset_ref, onehot_ref, after_ref = refs[2 * parts : 2 * parts + 4]
    out_refs = refs[2 * parts + 4 : 3 * parts + 4]
    gain_grad_ref, x_ref, weight_ref, cot_ref, grad_ref, part_ref, bias_ref = refs[3 * parts + 4 :]
    tokens = rows * parts
    depth = HEAD_DIM // parts
    scale = HEAD_DIM ** (-0.5)
    gather_rows(meta_ref, a_refs, rows, x_ref)
    gather_weight(meta_ref, a_refs, rows, weight_ref)
    gather_rows(meta_ref, c_refs, rows, cot_ref)
    weight = weight_ref[...]
    normed = x_ref[...]
    query = dot_nn(normed, weight[:, :HEAD_DIM]).astype(BF16)
    key = padded(dot_nn(normed, weight[:, HEAD_DIM : 2 * HEAD_DIM]).astype(BF16))
    value = padded(dot_nn(normed, weight[:, 2 * HEAD_DIM :]).astype(BF16))
    bias = toeplitz(offset_ref[0])
    blocks = tokens // ROW_BLOCK
    grad_query, grad_key, grad_value, score_sum = [], [], [], None
    for b in range(blocks):
        first = b * ROW_BLOCK
        window = slice(first, first + WINDOW)
        query_rows = query[first : first + ROW_BLOCK]
        cot_rows = cot_ref[first : first + ROW_BLOCK]
        probs = block_probs(query_rows, key[window], edge_bias(bias, first, tokens))
        grad_probs = dot_nt(cot_rows, value[window])
        delta = jnp.sum(probs * grad_probs, axis=-1, keepdims=True)
        grad_scores = probs * (grad_probs - delta)
        score_sum = grad_scores if score_sum is None else score_sum + grad_scores
        grad_packed = grad_scores.astype(BF16)
        grad_query.append(dot_nn(grad_packed, key[window]))
        grad_key.append(dot_tn(grad_packed, query_rows))
        grad_value.append(dot_tn(probs.astype(BF16), cot_rows))

    def joined(pieces):
        units = []
        for u in range((tokens + 2 * RADIUS) // ROW_BLOCK):
            total = None
            for b in range(blocks):
                if 0 <= u - b < WINDOW // ROW_BLOCK:
                    piece = pieces[b][(u - b) * ROW_BLOCK : (u - b + 1) * ROW_BLOCK]
                    total = piece if total is None else total + piece
            units.append(total)
        return jnp.concatenate(units, axis=0)[RADIUS : RADIUS + tokens]

    dqkv = jnp.concatenate(
        [
            (jnp.concatenate(grad_query, axis=0) * scale).astype(BF16),
            (joined(grad_key) * scale).astype(BF16),
            joined(grad_value).astype(BF16),
        ],
        axis=1,
    )
    grad_normed = dot_nt(dqkv, weight)
    gain_grad_ref[...] = jnp.sum(grad_normed * normed.astype(F32), axis=0, keepdims=True) / gain_ref[...]
    grad_ref[...] = grad_normed
    part_ref[...] = dot_tn(normed, dqkv)
    bias_grad = jnp.sum(onehot_ref[...] * diagonal_sums(score_sum), axis=1, keepdims=True)
    bias_ref[...] = jnp.broadcast_to(bias_grad, bias_ref.shape)
    buckets = bias_ref.shape[0] // parts
    for r, out_ref in enumerate(out_refs):
        source = lax.rem(meta_ref[0] + parts - r, parts)
        out_ref[:rows] = grad_ref[pl.ds(pl.multiple_of(source * rows, rows), rows)].astype(BF16)
        for j in range(3):
            out_ref[rows + j * depth : rows + (j + 1) * depth] = part_ref[
                pl.ds(pl.multiple_of(source * depth, depth), depth), j * HEAD_DIM : (j + 1) * HEAD_DIM
            ].astype(BF16)
        share = bias_ref[pl.ds(pl.multiple_of(source * buckets, buckets), buckets)]
        out_ref[rows + 3 * depth :] = jnp.concatenate(
            [share, jnp.zeros((16 - buckets, HEAD_DIM), F32)], axis=0
        ).astype(BF16)


def head_column(rows, first=0):
    return pl.BlockSpec((rows, HEAD_DIM), lambda i, meta: (0, i + first))


def whole_column(rows, heads, first=0):
    return pl.BlockSpec((rows, HEAD_DIM), lambda i, meta: (0, meta[0] * heads + first + i))


def offset_spec(heads, first=0):
    return pl.BlockSpec((1, 1, WINDOW), lambda i, meta: (meta[0] * heads + first + i, 0, 0))


def heads_backward(meta, a_slots, c_slots, gain, offsets, onehot, after, heads, first, count):
    parts = len(a_slots)
    rows = c_slots[0].shape[0]
    tokens = rows * parts
    buckets = onehot.shape[0]
    packed = a_slots[0].shape[0]
    made = packed + 16
    width = count * HEAD_DIM
    return pl.pallas_call(
        functools.partial(heads_backward_kernel, parts, rows),
        out_shape=(
            *[jax.ShapeDtypeStruct((made, width), BF16) for r in range(parts)],
            jax.ShapeDtypeStruct((1, width), F32),
        ),
        grid_spec=pltpu.PrefetchScalarGridSpec(
            num_scalar_prefetch=1,
            grid=(count,),
            in_specs=[
                *[head_column(packed, first)] * parts,
                whole_column(rows, heads, first),
                *[head_column(rows, first)] * (parts - 1),
                whole_column(1, heads, first),
                offset_spec(heads, first),
                pl.BlockSpec((buckets, WINDOW), lambda i, meta: (0, 0)),
                pl.BlockSpec(memory_space=pl.ANY),
            ],
            out_specs=(*[head_column(made)] * parts, head_column(1)),
            scratch_shapes=[
                pltpu.VMEM((tokens, HEAD_DIM), BF16),
                pltpu.VMEM((HEAD_DIM, 3 * HEAD_DIM), BF16),
                pltpu.VMEM((tokens, HEAD_DIM), BF16),
                pltpu.VMEM((tokens, HEAD_DIM), F32),
                pltpu.VMEM((HEAD_DIM, 3 * HEAD_DIM), F32),
                pltpu.VMEM((buckets, HEAD_DIM), F32),
            ],
        ),
        compiler_params=pltpu.CompilerParams(vmem_limit_bytes=VMEM_LIMIT),
        cost_estimate=pl.CostEstimate(
            flops=count * tokens * 400_000, bytes_accessed=tokens * width, transcendentals=0
        ),
        name="heads_backward",
    )(meta, *a_slots, *c_slots, gain, offsets, onehot, after)


def heads_forward_kernel(parts, rows, meta_ref, *refs):
    a_refs, i_refs = refs[:parts], refs[parts : 2 * parts]
    gain_ref, offset_ref = refs[2 * parts : 2 * parts + 2]
    out_refs = refs[2 * parts + 2 : 3 * parts + 2]
    inverse_ref, x_ref, weight_ref, made_ref, square_ref = refs[3 * parts + 2 :]
    tokens = rows * parts
    gather_rows(meta_ref, i_refs, rows, x_ref)
    gather_weight(meta_ref, a_refs, rows, weight_ref)
    gather_inverse(meta_ref, i_refs, rows, inverse_ref)
    weight = weight_ref[...]
    normed = (x_ref[...].astype(F32) * inverse_ref[...] * gain_ref[...]).astype(BF16)
    query = dot_nn(normed, weight[:, :HEAD_DIM]).astype(BF16)
    key = padded(dot_nn(normed, weight[:, HEAD_DIM : 2 * HEAD_DIM]).astype(BF16))
    value = padded(dot_nn(normed, weight[:, 2 * HEAD_DIM :]).astype(BF16))
    bias = toeplitz(offset_ref[0])
    for b in range(tokens // ROW_BLOCK):
        first = b * ROW_BLOCK
        window = slice(first, first + WINDOW)
        probs = block_probs(query[first : first + ROW_BLOCK], key[window], edge_bias(bias, first, tokens))
        attended = dot_nn(probs.astype(BF16), value[window])
        made_ref[first : first + ROW_BLOCK] = (
            x_ref[first : first + ROW_BLOCK].astype(F32) + attended
        ).astype(BF16)
    made = made_ref[...].astype(F32)
    squares = made * made

    @pl.when(pl.program_id(0) == 0)
    def first_head():
        square_ref[...] = squares

    @pl.when(pl.program_id(0) > 0)
    def later_head():
        square_ref[...] += squares

    for r, out_ref in enumerate(out_refs):
        source = lax.rem(meta_ref[0] + parts - r, parts)
        out_ref[:rows] = made_ref[pl.ds(pl.multiple_of(source * rows, rows), rows)]

    @pl.when(pl.program_id(0) == pl.num_programs(0) - 1)
    def last_head():
        total = jnp.sum(jnp.transpose(square_ref[...]), axis=0, keepdims=True)
        at_row = lax.broadcasted_iota(jnp.int32, (16, rows), 0)
        tail = jnp.zeros((16, rows), F32)
        rest = total
        for k in range(3):
            piece = rest.astype(BF16).astype(F32)
            rest = rest - piece
            for part in range(parts):
                row = jnp.broadcast_to(piece[:, part * rows : (part + 1) * rows], (16, rows))
                tail = jnp.where(at_row == 3 * part + k, row, tail)
        for out_ref in out_refs:
            out_ref[rows:] = tail.astype(BF16)


def heads_forward(meta, a_slots, i_slots, gain, offsets, heads, rows):
    parts = len(a_slots)
    tokens = rows * parts
    packed = a_slots[0].shape[0]
    width = heads * HEAD_DIM
    return pl.pallas_call(
        functools.partial(heads_forward_kernel, parts, rows),
        out_shape=(
            *[jax.ShapeDtypeStruct((rows + 16, width), BF16) for r in range(parts)],
        ),
        grid_spec=pltpu.PrefetchScalarGridSpec(
            num_scalar_prefetch=1,
            grid=(heads,),
            in_specs=[
                *[head_column(packed)] * parts,
                *[head_column(i_slots[0].shape[0])] * parts,
                whole_column(1, heads),
                offset_spec(heads),
            ],
            out_specs=(head_column(rows + 16),) * parts,
            scratch_shapes=[
                pltpu.VMEM((tokens, HEAD_DIM), F32),
                pltpu.VMEM((tokens, HEAD_DIM), BF16),
                pltpu.VMEM((HEAD_DIM, 3 * HEAD_DIM), BF16),
                pltpu.VMEM((tokens, HEAD_DIM), BF16),
                pltpu.VMEM((tokens, HEAD_DIM), F32),
            ],
        ),
        compiler_params=pltpu.CompilerParams(vmem_limit_bytes=VMEM_LIMIT),
        cost_estimate=pl.CostEstimate(
            flops=heads * tokens, bytes_accessed=tokens, transcendentals=0
        ),
        name="heads_forward",
    )(meta, *a_slots, *i_slots, gain, offsets)


def memory_kernel(parts, width, meta_ref, *refs):
    out_refs, other_refs = refs[:parts], refs[parts : 2 * parts - 1]
    gain_ref, *share_refs, memory_ref = refs[2 * parts - 1 :]
    wide = memory_ref.shape[1]
    rows = memory_ref.shape[0] // parts
    total = None
    for ref in (out_refs[0], *other_refs):
        tail = ref[rows:, wide - rows :].astype(F32)
        pieces = [
            tail[3 * p : 3 * p + 1] + tail[3 * p + 1 : 3 * p + 2] + tail[3 * p + 2 : 3 * p + 3]
            for p in range(parts)
        ]
        row = jnp.concatenate(pieces, axis=1)
        total = row if total is None else total + row
    inverse = lax.rsqrt(total / width + eps_norm)
    gain = gain_ref[:, pl.ds(pl.multiple_of(meta_ref[0] * wide, 128), wide)]
    spread_inverse = jnp.transpose(jnp.broadcast_to(inverse, (128, inverse.shape[1])))
    for r, out_ref in enumerate(out_refs):
        source = lax.rem(meta_ref[0] + parts - r, parts)
        memory_ref[pl.ds(pl.multiple_of(source * rows, rows), rows)] = out_ref[:rows]
    made = memory_ref[...].astype(F32)
    memory_ref[...] = (made * spread_inverse[:, :1] * gain).astype(BF16)
    for k, share_ref in enumerate(share_refs):
        size = share_ref.shape[0]
        share_ref[...] = memory_ref[k * size : (k + 1) * size]


def memory_rows(meta, outs, others, gain, width, shares):
    parts = len(outs)
    rows, wide = outs[0].shape[0] - 16, outs[0].shape[1]
    return pl.pallas_call(
        functools.partial(memory_kernel, parts, width),
        out_shape=[jax.ShapeDtypeStruct((rows * parts // shares, wide), BF16)] * shares,
        in_specs=[SMEM_SPEC] + [VMEM_SPEC] * (2 * parts),
        out_specs=[VMEM_SPEC] * shares,
        scratch_shapes=[pltpu.VMEM((rows * parts, wide), BF16)],
        compiler_params=pltpu.CompilerParams(vmem_limit_bytes=VMEM_LIMIT),
        cost_estimate=pl.CostEstimate(flops=rows, bytes_accessed=rows, transcendentals=0),
        name="memory_rows",
    )(meta, *outs, *others, gain)


def place_kernel(parts, meta_ref, *refs):
    out_ref = refs[parts]
    wide = refs[0].shape[1]
    for r in range(parts):
        source = lax.rem(meta_ref[0] + r, parts)
        out_ref[:, pl.ds(pl.multiple_of(source * wide, 128), wide)] = refs[r][: out_ref.shape[0]]


def place_columns(meta, slots):
    parts = len(slots)
    rows, wide = slots[0].shape[0] - 16, slots[0].shape[1]
    return pl.pallas_call(
        functools.partial(place_kernel, parts),
        out_shape=jax.ShapeDtypeStruct((rows, wide * parts), BF16),
        in_specs=[SMEM_SPEC] + [VMEM_SPEC] * parts,
        out_specs=VMEM_SPEC,
        compiler_params=pltpu.CompilerParams(vmem_limit_bytes=VMEM_LIMIT),
        cost_estimate=pl.CostEstimate(flops=0, bytes_accessed=rows, transcendentals=0),
        name="place_columns",
    )(meta, *slots)


def heads_finish_kernel(parts, chunks, meta_ref, *refs):
    g_refs = refs[: parts * chunks]
    x_ref, inverse_ref, gain_ref, cot_ref, out_ref, weight_ref, bias_ref, scaled_ref = refs[parts * chunks :]
    rows, width = x_ref.shape
    wide = width // parts // chunks
    heads = wide // HEAD_DIM
    depth = HEAD_DIM // parts
    buckets = bias_ref.shape[1]
    for c in range(chunks):
        for r in range(parts):
            g_ref = g_refs[c * parts + r]
            place = lax.rem(meta_ref[0] + r, parts) * chunks + c
            columns = pl.ds(pl.multiple_of(place * wide, 128), wide)
            scaled_ref[:, columns] = g_ref[:rows].astype(F32) * gain_ref[:, columns]
            for h in range(heads):
                lanes = slice(h * HEAD_DIM, (h + 1) * HEAD_DIM)
                for j in range(3):
                    weight_ref[j, place * heads + h] = g_ref[
                        rows + j * depth : rows + (j + 1) * depth, lanes
                    ].astype(F32)
                bias_ref[place * heads + h] = g_ref[rows + 3 * depth :, lanes].astype(F32)[:buckets]
    x = x_ref[...].astype(F32)
    scaled = scaled_ref[...]
    inverse = inverse_ref[:, :1]
    mean = jnp.mean(scaled * x, axis=-1, keepdims=True)
    result = inverse * scaled - x * (inverse * inverse * inverse * mean)
    out_ref[...] = (cot_ref[...].astype(F32) + result).astype(BF16)


def heads_finish(meta, g_chunks, x, inverse, gain, cotangent, buckets):
    chunks, parts = len(g_chunks), len(g_chunks[0])
    rows, width = x.shape
    heads = width // HEAD_DIM
    slots = [slot for g_slots in g_chunks for slot in g_slots]
    return pl.pallas_call(
        functools.partial(heads_finish_kernel, parts, chunks),
        out_shape=(
            jax.ShapeDtypeStruct((rows, width), BF16),
            jax.ShapeDtypeStruct((3, heads, HEAD_DIM // parts, HEAD_DIM), F32),
            jax.ShapeDtypeStruct((heads, buckets // parts, HEAD_DIM), F32),
        ),
        in_specs=[SMEM_SPEC] + [VMEM_SPEC] * (len(slots) + 4),
        out_specs=(VMEM_SPEC,) * 3,
        scratch_shapes=[pltpu.VMEM((rows, width), F32)],
        compiler_params=pltpu.CompilerParams(vmem_limit_bytes=VMEM_LIMIT),
        cost_estimate=pl.CostEstimate(flops=12 * rows * width, bytes_accessed=14 * rows * width, transcendentals=0),
        name="heads_finish",
    )(meta, *slots, x, inverse, gain, cotangent)


def offset_table(rel_bias):
    onehot = jnp.asarray(bucket_onehot(rel_bias.shape[0]))
    by_offset = jnp.dot(onehot, rel_bias, precision=lax.Precision.HIGHEST).T
    inside = jnp.arange(WINDOW, dtype=jnp.int32) <= 2 * RADIUS
    return jnp.where(inside[None, :], by_offset, masked_score)[:, None, :]


def shifted(value, axis, steps):
    count = lax.axis_size(axis)
    first, last = (max(0, -steps), min(count, count - steps))
    return lax.ppermute(value, axis, [(source, source + steps) for source in range(first, last)])


def spread_memory(shares, section, sections):
    last = sections - 1
    if len(shares) == sections:
        memory = jnp.where(section == last, shares[last], 0)
        for s in range(last):
            memory = memory + lax.ppermute(shares[s], "section", [(last, s)])
        return memory
    couple = jnp.where(section == last, shares[-1], 0)
    for s, share in enumerate(shares[:-1]):
        couple = couple + lax.ppermute(share, "section", [(last, 2 * s + 1)])
    half = couple.shape[0] // 2
    even = lax.ppermute(couple[:half], "section", [(s + 1, s) for s in range(0, sections, 2)])
    return jnp.where(section % 2 == 0, even, couple[half:])


def heads_body(
    embedded, carried, stash, returned, loss_grad, qkv_weight, rel_bias, norm_gain, final_gain
):
    section = lax.axis_index("section")
    sections = lax.axis_size("section")
    parts = lax.axis_size("seq")
    rows, width = embedded.shape
    heads = width // HEAD_DIM // parts
    buckets = rel_bias.shape[1]
    meta = jnp.stack(
        [lax.axis_index("seq"), section == 0, section == sections - 1]
    ).astype(jnp.int32)

    def exchanged(sends, direction):
        moved = [
            lax.ppermute(sends[r], "seq", [(i, (i + direction * r) % parts) for i in range(parts)])
            for r in range(1, parts)
        ]
        return [sends[0]] + moved

    inverse_b, *a_sends = pack_stash(meta, stash[0], norm_gain, qkv_weight[0], parts)
    a_slots = exchanged(a_sends, 1)
    kept, gone, inverse_b = lax.optimization_barrier((carried[0], returned[0], inverse_b))
    arrived = shifted(kept, "section", 1)
    came_back = shifted(gone, "section", -1)
    i_slots = exchanged(pack_rows(meta, embedded, arrived, parts, True), 1)
    *c_sends, cotangent = pack_rows(meta, loss_grad, came_back, parts, False)
    c_slots = exchanged(c_sends, 1)
    c_slots[0] = cotangent

    offsets = offset_table(rel_bias[0])
    onehot = jnp.asarray(bucket_onehot(buckets).T)
    o_sends = heads_forward(meta, a_slots, i_slots, norm_gain, offsets, heads, rows)
    o_sends, c_slots = lax.optimization_barrier((o_sends, c_slots))
    o_slots = exchanged(o_sends, -1)

    chunks = 2 if heads % 2 == 0 else 1
    count = heads // chunks

    def backward(c, after):
        return heads_backward(
            meta, a_slots, c_slots, norm_gain, offsets, onehot, after, heads, c * count, count
        )

    *g_sends, gain_grad = backward(0, o_sends[0])
    g_sends, o_slots = lax.optimization_barrier((g_sends, o_slots))
    g_chunks = [exchanged(g_sends, -1)]
    output = place_columns(meta, o_slots)
    shares = sections // 2 if sections % 2 == 0 else sections
    made = memory_rows(meta, o_sends, o_slots[1:], final_gain[None], width, shares)
    if chunks == 2:
        *g_sends, gain_part = backward(1, output)
        g_sends, made, g_chunks = lax.optimization_barrier((g_sends, made, g_chunks))
        g_chunks.append(exchanged(g_sends, -1))
        gain_grad = jnp.concatenate([gain_grad, gain_part], axis=1)
    memory = spread_memory(made, section, sections)

    input_grad, weight_grad, bias_wide = heads_finish(
        meta, g_chunks, stash[0], inverse_b, norm_gain, cotangent, buckets
    )
    bias_grad = bias_wide[:, :, 0].T
    return (
        output[None],
        input_grad[None],
        weight_grad[None],
        bias_grad[None],
        gain_grad,
        memory,
    )


def tokens_body(
    embedded, carried, stash, returned, loss_grad, qkv_weight, rel_bias, norm_gain, final_gain
):
    section_index = lax.axis_index("section")
    section_count = lax.axis_size("section")
    seq_index = lax.axis_index("seq")
    seq_count = lax.axis_size("seq")
    rows, width = embedded.shape
    heads = width // HEAD_DIM
    tokens = rows * seq_count
    shard = qkv_weight[0]
    up = [(i, i + 1) for i in range(seq_count - 1)]
    down = [(j, i) for i, j in up]
    group = 4 if heads % 4 == 0 else 1

    own_b, inverse_b = norm_rows(stash[0], norm_gain)
    before_b = lax.ppermute(own_b[rows - RADIUS :], "seq", up)
    after_b = lax.ppermute(own_b[:RADIUS], "seq", down)
    slots = [lax.all_gather(shard, "seq", axis=2, tiled=True)]

    section_up = [(i, (i + 1) % section_count) for i in range(section_count)]
    section_down = [(j, i) for i, j in section_up]
    inbound = lax.ppermute(
        jnp.where(section_index == section_count - 1, embedded, carried[0]), "section", section_up
    )
    cotangent = lax.ppermute(
        jnp.where(section_index == 0, loss_grad, returned[0]), "section", section_down
    )

    onehot = jnp.asarray(bucket_onehot(rel_bias.shape[1]))
    offsets = offset_table(rel_bias[0])
    first_key = RADIUS - seq_index * rows
    meta = jnp.stack([seq_index, first_key, first_key + tokens]).astype(jnp.int32)

    own_a, unused = norm_rows(inbound, norm_gain)
    before_a = lax.ppermute(own_a[rows - RADIUS :], "seq", up)
    after_a = lax.ppermute(own_a[:RADIUS], "seq", down)

    grad_own, lower, upper, offset_grad, *parts = backward_attention(
        meta, before_b, own_b, after_b, cotangent, offsets, slots, group, 0, heads
    )
    from_before = lax.ppermute(upper, "seq", up)
    from_after = lax.ppermute(lower, "seq", down)
    weight_sum = lax.psum_scatter(parts[0], "seq", scatter_dimension=2, tiled=True).astype(F32)

    output = forward_attention(meta, before_a, own_a, after_a, inbound, offsets, slots, group)
    final_normed, unused = norm_rows(output, final_gain[None])
    relaid = lax.all_to_all(final_normed, "seq", split_axis=1, concat_axis=0, tiled=True)
    kept = jnp.where(section_index == section_count - 1, relaid, jnp.zeros_like(relaid))
    memory = lax.psum_scatter(kept, "section", scatter_dimension=0, tiled=True)

    input_grad, gain_part = finish(
        grad_own, from_before, from_after, stash[0], inverse_b, norm_gain, cotangent
    )
    bias_part = jnp.dot(
        offset_grad[:, 0, :], onehot, precision=lax.Precision.HIGHEST
    ).T
    bias_sum = lax.psum_scatter(
        bias_part.astype(BF16), "seq", scatter_dimension=0, tiled=True
    ).astype(F32)
    gain_sum = lax.psum_scatter(
        gain_part.astype(BF16), "seq", scatter_dimension=1, tiled=True
    ).astype(F32)
    return (output[None], input_grad[None], weight_sum[None], bias_sum[None], gain_sum, memory)


def choose_body(embedded, carried, stash, returned, loss_grad, qkv_weight, rel_bias, norm_gain, final_gain):
    parts = lax.axis_size("seq")
    rows, width = embedded.shape
    even = width % (HEAD_DIM * parts) == 0 and HEAD_DIM % (32 * parts) == 0 and rows == 128
    even = even and rel_bias.shape[1] == 8 * parts and rows * parts % (16 * lax.axis_size("section")) == 0
    chosen = heads_body if even else tokens_body
    return chosen(
        embedded, carried, stash, returned, loss_grad, qkv_weight, rel_bias, norm_gain, final_gain
    )


def solution(mesh):
    in_specs = (
        P("seq", None),
        P("section", "seq", None),
        P("section", "seq", None),
        P("section", "seq", None),
        P("seq", None),
        P("section", None, None, "seq", None),
        P("section", None, None),
        P("section", None),
        P(),
    )
    out_specs = (
        P("section", "seq", None),
        P("section", "seq", None),
        P("section", None, None, "seq", None),
        P("section", "seq", None),
        P("section", "seq"),
        P("section", "seq"),
    )
    return jax.shard_map(choose_body, mesh=mesh, in_specs=in_specs, out_specs=out_specs, check_vma=False)
```

```python
import functools

import jax
import jax.numpy as jnp
import numpy as np
from jax import lax
from jax.experimental import pallas as pl
from jax.experimental.pallas import tpu as pltpu
from jax.sharding import PartitionSpec as P

RADIUS = 96
HEAD_DIM = 128
ROW_BLOCK = 64
WINDOW = ROW_BLOCK + 2 * RADIUS
eps_norm = 1e-06
bucket_edges = (1, 2, 3, 4, 5, 6, 7, 8, 11, 16, 22, 32, 45, 64, 90)
masked_score = -1e30
F32 = jnp.float32
BF16 = jnp.bfloat16
VMEM_LIMIT = 24 * 1024 * 1024


def bucket_onehot(bucket_count):
    offsets = np.arange(WINDOW) - RADIUS
    magnitude = np.abs(offsets)
    counted = np.zeros(offsets.shape, np.int32)
    for threshold in bucket_edges:
        counted = counted + (magnitude >= threshold)
    counted = counted + 16 * (offsets > 0)
    onehot = (counted[:, None] == np.arange(bucket_count)[None, :]) & (magnitude <= RADIUS)[:, None]
    return onehot.astype(np.float32)


def dot_nn(a, b):
    return lax.dot_general(a, b, (((1,), (0,)), ((), ())), preferred_element_type=F32)


def dot_nt(a, b):
    return lax.dot_general(a, b, (((1,), (1,)), ((), ())), preferred_element_type=F32)


def dot_tn(a, b):
    return lax.dot_general(a, b, (((0,), (0,)), ((), ())), preferred_element_type=F32)


def norm_kernel(x_ref, gain_ref, normed_ref, inverse_ref):
    x = x_ref[...].astype(F32)
    inverse = lax.rsqrt(jnp.mean(x * x, axis=-1, keepdims=True) + eps_norm)
    normed_ref[...] = (x * inverse * gain_ref[...]).astype(BF16)
    inverse_ref[...] = jnp.broadcast_to(inverse, inverse_ref.shape)


def norm_rows(x, gain):
    rows, width = x.shape
    return pl.pallas_call(
        norm_kernel,
        out_shape=(
            jax.ShapeDtypeStruct((rows, width), BF16),
            jax.ShapeDtypeStruct((rows, 128), F32),
        ),
        compiler_params=pltpu.CompilerParams(vmem_limit_bytes=VMEM_LIMIT),
        cost_estimate=pl.CostEstimate(
            flops=6 * rows * width, bytes_accessed=4 * rows * width, transcendentals=rows
        ),
        name="norm_rows",
    )(x, gain)


def load_weight(meta_ref, slot_refs, weight_ref, head, slots):
    depth = HEAD_DIM // slots
    for r, slot_ref in enumerate(slot_refs):
        if slots == 1:
            start = 0
        else:
            start = pl.multiple_of(lax.rem(meta_ref[0] + r, slots) * depth, depth)
        for j in range(3):
            weight_ref[head, pl.ds(start, depth), j * HEAD_DIM : (j + 1) * HEAD_DIM] = slot_ref[j, head]
    return weight_ref[head]


def key_mask(meta_ref, first_key):
    key = lax.broadcasted_iota(jnp.int32, (1, WINDOW), 1) + first_key
    inside = (key >= meta_ref[1]) & (key < meta_ref[2])
    return jnp.where(inside, 0.0, masked_score).astype(F32)


def toeplitz(row):
    return pltpu.roll(
        jnp.broadcast_to(row, (ROW_BLOCK, WINDOW)), 0, 1, stride=1, stride_axis=0
    )


def diagonal_sums(values):
    total = values[:8]
    for a in range(1, ROW_BLOCK // 8):
        total = total + pltpu.roll(values[8 * a : 8 * a + 8], WINDOW - 8 * a, 1)
    row = lax.broadcasted_iota(jnp.int32, total.shape, 0)
    for bit in (1, 2, 4):
        total = jnp.where((row & bit) != 0, pltpu.roll(total, WINDOW - bit, 1), total)
    return jnp.sum(total, axis=0, keepdims=True)


def block_probs(query_rows, key_rows, bias):
    scores = dot_nt(query_rows, key_rows) * (HEAD_DIM ** (-0.5)) + bias
    weights = jnp.exp(scores - jnp.max(scores, axis=-1, keepdims=True))
    return weights * (1.0 / jnp.sum(weights, axis=-1, keepdims=True))


def forward_kernel(slots, group, meta_ref, before_ref, own_ref, after_ref, x_ref, offset_ref, *rest):
    slot_refs = rest[:slots]
    out_ref, weight_ref = rest[slots:]
    rows = own_ref.shape[0]
    blocks = rows // ROW_BLOCK
    masks = [key_mask(meta_ref, b * ROW_BLOCK) for b in range(blocks)]
    for g in range(group):
        columns = slice(g * HEAD_DIM, (g + 1) * HEAD_DIM)
        weight = load_weight(meta_ref, slot_refs, weight_ref, g, slots)
        own = own_ref[:, columns]
        extended = jnp.concatenate([before_ref[:, columns], own, after_ref[:, columns]], axis=0)
        query = dot_nn(own, weight[:, :HEAD_DIM]).astype(BF16)
        key_value = dot_nn(extended, weight[:, HEAD_DIM:]).astype(BF16)
        key, value = key_value[:, :HEAD_DIM], key_value[:, HEAD_DIM:]
        bias = toeplitz(offset_ref[g])
        for b in range(blocks):
            first = b * ROW_BLOCK
            window = slice(first, first + WINDOW)
            probs = block_probs(query[first : first + ROW_BLOCK], key[window], bias + masks[b])
            attended = dot_nn(probs.astype(BF16), value[window])
            kept = x_ref[first : first + ROW_BLOCK, columns].astype(F32)
            out_ref[first : first + ROW_BLOCK, columns] = (kept + attended).astype(BF16)


def column_spec(rows, group, first):
    return pl.BlockSpec((rows, group * HEAD_DIM), lambda i, meta: (0, i + first))


def slot_specs(weight_slots, group):
    return [
        pl.BlockSpec((3, group, slot.shape[2], HEAD_DIM), lambda i, meta: (0, i, 0, 0))
        for slot in weight_slots
    ]


def forward_attention(meta, before, own, after, x, offsets, weight_slots, group):
    rows, width = own.shape
    heads = width // HEAD_DIM
    slots = len(weight_slots)
    return pl.pallas_call(
        functools.partial(forward_kernel, slots, group),
        out_shape=jax.ShapeDtypeStruct((rows, width), BF16),
        grid_spec=pltpu.PrefetchScalarGridSpec(
            num_scalar_prefetch=1,
            grid=(heads // group,),
            in_specs=[
                column_spec(RADIUS, group, 0),
                column_spec(rows, group, 0),
                column_spec(RADIUS, group, 0),
                column_spec(rows, group, 0),
                pl.BlockSpec((group, 1, WINDOW), lambda i, meta: (i, 0, 0)),
                *slot_specs(weight_slots, group),
            ],
            out_specs=column_spec(rows, group, 0),
            scratch_shapes=[pltpu.VMEM((group, HEAD_DIM, 3 * HEAD_DIM), BF16)],
        ),
        compiler_params=pltpu.CompilerParams(vmem_limit_bytes=VMEM_LIMIT),
        cost_estimate=pl.CostEstimate(
            flops=heads * 60_000_000, bytes_accessed=8 * rows * width, transcendentals=heads * 32768
        ),
        name="forward_attention",
    )(meta, before, own, after, x, offsets, *weight_slots)


def backward_kernel(slots, group, meta_ref, before_ref, own_ref, after_ref, cot_ref, offset_ref, *rest):
    slot_refs = rest[:slots]
    rest = rest[slots:]
    grad_ref, lower_ref, upper_ref, offset_grad_ref = rest[:4]
    part_refs = rest[4 : 4 + slots]
    weight_ref, part_ref = rest[4 + slots :]
    rows = own_ref.shape[0]
    blocks = rows // ROW_BLOCK
    scale = HEAD_DIM ** (-0.5)
    masks = [key_mask(meta_ref, b * ROW_BLOCK) for b in range(blocks)]
    for g in range(group):
        columns = slice(g * HEAD_DIM, (g + 1) * HEAD_DIM)
        weight = load_weight(meta_ref, slot_refs, weight_ref, g, slots)
        own = own_ref[:, columns]
        extended = jnp.concatenate([before_ref[:, columns], own, after_ref[:, columns]], axis=0)
        query = dot_nn(own, weight[:, :HEAD_DIM]).astype(BF16)
        key_value = dot_nn(extended, weight[:, HEAD_DIM:]).astype(BF16)
        key, value = key_value[:, :HEAD_DIM], key_value[:, HEAD_DIM:]
        bias = toeplitz(offset_ref[g])
        grad_query, grad_key, grad_value, score_sum = [], [], [], None
        for b in range(blocks):
            first = b * ROW_BLOCK
            window = slice(first, first + WINDOW)
            query_rows = query[first : first + ROW_BLOCK]
            cot_rows = cot_ref[first : first + ROW_BLOCK, columns]
            probs = block_probs(query_rows, key[window], bias + masks[b])
            grad_probs = dot_nt(cot_rows, value[window])
            delta = jnp.sum(probs * grad_probs, axis=-1, keepdims=True)
            grad_scores = probs * (grad_probs - delta)
            score_sum = grad_scores if score_sum is None else score_sum + grad_scores
            grad_packed = grad_scores.astype(BF16)
            grad_query.append(dot_nn(grad_packed, key[window]))
            grad_key.append(dot_tn(grad_packed, query_rows))
            grad_value.append(dot_tn(probs.astype(BF16), cot_rows))

        def joined(parts):
            pieces = []
            for u in range((rows + 2 * RADIUS) // ROW_BLOCK):
                total = None
                for b in range(blocks):
                    if 0 <= u - b < WINDOW // ROW_BLOCK:
                        piece = parts[b][(u - b) * ROW_BLOCK : (u - b + 1) * ROW_BLOCK]
                        total = piece if total is None else total + piece
                pieces.append(total)
            return jnp.concatenate(pieces, axis=0)

        dquery = (jnp.concatenate(grad_query, axis=0) * scale).astype(BF16)
        dkey = (joined(grad_key) * scale).astype(BF16)
        dvalue = joined(grad_value).astype(BF16)
        dkey_value = jnp.concatenate([dkey, dvalue], axis=1)
        grad_extended = dot_nt(dkey_value, weight[:, HEAD_DIM:])
        grad_ref[:, columns] = grad_extended[RADIUS : RADIUS + rows] + dot_nt(dquery, weight[:, :HEAD_DIM])
        lower_ref[:, columns] = grad_extended[:RADIUS].astype(BF16)
        upper_ref[:, columns] = grad_extended[RADIUS + rows :].astype(BF16)
        part_ref[g, :, :HEAD_DIM] = dot_tn(own, dquery)
        part_ref[g, :, HEAD_DIM:] = dot_tn(extended, dkey_value)
        depth = HEAD_DIM // slots
        for r in range(slots):
            if slots == 1:
                start = 0
            else:
                start = pl.multiple_of(lax.rem(meta_ref[0] + r, slots) * depth, depth)
            for j in range(3):
                part_refs[r][j, g] = part_ref[
                    g, pl.ds(start, depth), j * HEAD_DIM : (j + 1) * HEAD_DIM
                ].astype(part_refs[r].dtype)
        offset_grad_ref[g] = diagonal_sums(score_sum)


def backward_attention(meta, before, own, after, cotangent, offsets, weight_slots, group, first_head, heads):
    rows = own.shape[0]
    width = heads * HEAD_DIM
    slots = len(weight_slots)
    first = first_head // group
    slot_shape = weight_slots[0].shape
    part_types = [F32] + [BF16] * (slots - 1) if slots > 1 else [BF16]
    return pl.pallas_call(
        functools.partial(backward_kernel, slots, group),
        out_shape=(
            jax.ShapeDtypeStruct((rows, width), F32),
            jax.ShapeDtypeStruct((RADIUS, width), BF16),
            jax.ShapeDtypeStruct((RADIUS, width), BF16),
            jax.ShapeDtypeStruct((heads, 1, WINDOW), F32),
            *[jax.ShapeDtypeStruct(slot_shape, kind) for kind in part_types],
        ),
        grid_spec=pltpu.PrefetchScalarGridSpec(
            num_scalar_prefetch=1,
            grid=(heads // group,),
            in_specs=[
                column_spec(RADIUS, group, first),
                column_spec(rows, group, first),
                column_spec(RADIUS, group, first),
                column_spec(rows, group, first),
                pl.BlockSpec((group, 1, WINDOW), lambda i, meta: (i + first, 0, 0)),
                *slot_specs(weight_slots, group),
            ],
            out_specs=(
                column_spec(rows, group, 0),
                column_spec(RADIUS, group, 0),
                column_spec(RADIUS, group, 0),
                pl.BlockSpec((group, 1, WINDOW), lambda i, meta: (i, 0, 0)),
                *slot_specs(weight_slots, group),
            ),
            scratch_shapes=[
                pltpu.VMEM((group, HEAD_DIM, 3 * HEAD_DIM), BF16),
                pltpu.VMEM((group, HEAD_DIM, 3 * HEAD_DIM), F32),
            ],
        ),
        compiler_params=pltpu.CompilerParams(vmem_limit_bytes=VMEM_LIMIT),
        cost_estimate=pl.CostEstimate(
            flops=heads * 150_000_000, bytes_accessed=12 * rows * width, transcendentals=heads * 32768
        ),
        name="backward_attention",
    )(meta, before, own, after, cotangent, offsets, *weight_slots)


def finish_kernel(grad_ref, low_ref, high_ref, x_ref, inverse_ref, gain_ref, cot_ref, out_ref, gain_grad_ref):
    rows = x_ref.shape[0]
    grad = grad_ref[...]
    edge = jnp.zeros((rows - RADIUS, grad.shape[1]), F32)
    grad = grad + jnp.concatenate([low_ref[...].astype(F32), edge], axis=0)
    grad = grad + jnp.concatenate([edge, high_ref[...].astype(F32)], axis=0)
    x = x_ref[...].astype(F32)
    inverse = inverse_ref[:, :1]
    gain_grad_ref[...] = jnp.sum(grad * x * inverse, axis=0, keepdims=True)
    scaled = grad * gain_ref[...]
    mean = jnp.mean(scaled * x, axis=-1, keepdims=True)
    result = inverse * scaled - x * (inverse * inverse * inverse * mean)
    out_ref[...] = (cot_ref[...].astype(F32) + result).astype(BF16)


def finish(grad, low, high, x, inverse, gain, cotangent):
    rows, width = x.shape
    return pl.pallas_call(
        finish_kernel,
        out_shape=(
            jax.ShapeDtypeStruct((rows, width), BF16),
            jax.ShapeDtypeStruct((1, width), F32),
        ),
        compiler_params=pltpu.CompilerParams(vmem_limit_bytes=VMEM_LIMIT),
        cost_estimate=pl.CostEstimate(
            flops=16 * rows * width, bytes_accessed=14 * rows * width, transcendentals=0
        ),
        name="finish",
    )(grad, low, high, x, inverse, gain, cotangent)


def column_of(row, rows):
    return jnp.transpose(jnp.broadcast_to(row, (128, rows)))


def split_rows(inverse, pad_rows, width):
    high = inverse.astype(BF16)
    rest = inverse - high.astype(F32)
    middle = rest.astype(BF16)
    low = (rest - middle.astype(F32)).astype(BF16)
    wide = [jnp.transpose(jnp.broadcast_to(v.astype(F32), (v.shape[0], 128)))[:1] for v in (high, middle, low)]
    row = jnp.concatenate(wide + [jnp.zeros((pad_rows - 3, wide[0].shape[1]), F32)], axis=0)
    return row.astype(BF16)


def row_inverse(x):
    x = x.astype(F32)
    return lax.rsqrt(jnp.mean(x * x, axis=-1, keepdims=True) + eps_norm)


def pack_stash_kernel(parts, meta_ref, x_ref, gain_ref, weight_ref, inverse_ref, *refs):
    out_refs, normed_ref = refs[:parts], refs[parts]
    rows, width = x_ref.shape
    depth = weight_ref.shape[2]
    wide = width // parts
    heads = wide // HEAD_DIM
    inverse = row_inverse(x_ref[...])
    inverse_ref[...] = jnp.broadcast_to(inverse, inverse_ref.shape)
    normed_ref[...] = (x_ref[...].astype(F32) * inverse * gain_ref[...]).astype(BF16)
    for r, out_ref in enumerate(out_refs):
        target = lax.rem(meta_ref[0] + r, parts)
        out_ref[:rows] = normed_ref[:, pl.ds(pl.multiple_of(target * wide, 128), wide)]
        for j in range(3):
            for h in range(heads):
                out_ref[rows + j * depth : rows + (j + 1) * depth, h * HEAD_DIM : (h + 1) * HEAD_DIM] = weight_ref[
                    j, target * heads + h
                ]


def pack_rows_kernel(parts, with_inverse, meta_ref, edge_ref, inner_ref, *out_refs):
    rows, width = inner_ref.shape
    wide = width // parts
    edge = 1 if with_inverse else 2
    refs = out_refs[:parts]
    for r, out_ref in enumerate(refs):
        target = lax.rem(meta_ref[0] + r, parts)
        start = pl.multiple_of(target * wide, 128)

        @pl.when(meta_ref[edge] == 1)
        def use_edge():
            out_ref[:rows] = edge_ref[:, pl.ds(start, wide)]

        @pl.when(meta_ref[edge] == 0)
        def use_inner():
            out_ref[:rows] = inner_ref[:, pl.ds(start, wide)]

    def finish_with(source_ref):
        if with_inverse:
            tail = split_rows(row_inverse(source_ref[...]), 16, wide)
            for out_ref in refs:
                out_ref[rows:] = jnp.zeros((16, wide), BF16)
                out_ref[rows:, :rows] = tail
        else:
            out_refs[parts][...] = source_ref[...]

    @pl.when(meta_ref[edge] == 1)
    def finish_edge():
        finish_with(edge_ref)

    @pl.when(meta_ref[edge] == 0)
    def finish_inner():
        finish_with(inner_ref)


SMEM_SPEC = pl.BlockSpec(memory_space=pltpu.SMEM)
VMEM_SPEC = pl.BlockSpec(memory_space=pltpu.VMEM)


def pack_stash(meta, x, gain, weight, parts):
    rows, width = x.shape
    depth = weight.shape[2]
    shape = (rows + 3 * depth, width // parts)
    return pl.pallas_call(
        functools.partial(pack_stash_kernel, parts),
        out_shape=(
            jax.ShapeDtypeStruct((rows, 128), F32),
            *[jax.ShapeDtypeStruct(shape, BF16) for r in range(parts)],
        ),
        in_specs=[SMEM_SPEC, VMEM_SPEC, VMEM_SPEC, VMEM_SPEC],
        out_specs=(VMEM_SPEC,) * (parts + 1),
        scratch_shapes=[pltpu.VMEM((rows, width), BF16)],
        compiler_params=pltpu.CompilerParams(vmem_limit_bytes=VMEM_LIMIT),
        cost_estimate=pl.CostEstimate(flops=4 * rows * width, bytes_accessed=6 * rows * width, transcendentals=0),
        name="pack_stash",
    )(meta, x, gain, weight)


def pack_rows(meta, edge, inner, parts, with_inverse):
    rows, width = inner.shape
    shape = (rows + (16 if with_inverse else 0), width // parts)
    extra = () if with_inverse else (jax.ShapeDtypeStruct((rows, width), BF16),)
    return pl.pallas_call(
        functools.partial(pack_rows_kernel, parts, with_inverse),
        out_shape=(*[jax.ShapeDtypeStruct(shape, BF16) for r in range(parts)], *extra),
        in_specs=[SMEM_SPEC, VMEM_SPEC, VMEM_SPEC],
        out_specs=(VMEM_SPEC,) * (parts + len(extra)),
        compiler_params=pltpu.CompilerParams(vmem_limit_bytes=VMEM_LIMIT),
        cost_estimate=pl.CostEstimate(flops=4 * rows * width, bytes_accessed=6 * rows * width, transcendentals=0),
        name="pack_inbound" if with_inverse else "pack_cotangent",
    )(meta, edge, inner)


def gather_rows(meta_ref, refs, rows, x_ref):
    parts = len(refs)
    for r, ref in enumerate(refs):
        source = lax.rem(meta_ref[0] + parts - r, parts)
        x_ref[pl.ds(pl.multiple_of(source * rows, rows), rows)] = ref[:rows]


def gather_weight(meta_ref, refs, rows, weight_ref):
    parts = len(refs)
    depth = HEAD_DIM // parts
    for r, ref in enumerate(refs):
        source = lax.rem(meta_ref[0] + parts - r, parts)
        depth_at = pl.ds(pl.multiple_of(source * depth, depth), depth)
        for j in range(3):
            weight_ref[depth_at, j * HEAD_DIM : (j + 1) * HEAD_DIM] = ref[
                rows + j * depth : rows + (j + 1) * depth
            ]


def gather_inverse(meta_ref, refs, rows, inverse_ref):
    parts = len(refs)

    @pl.when(pl.program_id(0) == 0)
    def spread_inverse():
        for r, ref in enumerate(refs):
            source = lax.rem(meta_ref[0] + parts - r, parts)
            tail = ref[rows : rows + 16].astype(F32)
            inverse_ref[pl.ds(pl.multiple_of(source * rows, rows), rows)] = column_of(
                tail[:1] + tail[1:2] + tail[2:3], rows
            )


def block_mask(first_query, tokens):
    key = lax.broadcasted_iota(jnp.int32, (1, WINDOW), 1) + (first_query - RADIUS)
    return jnp.where((key >= 0) & (key < tokens), 0.0, masked_score).astype(F32)


def edge_bias(bias, first, tokens):
    if first < RADIUS or first + ROW_BLOCK + RADIUS > tokens:
        return bias + block_mask(first, tokens)
    return bias


def padded(rows):
    edge = jnp.zeros((RADIUS, rows.shape[1]), rows.dtype)
    return jnp.concatenate([edge, rows, edge], axis=0)


def heads_backward_kernel(parts, rows, meta_ref, *refs):
    a_refs, c_refs = refs[:parts], refs[parts : 2 * parts]
    gain_ref, offset_ref, onehot_ref, after_ref = refs[2 * parts : 2 * parts + 4]
    out_refs = refs[2 * parts + 4 : 3 * parts + 4]
    gain_grad_ref, x_ref, weight_ref, cot_ref, grad_ref, part_ref, bias_ref = refs[3 * parts + 4 :]
    tokens = rows * parts
    depth = HEAD_DIM // parts
    scale = HEAD_DIM ** (-0.5)
    gather_rows(meta_ref, a_refs, rows, x_ref)
    gather_weight(meta_ref, a_refs, rows, weight_ref)
    gather_rows(meta_ref, c_refs, rows, cot_ref)
    weight = weight_ref[...]
    normed = x_ref[...]
    query = dot_nn(normed, weight[:, :HEAD_DIM]).astype(BF16)
    key = padded(dot_nn(normed, weight[:, HEAD_DIM : 2 * HEAD_DIM]).astype(BF16))
    value = padded(dot_nn(normed, weight[:, 2 * HEAD_DIM :]).astype(BF16))
    bias = toeplitz(offset_ref[0])
    blocks = tokens // ROW_BLOCK
    grad_query, grad_key, grad_value, score_sum = [], [], [], None
    for b in range(blocks):
        first = b * ROW_BLOCK
        window = slice(first, first + WINDOW)
        query_rows = query[first : first + ROW_BLOCK]
        cot_rows = cot_ref[first : first + ROW_BLOCK]
        probs = block_probs(query_rows, key[window], edge_bias(bias, first, tokens))
        grad_probs = dot_nt(cot_rows, value[window])
        delta = jnp.sum(probs * grad_probs, axis=-1, keepdims=True)
        grad_scores = probs * (grad_probs - delta)
        score_sum = grad_scores if score_sum is None else score_sum + grad_scores
        grad_packed = grad_scores.astype(BF16)
        grad_query.append(dot_nn(grad_packed, key[window]))
        grad_key.append(dot_tn(grad_packed, query_rows))
        grad_value.append(dot_tn(probs.astype(BF16), cot_rows))

    def joined(pieces):
        units = []
        for u in range((tokens + 2 * RADIUS) // ROW_BLOCK):
            total = None
            for b in range(blocks):
                if 0 <= u - b < WINDOW // ROW_BLOCK:
                    piece = pieces[b][(u - b) * ROW_BLOCK : (u - b + 1) * ROW_BLOCK]
                    total = piece if total is None else total + piece
            units.append(total)
        return jnp.concatenate(units, axis=0)[RADIUS : RADIUS + tokens]

    dqkv = jnp.concatenate(
        [
            (jnp.concatenate(grad_query, axis=0) * scale).astype(BF16),
            (joined(grad_key) * scale).astype(BF16),
            joined(grad_value).astype(BF16),
        ],
        axis=1,
    )
    grad_normed = dot_nt(dqkv, weight)
    gain_grad_ref[...] = jnp.sum(grad_normed * normed.astype(F32), axis=0, keepdims=True) / gain_ref[...]
    grad_ref[...] = grad_normed
    part_ref[...] = dot_tn(normed, dqkv)
    bias_grad = jnp.sum(onehot_ref[...] * diagonal_sums(score_sum), axis=1, keepdims=True)
    bias_ref[...] = jnp.broadcast_to(bias_grad, bias_ref.shape)
    buckets = bias_ref.shape[0] // parts
    for r, out_ref in enumerate(out_refs):
        source = lax.rem(meta_ref[0] + parts - r, parts)
        out_ref[:rows] = grad_ref[pl.ds(pl.multiple_of(source * rows, rows), rows)].astype(BF16)
        for j in range(3):
            out_ref[rows + j * depth : rows + (j + 1) * depth] = part_ref[
                pl.ds(pl.multiple_of(source * depth, depth), depth), j * HEAD_DIM : (j + 1) * HEAD_DIM
            ].astype(BF16)
        share = bias_ref[pl.ds(pl.multiple_of(source * buckets, buckets), buckets)]
        out_ref[rows + 3 * depth :] = jnp.concatenate(
            [share, jnp.zeros((16 - buckets, HEAD_DIM), F32)], axis=0
        ).astype(BF16)


def head_column(rows, first=0):
    return pl.BlockSpec((rows, HEAD_DIM), lambda i, meta: (0, i + first))


def whole_column(rows, heads, first=0):
    return pl.BlockSpec((rows, HEAD_DIM), lambda i, meta: (0, meta[0] * heads + first + i))


def offset_spec(heads, first=0):
    return pl.BlockSpec((1, 1, WINDOW), lambda i, meta: (meta[0] * heads + first + i, 0, 0))


def heads_backward(meta, a_slots, c_slots, gain, offsets, onehot, after, heads, first, count):
    parts = len(a_slots)
    rows = c_slots[0].shape[0]
    tokens = rows * parts
    buckets = onehot.shape[0]
    packed = a_slots[0].shape[0]
    made = packed + 16
    width = count * HEAD_DIM
    return pl.pallas_call(
        functools.partial(heads_backward_kernel, parts, rows),
        out_shape=(
            *[jax.ShapeDtypeStruct((made, width), BF16) for r in range(parts)],
            jax.ShapeDtypeStruct((1, width), F32),
        ),
        grid_spec=pltpu.PrefetchScalarGridSpec(
            num_scalar_prefetch=1,
            grid=(count,),
            in_specs=[
                *[head_column(packed, first)] * parts,
                whole_column(rows, heads, first),
                *[head_column(rows, first)] * (parts - 1),
                whole_column(1, heads, first),
                offset_spec(heads, first),
                pl.BlockSpec((buckets, WINDOW), lambda i, meta: (0, 0)),
                pl.BlockSpec(memory_space=pl.ANY),
            ],
            out_specs=(*[head_column(made)] * parts, head_column(1)),
            scratch_shapes=[
                pltpu.VMEM((tokens, HEAD_DIM), BF16),
                pltpu.VMEM((HEAD_DIM, 3 * HEAD_DIM), BF16),
                pltpu.VMEM((tokens, HEAD_DIM), BF16),
                pltpu.VMEM((tokens, HEAD_DIM), F32),
                pltpu.VMEM((HEAD_DIM, 3 * HEAD_DIM), F32),
                pltpu.VMEM((buckets, HEAD_DIM), F32),
            ],
        ),
        compiler_params=pltpu.CompilerParams(vmem_limit_bytes=VMEM_LIMIT),
        cost_estimate=pl.CostEstimate(
            flops=count * tokens * 400_000, bytes_accessed=tokens * width, transcendentals=0
        ),
        name="heads_backward",
    )(meta, *a_slots, *c_slots, gain, offsets, onehot, after)


def heads_forward_kernel(parts, rows, meta_ref, *refs):
    a_refs, i_refs = refs[:parts], refs[parts : 2 * parts]
    gain_ref, offset_ref = refs[2 * parts : 2 * parts + 2]
    out_refs = refs[2 * parts + 2 : 3 * parts + 2]
    inverse_ref, x_ref, weight_ref, made_ref, square_ref = refs[3 * parts + 2 :]
    tokens = rows * parts
    gather_rows(meta_ref, i_refs, rows, x_ref)
    gather_weight(meta_ref, a_refs, rows, weight_ref)
    gather_inverse(meta_ref, i_refs, rows, inverse_ref)
    weight = weight_ref[...]
    normed = (x_ref[...].astype(F32) * inverse_ref[...] * gain_ref[...]).astype(BF16)
    query = dot_nn(normed, weight[:, :HEAD_DIM]).astype(BF16)
    key = padded(dot_nn(normed, weight[:, HEAD_DIM : 2 * HEAD_DIM]).astype(BF16))
    value = padded(dot_nn(normed, weight[:, 2 * HEAD_DIM :]).astype(BF16))
    bias = toeplitz(offset_ref[0])
    for b in range(tokens // ROW_BLOCK):
        first = b * ROW_BLOCK
        window = slice(first, first + WINDOW)
        probs = block_probs(query[first : first + ROW_BLOCK], key[window], edge_bias(bias, first, tokens))
        attended = dot_nn(probs.astype(BF16), value[window])
        made_ref[first : first + ROW_BLOCK] = (
            x_ref[first : first + ROW_BLOCK].astype(F32) + attended
        ).astype(BF16)
    made = made_ref[...].astype(F32)
    squares = made * made

    @pl.when(pl.program_id(0) == 0)
    def first_head():
        square_ref[...] = squares

    @pl.when(pl.program_id(0) > 0)
    def later_head():
        square_ref[...] += squares

    for r, out_ref in enumerate(out_refs):
        source = lax.rem(meta_ref[0] + parts - r, parts)
        out_ref[:rows] = made_ref[pl.ds(pl.multiple_of(source * rows, rows), rows)]

    @pl.when(pl.program_id(0) == pl.num_programs(0) - 1)
    def last_head():
        total = jnp.sum(jnp.transpose(square_ref[...]), axis=0, keepdims=True)
        at_row = lax.broadcasted_iota(jnp.int32, (16, rows), 0)
        tail = jnp.zeros((16, rows), F32)
        rest = total
        for k in range(3):
            piece = rest.astype(BF16).astype(F32)
            rest = rest - piece
            for part in range(parts):
                row = jnp.broadcast_to(piece[:, part * rows : (part + 1) * rows], (16, rows))
                tail = jnp.where(at_row == 3 * part + k, row, tail)
        for out_ref in out_refs:
            out_ref[rows:] = tail.astype(BF16)


def heads_forward(meta, a_slots, i_slots, gain, offsets, heads, rows):
    parts = len(a_slots)
    tokens = rows * parts
    packed = a_slots[0].shape[0]
    width = heads * HEAD_DIM
    return pl.pallas_call(
        functools.partial(heads_forward_kernel, parts, rows),
        out_shape=(
            *[jax.ShapeDtypeStruct((rows + 16, width), BF16) for r in range(parts)],
        ),
        grid_spec=pltpu.PrefetchScalarGridSpec(
            num_scalar_prefetch=1,
            grid=(heads,),
            in_specs=[
                *[head_column(packed)] * parts,
                *[head_column(i_slots[0].shape[0])] * parts,
                whole_column(1, heads),
                offset_spec(heads),
            ],
            out_specs=(head_column(rows + 16),) * parts,
            scratch_shapes=[
                pltpu.VMEM((tokens, HEAD_DIM), F32),
                pltpu.VMEM((tokens, HEAD_DIM), BF16),
                pltpu.VMEM((HEAD_DIM, 3 * HEAD_DIM), BF16),
                pltpu.VMEM((tokens, HEAD_DIM), BF16),
                pltpu.VMEM((tokens, HEAD_DIM), F32),
            ],
        ),
        compiler_params=pltpu.CompilerParams(vmem_limit_bytes=VMEM_LIMIT),
        cost_estimate=pl.CostEstimate(
            flops=heads * tokens, bytes_accessed=tokens, transcendentals=0
        ),
        name="heads_forward",
    )(meta, *a_slots, *i_slots, gain, offsets)


def memory_kernel(parts, width, meta_ref, *refs):
    out_refs, other_refs = refs[:parts], refs[parts : 2 * parts - 1]
    gain_ref, *share_refs, memory_ref = refs[2 * parts - 1 :]
    wide = memory_ref.shape[1]
    rows = memory_ref.shape[0] // parts
    total = None
    for ref in (out_refs[0], *other_refs):
        tail = ref[rows:, wide - rows :].astype(F32)
        pieces = [
            tail[3 * p : 3 * p + 1] + tail[3 * p + 1 : 3 * p + 2] + tail[3 * p + 2 : 3 * p + 3]
            for p in range(parts)
        ]
        row = jnp.concatenate(pieces, axis=1)
        total = row if total is None else total + row
    inverse = lax.rsqrt(total / width + eps_norm)
    gain = gain_ref[:, pl.ds(pl.multiple_of(meta_ref[0] * wide, 128), wide)]
    spread_inverse = jnp.transpose(jnp.broadcast_to(inverse, (128, inverse.shape[1])))
    for r, out_ref in enumerate(out_refs):
        source = lax.rem(meta_ref[0] + parts - r, parts)
        memory_ref[pl.ds(pl.multiple_of(source * rows, rows), rows)] = out_ref[:rows]
    made = memory_ref[...].astype(F32)
    memory_ref[...] = (made * spread_inverse[:, :1] * gain).astype(BF16)
    for k, share_ref in enumerate(share_refs):
        size = share_ref.shape[0]
        share_ref[...] = memory_ref[k * size : (k + 1) * size]


def memory_rows(meta, outs, others, gain, width, shares):
    parts = len(outs)
    rows, wide = outs[0].shape[0] - 16, outs[0].shape[1]
    return pl.pallas_call(
        functools.partial(memory_kernel, parts, width),
        out_shape=[jax.ShapeDtypeStruct((rows * parts // shares, wide), BF16)] * shares,
        in_specs=[SMEM_SPEC] + [VMEM_SPEC] * (2 * parts),
        out_specs=[VMEM_SPEC] * shares,
        scratch_shapes=[pltpu.VMEM((rows * parts, wide), BF16)],
        compiler_params=pltpu.CompilerParams(vmem_limit_bytes=VMEM_LIMIT),
        cost_estimate=pl.CostEstimate(flops=rows, bytes_accessed=rows, transcendentals=0),
        name="memory_rows",
    )(meta, *outs, *others, gain)


def place_kernel(parts, meta_ref, *refs):
    out_ref = refs[parts]
    wide = refs[0].shape[1]
    for r in range(parts):
        source = lax.rem(meta_ref[0] + r, parts)
        out_ref[:, pl.ds(pl.multiple_of(source * wide, 128), wide)] = refs[r][: out_ref.shape[0]]


def place_columns(meta, slots):
    parts = len(slots)
    rows, wide = slots[0].shape[0] - 16, slots[0].shape[1]
    return pl.pallas_call(
        functools.partial(place_kernel, parts),
        out_shape=jax.ShapeDtypeStruct((rows, wide * parts), BF16),
        in_specs=[SMEM_SPEC] + [VMEM_SPEC] * parts,
        out_specs=VMEM_SPEC,
        compiler_params=pltpu.CompilerParams(vmem_limit_bytes=VMEM_LIMIT),
        cost_estimate=pl.CostEstimate(flops=0, bytes_accessed=rows, transcendentals=0),
        name="place_columns",
    )(meta, *slots)


def heads_finish_kernel(parts, chunks, meta_ref, *refs):
    g_refs = refs[: parts * chunks]
    x_ref, inverse_ref, gain_ref, cot_ref, out_ref, weight_ref, bias_ref, scaled_ref = refs[parts * chunks :]
    rows, width = x_ref.shape
    wide = width // parts // chunks
    heads = wide // HEAD_DIM
    depth = HEAD_DIM // parts
    buckets = bias_ref.shape[1]
    for c in range(chunks):
        for r in range(parts):
            g_ref = g_refs[c * parts + r]
            place = lax.rem(meta_ref[0] + r, parts) * chunks + c
            columns = pl.ds(pl.multiple_of(place * wide, 128), wide)
            scaled_ref[:, columns] = g_ref[:rows].astype(F32) * gain_ref[:, columns]
            for h in range(heads):
                lanes = slice(h * HEAD_DIM, (h + 1) * HEAD_DIM)
                for j in range(3):
                    weight_ref[j, place * heads + h] = g_ref[
                        rows + j * depth : rows + (j + 1) * depth, lanes
                    ].astype(F32)
                bias_ref[place * heads + h] = g_ref[rows + 3 * depth :, lanes].astype(F32)[:buckets]
    x = x_ref[...].astype(F32)
    scaled = scaled_ref[...]
    inverse = inverse_ref[:, :1]
    mean = jnp.mean(scaled * x, axis=-1, keepdims=True)
    result = inverse * scaled - x * (inverse * inverse * inverse * mean)
    out_ref[...] = (cot_ref[...].astype(F32) + result).astype(BF16)


def heads_finish(meta, g_chunks, x, inverse, gain, cotangent, buckets):
    chunks, parts = len(g_chunks), len(g_chunks[0])
    rows, width = x.shape
    heads = width // HEAD_DIM
    slots = [slot for g_slots in g_chunks for slot in g_slots]
    return pl.pallas_call(
        functools.partial(heads_finish_kernel, parts, chunks),
        out_shape=(
            jax.ShapeDtypeStruct((rows, width), BF16),
            jax.ShapeDtypeStruct((3, heads, HEAD_DIM // parts, HEAD_DIM), F32),
            jax.ShapeDtypeStruct((heads, buckets // parts, HEAD_DIM), F32),
        ),
        in_specs=[SMEM_SPEC] + [VMEM_SPEC] * (len(slots) + 4),
        out_specs=(VMEM_SPEC,) * 3,
        scratch_shapes=[pltpu.VMEM((rows, width), F32)],
        compiler_params=pltpu.CompilerParams(vmem_limit_bytes=VMEM_LIMIT),
        cost_estimate=pl.CostEstimate(flops=12 * rows * width, bytes_accessed=14 * rows * width, transcendentals=0),
        name="heads_finish",
    )(meta, *slots, x, inverse, gain, cotangent)


def offset_table(rel_bias):
    onehot = jnp.asarray(bucket_onehot(rel_bias.shape[0]))
    by_offset = jnp.dot(onehot, rel_bias, precision=lax.Precision.HIGHEST).T
    inside = jnp.arange(WINDOW, dtype=jnp.int32) <= 2 * RADIUS
    return jnp.where(inside[None, :], by_offset, masked_score)[:, None, :]


def shifted(value, axis, steps):
    count = lax.axis_size(axis)
    first, last = (max(0, -steps), min(count, count - steps))
    return lax.ppermute(value, axis, [(source, source + steps) for source in range(first, last)])


def spread_memory(lower, upper, section, sections, later):
    size = sections
    while True:
        half = size // 2
        pairs = [(top, top - half) for top in range(size - 1, sections, size)]
        got = lax.ppermute(lower, "section", pairs)
        if size == sections:
            got, later = lax.optimization_barrier((got, later))
        held = jnp.where(section % size == size - 1, upper, got)
        if half == 1:
            return held
        middle = held.shape[0] // 2
        lower, upper, size = held[:middle], held[middle:], half


def heads_body(
    embedded, carried, stash, returned, loss_grad, qkv_weight, rel_bias, norm_gain, final_gain
):
    section = lax.axis_index("section")
    sections = lax.axis_size("section")
    parts = lax.axis_size("seq")
    rows, width = embedded.shape
    heads = width // HEAD_DIM // parts
    buckets = rel_bias.shape[1]
    meta = jnp.stack(
        [lax.axis_index("seq"), section == 0, section == sections - 1]
    ).astype(jnp.int32)

    def exchanged(sends, direction):
        moved = [
            lax.ppermute(sends[r], "seq", [(i, (i + direction * r) % parts) for i in range(parts)])
            for r in range(1, parts)
        ]
        return [sends[0]] + moved

    inverse_b, *a_sends = pack_stash(meta, stash[0], norm_gain, qkv_weight[0], parts)
    a_slots = exchanged(a_sends, 1)
    arrived = shifted(carried[0], "section", 1)
    came_back = shifted(returned[0], "section", -1)
    i_slots = exchanged(pack_rows(meta, embedded, arrived, parts, True), 1)
    *c_sends, cotangent = pack_rows(meta, loss_grad, came_back, parts, False)
    c_sends, a_slots, i_slots = lax.optimization_barrier((c_sends, a_slots, i_slots))
    c_slots = exchanged(c_sends, 1)
    c_slots[0] = cotangent

    offsets = offset_table(rel_bias[0])
    onehot = jnp.asarray(bucket_onehot(buckets).T)
    o_sends = heads_forward(meta, a_slots, i_slots, norm_gain, offsets, heads, rows)
    o_sends, c_slots = lax.optimization_barrier((o_sends, c_slots))
    o_slots = exchanged(o_sends, -1)

    chunks = 2 if heads % 2 == 0 else 1
    count = heads // chunks

    def backward(c, after):
        return heads_backward(
            meta, a_slots, c_slots, norm_gain, offsets, onehot, after, heads, c * count, count
        )

    *g_sends, gain_grad = backward(0, o_sends[0])
    g_sends, o_slots = lax.optimization_barrier((g_sends, o_slots))
    g_chunks = [exchanged(g_sends, -1)]
    output = place_columns(meta, o_slots)
    lower, upper = memory_rows(meta, o_sends, o_slots[1:], final_gain[None], width, 2)
    if chunks == 2:
        *g_sends, gain_part = backward(1, output)
        g_sends, g_chunks = lax.optimization_barrier((g_sends, g_chunks))
        g_chunks.append(exchanged(g_sends, -1))
        gain_grad = jnp.concatenate([gain_grad, gain_part], axis=1)
    memory = spread_memory(lower, upper, section, sections, g_chunks[0])

    input_grad, weight_grad, bias_wide = heads_finish(
        meta, g_chunks, stash[0], inverse_b, norm_gain, cotangent, buckets
    )
    bias_grad = bias_wide[:, :, 0].T
    return (
        output[None],
        input_grad[None],
        weight_grad[None],
        bias_grad[None],
        gain_grad,
        memory,
    )


def tokens_body(
    embedded, carried, stash, returned, loss_grad, qkv_weight, rel_bias, norm_gain, final_gain
):
    section_index = lax.axis_index("section")
    section_count = lax.axis_size("section")
    seq_index = lax.axis_index("seq")
    seq_count = lax.axis_size("seq")
    rows, width = embedded.shape
    heads = width // HEAD_DIM
    tokens = rows * seq_count
    shard = qkv_weight[0]
    up = [(i, i + 1) for i in range(seq_count - 1)]
    down = [(j, i) for i, j in up]
    group = 4 if heads % 4 == 0 else 1

    own_b, inverse_b = norm_rows(stash[0], norm_gain)
    before_b = lax.ppermute(own_b[rows - RADIUS :], "seq", up)
    after_b = lax.ppermute(own_b[:RADIUS], "seq", down)
    slots = [lax.all_gather(shard, "seq", axis=2, tiled=True)]

    section_up = [(i, (i + 1) % section_count) for i in range(section_count)]
    section_down = [(j, i) for i, j in section_up]
    inbound = lax.ppermute(
        jnp.where(section_index == section_count - 1, embedded, carried[0]), "section", section_up
    )
    cotangent = lax.ppermute(
        jnp.where(section_index == 0, loss_grad, returned[0]), "section", section_down
    )

    onehot = jnp.asarray(bucket_onehot(rel_bias.shape[1]))
    offsets = offset_table(rel_bias[0])
    first_key = RADIUS - seq_index * rows
    meta = jnp.stack([seq_index, first_key, first_key + tokens]).astype(jnp.int32)

    own_a, unused = norm_rows(inbound, norm_gain)
    before_a = lax.ppermute(own_a[rows - RADIUS :], "seq", up)
    after_a = lax.ppermute(own_a[:RADIUS], "seq", down)

    grad_own, lower, upper, offset_grad, *parts = backward_attention(
        meta, before_b, own_b, after_b, cotangent, offsets, slots, group, 0, heads
    )
    from_before = lax.ppermute(upper, "seq", up)
    from_after = lax.ppermute(lower, "seq", down)
    weight_sum = lax.psum_scatter(parts[0], "seq", scatter_dimension=2, tiled=True).astype(F32)

    output = forward_attention(meta, before_a, own_a, after_a, inbound, offsets, slots, group)
    final_normed, unused = norm_rows(output, final_gain[None])
    relaid = lax.all_to_all(final_normed, "seq", split_axis=1, concat_axis=0, tiled=True)
    kept = jnp.where(section_index == section_count - 1, relaid, jnp.zeros_like(relaid))
    memory = lax.psum_scatter(kept, "section", scatter_dimension=0, tiled=True)

    input_grad, gain_part = finish(
        grad_own, from_before, from_after, stash[0], inverse_b, norm_gain, cotangent
    )
    bias_part = jnp.dot(
        offset_grad[:, 0, :], onehot, precision=lax.Precision.HIGHEST
    ).T
    bias_sum = lax.psum_scatter(
        bias_part.astype(BF16), "seq", scatter_dimension=0, tiled=True
    ).astype(F32)
    gain_sum = lax.psum_scatter(
        gain_part.astype(BF16), "seq", scatter_dimension=1, tiled=True
    ).astype(F32)
    return (output[None], input_grad[None], weight_sum[None], bias_sum[None], gain_sum, memory)


def choose_body(embedded, carried, stash, returned, loss_grad, qkv_weight, rel_bias, norm_gain, final_gain):
    parts = lax.axis_size("seq")
    rows, width = embedded.shape
    even = width % (HEAD_DIM * parts) == 0 and HEAD_DIM % (32 * parts) == 0 and rows == 128
    sections = lax.axis_size("section")
    even = even and sections > 1 and sections & (sections - 1) == 0
    even = even and rel_bias.shape[1] == 8 * parts and rows * parts % (16 * sections) == 0
    chosen = heads_body if even else tokens_body
    return chosen(
        embedded, carried, stash, returned, loss_grad, qkv_weight, rel_bias, norm_gain, final_gain
    )


def solution(mesh):
    in_specs = (
        P("seq", None),
        P("section", "seq", None),
        P("section", "seq", None),
        P("section", "seq", None),
        P("seq", None),
        P("section", None, None, "seq", None),
        P("section", None, None),
        P("section", None),
        P(),
    )
    out_specs = (
        P("section", "seq", None),
        P("section", "seq", None),
        P("section", None, None, "seq", None),
        P("section", "seq", None),
        P("section", "seq"),
        P("section", "seq"),
    )
    return jax.shard_map(choose_body, mesh=mesh, in_specs=in_specs, out_specs=out_specs, check_vma=False)
```

```python
import functools

import jax
import jax.numpy as jnp
import numpy as np
from jax import lax
from jax.experimental import pallas as pl
from jax.experimental.pallas import tpu as pltpu
from jax.sharding import PartitionSpec as P

RADIUS = 96
HEAD_DIM = 128
ROW_BLOCK = 64
WINDOW = ROW_BLOCK + 2 * RADIUS
eps_norm = 1e-06
bucket_edges = (1, 2, 3, 4, 5, 6, 7, 8, 11, 16, 22, 32, 45, 64, 90)
masked_score = -1e30
F32 = jnp.float32
BF16 = jnp.bfloat16
VMEM_LIMIT = 24 * 1024 * 1024


def bucket_onehot(bucket_count):
    offsets = np.arange(WINDOW) - RADIUS
    magnitude = np.abs(offsets)
    counted = np.zeros(offsets.shape, np.int32)
    for threshold in bucket_edges:
        counted = counted + (magnitude >= threshold)
    counted = counted + 16 * (offsets > 0)
    onehot = (counted[:, None] == np.arange(bucket_count)[None, :]) & (magnitude <= RADIUS)[:, None]
    return onehot.astype(np.float32)


def dot_nn(a, b):
    return lax.dot_general(a, b, (((1,), (0,)), ((), ())), preferred_element_type=F32)


def dot_nt(a, b):
    return lax.dot_general(a, b, (((1,), (1,)), ((), ())), preferred_element_type=F32)


def dot_tn(a, b):
    return lax.dot_general(a, b, (((0,), (0,)), ((), ())), preferred_element_type=F32)


def norm_kernel(x_ref, gain_ref, normed_ref, inverse_ref):
    x = x_ref[...].astype(F32)
    inverse = lax.rsqrt(jnp.mean(x * x, axis=-1, keepdims=True) + eps_norm)
    normed_ref[...] = (x * inverse * gain_ref[...]).astype(BF16)
    inverse_ref[...] = jnp.broadcast_to(inverse, inverse_ref.shape)


def norm_rows(x, gain):
    rows, width = x.shape
    return pl.pallas_call(
        norm_kernel,
        out_shape=(
            jax.ShapeDtypeStruct((rows, width), BF16),
            jax.ShapeDtypeStruct((rows, 128), F32),
        ),
        compiler_params=pltpu.CompilerParams(vmem_limit_bytes=VMEM_LIMIT),
        cost_estimate=pl.CostEstimate(
            flops=6 * rows * width, bytes_accessed=4 * rows * width, transcendentals=rows
        ),
        name="norm_rows",
    )(x, gain)


def load_weight(meta_ref, slot_refs, weight_ref, head, slots):
    depth = HEAD_DIM // slots
    for r, slot_ref in enumerate(slot_refs):
        if slots == 1:
            start = 0
        else:
            start = pl.multiple_of(lax.rem(meta_ref[0] + r, slots) * depth, depth)
        for j in range(3):
            weight_ref[head, pl.ds(start, depth), j * HEAD_DIM : (j + 1) * HEAD_DIM] = slot_ref[j, head]
    return weight_ref[head]


def key_mask(meta_ref, first_key):
    key = lax.broadcasted_iota(jnp.int32, (1, WINDOW), 1) + first_key
    inside = (key >= meta_ref[1]) & (key < meta_ref[2])
    return jnp.where(inside, 0.0, masked_score).astype(F32)


def toeplitz(row):
    return pltpu.roll(
        jnp.broadcast_to(row, (ROW_BLOCK, WINDOW)), 0, 1, stride=1, stride_axis=0
    )


def diagonal_sums(values):
    total = values[:8]
    for a in range(1, ROW_BLOCK // 8):
        total = total + pltpu.roll(values[8 * a : 8 * a + 8], WINDOW - 8 * a, 1)
    row = lax.broadcasted_iota(jnp.int32, total.shape, 0)
    for bit in (1, 2, 4):
        total = jnp.where((row & bit) != 0, pltpu.roll(total, WINDOW - bit, 1), total)
    return jnp.sum(total, axis=0, keepdims=True)


def block_probs(query_rows, key_rows, bias):
    return score_probs(dot_nt(query_rows, key_rows), bias)


def score_probs(products, bias):
    scores = products * (HEAD_DIM ** (-0.5)) + bias
    weights = jnp.exp(scores - jnp.max(scores, axis=-1, keepdims=True))
    return weights * (1.0 / jnp.sum(weights, axis=-1, keepdims=True))


def forward_kernel(slots, group, meta_ref, before_ref, own_ref, after_ref, x_ref, offset_ref, *rest):
    slot_refs = rest[:slots]
    out_ref, weight_ref = rest[slots:]
    rows = own_ref.shape[0]
    blocks = rows // ROW_BLOCK
    masks = [key_mask(meta_ref, b * ROW_BLOCK) for b in range(blocks)]
    for g in range(group):
        columns = slice(g * HEAD_DIM, (g + 1) * HEAD_DIM)
        weight = load_weight(meta_ref, slot_refs, weight_ref, g, slots)
        own = own_ref[:, columns]
        extended = jnp.concatenate([before_ref[:, columns], own, after_ref[:, columns]], axis=0)
        query = dot_nn(own, weight[:, :HEAD_DIM]).astype(BF16)
        key_value = dot_nn(extended, weight[:, HEAD_DIM:]).astype(BF16)
        key, value = key_value[:, :HEAD_DIM], key_value[:, HEAD_DIM:]
        bias = toeplitz(offset_ref[g])
        for b in range(blocks):
            first = b * ROW_BLOCK
            window = slice(first, first + WINDOW)
            probs = block_probs(query[first : first + ROW_BLOCK], key[window], bias + masks[b])
            attended = dot_nn(probs.astype(BF16), value[window])
            kept = x_ref[first : first + ROW_BLOCK, columns].astype(F32)
            out_ref[first : first + ROW_BLOCK, columns] = (kept + attended).astype(BF16)


def column_spec(rows, group, first):
    return pl.BlockSpec((rows, group * HEAD_DIM), lambda i, meta: (0, i + first))


def slot_specs(weight_slots, group):
    return [
        pl.BlockSpec((3, group, slot.shape[2], HEAD_DIM), lambda i, meta: (0, i, 0, 0))
        for slot in weight_slots
    ]


def forward_attention(meta, before, own, after, x, offsets, weight_slots, group):
    rows, width = own.shape
    heads = width // HEAD_DIM
    slots = len(weight_slots)
    return pl.pallas_call(
        functools.partial(forward_kernel, slots, group),
        out_shape=jax.ShapeDtypeStruct((rows, width), BF16),
        grid_spec=pltpu.PrefetchScalarGridSpec(
            num_scalar_prefetch=1,
            grid=(heads // group,),
            in_specs=[
                column_spec(RADIUS, group, 0),
                column_spec(rows, group, 0),
                column_spec(RADIUS, group, 0),
                column_spec(rows, group, 0),
                pl.BlockSpec((group, 1, WINDOW), lambda i, meta: (i, 0, 0)),
                *slot_specs(weight_slots, group),
            ],
            out_specs=column_spec(rows, group, 0),
            scratch_shapes=[pltpu.VMEM((group, HEAD_DIM, 3 * HEAD_DIM), BF16)],
        ),
        compiler_params=pltpu.CompilerParams(vmem_limit_bytes=VMEM_LIMIT),
        cost_estimate=pl.CostEstimate(
            flops=heads * 60_000_000, bytes_accessed=8 * rows * width, transcendentals=heads * 32768
        ),
        name="forward_attention",
    )(meta, before, own, after, x, offsets, *weight_slots)


def backward_kernel(slots, group, meta_ref, before_ref, own_ref, after_ref, cot_ref, offset_ref, *rest):
    slot_refs = rest[:slots]
    rest = rest[slots:]
    grad_ref, lower_ref, upper_ref, offset_grad_ref = rest[:4]
    part_refs = rest[4 : 4 + slots]
    weight_ref, part_ref = rest[4 + slots :]
    rows = own_ref.shape[0]
    blocks = rows // ROW_BLOCK
    scale = HEAD_DIM ** (-0.5)
    masks = [key_mask(meta_ref, b * ROW_BLOCK) for b in range(blocks)]
    for g in range(group):
        columns = slice(g * HEAD_DIM, (g + 1) * HEAD_DIM)
        weight = load_weight(meta_ref, slot_refs, weight_ref, g, slots)
        own = own_ref[:, columns]
        extended = jnp.concatenate([before_ref[:, columns], own, after_ref[:, columns]], axis=0)
        query = dot_nn(own, weight[:, :HEAD_DIM]).astype(BF16)
        key_value = dot_nn(extended, weight[:, HEAD_DIM:]).astype(BF16)
        key, value = key_value[:, :HEAD_DIM], key_value[:, HEAD_DIM:]
        bias = toeplitz(offset_ref[g])
        grad_query, grad_key, grad_value, score_sum = [], [], [], None
        for b in range(blocks):
            first = b * ROW_BLOCK
            window = slice(first, first + WINDOW)
            query_rows = query[first : first + ROW_BLOCK]
            cot_rows = cot_ref[first : first + ROW_BLOCK, columns]
            probs = block_probs(query_rows, key[window], bias + masks[b])
            grad_probs = dot_nt(cot_rows, value[window])
            delta = jnp.sum(probs * grad_probs, axis=-1, keepdims=True)
            grad_scores = probs * (grad_probs - delta)
            score_sum = grad_scores if score_sum is None else score_sum + grad_scores
            grad_packed = grad_scores.astype(BF16)
            grad_query.append(dot_nn(grad_packed, key[window]))
            grad_key.append(dot_tn(grad_packed, query_rows))
            grad_value.append(dot_tn(probs.astype(BF16), cot_rows))

        def joined(parts):
            pieces = []
            for u in range((rows + 2 * RADIUS) // ROW_BLOCK):
                total = None
                for b in range(blocks):
                    if 0 <= u - b < WINDOW // ROW_BLOCK:
                        piece = parts[b][(u - b) * ROW_BLOCK : (u - b + 1) * ROW_BLOCK]
                        total = piece if total is None else total + piece
                pieces.append(total)
            return jnp.concatenate(pieces, axis=0)

        dquery = (jnp.concatenate(grad_query, axis=0) * scale).astype(BF16)
        dkey = (joined(grad_key) * scale).astype(BF16)
        dvalue = joined(grad_value).astype(BF16)
        dkey_value = jnp.concatenate([dkey, dvalue], axis=1)
        grad_extended = dot_nt(dkey_value, weight[:, HEAD_DIM:])
        grad_ref[:, columns] = grad_extended[RADIUS : RADIUS + rows] + dot_nt(dquery, weight[:, :HEAD_DIM])
        lower_ref[:, columns] = grad_extended[:RADIUS].astype(BF16)
        upper_ref[:, columns] = grad_extended[RADIUS + rows :].astype(BF16)
        part_ref[g, :, :HEAD_DIM] = dot_tn(own, dquery)
        part_ref[g, :, HEAD_DIM:] = dot_tn(extended, dkey_value)
        depth = HEAD_DIM // slots
        for r in range(slots):
            if slots == 1:
                start = 0
            else:
                start = pl.multiple_of(lax.rem(meta_ref[0] + r, slots) * depth, depth)
            for j in range(3):
                part_refs[r][j, g] = part_ref[
                    g, pl.ds(start, depth), j * HEAD_DIM : (j + 1) * HEAD_DIM
                ].astype(part_refs[r].dtype)
        offset_grad_ref[g] = diagonal_sums(score_sum)


def backward_attention(meta, before, own, after, cotangent, offsets, weight_slots, group, first_head, heads):
    rows = own.shape[0]
    width = heads * HEAD_DIM
    slots = len(weight_slots)
    first = first_head // group
    slot_shape = weight_slots[0].shape
    part_types = [F32] + [BF16] * (slots - 1) if slots > 1 else [BF16]
    return pl.pallas_call(
        functools.partial(backward_kernel, slots, group),
        out_shape=(
            jax.ShapeDtypeStruct((rows, width), F32),
            jax.ShapeDtypeStruct((RADIUS, width), BF16),
            jax.ShapeDtypeStruct((RADIUS, width), BF16),
            jax.ShapeDtypeStruct((heads, 1, WINDOW), F32),
            *[jax.ShapeDtypeStruct(slot_shape, kind) for kind in part_types],
        ),
        grid_spec=pltpu.PrefetchScalarGridSpec(
            num_scalar_prefetch=1,
            grid=(heads // group,),
            in_specs=[
                column_spec(RADIUS, group, first),
                column_spec(rows, group, first),
                column_spec(RADIUS, group, first),
                column_spec(rows, group, first),
                pl.BlockSpec((group, 1, WINDOW), lambda i, meta: (i + first, 0, 0)),
                *slot_specs(weight_slots, group),
            ],
            out_specs=(
                column_spec(rows, group, 0),
                column_spec(RADIUS, group, 0),
                column_spec(RADIUS, group, 0),
                pl.BlockSpec((group, 1, WINDOW), lambda i, meta: (i, 0, 0)),
                *slot_specs(weight_slots, group),
            ),
            scratch_shapes=[
                pltpu.VMEM((group, HEAD_DIM, 3 * HEAD_DIM), BF16),
                pltpu.VMEM((group, HEAD_DIM, 3 * HEAD_DIM), F32),
            ],
        ),
        compiler_params=pltpu.CompilerParams(vmem_limit_bytes=VMEM_LIMIT),
        cost_estimate=pl.CostEstimate(
            flops=heads * 150_000_000, bytes_accessed=12 * rows * width, transcendentals=heads * 32768
        ),
        name="backward_attention",
    )(meta, before, own, after, cotangent, offsets, *weight_slots)


def finish_kernel(grad_ref, low_ref, high_ref, x_ref, inverse_ref, gain_ref, cot_ref, out_ref, gain_grad_ref):
    rows = x_ref.shape[0]
    grad = grad_ref[...]
    edge = jnp.zeros((rows - RADIUS, grad.shape[1]), F32)
    grad = grad + jnp.concatenate([low_ref[...].astype(F32), edge], axis=0)
    grad = grad + jnp.concatenate([edge, high_ref[...].astype(F32)], axis=0)
    x = x_ref[...].astype(F32)
    inverse = inverse_ref[:, :1]
    gain_grad_ref[...] = jnp.sum(grad * x * inverse, axis=0, keepdims=True)
    scaled = grad * gain_ref[...]
    mean = jnp.mean(scaled * x, axis=-1, keepdims=True)
    result = inverse * scaled - x * (inverse * inverse * inverse * mean)
    out_ref[...] = (cot_ref[...].astype(F32) + result).astype(BF16)


def finish(grad, low, high, x, inverse, gain, cotangent):
    rows, width = x.shape
    return pl.pallas_call(
        finish_kernel,
        out_shape=(
            jax.ShapeDtypeStruct((rows, width), BF16),
            jax.ShapeDtypeStruct((1, width), F32),
        ),
        compiler_params=pltpu.CompilerParams(vmem_limit_bytes=VMEM_LIMIT),
        cost_estimate=pl.CostEstimate(
            flops=16 * rows * width, bytes_accessed=14 * rows * width, transcendentals=0
        ),
        name="finish",
    )(grad, low, high, x, inverse, gain, cotangent)


def column_of(row, rows):
    return jnp.transpose(jnp.broadcast_to(row, (128, rows)))


def split_rows(inverse, pad_rows, width):
    high = inverse.astype(BF16)
    rest = inverse - high.astype(F32)
    middle = rest.astype(BF16)
    low = (rest - middle.astype(F32)).astype(BF16)
    wide = [jnp.transpose(jnp.broadcast_to(v.astype(F32), (v.shape[0], 128)))[:1] for v in (high, middle, low)]
    row = jnp.concatenate(wide + [jnp.zeros((pad_rows - 3, wide[0].shape[1]), F32)], axis=0)
    return row.astype(BF16)


def row_inverse(x):
    x = x.astype(F32)
    return lax.rsqrt(jnp.mean(x * x, axis=-1, keepdims=True) + eps_norm)


def pack_stash_kernel(parts, meta_ref, x_ref, gain_ref, weight_ref, inverse_ref, *refs):
    out_refs, normed_ref = refs[:parts], refs[parts]
    rows, width = x_ref.shape
    depth = weight_ref.shape[2]
    wide = width // parts
    heads = wide // HEAD_DIM
    inverse = row_inverse(x_ref[...])
    inverse_ref[...] = jnp.broadcast_to(inverse, inverse_ref.shape)
    normed_ref[...] = (x_ref[...].astype(F32) * inverse * gain_ref[...]).astype(BF16)
    for r, out_ref in enumerate(out_refs):
        target = lax.rem(meta_ref[0] + r, parts)
        out_ref[:rows] = normed_ref[:, pl.ds(pl.multiple_of(target * wide, 128), wide)]
        for j in range(3):
            for h in range(heads):
                out_ref[rows + j * depth : rows + (j + 1) * depth, h * HEAD_DIM : (h + 1) * HEAD_DIM] = weight_ref[
                    j, target * heads + h
                ]


def pack_rows_kernel(parts, with_inverse, meta_ref, edge_ref, inner_ref, *out_refs):
    rows, width = inner_ref.shape
    wide = width // parts
    edge = 1 if with_inverse else 2
    refs = out_refs[:parts]
    for r, out_ref in enumerate(refs):
        target = lax.rem(meta_ref[0] + r, parts)
        start = pl.multiple_of(target * wide, 128)

        @pl.when(meta_ref[edge] == 1)
        def use_edge():
            out_ref[:rows] = edge_ref[:, pl.ds(start, wide)]

        @pl.when(meta_ref[edge] == 0)
        def use_inner():
            out_ref[:rows] = inner_ref[:, pl.ds(start, wide)]

    def finish_with(source_ref):
        if with_inverse:
            tail = split_rows(row_inverse(source_ref[...]), 16, wide)
            for out_ref in refs:
                out_ref[rows:] = jnp.zeros((16, wide), BF16)
                out_ref[rows:, :rows] = tail
        else:
            out_refs[parts][...] = source_ref[...]

    @pl.when(meta_ref[edge] == 1)
    def finish_edge():
        finish_with(edge_ref)

    @pl.when(meta_ref[edge] == 0)
    def finish_inner():
        finish_with(inner_ref)


SMEM_SPEC = pl.BlockSpec(memory_space=pltpu.SMEM)
VMEM_SPEC = pl.BlockSpec(memory_space=pltpu.VMEM)


def pack_stash(meta, x, gain, weight, parts):
    rows, width = x.shape
    depth = weight.shape[2]
    shape = (rows + 3 * depth, width // parts)
    return pl.pallas_call(
        functools.partial(pack_stash_kernel, parts),
        out_shape=(
            jax.ShapeDtypeStruct((rows, 128), F32),
            *[jax.ShapeDtypeStruct(shape, BF16) for r in range(parts)],
        ),
        in_specs=[SMEM_SPEC, VMEM_SPEC, VMEM_SPEC, VMEM_SPEC],
        out_specs=(VMEM_SPEC,) * (parts + 1),
        scratch_shapes=[pltpu.VMEM((rows, width), BF16)],
        compiler_params=pltpu.CompilerParams(vmem_limit_bytes=VMEM_LIMIT),
        cost_estimate=pl.CostEstimate(flops=4 * rows * width, bytes_accessed=6 * rows * width, transcendentals=0),
        name="pack_stash",
    )(meta, x, gain, weight)


def pack_rows(meta, edge, inner, parts, with_inverse):
    rows, width = inner.shape
    shape = (rows + (16 if with_inverse else 0), width // parts)
    extra = () if with_inverse else (jax.ShapeDtypeStruct((rows, width), BF16),)
    return pl.pallas_call(
        functools.partial(pack_rows_kernel, parts, with_inverse),
        out_shape=(*[jax.ShapeDtypeStruct(shape, BF16) for r in range(parts)], *extra),
        in_specs=[SMEM_SPEC, VMEM_SPEC, VMEM_SPEC],
        out_specs=(VMEM_SPEC,) * (parts + len(extra)),
        compiler_params=pltpu.CompilerParams(vmem_limit_bytes=VMEM_LIMIT),
        cost_estimate=pl.CostEstimate(flops=4 * rows * width, bytes_accessed=6 * rows * width, transcendentals=0),
        name="pack_inbound" if with_inverse else "pack_cotangent",
    )(meta, edge, inner)


def gather_rows(meta_ref, refs, rows, x_ref):
    parts = len(refs)
    for r, ref in enumerate(refs):
        source = lax.rem(meta_ref[0] + parts - r, parts)
        x_ref[pl.ds(pl.multiple_of(source * rows, rows), rows)] = ref[:rows]


def gather_weight(meta_ref, refs, rows, weight_ref):
    parts = len(refs)
    depth = HEAD_DIM // parts
    for r, ref in enumerate(refs):
        source = lax.rem(meta_ref[0] + parts - r, parts)
        depth_at = pl.ds(pl.multiple_of(source * depth, depth), depth)
        for j in range(3):
            weight_ref[depth_at, j * HEAD_DIM : (j + 1) * HEAD_DIM] = ref[
                rows + j * depth : rows + (j + 1) * depth
            ]


def gather_inverse(meta_ref, refs, rows, inverse_ref):
    parts = len(refs)

    @pl.when(pl.program_id(0) == 0)
    def spread_inverse():
        for r, ref in enumerate(refs):
            source = lax.rem(meta_ref[0] + parts - r, parts)
            tail = ref[rows : rows + 16].astype(F32)
            inverse_ref[pl.ds(pl.multiple_of(source * rows, rows), rows)] = column_of(
                tail[:1] + tail[1:2] + tail[2:3], rows
            )


def block_mask(first_query, tokens):
    key = lax.broadcasted_iota(jnp.int32, (1, WINDOW), 1) + (first_query - RADIUS)
    return jnp.where((key >= 0) & (key < tokens), 0.0, masked_score).astype(F32)


def edge_bias(bias, first, tokens):
    if first < RADIUS or first + ROW_BLOCK + RADIUS > tokens:
        return bias + block_mask(first, tokens)
    return bias


def padded(rows):
    edge = jnp.zeros((RADIUS, rows.shape[1]), rows.dtype)
    return jnp.concatenate([edge, rows, edge], axis=0)


def heads_backward_kernel(parts, rows, meta_ref, *refs):
    a_refs, c_refs = refs[:parts], refs[parts : 2 * parts]
    gain_ref, offset_ref, onehot_ref, after_ref = refs[2 * parts : 2 * parts + 4]
    out_refs = refs[2 * parts + 4 : 3 * parts + 4]
    gain_grad_ref, x_ref, weight_ref, cot_ref, grad_ref, part_ref, bias_ref = refs[3 * parts + 4 :]
    tokens = rows * parts
    depth = HEAD_DIM // parts
    scale = HEAD_DIM ** (-0.5)
    gather_rows(meta_ref, a_refs, rows, x_ref)
    gather_weight(meta_ref, a_refs, rows, weight_ref)
    gather_rows(meta_ref, c_refs, rows, cot_ref)
    weight = weight_ref[...]
    normed = x_ref[...]
    query = dot_nn(normed, weight[:, :HEAD_DIM]).astype(BF16)
    key = padded(dot_nn(normed, weight[:, HEAD_DIM : 2 * HEAD_DIM]).astype(BF16))
    value = padded(dot_nn(normed, weight[:, 2 * HEAD_DIM :]).astype(BF16))
    bias = toeplitz(offset_ref[0])
    blocks = tokens // ROW_BLOCK
    starts = range(0, tokens, ROW_BLOCK)
    cot = cot_ref[...]
    query_rows = [query[f : f + ROW_BLOCK] for f in starts]
    cot_rows = [cot[f : f + ROW_BLOCK] for f in starts]
    products = [dot_nt(rows_q, key[f : f + WINDOW]) for f, rows_q in zip(starts, query_rows)]
    grad_probs = [dot_nt(rows_c, value[f : f + WINDOW]) for f, rows_c in zip(starts, cot_rows)]
    packed, grad_packed, score_sum = [], [], None
    for f, product, grads in zip(starts, products, grad_probs):
        probs = score_probs(product, edge_bias(bias, f, tokens))
        delta = jnp.sum(probs * grads, axis=-1, keepdims=True)
        grad_scores = probs * (grads - delta)
        score_sum = grad_scores if score_sum is None else score_sum + grad_scores
        packed.append(probs.astype(BF16))
        grad_packed.append(grad_scores.astype(BF16))
    grad_query = [dot_nn(part, key[f : f + WINDOW]) for f, part in zip(starts, grad_packed)]
    grad_key = [dot_tn(part, rows_q) for part, rows_q in zip(grad_packed, query_rows)]
    grad_value = [dot_tn(part, rows_c) for part, rows_c in zip(packed, cot_rows)]

    def joined(pieces):
        units = []
        for u in range((tokens + 2 * RADIUS) // ROW_BLOCK):
            total = None
            for b in range(blocks):
                if 0 <= u - b < WINDOW // ROW_BLOCK:
                    piece = pieces[b][(u - b) * ROW_BLOCK : (u - b + 1) * ROW_BLOCK]
                    total = piece if total is None else total + piece
            units.append(total)
        return jnp.concatenate(units, axis=0)[RADIUS : RADIUS + tokens]

    dqkv = jnp.concatenate(
        [
            (jnp.concatenate(grad_query, axis=0) * scale).astype(BF16),
            (joined(grad_key) * scale).astype(BF16),
            joined(grad_value).astype(BF16),
        ],
        axis=1,
    )
    grad_normed = dot_nt(dqkv, weight)
    gain_grad_ref[...] = jnp.sum(grad_normed * normed.astype(F32), axis=0, keepdims=True) / gain_ref[...]
    grad_ref[...] = grad_normed
    part_ref[...] = dot_tn(normed, dqkv)
    bias_grad = jnp.sum(onehot_ref[...] * diagonal_sums(score_sum), axis=1, keepdims=True)
    bias_ref[...] = jnp.broadcast_to(bias_grad, bias_ref.shape)
    buckets = bias_ref.shape[0] // parts
    for r, out_ref in enumerate(out_refs):
        source = lax.rem(meta_ref[0] + parts - r, parts)
        out_ref[:rows] = grad_ref[pl.ds(pl.multiple_of(source * rows, rows), rows)].astype(BF16)
        for j in range(3):
            out_ref[rows + j * depth : rows + (j + 1) * depth] = part_ref[
                pl.ds(pl.multiple_of(source * depth, depth), depth), j * HEAD_DIM : (j + 1) * HEAD_DIM
            ].astype(BF16)
        share = bias_ref[pl.ds(pl.multiple_of(source * buckets, buckets), buckets)]
        out_ref[rows + 3 * depth :] = jnp.concatenate(
            [share, jnp.zeros((16 - buckets, HEAD_DIM), F32)], axis=0
        ).astype(BF16)


def head_column(rows, first=0):
    return pl.BlockSpec((rows, HEAD_DIM), lambda i, meta: (0, i + first))


def whole_column(rows, heads, first=0):
    return pl.BlockSpec((rows, HEAD_DIM), lambda i, meta: (0, meta[0] * heads + first + i))


def offset_spec(heads, first=0):
    return pl.BlockSpec((1, 1, WINDOW), lambda i, meta: (meta[0] * heads + first + i, 0, 0))


def heads_backward(meta, a_slots, c_slots, gain, offsets, onehot, after, heads, first, count):
    parts = len(a_slots)
    rows = c_slots[0].shape[0]
    tokens = rows * parts
    buckets = onehot.shape[0]
    packed = a_slots[0].shape[0]
    made = packed + 16
    width = count * HEAD_DIM
    return pl.pallas_call(
        functools.partial(heads_backward_kernel, parts, rows),
        out_shape=(
            *[jax.ShapeDtypeStruct((made, width), BF16) for r in range(parts)],
            jax.ShapeDtypeStruct((1, width), F32),
        ),
        grid_spec=pltpu.PrefetchScalarGridSpec(
            num_scalar_prefetch=1,
            grid=(count,),
            in_specs=[
                *[head_column(packed, first)] * parts,
                whole_column(rows, heads, first),
                *[head_column(rows, first)] * (parts - 1),
                whole_column(1, heads, first),
                offset_spec(heads, first),
                pl.BlockSpec((buckets, WINDOW), lambda i, meta: (0, 0)),
                pl.BlockSpec(memory_space=pl.ANY),
            ],
            out_specs=(*[head_column(made)] * parts, head_column(1)),
            scratch_shapes=[
                pltpu.VMEM((tokens, HEAD_DIM), BF16),
                pltpu.VMEM((HEAD_DIM, 3 * HEAD_DIM), BF16),
                pltpu.VMEM((tokens, HEAD_DIM), BF16),
                pltpu.VMEM((tokens, HEAD_DIM), F32),
                pltpu.VMEM((HEAD_DIM, 3 * HEAD_DIM), F32),
                pltpu.VMEM((buckets, HEAD_DIM), F32),
            ],
        ),
        compiler_params=pltpu.CompilerParams(vmem_limit_bytes=VMEM_LIMIT),
        cost_estimate=pl.CostEstimate(
            flops=count * tokens * 400_000, bytes_accessed=tokens * width, transcendentals=0
        ),
        name="heads_backward",
    )(meta, *a_slots, *c_slots, gain, offsets, onehot, after)


def heads_forward_kernel(parts, rows, meta_ref, *refs):
    a_refs, i_refs = refs[:parts], refs[parts : 2 * parts]
    gain_ref, offset_ref = refs[2 * parts : 2 * parts + 2]
    out_refs = refs[2 * parts + 2 : 3 * parts + 2]
    sums_ref, inverse_ref, x_ref, weight_ref, made_ref, square_ref = refs[3 * parts + 2 :]
    tokens = rows * parts
    gather_rows(meta_ref, i_refs, rows, x_ref)
    gather_weight(meta_ref, a_refs, rows, weight_ref)
    gather_inverse(meta_ref, i_refs, rows, inverse_ref)
    weight = weight_ref[...]
    normed = (x_ref[...].astype(F32) * inverse_ref[...] * gain_ref[...]).astype(BF16)
    query = dot_nn(normed, weight[:, :HEAD_DIM]).astype(BF16)
    key = padded(dot_nn(normed, weight[:, HEAD_DIM : 2 * HEAD_DIM]).astype(BF16))
    value = padded(dot_nn(normed, weight[:, 2 * HEAD_DIM :]).astype(BF16))
    bias = toeplitz(offset_ref[0])
    starts = range(0, tokens, ROW_BLOCK)
    products = [dot_nt(query[f : f + ROW_BLOCK], key[f : f + WINDOW]) for f in starts]
    packed = [
        score_probs(product, edge_bias(bias, f, tokens)).astype(BF16) for f, product in zip(starts, products)
    ]
    attended = [dot_nn(part, value[f : f + WINDOW]) for f, part in zip(starts, packed)]
    for f, part in zip(starts, attended):
        made_ref[f : f + ROW_BLOCK] = (x_ref[f : f + ROW_BLOCK].astype(F32) + part).astype(BF16)
    made = made_ref[...].astype(F32)
    squares = made * made

    @pl.when(pl.program_id(0) == 0)
    def first_head():
        square_ref[...] = squares

    @pl.when(pl.program_id(0) > 0)
    def later_head():
        square_ref[...] += squares

    for r, out_ref in enumerate(out_refs):
        source = lax.rem(meta_ref[0] + parts - r, parts)
        out_ref[...] = made_ref[pl.ds(pl.multiple_of(source * rows, rows), rows)]

    @pl.when(pl.program_id(0) == pl.num_programs(0) - 1)
    def last_head():
        total = jnp.sum(jnp.transpose(square_ref[...]), axis=0, keepdims=True)
        sums_ref[...] = jnp.broadcast_to(total, sums_ref.shape)


def heads_forward(meta, a_slots, i_slots, gain, offsets, heads, rows):
    parts = len(a_slots)
    tokens = rows * parts
    packed = a_slots[0].shape[0]
    width = heads * HEAD_DIM
    return pl.pallas_call(
        functools.partial(heads_forward_kernel, parts, rows),
        out_shape=(
            *[jax.ShapeDtypeStruct((rows, width), BF16) for r in range(parts)],
            jax.ShapeDtypeStruct((8, tokens), F32),
        ),
        grid_spec=pltpu.PrefetchScalarGridSpec(
            num_scalar_prefetch=1,
            grid=(heads,),
            in_specs=[
                *[head_column(packed)] * parts,
                *[head_column(i_slots[0].shape[0])] * parts,
                whole_column(1, heads),
                offset_spec(heads),
            ],
            out_specs=(
                *[head_column(rows)] * parts,
                pl.BlockSpec((8, tokens), lambda i, meta: (0, 0)),
            ),
            scratch_shapes=[
                pltpu.VMEM((tokens, HEAD_DIM), F32),
                pltpu.VMEM((tokens, HEAD_DIM), BF16),
                pltpu.VMEM((HEAD_DIM, 3 * HEAD_DIM), BF16),
                pltpu.VMEM((tokens, HEAD_DIM), BF16),
                pltpu.VMEM((tokens, HEAD_DIM), F32),
            ],
        ),
        compiler_params=pltpu.CompilerParams(vmem_limit_bytes=VMEM_LIMIT),
        cost_estimate=pl.CostEstimate(
            flops=heads * tokens, bytes_accessed=tokens, transcendentals=0
        ),
        name="heads_forward",
    )(meta, *a_slots, *i_slots, gain, offsets)


def memory_kernel(parts, width, meta_ref, *refs):
    out_refs, sum_refs = refs[:parts], refs[parts : 2 * parts]
    gain_ref, after_ref, *share_refs, memory_ref = refs[2 * parts :]
    wide = memory_ref.shape[1]
    rows = memory_ref.shape[0] // parts
    total = sum_refs[0][:1]
    for sum_ref in sum_refs[1:]:
        total = total + sum_ref[:1]
    inverse = lax.rsqrt(total / width + eps_norm)
    gain = gain_ref[:, pl.ds(pl.multiple_of(meta_ref[0] * wide, 128), wide)]
    spread_inverse = jnp.transpose(jnp.broadcast_to(inverse, (128, inverse.shape[1])))
    for r, out_ref in enumerate(out_refs):
        source = lax.rem(meta_ref[0] + parts - r, parts)
        memory_ref[pl.ds(pl.multiple_of(source * rows, rows), rows)] = out_ref[...]
    made = memory_ref[...].astype(F32)
    memory_ref[...] = (made * spread_inverse[:, :1] * gain).astype(BF16)
    for k, share_ref in enumerate(share_refs):
        size = share_ref.shape[0]
        share_ref[...] = memory_ref[k * size : (k + 1) * size]


def memory_rows(meta, outs, sums, gain, after, width, shares):
    parts = len(outs)
    rows, wide = outs[0].shape
    return pl.pallas_call(
        functools.partial(memory_kernel, parts, width),
        out_shape=[jax.ShapeDtypeStruct((rows * parts // shares, wide), BF16)] * shares,
        in_specs=[SMEM_SPEC] + [VMEM_SPEC] * (2 * parts + 1) + [pl.BlockSpec(memory_space=pl.ANY)],
        out_specs=[VMEM_SPEC] * shares,
        scratch_shapes=[pltpu.VMEM((rows * parts, wide), BF16)],
        compiler_params=pltpu.CompilerParams(vmem_limit_bytes=VMEM_LIMIT),
        cost_estimate=pl.CostEstimate(flops=rows, bytes_accessed=rows, transcendentals=0),
        name="memory_rows",
    )(meta, *outs, *sums, gain, after)


def place_kernel(parts, meta_ref, *refs):
    out_ref = refs[parts]
    wide = refs[0].shape[1]
    for r in range(parts):
        source = lax.rem(meta_ref[0] + r, parts)
        out_ref[:, pl.ds(pl.multiple_of(source * wide, 128), wide)] = refs[r][...]


def place_columns(meta, slots):
    parts = len(slots)
    rows, wide = slots[0].shape
    return pl.pallas_call(
        functools.partial(place_kernel, parts),
        out_shape=jax.ShapeDtypeStruct((rows, wide * parts), BF16),
        in_specs=[SMEM_SPEC] + [VMEM_SPEC] * parts,
        out_specs=VMEM_SPEC,
        compiler_params=pltpu.CompilerParams(vmem_limit_bytes=VMEM_LIMIT),
        cost_estimate=pl.CostEstimate(flops=0, bytes_accessed=rows, transcendentals=0),
        name="place_columns",
    )(meta, *slots)


def heads_finish_kernel(parts, chunks, meta_ref, *refs):
    g_refs = refs[: parts * chunks]
    x_ref, inverse_ref, gain_ref, cot_ref, out_ref, weight_ref, bias_ref, scaled_ref = refs[parts * chunks :]
    rows, width = x_ref.shape
    wide = width // parts // chunks
    heads = wide // HEAD_DIM
    depth = HEAD_DIM // parts
    buckets = bias_ref.shape[1]
    for c in range(chunks):
        for r in range(parts):
            g_ref = g_refs[c * parts + r]
            place = lax.rem(meta_ref[0] + r, parts) * chunks + c
            columns = pl.ds(pl.multiple_of(place * wide, 128), wide)
            scaled_ref[:, columns] = g_ref[:rows].astype(F32) * gain_ref[:, columns]
            for h in range(heads):
                lanes = slice(h * HEAD_DIM, (h + 1) * HEAD_DIM)
                for j in range(3):
                    weight_ref[j, place * heads + h] = g_ref[
                        rows + j * depth : rows + (j + 1) * depth, lanes
                    ].astype(F32)
                bias_ref[place * heads + h] = g_ref[rows + 3 * depth :, lanes].astype(F32)[:buckets]
    x = x_ref[...].astype(F32)
    scaled = scaled_ref[...]
    inverse = inverse_ref[:, :1]
    mean = jnp.mean(scaled * x, axis=-1, keepdims=True)
    result = inverse * scaled - x * (inverse * inverse * inverse * mean)
    out_ref[...] = (cot_ref[...].astype(F32) + result).astype(BF16)


def heads_finish(meta, g_chunks, x, inverse, gain, cotangent, buckets):
    chunks, parts = len(g_chunks), len(g_chunks[0])
    rows, width = x.shape
    heads = width // HEAD_DIM
    slots = [slot for g_slots in g_chunks for slot in g_slots]
    return pl.pallas_call(
        functools.partial(heads_finish_kernel, parts, chunks),
        out_shape=(
            jax.ShapeDtypeStruct((rows, width), BF16),
            jax.ShapeDtypeStruct((3, heads, HEAD_DIM // parts, HEAD_DIM), F32),
            jax.ShapeDtypeStruct((heads, buckets // parts, HEAD_DIM), F32),
        ),
        in_specs=[SMEM_SPEC] + [VMEM_SPEC] * (len(slots) + 4),
        out_specs=(VMEM_SPEC,) * 3,
        scratch_shapes=[pltpu.VMEM((rows, width), F32)],
        compiler_params=pltpu.CompilerParams(vmem_limit_bytes=VMEM_LIMIT),
        cost_estimate=pl.CostEstimate(flops=12 * rows * width, bytes_accessed=14 * rows * width, transcendentals=0),
        name="heads_finish",
    )(meta, *slots, x, inverse, gain, cotangent)


def offset_table(rel_bias):
    onehot = jnp.asarray(bucket_onehot(rel_bias.shape[0]))
    by_offset = jnp.dot(onehot, rel_bias, precision=lax.Precision.HIGHEST).T
    inside = jnp.arange(WINDOW, dtype=jnp.int32) <= 2 * RADIUS
    return jnp.where(inside[None, :], by_offset, masked_score)[:, None, :]


def shifted(value, axis, steps):
    count = lax.axis_size(axis)
    first, last = (max(0, -steps), min(count, count - steps))
    return lax.ppermute(value, axis, [(source, source + steps) for source in range(first, last)])


def spread_memory(shares, section, sections):
    last = sections - 1
    couple = jnp.where(section == last, shares[-1], 0)
    for s, share in enumerate(shares[:-1]):
        couple = couple + lax.ppermute(share, "section", [(last, 2 * s + 1)])
    half = couple.shape[0] // 2
    even = lax.ppermute(couple[:half], "section", [(s + 1, s) for s in range(0, sections, 2)])
    return jnp.where(section % 2 == 0, even, couple[half:])


def heads_body(
    embedded, carried, stash, returned, loss_grad, qkv_weight, rel_bias, norm_gain, final_gain
):
    section = lax.axis_index("section")
    sections = lax.axis_size("section")
    parts = lax.axis_size("seq")
    rows, width = embedded.shape
    heads = width // HEAD_DIM // parts
    buckets = rel_bias.shape[1]
    meta = jnp.stack(
        [lax.axis_index("seq"), section == 0, section == sections - 1]
    ).astype(jnp.int32)

    def exchanged(sends, direction):
        moved = [
            lax.ppermute(sends[r], "seq", [(i, (i + direction * r) % parts) for i in range(parts)])
            for r in range(1, parts)
        ]
        return [sends[0]] + moved

    inverse_b, *a_sends = pack_stash(meta, stash[0], norm_gain, qkv_weight[0], parts)
    a_slots = exchanged(a_sends, 1)
    arrived = shifted(carried[0], "section", 1)
    came_back = shifted(returned[0], "section", -1)
    i_slots = exchanged(pack_rows(meta, embedded, arrived, parts, True), 1)
    *c_sends, cotangent = pack_rows(meta, loss_grad, came_back, parts, False)
    c_slots = exchanged(c_sends, 1)
    c_slots[0] = cotangent

    offsets = offset_table(rel_bias[0])
    onehot = jnp.asarray(bucket_onehot(buckets).T)
    *o_sends, sums = heads_forward(meta, a_slots, i_slots, norm_gain, offsets, heads, rows)
    all_sums = exchanged([sums] * parts, 1)
    o_sends, c_slots = lax.optimization_barrier((o_sends, c_slots))
    o_slots = exchanged(o_sends, -1)

    *g_sends, gain_grad = heads_backward(
        meta, a_slots, c_slots, norm_gain, offsets, onehot, o_sends[0], heads, 0, heads
    )
    g_sends, o_slots = lax.optimization_barrier((g_sends, o_slots))
    g_chunks = [exchanged(g_sends, -1)]
    output = place_columns(meta, o_slots)
    shares = memory_rows(meta, o_sends, all_sums, final_gain[None], gain_grad, width, sections // 2)
    memory = spread_memory(shares, section, sections)

    input_grad, weight_grad, bias_wide = heads_finish(
        meta, g_chunks, stash[0], inverse_b, norm_gain, cotangent, buckets
    )
    bias_grad = bias_wide[:, :, 0].T
    return (
        output[None],
        input_grad[None],
        weight_grad[None],
        bias_grad[None],
        gain_grad,
        memory,
    )


def tokens_body(
    embedded, carried, stash, returned, loss_grad, qkv_weight, rel_bias, norm_gain, final_gain
):
    section_index = lax.axis_index("section")
    section_count = lax.axis_size("section")
    seq_index = lax.axis_index("seq")
    seq_count = lax.axis_size("seq")
    rows, width = embedded.shape
    heads = width // HEAD_DIM
    tokens = rows * seq_count
    shard = qkv_weight[0]
    up = [(i, i + 1) for i in range(seq_count - 1)]
    down = [(j, i) for i, j in up]
    group = 4 if heads % 4 == 0 else 1

    own_b, inverse_b = norm_rows(stash[0], norm_gain)
    before_b = lax.ppermute(own_b[rows - RADIUS :], "seq", up)
    after_b = lax.ppermute(own_b[:RADIUS], "seq", down)
    slots = [lax.all_gather(shard, "seq", axis=2, tiled=True)]

    section_up = [(i, (i + 1) % section_count) for i in range(section_count)]
    section_down = [(j, i) for i, j in section_up]
    inbound = lax.ppermute(
        jnp.where(section_index == section_count - 1, embedded, carried[0]), "section", section_up
    )
    cotangent = lax.ppermute(
        jnp.where(section_index == 0, loss_grad, returned[0]), "section", section_down
    )

    onehot = jnp.asarray(bucket_onehot(rel_bias.shape[1]))
    offsets = offset_table(rel_bias[0])
    first_key = RADIUS - seq_index * rows
    meta = jnp.stack([seq_index, first_key, first_key + tokens]).astype(jnp.int32)

    own_a, unused = norm_rows(inbound, norm_gain)
    before_a = lax.ppermute(own_a[rows - RADIUS :], "seq", up)
    after_a = lax.ppermute(own_a[:RADIUS], "seq", down)

    grad_own, lower, upper, offset_grad, *parts = backward_attention(
        meta, before_b, own_b, after_b, cotangent, offsets, slots, group, 0, heads
    )
    from_before = lax.ppermute(upper, "seq", up)
    from_after = lax.ppermute(lower, "seq", down)
    weight_sum = lax.psum_scatter(parts[0], "seq", scatter_dimension=2, tiled=True).astype(F32)

    output = forward_attention(meta, before_a, own_a, after_a, inbound, offsets, slots, group)
    final_normed, unused = norm_rows(output, final_gain[None])
    relaid = lax.all_to_all(final_normed, "seq", split_axis=1, concat_axis=0, tiled=True)
    kept = jnp.where(section_index == section_count - 1, relaid, jnp.zeros_like(relaid))
    memory = lax.psum_scatter(kept, "section", scatter_dimension=0, tiled=True)

    input_grad, gain_part = finish(
        grad_own, from_before, from_after, stash[0], inverse_b, norm_gain, cotangent
    )
    bias_part = jnp.dot(
        offset_grad[:, 0, :], onehot, precision=lax.Precision.HIGHEST
    ).T
    bias_sum = lax.psum_scatter(
        bias_part.astype(BF16), "seq", scatter_dimension=0, tiled=True
    ).astype(F32)
    gain_sum = lax.psum_scatter(
        gain_part.astype(BF16), "seq", scatter_dimension=1, tiled=True
    ).astype(F32)
    return (output[None], input_grad[None], weight_sum[None], bias_sum[None], gain_sum, memory)


def choose_body(embedded, carried, stash, returned, loss_grad, qkv_weight, rel_bias, norm_gain, final_gain):
    parts = lax.axis_size("seq")
    rows, width = embedded.shape
    even = width % (HEAD_DIM * parts) == 0 and HEAD_DIM % (32 * parts) == 0 and rows == 128
    sections = lax.axis_size("section")
    even = even and sections % 2 == 0
    even = even and rel_bias.shape[1] == 8 * parts and rows * parts % (16 * sections) == 0
    chosen = heads_body if even else tokens_body
    return chosen(
        embedded, carried, stash, returned, loss_grad, qkv_weight, rel_bias, norm_gain, final_gain
    )


def solution(mesh):
    in_specs = (
        P("seq", None),
        P("section", "seq", None),
        P("section", "seq", None),
        P("section", "seq", None),
        P("seq", None),
        P("section", None, None, "seq", None),
        P("section", None, None),
        P("section", None),
        P(),
    )
    out_specs = (
        P("section", "seq", None),
        P("section", "seq", None),
        P("section", None, None, "seq", None),
        P("section", "seq", None),
        P("section", "seq"),
        P("section", "seq"),
    )
    return jax.shard_map(choose_body, mesh=mesh, in_specs=in_specs, out_specs=out_specs, check_vma=False)
```

```python
import functools

import jax
import jax.numpy as jnp
import numpy as np
from jax import lax
from jax.experimental import pallas as pl
from jax.experimental.pallas import tpu as pltpu
from jax.sharding import PartitionSpec as P

RADIUS = 96
HEAD_DIM = 128
ROW_BLOCK = 64
WINDOW = ROW_BLOCK + 2 * RADIUS
eps_norm = 1e-06
bucket_edges = (1, 2, 3, 4, 5, 6, 7, 8, 11, 16, 22, 32, 45, 64, 90)
masked_score = -1e30
F32 = jnp.float32
BF16 = jnp.bfloat16
VMEM_LIMIT = 24 * 1024 * 1024


def bucket_onehot(bucket_count):
    offsets = np.arange(WINDOW) - RADIUS
    magnitude = np.abs(offsets)
    counted = np.zeros(offsets.shape, np.int32)
    for threshold in bucket_edges:
        counted = counted + (magnitude >= threshold)
    counted = counted + 16 * (offsets > 0)
    onehot = (counted[:, None] == np.arange(bucket_count)[None, :]) & (magnitude <= RADIUS)[:, None]
    return onehot.astype(np.float32)


def dot_nn(a, b):
    return lax.dot_general(a, b, (((1,), (0,)), ((), ())), preferred_element_type=F32)


def dot_nt(a, b):
    return lax.dot_general(a, b, (((1,), (1,)), ((), ())), preferred_element_type=F32)


def dot_tn(a, b):
    return lax.dot_general(a, b, (((0,), (0,)), ((), ())), preferred_element_type=F32)


def norm_kernel(x_ref, gain_ref, normed_ref, inverse_ref):
    x = x_ref[...].astype(F32)
    inverse = lax.rsqrt(jnp.mean(x * x, axis=-1, keepdims=True) + eps_norm)
    normed_ref[...] = (x * inverse * gain_ref[...]).astype(BF16)
    inverse_ref[...] = jnp.broadcast_to(inverse, inverse_ref.shape)


def norm_rows(x, gain):
    rows, width = x.shape
    return pl.pallas_call(
        norm_kernel,
        out_shape=(
            jax.ShapeDtypeStruct((rows, width), BF16),
            jax.ShapeDtypeStruct((rows, 128), F32),
        ),
        compiler_params=pltpu.CompilerParams(vmem_limit_bytes=VMEM_LIMIT),
        cost_estimate=pl.CostEstimate(
            flops=6 * rows * width, bytes_accessed=4 * rows * width, transcendentals=rows
        ),
        name="norm_rows",
    )(x, gain)


def load_weight(meta_ref, slot_refs, weight_ref, head, slots):
    depth = HEAD_DIM // slots
    for r, slot_ref in enumerate(slot_refs):
        if slots == 1:
            start = 0
        else:
            start = pl.multiple_of(lax.rem(meta_ref[0] + r, slots) * depth, depth)
        for j in range(3):
            weight_ref[head, pl.ds(start, depth), j * HEAD_DIM : (j + 1) * HEAD_DIM] = slot_ref[j, head]
    return weight_ref[head]


def key_mask(meta_ref, first_key):
    key = lax.broadcasted_iota(jnp.int32, (1, WINDOW), 1) + first_key
    inside = (key >= meta_ref[1]) & (key < meta_ref[2])
    return jnp.where(inside, 0.0, masked_score).astype(F32)


def toeplitz(row):
    return pltpu.roll(
        jnp.broadcast_to(row, (ROW_BLOCK, WINDOW)), 0, 1, stride=1, stride_axis=0
    )


def diagonal_sums(values):
    total = values[:8]
    for a in range(1, ROW_BLOCK // 8):
        total = total + pltpu.roll(values[8 * a : 8 * a + 8], WINDOW - 8 * a, 1)
    row = lax.broadcasted_iota(jnp.int32, total.shape, 0)
    for bit in (1, 2, 4):
        total = jnp.where((row & bit) != 0, pltpu.roll(total, WINDOW - bit, 1), total)
    return jnp.sum(total, axis=0, keepdims=True)


def block_probs(query_rows, key_rows, bias):
    return score_probs(dot_nt(query_rows, key_rows), bias)


def score_probs(products, bias):
    scores = products * (HEAD_DIM ** (-0.5)) + bias
    weights = jnp.exp(scores - jnp.max(scores, axis=-1, keepdims=True))
    return weights * (1.0 / jnp.sum(weights, axis=-1, keepdims=True))


def forward_kernel(slots, group, meta_ref, before_ref, own_ref, after_ref, x_ref, offset_ref, *rest):
    slot_refs = rest[:slots]
    out_ref, weight_ref = rest[slots:]
    rows = own_ref.shape[0]
    blocks = rows // ROW_BLOCK
    masks = [key_mask(meta_ref, b * ROW_BLOCK) for b in range(blocks)]
    for g in range(group):
        columns = slice(g * HEAD_DIM, (g + 1) * HEAD_DIM)
        weight = load_weight(meta_ref, slot_refs, weight_ref, g, slots)
        own = own_ref[:, columns]
        extended = jnp.concatenate([before_ref[:, columns], own, after_ref[:, columns]], axis=0)
        query = dot_nn(own, weight[:, :HEAD_DIM]).astype(BF16)
        key_value = dot_nn(extended, weight[:, HEAD_DIM:]).astype(BF16)
        key, value = key_value[:, :HEAD_DIM], key_value[:, HEAD_DIM:]
        bias = toeplitz(offset_ref[g])
        for b in range(blocks):
            first = b * ROW_BLOCK
            window = slice(first, first + WINDOW)
            probs = block_probs(query[first : first + ROW_BLOCK], key[window], bias + masks[b])
            attended = dot_nn(probs.astype(BF16), value[window])
            kept = x_ref[first : first + ROW_BLOCK, columns].astype(F32)
            out_ref[first : first + ROW_BLOCK, columns] = (kept + attended).astype(BF16)


def column_spec(rows, group, first):
    return pl.BlockSpec((rows, group * HEAD_DIM), lambda i, meta: (0, i + first))


def slot_specs(weight_slots, group):
    return [
        pl.BlockSpec((3, group, slot.shape[2], HEAD_DIM), lambda i, meta: (0, i, 0, 0))
        for slot in weight_slots
    ]


def forward_attention(meta, before, own, after, x, offsets, weight_slots, group):
    rows, width = own.shape
    heads = width // HEAD_DIM
    slots = len(weight_slots)
    return pl.pallas_call(
        functools.partial(forward_kernel, slots, group),
        out_shape=jax.ShapeDtypeStruct((rows, width), BF16),
        grid_spec=pltpu.PrefetchScalarGridSpec(
            num_scalar_prefetch=1,
            grid=(heads // group,),
            in_specs=[
                column_spec(RADIUS, group, 0),
                column_spec(rows, group, 0),
                column_spec(RADIUS, group, 0),
                column_spec(rows, group, 0),
                pl.BlockSpec((group, 1, WINDOW), lambda i, meta: (i, 0, 0)),
                *slot_specs(weight_slots, group),
            ],
            out_specs=column_spec(rows, group, 0),
            scratch_shapes=[pltpu.VMEM((group, HEAD_DIM, 3 * HEAD_DIM), BF16)],
        ),
        compiler_params=pltpu.CompilerParams(vmem_limit_bytes=VMEM_LIMIT),
        cost_estimate=pl.CostEstimate(
            flops=heads * 60_000_000, bytes_accessed=8 * rows * width, transcendentals=heads * 32768
        ),
        name="forward_attention",
    )(meta, before, own, after, x, offsets, *weight_slots)


def backward_kernel(slots, group, meta_ref, before_ref, own_ref, after_ref, cot_ref, offset_ref, *rest):
    slot_refs = rest[:slots]
    rest = rest[slots:]
    grad_ref, lower_ref, upper_ref, offset_grad_ref = rest[:4]
    part_refs = rest[4 : 4 + slots]
    weight_ref, part_ref = rest[4 + slots :]
    rows = own_ref.shape[0]
    blocks = rows // ROW_BLOCK
    scale = HEAD_DIM ** (-0.5)
    masks = [key_mask(meta_ref, b * ROW_BLOCK) for b in range(blocks)]
    for g in range(group):
        columns = slice(g * HEAD_DIM, (g + 1) * HEAD_DIM)
        weight = load_weight(meta_ref, slot_refs, weight_ref, g, slots)
        own = own_ref[:, columns]
        extended = jnp.concatenate([before_ref[:, columns], own, after_ref[:, columns]], axis=0)
        query = dot_nn(own, weight[:, :HEAD_DIM]).astype(BF16)
        key_value = dot_nn(extended, weight[:, HEAD_DIM:]).astype(BF16)
        key, value = key_value[:, :HEAD_DIM], key_value[:, HEAD_DIM:]
        bias = toeplitz(offset_ref[g])
        grad_query, grad_key, grad_value, score_sum = [], [], [], None
        for b in range(blocks):
            first = b * ROW_BLOCK
            window = slice(first, first + WINDOW)
            query_rows = query[first : first + ROW_BLOCK]
            cot_rows = cot_ref[first : first + ROW_BLOCK, columns]
            probs = block_probs(query_rows, key[window], bias + masks[b])
            grad_probs = dot_nt(cot_rows, value[window])
            delta = jnp.sum(probs * grad_probs, axis=-1, keepdims=True)
            grad_scores = probs * (grad_probs - delta)
            score_sum = grad_scores if score_sum is None else score_sum + grad_scores
            grad_packed = grad_scores.astype(BF16)
            grad_query.append(dot_nn(grad_packed, key[window]))
            grad_key.append(dot_tn(grad_packed, query_rows))
            grad_value.append(dot_tn(probs.astype(BF16), cot_rows))

        def joined(parts):
            pieces = []
            for u in range((rows + 2 * RADIUS) // ROW_BLOCK):
                total = None
                for b in range(blocks):
                    if 0 <= u - b < WINDOW // ROW_BLOCK:
                        piece = parts[b][(u - b) * ROW_BLOCK : (u - b + 1) * ROW_BLOCK]
                        total = piece if total is None else total + piece
                pieces.append(total)
            return jnp.concatenate(pieces, axis=0)

        dquery = (jnp.concatenate(grad_query, axis=0) * scale).astype(BF16)
        dkey = (joined(grad_key) * scale).astype(BF16)
        dvalue = joined(grad_value).astype(BF16)
        dkey_value = jnp.concatenate([dkey, dvalue], axis=1)
        grad_extended = dot_nt(dkey_value, weight[:, HEAD_DIM:])
        grad_ref[:, columns] = grad_extended[RADIUS : RADIUS + rows] + dot_nt(dquery, weight[:, :HEAD_DIM])
        lower_ref[:, columns] = grad_extended[:RADIUS].astype(BF16)
        upper_ref[:, columns] = grad_extended[RADIUS + rows :].astype(BF16)
        part_ref[g, :, :HEAD_DIM] = dot_tn(own, dquery)
        part_ref[g, :, HEAD_DIM:] = dot_tn(extended, dkey_value)
        depth = HEAD_DIM // slots
        for r in range(slots):
            if slots == 1:
                start = 0
            else:
                start = pl.multiple_of(lax.rem(meta_ref[0] + r, slots) * depth, depth)
            for j in range(3):
                part_refs[r][j, g] = part_ref[
                    g, pl.ds(start, depth), j * HEAD_DIM : (j + 1) * HEAD_DIM
                ].astype(part_refs[r].dtype)
        offset_grad_ref[g] = diagonal_sums(score_sum)


def backward_attention(meta, before, own, after, cotangent, offsets, weight_slots, group, first_head, heads):
    rows = own.shape[0]
    width = heads * HEAD_DIM
    slots = len(weight_slots)
    first = first_head // group
    slot_shape = weight_slots[0].shape
    part_types = [F32] + [BF16] * (slots - 1) if slots > 1 else [BF16]
    return pl.pallas_call(
        functools.partial(backward_kernel, slots, group),
        out_shape=(
            jax.ShapeDtypeStruct((rows, width), F32),
            jax.ShapeDtypeStruct((RADIUS, width), BF16),
            jax.ShapeDtypeStruct((RADIUS, width), BF16),
            jax.ShapeDtypeStruct((heads, 1, WINDOW), F32),
            *[jax.ShapeDtypeStruct(slot_shape, kind) for kind in part_types],
        ),
        grid_spec=pltpu.PrefetchScalarGridSpec(
            num_scalar_prefetch=1,
            grid=(heads // group,),
            in_specs=[
                column_spec(RADIUS, group, first),
                column_spec(rows, group, first),
                column_spec(RADIUS, group, first),
                column_spec(rows, group, first),
                pl.BlockSpec((group, 1, WINDOW), lambda i, meta: (i + first, 0, 0)),
                *slot_specs(weight_slots, group),
            ],
            out_specs=(
                column_spec(rows, group, 0),
                column_spec(RADIUS, group, 0),
                column_spec(RADIUS, group, 0),
                pl.BlockSpec((group, 1, WINDOW), lambda i, meta: (i, 0, 0)),
                *slot_specs(weight_slots, group),
            ),
            scratch_shapes=[
                pltpu.VMEM((group, HEAD_DIM, 3 * HEAD_DIM), BF16),
                pltpu.VMEM((group, HEAD_DIM, 3 * HEAD_DIM), F32),
            ],
        ),
        compiler_params=pltpu.CompilerParams(vmem_limit_bytes=VMEM_LIMIT),
        cost_estimate=pl.CostEstimate(
            flops=heads * 150_000_000, bytes_accessed=12 * rows * width, transcendentals=heads * 32768
        ),
        name="backward_attention",
    )(meta, before, own, after, cotangent, offsets, *weight_slots)


def finish_kernel(grad_ref, low_ref, high_ref, x_ref, inverse_ref, gain_ref, cot_ref, out_ref, gain_grad_ref):
    rows = x_ref.shape[0]
    grad = grad_ref[...]
    edge = jnp.zeros((rows - RADIUS, grad.shape[1]), F32)
    grad = grad + jnp.concatenate([low_ref[...].astype(F32), edge], axis=0)
    grad = grad + jnp.concatenate([edge, high_ref[...].astype(F32)], axis=0)
    x = x_ref[...].astype(F32)
    inverse = inverse_ref[:, :1]
    gain_grad_ref[...] = jnp.sum(grad * x * inverse, axis=0, keepdims=True)
    scaled = grad * gain_ref[...]
    mean = jnp.mean(scaled * x, axis=-1, keepdims=True)
    result = inverse * scaled - x * (inverse * inverse * inverse * mean)
    out_ref[...] = (cot_ref[...].astype(F32) + result).astype(BF16)


def finish(grad, low, high, x, inverse, gain, cotangent):
    rows, width = x.shape
    return pl.pallas_call(
        finish_kernel,
        out_shape=(
            jax.ShapeDtypeStruct((rows, width), BF16),
            jax.ShapeDtypeStruct((1, width), F32),
        ),
        compiler_params=pltpu.CompilerParams(vmem_limit_bytes=VMEM_LIMIT),
        cost_estimate=pl.CostEstimate(
            flops=16 * rows * width, bytes_accessed=14 * rows * width, transcendentals=0
        ),
        name="finish",
    )(grad, low, high, x, inverse, gain, cotangent)


def column_of(row, rows):
    return jnp.transpose(jnp.broadcast_to(row, (128, rows)))


def split_rows(inverse, pad_rows, width):
    high = inverse.astype(BF16)
    rest = inverse - high.astype(F32)
    middle = rest.astype(BF16)
    low = (rest - middle.astype(F32)).astype(BF16)
    wide = [jnp.transpose(jnp.broadcast_to(v.astype(F32), (v.shape[0], 128)))[:1] for v in (high, middle, low)]
    row = jnp.concatenate(wide + [jnp.zeros((pad_rows - 3, wide[0].shape[1]), F32)], axis=0)
    return row.astype(BF16)


def row_inverse(x):
    x = x.astype(F32)
    return lax.rsqrt(jnp.mean(x * x, axis=-1, keepdims=True) + eps_norm)


def pack_stash_kernel(parts, pieces, meta_ref, x_hbm, gain_hbm, weight_hbm, inverse_ref, *refs):
    out_refs = refs[:parts]
    x_ref, gain_ref, weight_ref, normed_ref, sems = refs[parts:]
    rows, width = x_ref.shape
    depth = weight_ref.shape[2]
    wide = width // parts
    heads = wide // HEAD_DIM
    step = rows // pieces
    gain_copy = pltpu.make_async_copy(gain_hbm, gain_ref, sems.at[0])
    x_copies = [
        pltpu.make_async_copy(x_hbm.at[pl.ds(k * step, step)], x_ref.at[pl.ds(k * step, step)], sems.at[1 + k])
        for k in range(pieces)
    ]
    weight_copies = [
        pltpu.make_async_copy(weight_hbm.at[j], weight_ref.at[j], sems.at[1 + pieces + j]) for j in range(3)
    ]
    for copy in (gain_copy, *x_copies, *weight_copies):
        copy.start()
    gain_copy.wait()
    gain = gain_ref[...]
    for k, copy in enumerate(x_copies):
        copy.wait()
        part = slice(k * step, (k + 1) * step)
        inverse = row_inverse(x_ref[part])
        inverse_ref[part] = jnp.broadcast_to(inverse, (step, 128))
        normed_ref[part] = (x_ref[part].astype(F32) * inverse * gain).astype(BF16)
    for r, out_ref in enumerate(out_refs):
        target = lax.rem(meta_ref[0] + r, parts)
        out_ref[:rows] = normed_ref[:, pl.ds(pl.multiple_of(target * wide, 128), wide)]
    for j, copy in enumerate(weight_copies):
        copy.wait()
        for r, out_ref in enumerate(out_refs):
            target = lax.rem(meta_ref[0] + r, parts)
            for h in range(heads):
                out_ref[rows + j * depth : rows + (j + 1) * depth, h * HEAD_DIM : (h + 1) * HEAD_DIM] = weight_ref[
                    j, target * heads + h
                ]


def pack_rows_kernel(parts, with_inverse, meta_ref, edge_ref, inner_ref, *out_refs):
    rows, width = inner_ref.shape
    wide = width // parts
    edge = 1 if with_inverse else 2
    refs = out_refs[:parts]
    for r, out_ref in enumerate(refs):
        target = lax.rem(meta_ref[0] + r, parts)
        start = pl.multiple_of(target * wide, 128)

        @pl.when(meta_ref[edge] == 1)
        def use_edge():
            out_ref[:rows] = edge_ref[:, pl.ds(start, wide)]

        @pl.when(meta_ref[edge] == 0)
        def use_inner():
            out_ref[:rows] = inner_ref[:, pl.ds(start, wide)]

    def finish_with(source_ref):
        if with_inverse:
            tail = split_rows(row_inverse(source_ref[...]), 16, wide)
            for out_ref in refs:
                out_ref[rows:] = jnp.zeros((16, wide), BF16)
                out_ref[rows:, :rows] = tail
        else:
            out_refs[parts][...] = source_ref[...]

    @pl.when(meta_ref[edge] == 1)
    def finish_edge():
        finish_with(edge_ref)

    @pl.when(meta_ref[edge] == 0)
    def finish_inner():
        finish_with(inner_ref)


SMEM_SPEC = pl.BlockSpec(memory_space=pltpu.SMEM)
VMEM_SPEC = pl.BlockSpec(memory_space=pltpu.VMEM)


def pack_stash(meta, x, gain, weight, parts):
    rows, width = x.shape
    depth = weight.shape[2]
    shape = (rows + 3 * depth, width // parts)
    return pl.pallas_call(
        functools.partial(pack_stash_kernel, parts, 4),
        out_shape=(
            jax.ShapeDtypeStruct((rows, 128), F32),
            *[jax.ShapeDtypeStruct(shape, BF16) for r in range(parts)],
        ),
        in_specs=[SMEM_SPEC] + [pl.BlockSpec(memory_space=pl.ANY)] * 3,
        out_specs=(VMEM_SPEC,) * (parts + 1),
        scratch_shapes=[
            pltpu.VMEM((rows, width), BF16),
            pltpu.VMEM((1, width), F32),
            pltpu.VMEM(weight.shape, BF16),
            pltpu.VMEM((rows, width), BF16),
            pltpu.SemaphoreType.DMA((8,)),
        ],
        compiler_params=pltpu.CompilerParams(vmem_limit_bytes=VMEM_LIMIT),
        cost_estimate=pl.CostEstimate(flops=4 * rows * width, bytes_accessed=6 * rows * width, transcendentals=0),
        name="pack_stash",
    )(meta, x, gain, weight)


def pack_rows(meta, edge, inner, parts, with_inverse):
    rows, width = inner.shape
    shape = (rows + (16 if with_inverse else 0), width // parts)
    extra = () if with_inverse else (jax.ShapeDtypeStruct((rows, width), BF16),)
    return pl.pallas_call(
        functools.partial(pack_rows_kernel, parts, with_inverse),
        out_shape=(*[jax.ShapeDtypeStruct(shape, BF16) for r in range(parts)], *extra),
        in_specs=[SMEM_SPEC, VMEM_SPEC, VMEM_SPEC],
        out_specs=(VMEM_SPEC,) * (parts + len(extra)),
        compiler_params=pltpu.CompilerParams(vmem_limit_bytes=VMEM_LIMIT),
        cost_estimate=pl.CostEstimate(flops=4 * rows * width, bytes_accessed=6 * rows * width, transcendentals=0),
        name="pack_inbound" if with_inverse else "pack_cotangent",
    )(meta, edge, inner)


def gather_rows(meta_ref, refs, rows, x_ref):
    parts = len(refs)
    for r, ref in enumerate(refs):
        source = lax.rem(meta_ref[0] + parts - r, parts)
        x_ref[pl.ds(pl.multiple_of(source * rows, rows), rows)] = ref[:rows]


def gather_weight(meta_ref, refs, rows, weight_ref):
    parts = len(refs)
    depth = HEAD_DIM // parts
    for r, ref in enumerate(refs):
        source = lax.rem(meta_ref[0] + parts - r, parts)
        depth_at = pl.ds(pl.multiple_of(source * depth, depth), depth)
        for j in range(3):
            weight_ref[depth_at, j * HEAD_DIM : (j + 1) * HEAD_DIM] = ref[
                rows + j * depth : rows + (j + 1) * depth
            ]


def gather_inverse(meta_ref, refs, rows, inverse_ref):
    parts = len(refs)

    @pl.when(pl.program_id(0) == 0)
    def spread_inverse():
        for r, ref in enumerate(refs):
            source = lax.rem(meta_ref[0] + parts - r, parts)
            tail = ref[rows : rows + 16].astype(F32)
            inverse_ref[pl.ds(pl.multiple_of(source * rows, rows), rows)] = column_of(
                tail[:1] + tail[1:2] + tail[2:3], rows
            )


def block_mask(first_query, tokens):
    key = lax.broadcasted_iota(jnp.int32, (1, WINDOW), 1) + (first_query - RADIUS)
    return jnp.where((key >= 0) & (key < tokens), 0.0, masked_score).astype(F32)


def edge_bias(bias, first, tokens):
    if first < RADIUS or first + ROW_BLOCK + RADIUS > tokens:
        return bias + block_mask(first, tokens)
    return bias


def padded(rows):
    edge = jnp.zeros((RADIUS, rows.shape[1]), rows.dtype)
    return jnp.concatenate([edge, rows, edge], axis=0)


def heads_backward_kernel(parts, rows, meta_ref, *refs):
    a_refs, c_refs = refs[:parts], refs[parts : 2 * parts]
    gain_ref, offset_ref, onehot_ref, after_ref = refs[2 * parts : 2 * parts + 4]
    out_refs = refs[2 * parts + 4 : 3 * parts + 4]
    gain_grad_ref, x_ref, weight_ref, cot_ref, grad_ref, part_ref, bias_ref = refs[3 * parts + 4 :]
    tokens = rows * parts
    depth = HEAD_DIM // parts
    scale = HEAD_DIM ** (-0.5)
    gather_rows(meta_ref, a_refs, rows, x_ref)
    gather_weight(meta_ref, a_refs, rows, weight_ref)
    gather_rows(meta_ref, c_refs, rows, cot_ref)
    weight = weight_ref[...]
    normed = x_ref[...]
    query = dot_nn(normed, weight[:, :HEAD_DIM]).astype(BF16)
    key = padded(dot_nn(normed, weight[:, HEAD_DIM : 2 * HEAD_DIM]).astype(BF16))
    value = padded(dot_nn(normed, weight[:, 2 * HEAD_DIM :]).astype(BF16))
    bias = toeplitz(offset_ref[0])
    blocks = tokens // ROW_BLOCK
    starts = range(0, tokens, ROW_BLOCK)
    cot = cot_ref[...]
    query_rows = [query[f : f + ROW_BLOCK] for f in starts]
    cot_rows = [cot[f : f + ROW_BLOCK] for f in starts]
    products = [dot_nt(rows_q, key[f : f + WINDOW]) for f, rows_q in zip(starts, query_rows)]
    grad_probs = [dot_nt(rows_c, value[f : f + WINDOW]) for f, rows_c in zip(starts, cot_rows)]
    packed, grad_packed, score_sum = [], [], None
    for f, product, grads in zip(starts, products, grad_probs):
        probs = score_probs(product, edge_bias(bias, f, tokens))
        delta = jnp.sum(probs * grads, axis=-1, keepdims=True)
        grad_scores = probs * (grads - delta)
        score_sum = grad_scores if score_sum is None else score_sum + grad_scores
        packed.append(probs.astype(BF16))
        grad_packed.append(grad_scores.astype(BF16))
    grad_query = [dot_nn(part, key[f : f + WINDOW]) for f, part in zip(starts, grad_packed)]
    grad_key = [dot_tn(part, rows_q) for part, rows_q in zip(grad_packed, query_rows)]
    grad_value = [dot_tn(part, rows_c) for part, rows_c in zip(packed, cot_rows)]

    def joined(pieces):
        units = []
        for u in range((tokens + 2 * RADIUS) // ROW_BLOCK):
            total = None
            for b in range(blocks):
                if 0 <= u - b < WINDOW // ROW_BLOCK:
                    piece = pieces[b][(u - b) * ROW_BLOCK : (u - b + 1) * ROW_BLOCK]
                    total = piece if total is None else total + piece
            units.append(total)
        return jnp.concatenate(units, axis=0)[RADIUS : RADIUS + tokens]

    dqkv = jnp.concatenate(
        [
            (jnp.concatenate(grad_query, axis=0) * scale).astype(BF16),
            (joined(grad_key) * scale).astype(BF16),
            joined(grad_value).astype(BF16),
        ],
        axis=1,
    )
    grad_normed = dot_nt(dqkv, weight)
    gain_grad_ref[...] = jnp.sum(grad_normed * normed.astype(F32), axis=0, keepdims=True) / gain_ref[...]
    grad_ref[...] = grad_normed
    part_ref[...] = dot_tn(normed, dqkv)
    bias_grad = jnp.sum(onehot_ref[...] * diagonal_sums(score_sum), axis=1, keepdims=True)
    bias_ref[...] = jnp.broadcast_to(bias_grad, bias_ref.shape)
    buckets = bias_ref.shape[0] // parts
    for r, out_ref in enumerate(out_refs):
        source = lax.rem(meta_ref[0] + parts - r, parts)
        out_ref[:rows] = grad_ref[pl.ds(pl.multiple_of(source * rows, rows), rows)].astype(BF16)
        for j in range(3):
            out_ref[rows + j * depth : rows + (j + 1) * depth] = part_ref[
                pl.ds(pl.multiple_of(source * depth, depth), depth), j * HEAD_DIM : (j + 1) * HEAD_DIM
            ].astype(BF16)
        share = bias_ref[pl.ds(pl.multiple_of(source * buckets, buckets), buckets)]
        out_ref[rows + 3 * depth :] = jnp.concatenate(
            [share, jnp.zeros((16 - buckets, HEAD_DIM), F32)], axis=0
        ).astype(BF16)


def head_column(rows, first=0):
    return pl.BlockSpec((rows, HEAD_DIM), lambda i, meta: (0, i + first))


def whole_column(rows, heads, first=0):
    return pl.BlockSpec((rows, HEAD_DIM), lambda i, meta: (0, meta[0] * heads + first + i))


def offset_spec(heads, first=0):
    return pl.BlockSpec((1, 1, WINDOW), lambda i, meta: (meta[0] * heads + first + i, 0, 0))


def heads_backward(meta, a_slots, c_slots, gain, offsets, onehot, after, heads, first, count):
    parts = len(a_slots)
    rows = c_slots[0].shape[0]
    tokens = rows * parts
    buckets = onehot.shape[0]
    packed = a_slots[0].shape[0]
    made = packed + 16
    width = count * HEAD_DIM
    return pl.pallas_call(
        functools.partial(heads_backward_kernel, parts, rows),
        out_shape=(
            *[jax.ShapeDtypeStruct((made, width), BF16) for r in range(parts)],
            jax.ShapeDtypeStruct((1, width), F32),
        ),
        grid_spec=pltpu.PrefetchScalarGridSpec(
            num_scalar_prefetch=1,
            grid=(count,),
            in_specs=[
                *[head_column(packed, first)] * parts,
                whole_column(rows, heads, first),
                *[head_column(rows, first)] * (parts - 1),
                whole_column(1, heads, first),
                offset_spec(heads, first),
                pl.BlockSpec((buckets, WINDOW), lambda i, meta: (0, 0)),
                pl.BlockSpec(memory_space=pl.ANY),
            ],
            out_specs=(*[head_column(made)] * parts, head_column(1)),
            scratch_shapes=[
                pltpu.VMEM((tokens, HEAD_DIM), BF16),
                pltpu.VMEM((HEAD_DIM, 3 * HEAD_DIM), BF16),
                pltpu.VMEM((tokens, HEAD_DIM), BF16),
                pltpu.VMEM((tokens, HEAD_DIM), F32),
                pltpu.VMEM((HEAD_DIM, 3 * HEAD_DIM), F32),
                pltpu.VMEM((buckets, HEAD_DIM), F32),
            ],
        ),
        compiler_params=pltpu.CompilerParams(vmem_limit_bytes=VMEM_LIMIT),
        cost_estimate=pl.CostEstimate(
            flops=count * tokens * 400_000, bytes_accessed=tokens * width, transcendentals=0
        ),
        name="heads_backward",
    )(meta, *a_slots, *c_slots, gain, offsets, onehot, after)


def heads_forward_kernel(parts, rows, meta_ref, *refs):
    a_refs, i_refs = refs[:parts], refs[parts : 2 * parts]
    gain_ref, offset_ref = refs[2 * parts : 2 * parts + 2]
    out_refs = refs[2 * parts + 2 : 3 * parts + 2]
    inverse_ref, x_ref, weight_ref, made_ref, square_ref = refs[3 * parts + 2 :]
    tokens = rows * parts
    gather_rows(meta_ref, i_refs, rows, x_ref)
    gather_weight(meta_ref, a_refs, rows, weight_ref)
    gather_inverse(meta_ref, i_refs, rows, inverse_ref)
    weight = weight_ref[...]
    normed = (x_ref[...].astype(F32) * inverse_ref[...] * gain_ref[...]).astype(BF16)
    query = dot_nn(normed, weight[:, :HEAD_DIM]).astype(BF16)
    key = padded(dot_nn(normed, weight[:, HEAD_DIM : 2 * HEAD_DIM]).astype(BF16))
    value = padded(dot_nn(normed, weight[:, 2 * HEAD_DIM :]).astype(BF16))
    bias = toeplitz(offset_ref[0])
    starts = range(0, tokens, ROW_BLOCK)
    products = [dot_nt(query[f : f + ROW_BLOCK], key[f : f + WINDOW]) for f in starts]
    packed = [
        score_probs(product, edge_bias(bias, f, tokens)).astype(BF16) for f, product in zip(starts, products)
    ]
    attended = [dot_nn(part, value[f : f + WINDOW]) for f, part in zip(starts, packed)]
    for f, part in zip(starts, attended):
        made_ref[f : f + ROW_BLOCK] = (x_ref[f : f + ROW_BLOCK].astype(F32) + part).astype(BF16)
    made = made_ref[...].astype(F32)
    squares = made * made

    @pl.when(pl.program_id(0) == 0)
    def first_head():
        square_ref[...] = squares

    @pl.when(pl.program_id(0) > 0)
    def later_head():
        square_ref[...] += squares

    for r, out_ref in enumerate(out_refs):
        source = lax.rem(meta_ref[0] + parts - r, parts)
        out_ref[:rows] = made_ref[pl.ds(pl.multiple_of(source * rows, rows), rows)]

    @pl.when(pl.program_id(0) < pl.num_programs(0) - 1)
    def no_sums():
        for out_ref in out_refs:
            out_ref[rows:] = jnp.zeros((16, HEAD_DIM), BF16)

    @pl.when(pl.program_id(0) == pl.num_programs(0) - 1)
    def last_head():
        rest = jnp.sum(jnp.transpose(square_ref[...]), axis=0, keepdims=True)
        at_row = lax.broadcasted_iota(jnp.int32, (16, rows), 0)
        tail = jnp.zeros((16, rows), F32)
        for k in range(3):
            piece = rest.astype(BF16).astype(F32)
            rest = rest - piece
            for part in range(parts):
                row = jnp.broadcast_to(piece[:, part * rows : (part + 1) * rows], (16, rows))
                tail = jnp.where(at_row == 3 * part + k, row, tail)
        for out_ref in out_refs:
            out_ref[rows:] = tail.astype(BF16)


def heads_forward(meta, a_slots, i_slots, gain, offsets, heads, rows):
    parts = len(a_slots)
    tokens = rows * parts
    packed = a_slots[0].shape[0]
    width = heads * HEAD_DIM
    return pl.pallas_call(
        functools.partial(heads_forward_kernel, parts, rows),
        out_shape=(
            *[jax.ShapeDtypeStruct((rows + 16, width), BF16) for r in range(parts)],
        ),
        grid_spec=pltpu.PrefetchScalarGridSpec(
            num_scalar_prefetch=1,
            grid=(heads,),
            in_specs=[
                *[head_column(packed)] * parts,
                *[head_column(i_slots[0].shape[0])] * parts,
                whole_column(1, heads),
                offset_spec(heads),
            ],
            out_specs=(head_column(rows + 16),) * parts,
            scratch_shapes=[
                pltpu.VMEM((tokens, HEAD_DIM), F32),
                pltpu.VMEM((tokens, HEAD_DIM), BF16),
                pltpu.VMEM((HEAD_DIM, 3 * HEAD_DIM), BF16),
                pltpu.VMEM((tokens, HEAD_DIM), BF16),
                pltpu.VMEM((tokens, HEAD_DIM), F32),
            ],
        ),
        compiler_params=pltpu.CompilerParams(vmem_limit_bytes=VMEM_LIMIT),
        cost_estimate=pl.CostEstimate(
            flops=heads * tokens, bytes_accessed=tokens, transcendentals=0
        ),
        name="heads_forward",
    )(meta, *a_slots, *i_slots, gain, offsets)


def memory_kernel(parts, width, meta_ref, *refs):
    out_refs, other_refs = refs[:parts], refs[parts : 2 * parts - 1]
    gain_ref, *share_refs, memory_ref = refs[2 * parts - 1 :]
    wide = memory_ref.shape[1]
    rows = memory_ref.shape[0] // parts
    total = None
    for ref in (out_refs[0], *other_refs):
        tail = ref[rows:, wide - rows :].astype(F32)
        pieces = [
            tail[3 * p : 3 * p + 1] + tail[3 * p + 1 : 3 * p + 2] + tail[3 * p + 2 : 3 * p + 3]
            for p in range(parts)
        ]
        row = jnp.concatenate(pieces, axis=1)
        total = row if total is None else total + row
    inverse = lax.rsqrt(total / width + eps_norm)
    gain = gain_ref[:, pl.ds(pl.multiple_of(meta_ref[0] * wide, 128), wide)]
    spread_inverse = jnp.transpose(jnp.broadcast_to(inverse, (128, inverse.shape[1])))
    for r, out_ref in enumerate(out_refs):
        source = lax.rem(meta_ref[0] + parts - r, parts)
        memory_ref[pl.ds(pl.multiple_of(source * rows, rows), rows)] = out_ref[:rows]
    made = memory_ref[...].astype(F32)
    memory_ref[...] = (made * spread_inverse[:, :1] * gain).astype(BF16)
    for k, share_ref in enumerate(share_refs):
        size = share_ref.shape[0]
        share_ref[...] = memory_ref[k * size : (k + 1) * size]


def memory_rows(meta, outs, others, gain, width, shares):
    parts = len(outs)
    rows, wide = outs[0].shape[0] - 16, outs[0].shape[1]
    return pl.pallas_call(
        functools.partial(memory_kernel, parts, width),
        out_shape=[jax.ShapeDtypeStruct((rows * parts // shares, wide), BF16)] * shares,
        in_specs=[SMEM_SPEC] + [VMEM_SPEC] * (2 * parts),
        out_specs=[VMEM_SPEC] * shares,
        scratch_shapes=[pltpu.VMEM((rows * parts, wide), BF16)],
        compiler_params=pltpu.CompilerParams(vmem_limit_bytes=VMEM_LIMIT),
        cost_estimate=pl.CostEstimate(flops=rows, bytes_accessed=rows, transcendentals=0),
        name="memory_rows",
    )(meta, *outs, *others, gain)


def place_kernel(parts, meta_ref, *refs):
    out_ref = refs[parts]
    wide = refs[0].shape[1]
    for r in range(parts):
        source = lax.rem(meta_ref[0] + r, parts)
        out_ref[:, pl.ds(pl.multiple_of(source * wide, 128), wide)] = refs[r][: out_ref.shape[0]]


def place_columns(meta, slots):
    parts = len(slots)
    rows, wide = slots[0].shape[0] - 16, slots[0].shape[1]
    return pl.pallas_call(
        functools.partial(place_kernel, parts),
        out_shape=jax.ShapeDtypeStruct((rows, wide * parts), BF16),
        in_specs=[SMEM_SPEC] + [VMEM_SPEC] * parts,
        out_specs=VMEM_SPEC,
        compiler_params=pltpu.CompilerParams(vmem_limit_bytes=VMEM_LIMIT),
        cost_estimate=pl.CostEstimate(flops=0, bytes_accessed=rows, transcendentals=0),
        name="place_columns",
    )(meta, *slots)


def heads_finish_kernel(parts, chunks, meta_ref, *refs):
    g_refs = refs[: parts * chunks]
    x_ref, inverse_ref, gain_ref, cot_ref, out_ref, weight_ref, bias_ref, scaled_ref = refs[parts * chunks :]
    rows, width = x_ref.shape
    wide = width // parts // chunks
    heads = wide // HEAD_DIM
    depth = HEAD_DIM // parts
    buckets = bias_ref.shape[1]
    for c in range(chunks):
        for r in range(parts):
            g_ref = g_refs[c * parts + r]
            place = lax.rem(meta_ref[0] + r, parts) * chunks + c
            columns = pl.ds(pl.multiple_of(place * wide, 128), wide)
            scaled_ref[:, columns] = g_ref[:rows].astype(F32) * gain_ref[:, columns]
            for h in range(heads):
                lanes = slice(h * HEAD_DIM, (h + 1) * HEAD_DIM)
                for j in range(3):
                    weight_ref[j, place * heads + h] = g_ref[
                        rows + j * depth : rows + (j + 1) * depth, lanes
                    ].astype(F32)
                bias_ref[place * heads + h] = g_ref[rows + 3 * depth :, lanes].astype(F32)[:buckets]
    x = x_ref[...].astype(F32)
    scaled = scaled_ref[...]
    inverse = inverse_ref[:, :1]
    mean = jnp.mean(scaled * x, axis=-1, keepdims=True)
    result = inverse * scaled - x * (inverse * inverse * inverse * mean)
    out_ref[...] = (cot_ref[...].astype(F32) + result).astype(BF16)


def heads_finish(meta, g_chunks, x, inverse, gain, cotangent, buckets):
    chunks, parts = len(g_chunks), len(g_chunks[0])
    rows, width = x.shape
    heads = width // HEAD_DIM
    slots = [slot for g_slots in g_chunks for slot in g_slots]
    return pl.pallas_call(
        functools.partial(heads_finish_kernel, parts, chunks),
        out_shape=(
            jax.ShapeDtypeStruct((rows, width), BF16),
            jax.ShapeDtypeStruct((3, heads, HEAD_DIM // parts, HEAD_DIM), F32),
            jax.ShapeDtypeStruct((heads, buckets // parts, HEAD_DIM), F32),
        ),
        in_specs=[SMEM_SPEC] + [VMEM_SPEC] * (len(slots) + 4),
        out_specs=(VMEM_SPEC,) * 3,
        scratch_shapes=[pltpu.VMEM((rows, width), F32)],
        compiler_params=pltpu.CompilerParams(vmem_limit_bytes=VMEM_LIMIT),
        cost_estimate=pl.CostEstimate(flops=12 * rows * width, bytes_accessed=14 * rows * width, transcendentals=0),
        name="heads_finish",
    )(meta, *slots, x, inverse, gain, cotangent)


def offset_table(rel_bias):
    onehot = jnp.asarray(bucket_onehot(rel_bias.shape[0]))
    by_offset = jnp.dot(onehot, rel_bias, precision=lax.Precision.HIGHEST).T
    inside = jnp.arange(WINDOW, dtype=jnp.int32) <= 2 * RADIUS
    return jnp.where(inside[None, :], by_offset, masked_score)[:, None, :]


def shifted(value, axis, steps):
    count = lax.axis_size(axis)
    first, last = (max(0, -steps), min(count, count - steps))
    return lax.ppermute(value, axis, [(source, source + steps) for source in range(first, last)])


def spread_memory(shares, section, sections):
    last = sections - 1
    couple = jnp.where(section == last, shares[-1], 0)
    for s, share in enumerate(shares[:-1]):
        couple = couple + lax.ppermute(share, "section", [(last, 2 * s + 1)])
    half = couple.shape[0] // 2
    even = lax.ppermute(couple[:half], "section", [(s + 1, s) for s in range(0, sections, 2)])
    return jnp.where(section % 2 == 0, even, couple[half:])


def heads_body(
    embedded, carried, stash, returned, loss_grad, qkv_weight, rel_bias, norm_gain, final_gain
):
    section = lax.axis_index("section")
    sections = lax.axis_size("section")
    parts = lax.axis_size("seq")
    rows, width = embedded.shape
    heads = width // HEAD_DIM // parts
    buckets = rel_bias.shape[1]
    meta = jnp.stack(
        [lax.axis_index("seq"), section == 0, section == sections - 1]
    ).astype(jnp.int32)

    def exchanged(sends, direction):
        moved = [
            lax.ppermute(sends[r], "seq", [(i, (i + direction * r) % parts) for i in range(parts)])
            for r in range(1, parts)
        ]
        return [sends[0]] + moved

    inverse_b, *a_sends = pack_stash(meta, stash[0], norm_gain, qkv_weight[0], parts)
    a_slots = exchanged(a_sends, 1)
    arrived = shifted(carried[0], "section", 1)
    came_back = shifted(returned[0], "section", -1)
    i_slots = exchanged(pack_rows(meta, embedded, arrived, parts, True), 1)
    *c_sends, cotangent = pack_rows(meta, loss_grad, came_back, parts, False)
    c_slots = exchanged(c_sends, 1)
    c_slots[0] = cotangent

    offsets = offset_table(rel_bias[0])
    onehot = jnp.asarray(bucket_onehot(buckets).T)
    o_sends = heads_forward(meta, a_slots, i_slots, norm_gain, offsets, heads, rows)
    o_sends, c_slots = lax.optimization_barrier((o_sends, c_slots))
    o_slots = exchanged(o_sends, -1)

    *g_sends, gain_grad = heads_backward(
        meta, a_slots, c_slots, norm_gain, offsets, onehot, o_sends[0], heads, 0, heads
    )
    g_sends, o_slots = lax.optimization_barrier((g_sends, o_slots))
    g_chunks = [exchanged(g_sends, -1)]
    output = place_columns(meta, o_slots)
    shares = memory_rows(meta, o_sends, o_slots[1:], final_gain[None], width, sections // 2)
    memory = spread_memory(shares, section, sections)

    input_grad, weight_grad, bias_wide = heads_finish(
        meta, g_chunks, stash[0], inverse_b, norm_gain, cotangent, buckets
    )
    bias_grad = bias_wide[:, :, 0].T
    return (
        output[None],
        input_grad[None],
        weight_grad[None],
        bias_grad[None],
        gain_grad,
        memory,
    )


def tokens_body(
    embedded, carried, stash, returned, loss_grad, qkv_weight, rel_bias, norm_gain, final_gain
):
    section_index = lax.axis_index("section")
    section_count = lax.axis_size("section")
    seq_index = lax.axis_index("seq")
    seq_count = lax.axis_size("seq")
    rows, width = embedded.shape
    heads = width // HEAD_DIM
    tokens = rows * seq_count
    shard = qkv_weight[0]
    up = [(i, i + 1) for i in range(seq_count - 1)]
    down = [(j, i) for i, j in up]
    group = 4 if heads % 4 == 0 else 1

    own_b, inverse_b = norm_rows(stash[0], norm_gain)
    before_b = lax.ppermute(own_b[rows - RADIUS :], "seq", up)
    after_b = lax.ppermute(own_b[:RADIUS], "seq", down)
    slots = [lax.all_gather(shard, "seq", axis=2, tiled=True)]

    section_up = [(i, (i + 1) % section_count) for i in range(section_count)]
    section_down = [(j, i) for i, j in section_up]
    inbound = lax.ppermute(
        jnp.where(section_index == section_count - 1, embedded, carried[0]), "section", section_up
    )
    cotangent = lax.ppermute(
        jnp.where(section_index == 0, loss_grad, returned[0]), "section", section_down
    )

    onehot = jnp.asarray(bucket_onehot(rel_bias.shape[1]))
    offsets = offset_table(rel_bias[0])
    first_key = RADIUS - seq_index * rows
    meta = jnp.stack([seq_index, first_key, first_key + tokens]).astype(jnp.int32)

    own_a, unused = norm_rows(inbound, norm_gain)
    before_a = lax.ppermute(own_a[rows - RADIUS :], "seq", up)
    after_a = lax.ppermute(own_a[:RADIUS], "seq", down)

    grad_own, lower, upper, offset_grad, *parts = backward_attention(
        meta, before_b, own_b, after_b, cotangent, offsets, slots, group, 0, heads
    )
    from_before = lax.ppermute(upper, "seq", up)
    from_after = lax.ppermute(lower, "seq", down)
    weight_sum = lax.psum_scatter(parts[0], "seq", scatter_dimension=2, tiled=True).astype(F32)

    output = forward_attention(meta, before_a, own_a, after_a, inbound, offsets, slots, group)
    final_normed, unused = norm_rows(output, final_gain[None])
    relaid = lax.all_to_all(final_normed, "seq", split_axis=1, concat_axis=0, tiled=True)
    kept = jnp.where(section_index == section_count - 1, relaid, jnp.zeros_like(relaid))
    memory = lax.psum_scatter(kept, "section", scatter_dimension=0, tiled=True)

    input_grad, gain_part = finish(
        grad_own, from_before, from_after, stash[0], inverse_b, norm_gain, cotangent
    )
    bias_part = jnp.dot(
        offset_grad[:, 0, :], onehot, precision=lax.Precision.HIGHEST
    ).T
    bias_sum = lax.psum_scatter(
        bias_part.astype(BF16), "seq", scatter_dimension=0, tiled=True
    ).astype(F32)
    gain_sum = lax.psum_scatter(
        gain_part.astype(BF16), "seq", scatter_dimension=1, tiled=True
    ).astype(F32)
    return (output[None], input_grad[None], weight_sum[None], bias_sum[None], gain_sum, memory)


def choose_body(embedded, carried, stash, returned, loss_grad, qkv_weight, rel_bias, norm_gain, final_gain):
    parts = lax.axis_size("seq")
    rows, width = embedded.shape
    even = width % (HEAD_DIM * parts) == 0 and HEAD_DIM % (32 * parts) == 0 and rows == 128
    sections = lax.axis_size("section")
    even = even and sections % 2 == 0
    even = even and rel_bias.shape[1] == 8 * parts and rows * parts % (16 * sections) == 0
    chosen = heads_body if even else tokens_body
    return chosen(
        embedded, carried, stash, returned, loss_grad, qkv_weight, rel_bias, norm_gain, final_gain
    )


def solution(mesh):
    in_specs = (
        P("seq", None),
        P("section", "seq", None),
        P("section", "seq", None),
        P("section", "seq", None),
        P("seq", None),
        P("section", None, None, "seq", None),
        P("section", None, None),
        P("section", None),
        P(),
    )
    out_specs = (
        P("section", "seq", None),
        P("section", "seq", None),
        P("section", None, None, "seq", None),
        P("section", "seq", None),
        P("section", "seq"),
        P("section", "seq"),
    )
    return jax.shard_map(choose_body, mesh=mesh, in_specs=in_specs, out_specs=out_specs, check_vma=False)
```

```python
import functools

import jax
import jax.numpy as jnp
import numpy as np
from jax import lax
from jax.experimental import pallas as pl
from jax.experimental.pallas import tpu as pltpu
from jax.sharding import PartitionSpec as P

RADIUS = 96
HEAD_DIM = 128
ROW_BLOCK = 64
WINDOW = ROW_BLOCK + 2 * RADIUS
eps_norm = 1e-06
bucket_edges = (1, 2, 3, 4, 5, 6, 7, 8, 11, 16, 22, 32, 45, 64, 90)
masked_score = -1e30
F32 = jnp.float32
BF16 = jnp.bfloat16
VMEM_LIMIT = 24 * 1024 * 1024
EXTRA = 8


def bucket_onehot(bucket_count):
    offsets = np.arange(WINDOW) - RADIUS
    magnitude = np.abs(offsets)
    counted = np.zeros(offsets.shape, np.int32)
    for threshold in bucket_edges:
        counted = counted + (magnitude >= threshold)
    counted = counted + 16 * (offsets > 0)
    onehot = (counted[:, None] == np.arange(bucket_count)[None, :]) & (magnitude <= RADIUS)[:, None]
    return onehot.astype(np.float32)


def dot_nn(a, b):
    return lax.dot_general(a, b, (((1,), (0,)), ((), ())), preferred_element_type=F32)


def dot_nt(a, b):
    return lax.dot_general(a, b, (((1,), (1,)), ((), ())), preferred_element_type=F32)


def dot_tn(a, b):
    return lax.dot_general(a, b, (((0,), (0,)), ((), ())), preferred_element_type=F32)


def norm_kernel(x_ref, gain_ref, normed_ref, inverse_ref):
    x = x_ref[...].astype(F32)
    inverse = lax.rsqrt(jnp.mean(x * x, axis=-1, keepdims=True) + eps_norm)
    normed_ref[...] = (x * inverse * gain_ref[...]).astype(BF16)
    inverse_ref[...] = jnp.broadcast_to(inverse, inverse_ref.shape)


def norm_rows(x, gain):
    rows, width = x.shape
    return pl.pallas_call(
        norm_kernel,
        out_shape=(
            jax.ShapeDtypeStruct((rows, width), BF16),
            jax.ShapeDtypeStruct((rows, 128), F32),
        ),
        compiler_params=pltpu.CompilerParams(vmem_limit_bytes=VMEM_LIMIT),
        cost_estimate=pl.CostEstimate(
            flops=6 * rows * width, bytes_accessed=4 * rows * width, transcendentals=rows
        ),
        name="norm_rows",
    )(x, gain)


def load_weight(meta_ref, slot_refs, weight_ref, head, slots):
    depth = HEAD_DIM // slots
    for r, slot_ref in enumerate(slot_refs):
        if slots == 1:
            start = 0
        else:
            start = pl.multiple_of(lax.rem(meta_ref[0] + r, slots) * depth, depth)
        for j in range(3):
            weight_ref[head, pl.ds(start, depth), j * HEAD_DIM : (j + 1) * HEAD_DIM] = slot_ref[j, head]
    return weight_ref[head]


def key_mask(meta_ref, first_key):
    key = lax.broadcasted_iota(jnp.int32, (1, WINDOW), 1) + first_key
    inside = (key >= meta_ref[1]) & (key < meta_ref[2])
    return jnp.where(inside, 0.0, masked_score).astype(F32)


def toeplitz(row):
    return pltpu.roll(
        jnp.broadcast_to(row, (ROW_BLOCK, WINDOW)), 0, 1, stride=1, stride_axis=0
    )


def diagonal_sums(values):
    total = values[:8]
    for a in range(1, ROW_BLOCK // 8):
        total = total + pltpu.roll(values[8 * a : 8 * a + 8], WINDOW - 8 * a, 1)
    row = lax.broadcasted_iota(jnp.int32, total.shape, 0)
    for bit in (1, 2, 4):
        total = jnp.where((row & bit) != 0, pltpu.roll(total, WINDOW - bit, 1), total)
    return jnp.sum(total, axis=0, keepdims=True)


def block_probs(query_rows, key_rows, bias):
    return score_probs(dot_nt(query_rows, key_rows), bias)


def score_probs(products, bias):
    scores = products * (HEAD_DIM ** (-0.5)) + bias
    weights = jnp.exp(scores - jnp.max(scores, axis=-1, keepdims=True))
    return weights * (1.0 / jnp.sum(weights, axis=-1, keepdims=True))


def forward_kernel(slots, group, meta_ref, before_ref, own_ref, after_ref, x_ref, offset_ref, *rest):
    slot_refs = rest[:slots]
    out_ref, weight_ref = rest[slots:]
    rows = own_ref.shape[0]
    blocks = rows // ROW_BLOCK
    masks = [key_mask(meta_ref, b * ROW_BLOCK) for b in range(blocks)]
    for g in range(group):
        columns = slice(g * HEAD_DIM, (g + 1) * HEAD_DIM)
        weight = load_weight(meta_ref, slot_refs, weight_ref, g, slots)
        own = own_ref[:, columns]
        extended = jnp.concatenate([before_ref[:, columns], own, after_ref[:, columns]], axis=0)
        query = dot_nn(own, weight[:, :HEAD_DIM]).astype(BF16)
        key_value = dot_nn(extended, weight[:, HEAD_DIM:]).astype(BF16)
        key, value = key_value[:, :HEAD_DIM], key_value[:, HEAD_DIM:]
        bias = toeplitz(offset_ref[g])
        for b in range(blocks):
            first = b * ROW_BLOCK
            window = slice(first, first + WINDOW)
            probs = block_probs(query[first : first + ROW_BLOCK], key[window], bias + masks[b])
            attended = dot_nn(probs.astype(BF16), value[window])
            kept = x_ref[first : first + ROW_BLOCK, columns].astype(F32)
            out_ref[first : first + ROW_BLOCK, columns] = (kept + attended).astype(BF16)


def column_spec(rows, group, first):
    return pl.BlockSpec((rows, group * HEAD_DIM), lambda i, meta: (0, i + first))


def slot_specs(weight_slots, group):
    return [
        pl.BlockSpec((3, group, slot.shape[2], HEAD_DIM), lambda i, meta: (0, i, 0, 0))
        for slot in weight_slots
    ]


def forward_attention(meta, before, own, after, x, offsets, weight_slots, group):
    rows, width = own.shape
    heads = width // HEAD_DIM
    slots = len(weight_slots)
    return pl.pallas_call(
        functools.partial(forward_kernel, slots, group),
        out_shape=jax.ShapeDtypeStruct((rows, width), BF16),
        grid_spec=pltpu.PrefetchScalarGridSpec(
            num_scalar_prefetch=1,
            grid=(heads // group,),
            in_specs=[
                column_spec(RADIUS, group, 0),
                column_spec(rows, group, 0),
                column_spec(RADIUS, group, 0),
                column_spec(rows, group, 0),
                pl.BlockSpec((group, 1, WINDOW), lambda i, meta: (i, 0, 0)),
                *slot_specs(weight_slots, group),
            ],
            out_specs=column_spec(rows, group, 0),
            scratch_shapes=[pltpu.VMEM((group, HEAD_DIM, 3 * HEAD_DIM), BF16)],
        ),
        compiler_params=pltpu.CompilerParams(vmem_limit_bytes=VMEM_LIMIT),
        cost_estimate=pl.CostEstimate(
            flops=heads * 60_000_000, bytes_accessed=8 * rows * width, transcendentals=heads * 32768
        ),
        name="forward_attention",
    )(meta, before, own, after, x, offsets, *weight_slots)


def backward_kernel(slots, group, meta_ref, before_ref, own_ref, after_ref, cot_ref, offset_ref, *rest):
    slot_refs = rest[:slots]
    rest = rest[slots:]
    grad_ref, lower_ref, upper_ref, offset_grad_ref = rest[:4]
    part_refs = rest[4 : 4 + slots]
    weight_ref, part_ref = rest[4 + slots :]
    rows = own_ref.shape[0]
    blocks = rows // ROW_BLOCK
    scale = HEAD_DIM ** (-0.5)
    masks = [key_mask(meta_ref, b * ROW_BLOCK) for b in range(blocks)]
    for g in range(group):
        columns = slice(g * HEAD_DIM, (g + 1) * HEAD_DIM)
        weight = load_weight(meta_ref, slot_refs, weight_ref, g, slots)
        own = own_ref[:, columns]
        extended = jnp.concatenate([before_ref[:, columns], own, after_ref[:, columns]], axis=0)
        query = dot_nn(own, weight[:, :HEAD_DIM]).astype(BF16)
        key_value = dot_nn(extended, weight[:, HEAD_DIM:]).astype(BF16)
        key, value = key_value[:, :HEAD_DIM], key_value[:, HEAD_DIM:]
        bias = toeplitz(offset_ref[g])
        grad_query, grad_key, grad_value, score_sum = [], [], [], None
        for b in range(blocks):
            first = b * ROW_BLOCK
            window = slice(first, first + WINDOW)
            query_rows = query[first : first + ROW_BLOCK]
            cot_rows = cot_ref[first : first + ROW_BLOCK, columns]
            probs = block_probs(query_rows, key[window], bias + masks[b])
            grad_probs = dot_nt(cot_rows, value[window])
            delta = jnp.sum(probs * grad_probs, axis=-1, keepdims=True)
            grad_scores = probs * (grad_probs - delta)
            score_sum = grad_scores if score_sum is None else score_sum + grad_scores
            grad_packed = grad_scores.astype(BF16)
            grad_query.append(dot_nn(grad_packed, key[window]))
            grad_key.append(dot_tn(grad_packed, query_rows))
            grad_value.append(dot_tn(probs.astype(BF16), cot_rows))

        def joined(parts):
            pieces = []
            for u in range((rows + 2 * RADIUS) // ROW_BLOCK):
                total = None
                for b in range(blocks):
                    if 0 <= u - b < WINDOW // ROW_BLOCK:
                        piece = parts[b][(u - b) * ROW_BLOCK : (u - b + 1) * ROW_BLOCK]
                        total = piece if total is None else total + piece
                pieces.append(total)
            return jnp.concatenate(pieces, axis=0)

        dquery = (jnp.concatenate(grad_query, axis=0) * scale).astype(BF16)
        dkey = (joined(grad_key) * scale).astype(BF16)
        dvalue = joined(grad_value).astype(BF16)
        dkey_value = jnp.concatenate([dkey, dvalue], axis=1)
        grad_extended = dot_nt(dkey_value, weight[:, HEAD_DIM:])
        grad_ref[:, columns] = grad_extended[RADIUS : RADIUS + rows] + dot_nt(dquery, weight[:, :HEAD_DIM])
        lower_ref[:, columns] = grad_extended[:RADIUS].astype(BF16)
        upper_ref[:, columns] = grad_extended[RADIUS + rows :].astype(BF16)
        part_ref[g, :, :HEAD_DIM] = dot_tn(own, dquery)
        part_ref[g, :, HEAD_DIM:] = dot_tn(extended, dkey_value)
        depth = HEAD_DIM // slots
        for r in range(slots):
            if slots == 1:
                start = 0
            else:
                start = pl.multiple_of(lax.rem(meta_ref[0] + r, slots) * depth, depth)
            for j in range(3):
                part_refs[r][j, g] = part_ref[
                    g, pl.ds(start, depth), j * HEAD_DIM : (j + 1) * HEAD_DIM
                ].astype(part_refs[r].dtype)
        offset_grad_ref[g] = diagonal_sums(score_sum)


def backward_attention(meta, before, own, after, cotangent, offsets, weight_slots, group, first_head, heads):
    rows = own.shape[0]
    width = heads * HEAD_DIM
    slots = len(weight_slots)
    first = first_head // group
    slot_shape = weight_slots[0].shape
    part_types = [F32] + [BF16] * (slots - 1) if slots > 1 else [BF16]
    return pl.pallas_call(
        functools.partial(backward_kernel, slots, group),
        out_shape=(
            jax.ShapeDtypeStruct((rows, width), F32),
            jax.ShapeDtypeStruct((RADIUS, width), BF16),
            jax.ShapeDtypeStruct((RADIUS, width), BF16),
            jax.ShapeDtypeStruct((heads, 1, WINDOW), F32),
            *[jax.ShapeDtypeStruct(slot_shape, kind) for kind in part_types],
        ),
        grid_spec=pltpu.PrefetchScalarGridSpec(
            num_scalar_prefetch=1,
            grid=(heads // group,),
            in_specs=[
                column_spec(RADIUS, group, first),
                column_spec(rows, group, first),
                column_spec(RADIUS, group, first),
                column_spec(rows, group, first),
                pl.BlockSpec((group, 1, WINDOW), lambda i, meta: (i + first, 0, 0)),
                *slot_specs(weight_slots, group),
            ],
            out_specs=(
                column_spec(rows, group, 0),
                column_spec(RADIUS, group, 0),
                column_spec(RADIUS, group, 0),
                pl.BlockSpec((group, 1, WINDOW), lambda i, meta: (i, 0, 0)),
                *slot_specs(weight_slots, group),
            ),
            scratch_shapes=[
                pltpu.VMEM((group, HEAD_DIM, 3 * HEAD_DIM), BF16),
                pltpu.VMEM((group, HEAD_DIM, 3 * HEAD_DIM), F32),
            ],
        ),
        compiler_params=pltpu.CompilerParams(vmem_limit_bytes=VMEM_LIMIT),
        cost_estimate=pl.CostEstimate(
            flops=heads * 150_000_000, bytes_accessed=12 * rows * width, transcendentals=heads * 32768
        ),
        name="backward_attention",
    )(meta, before, own, after, cotangent, offsets, *weight_slots)


def finish_kernel(grad_ref, low_ref, high_ref, x_ref, inverse_ref, gain_ref, cot_ref, out_ref, gain_grad_ref):
    rows = x_ref.shape[0]
    grad = grad_ref[...]
    edge = jnp.zeros((rows - RADIUS, grad.shape[1]), F32)
    grad = grad + jnp.concatenate([low_ref[...].astype(F32), edge], axis=0)
    grad = grad + jnp.concatenate([edge, high_ref[...].astype(F32)], axis=0)
    x = x_ref[...].astype(F32)
    inverse = inverse_ref[:, :1]
    gain_grad_ref[...] = jnp.sum(grad * x * inverse, axis=0, keepdims=True)
    scaled = grad * gain_ref[...]
    mean = jnp.mean(scaled * x, axis=-1, keepdims=True)
    result = inverse * scaled - x * (inverse * inverse * inverse * mean)
    out_ref[...] = (cot_ref[...].astype(F32) + result).astype(BF16)


def finish(grad, low, high, x, inverse, gain, cotangent):
    rows, width = x.shape
    return pl.pallas_call(
        finish_kernel,
        out_shape=(
            jax.ShapeDtypeStruct((rows, width), BF16),
            jax.ShapeDtypeStruct((1, width), F32),
        ),
        compiler_params=pltpu.CompilerParams(vmem_limit_bytes=VMEM_LIMIT),
        cost_estimate=pl.CostEstimate(
            flops=16 * rows * width, bytes_accessed=14 * rows * width, transcendentals=0
        ),
        name="finish",
    )(grad, low, high, x, inverse, gain, cotangent)


def column_of(row, rows):
    return jnp.transpose(jnp.broadcast_to(row, (128, rows)))


def split_rows(inverse, pad_rows, width):
    high = inverse.astype(BF16)
    rest = inverse - high.astype(F32)
    middle = rest.astype(BF16)
    low = (rest - middle.astype(F32)).astype(BF16)
    wide = [jnp.transpose(jnp.broadcast_to(v.astype(F32), (v.shape[0], 128)))[:1] for v in (high, middle, low)]
    row = jnp.concatenate(wide + [jnp.zeros((pad_rows - 3, wide[0].shape[1]), F32)], axis=0)
    return row.astype(BF16)


def row_inverse(x):
    x = x.astype(F32)
    return lax.rsqrt(jnp.mean(x * x, axis=-1, keepdims=True) + eps_norm)


def pack_stash_kernel(parts, pieces, meta_ref, x_hbm, gain_hbm, weight_hbm, inverse_ref, *refs):
    out_refs = refs[:parts]
    x_ref, gain_ref, weight_ref, normed_ref, sems = refs[parts:]
    rows, width = x_ref.shape
    depth = weight_ref.shape[2]
    wide = width // parts
    heads = wide // HEAD_DIM
    step = rows // pieces
    gain_copy = pltpu.make_async_copy(gain_hbm, gain_ref, sems.at[0])
    x_copies = [
        pltpu.make_async_copy(x_hbm.at[pl.ds(k * step, step)], x_ref.at[pl.ds(k * step, step)], sems.at[1 + k])
        for k in range(pieces)
    ]
    weight_copies = [
        pltpu.make_async_copy(weight_hbm.at[j], weight_ref.at[j], sems.at[1 + pieces + j]) for j in range(3)
    ]
    for copy in (gain_copy, *x_copies, *weight_copies):
        copy.start()
    gain_copy.wait()
    gain = gain_ref[...]
    for k, copy in enumerate(x_copies):
        copy.wait()
        part = slice(k * step, (k + 1) * step)
        inverse = row_inverse(x_ref[part])
        inverse_ref[part] = jnp.broadcast_to(inverse, (step, 128))
        normed_ref[part] = (x_ref[part].astype(F32) * inverse * gain).astype(BF16)
    for r, out_ref in enumerate(out_refs):
        target = lax.rem(meta_ref[0] + r, parts)
        out_ref[:rows] = normed_ref[:, pl.ds(pl.multiple_of(target * wide, 128), wide)]
    for j, copy in enumerate(weight_copies):
        copy.wait()
        for r, out_ref in enumerate(out_refs):
            target = lax.rem(meta_ref[0] + r, parts)
            for h in range(heads):
                out_ref[rows + j * depth : rows + (j + 1) * depth, h * HEAD_DIM : (h + 1) * HEAD_DIM] = weight_ref[
                    j, target * heads + h
                ]


def pack_rows_kernel(parts, with_inverse, meta_ref, edge_ref, inner_ref, *out_refs):
    rows, width = inner_ref.shape
    wide = width // parts
    edge = 1 if with_inverse else 2
    refs = out_refs[:parts]
    for r, out_ref in enumerate(refs):
        target = lax.rem(meta_ref[0] + r, parts)
        start = pl.multiple_of(target * wide, 128)

        @pl.when(meta_ref[edge] == 1)
        def use_edge():
            out_ref[:rows] = edge_ref[:, pl.ds(start, wide)]

        @pl.when(meta_ref[edge] == 0)
        def use_inner():
            out_ref[:rows] = inner_ref[:, pl.ds(start, wide)]

    def finish_with(source_ref):
        if with_inverse:
            tail = split_rows(row_inverse(source_ref[...]), EXTRA, wide)
            for out_ref in refs:
                out_ref[rows:] = jnp.zeros((EXTRA, wide), BF16)
                out_ref[rows:, :rows] = tail
        else:
            out_refs[parts][...] = source_ref[...]

    @pl.when(meta_ref[edge] == 1)
    def finish_edge():
        finish_with(edge_ref)

    @pl.when(meta_ref[edge] == 0)
    def finish_inner():
        finish_with(inner_ref)


SMEM_SPEC = pl.BlockSpec(memory_space=pltpu.SMEM)
VMEM_SPEC = pl.BlockSpec(memory_space=pltpu.VMEM)


def pack_stash(meta, x, gain, weight, parts):
    rows, width = x.shape
    depth = weight.shape[2]
    shape = (rows + 3 * depth, width // parts)
    return pl.pallas_call(
        functools.partial(pack_stash_kernel, parts, 4),
        out_shape=(
            jax.ShapeDtypeStruct((rows, 128), F32),
            *[jax.ShapeDtypeStruct(shape, BF16) for r in range(parts)],
        ),
        in_specs=[SMEM_SPEC] + [pl.BlockSpec(memory_space=pl.ANY)] * 3,
        out_specs=(VMEM_SPEC,) * (parts + 1),
        scratch_shapes=[
            pltpu.VMEM((rows, width), BF16),
            pltpu.VMEM((1, width), F32),
            pltpu.VMEM(weight.shape, BF16),
            pltpu.VMEM((rows, width), BF16),
            pltpu.SemaphoreType.DMA((8,)),
        ],
        compiler_params=pltpu.CompilerParams(vmem_limit_bytes=58 * 1024 * 1024),
        cost_estimate=pl.CostEstimate(flops=4 * rows * width, bytes_accessed=6 * rows * width, transcendentals=0),
        name="pack_stash",
    )(meta, x, gain, weight)


def pack_rows(meta, edge, inner, parts, with_inverse):
    rows, width = inner.shape
    shape = (rows + (EXTRA if with_inverse else 0), width // parts)
    extra = () if with_inverse else (jax.ShapeDtypeStruct((rows, width), BF16),)
    return pl.pallas_call(
        functools.partial(pack_rows_kernel, parts, with_inverse),
        out_shape=(*[jax.ShapeDtypeStruct(shape, BF16) for r in range(parts)], *extra),
        in_specs=[SMEM_SPEC, VMEM_SPEC, VMEM_SPEC],
        out_specs=(VMEM_SPEC,) * (parts + len(extra)),
        compiler_params=pltpu.CompilerParams(vmem_limit_bytes=VMEM_LIMIT),
        cost_estimate=pl.CostEstimate(flops=4 * rows * width, bytes_accessed=6 * rows * width, transcendentals=0),
        name="pack_inbound" if with_inverse else "pack_cotangent",
    )(meta, edge, inner)


def gather_rows(meta_ref, refs, rows, x_ref):
    parts = len(refs)
    for r, ref in enumerate(refs):
        source = lax.rem(meta_ref[0] + parts - r, parts)
        x_ref[pl.ds(pl.multiple_of(source * rows, rows), rows)] = ref[:rows]


def gather_weight(meta_ref, refs, rows, weight_ref):
    parts = len(refs)
    depth = HEAD_DIM // parts
    for r, ref in enumerate(refs):
        source = lax.rem(meta_ref[0] + parts - r, parts)
        depth_at = pl.ds(pl.multiple_of(source * depth, depth), depth)
        for j in range(3):
            weight_ref[depth_at, j * HEAD_DIM : (j + 1) * HEAD_DIM] = ref[
                rows + j * depth : rows + (j + 1) * depth
            ]


def gather_inverse(meta_ref, refs, rows, inverse_ref):
    parts = len(refs)

    @pl.when(pl.program_id(0) == 0)
    def spread_inverse():
        for r, ref in enumerate(refs):
            source = lax.rem(meta_ref[0] + parts - r, parts)
            tail = ref[rows : rows + EXTRA].astype(F32)
            inverse_ref[pl.ds(pl.multiple_of(source * rows, rows), rows)] = column_of(
                tail[:1] + tail[1:2] + tail[2:3], rows
            )


def block_mask(first_query, tokens):
    key = lax.broadcasted_iota(jnp.int32, (1, WINDOW), 1) + (first_query - RADIUS)
    return jnp.where((key >= 0) & (key < tokens), 0.0, masked_score).astype(F32)


def edge_bias(bias, first, tokens):
    if first < RADIUS or first + ROW_BLOCK + RADIUS > tokens:
        return bias + block_mask(first, tokens)
    return bias


def padded(rows):
    edge = jnp.zeros((RADIUS, rows.shape[1]), rows.dtype)
    return jnp.concatenate([edge, rows, edge], axis=0)


def heads_backward_kernel(parts, rows, meta_ref, *refs):
    a_refs, c_refs = refs[:parts], refs[parts : 2 * parts]
    gain_ref, offset_ref, onehot_ref, after_ref = refs[2 * parts : 2 * parts + 4]
    out_refs = refs[2 * parts + 4 : 3 * parts + 4]
    gain_grad_ref, x_ref, weight_ref, cot_ref, grad_ref, part_ref, bias_ref = refs[3 * parts + 4 :]
    tokens = rows * parts
    depth = HEAD_DIM // parts
    scale = HEAD_DIM ** (-0.5)
    gather_rows(meta_ref, a_refs, rows, x_ref)
    gather_weight(meta_ref, a_refs, rows, weight_ref)
    gather_rows(meta_ref, c_refs, rows, cot_ref)
    weight = weight_ref[...]
    normed = x_ref[...]
    query = dot_nn(normed, weight[:, :HEAD_DIM]).astype(BF16)
    key = padded(dot_nn(normed, weight[:, HEAD_DIM : 2 * HEAD_DIM]).astype(BF16))
    value = padded(dot_nn(normed, weight[:, 2 * HEAD_DIM :]).astype(BF16))
    bias = toeplitz(offset_ref[0])
    blocks = tokens // ROW_BLOCK
    starts = range(0, tokens, ROW_BLOCK)
    cot = cot_ref[...]
    query_rows = [query[f : f + ROW_BLOCK] for f in starts]
    cot_rows = [cot[f : f + ROW_BLOCK] for f in starts]
    products = [dot_nt(rows_q, key[f : f + WINDOW]) for f, rows_q in zip(starts, query_rows)]
    grad_probs = [dot_nt(rows_c, value[f : f + WINDOW]) for f, rows_c in zip(starts, cot_rows)]
    packed, grad_packed, score_sum = [], [], None
    for f, product, grads in zip(starts, products, grad_probs):
        probs = score_probs(product, edge_bias(bias, f, tokens))
        delta = jnp.sum(probs * grads, axis=-1, keepdims=True)
        grad_scores = probs * (grads - delta)
        score_sum = grad_scores if score_sum is None else score_sum + grad_scores
        packed.append(probs.astype(BF16))
        grad_packed.append(grad_scores.astype(BF16))
    grad_query = [dot_nn(part, key[f : f + WINDOW]) for f, part in zip(starts, grad_packed)]
    grad_key = [dot_tn(part, rows_q) for part, rows_q in zip(grad_packed, query_rows)]
    grad_value = [dot_tn(part, rows_c) for part, rows_c in zip(packed, cot_rows)]

    def joined(pieces):
        units = []
        for u in range((tokens + 2 * RADIUS) // ROW_BLOCK):
            total = None
            for b in range(blocks):
                if 0 <= u - b < WINDOW // ROW_BLOCK:
                    piece = pieces[b][(u - b) * ROW_BLOCK : (u - b + 1) * ROW_BLOCK]
                    total = piece if total is None else total + piece
            units.append(total)
        return jnp.concatenate(units, axis=0)[RADIUS : RADIUS + tokens]

    dqkv = jnp.concatenate(
        [
            (jnp.concatenate(grad_query, axis=0) * scale).astype(BF16),
            (joined(grad_key) * scale).astype(BF16),
            joined(grad_value).astype(BF16),
        ],
        axis=1,
    )
    grad_normed = dot_nt(dqkv, weight)
    gain_grad_ref[...] = jnp.sum(grad_normed * normed.astype(F32), axis=0, keepdims=True) / gain_ref[...]
    grad_ref[...] = grad_normed
    part_ref[...] = dot_tn(normed, dqkv)
    bias_grad = jnp.sum(onehot_ref[...] * diagonal_sums(score_sum), axis=1, keepdims=True)
    bias_ref[...] = jnp.broadcast_to(bias_grad, bias_ref.shape)
    buckets = bias_ref.shape[0] // parts
    for r, out_ref in enumerate(out_refs):
        source = lax.rem(meta_ref[0] + parts - r, parts)
        out_ref[:rows] = grad_ref[pl.ds(pl.multiple_of(source * rows, rows), rows)].astype(BF16)
        for j in range(3):
            out_ref[rows + j * depth : rows + (j + 1) * depth] = part_ref[
                pl.ds(pl.multiple_of(source * depth, depth), depth), j * HEAD_DIM : (j + 1) * HEAD_DIM
            ].astype(BF16)
        share = bias_ref[pl.ds(pl.multiple_of(source * buckets, buckets), buckets)]
        out_ref[rows + 3 * depth :] = share.astype(BF16)


def head_column(rows, first=0):
    return pl.BlockSpec((rows, HEAD_DIM), lambda i, meta: (0, i + first))


def whole_column(rows, heads, first=0):
    return pl.BlockSpec((rows, HEAD_DIM), lambda i, meta: (0, meta[0] * heads + first + i))


def offset_spec(heads, first=0):
    return pl.BlockSpec((1, 1, WINDOW), lambda i, meta: (meta[0] * heads + first + i, 0, 0))


def heads_backward(meta, a_slots, c_slots, gain, offsets, onehot, after, heads, first, count):
    parts = len(a_slots)
    rows = c_slots[0].shape[0]
    tokens = rows * parts
    buckets = onehot.shape[0]
    packed = a_slots[0].shape[0]
    made = packed + buckets // parts
    width = count * HEAD_DIM
    return pl.pallas_call(
        functools.partial(heads_backward_kernel, parts, rows),
        out_shape=(
            *[jax.ShapeDtypeStruct((made, width), BF16) for r in range(parts)],
            jax.ShapeDtypeStruct((1, width), F32),
        ),
        grid_spec=pltpu.PrefetchScalarGridSpec(
            num_scalar_prefetch=1,
            grid=(count,),
            in_specs=[
                *[head_column(packed, first)] * parts,
                whole_column(rows, heads, first),
                *[head_column(rows, first)] * (parts - 1),
                whole_column(1, heads, first),
                offset_spec(heads, first),
                pl.BlockSpec((buckets, WINDOW), lambda i, meta: (0, 0)),
                pl.BlockSpec(memory_space=pl.ANY),
            ],
            out_specs=(*[head_column(made)] * parts, head_column(1)),
            scratch_shapes=[
                pltpu.VMEM((tokens, HEAD_DIM), BF16),
                pltpu.VMEM((HEAD_DIM, 3 * HEAD_DIM), BF16),
                pltpu.VMEM((tokens, HEAD_DIM), BF16),
                pltpu.VMEM((tokens, HEAD_DIM), F32),
                pltpu.VMEM((HEAD_DIM, 3 * HEAD_DIM), F32),
                pltpu.VMEM((buckets, HEAD_DIM), F32),
            ],
        ),
        compiler_params=pltpu.CompilerParams(vmem_limit_bytes=VMEM_LIMIT),
        cost_estimate=pl.CostEstimate(
            flops=count * tokens * 400_000, bytes_accessed=tokens * width, transcendentals=0
        ),
        name="heads_backward",
    )(meta, *a_slots, *c_slots, gain, offsets, onehot, after)


def heads_forward_kernel(parts, rows, meta_ref, *refs):
    a_refs, i_refs = refs[:parts], refs[parts : 2 * parts]
    gain_ref, offset_ref = refs[2 * parts : 2 * parts + 2]
    out_refs = refs[2 * parts + 2 : 3 * parts + 2]
    inverse_ref, x_ref, weight_ref, made_ref, square_ref = refs[3 * parts + 2 :]
    tokens = rows * parts
    gather_rows(meta_ref, i_refs, rows, x_ref)
    gather_weight(meta_ref, a_refs, rows, weight_ref)
    gather_inverse(meta_ref, i_refs, rows, inverse_ref)
    weight = weight_ref[...]
    normed = (x_ref[...].astype(F32) * inverse_ref[...] * gain_ref[...]).astype(BF16)
    query = dot_nn(normed, weight[:, :HEAD_DIM]).astype(BF16)
    key = padded(dot_nn(normed, weight[:, HEAD_DIM : 2 * HEAD_DIM]).astype(BF16))
    value = padded(dot_nn(normed, weight[:, 2 * HEAD_DIM :]).astype(BF16))
    bias = toeplitz(offset_ref[0])
    starts = range(0, tokens, ROW_BLOCK)
    products = [dot_nt(query[f : f + ROW_BLOCK], key[f : f + WINDOW]) for f in starts]
    packed = [
        score_probs(product, edge_bias(bias, f, tokens)).astype(BF16) for f, product in zip(starts, products)
    ]
    attended = [dot_nn(part, value[f : f + WINDOW]) for f, part in zip(starts, packed)]
    for f, part in zip(starts, attended):
        made_ref[f : f + ROW_BLOCK] = (x_ref[f : f + ROW_BLOCK].astype(F32) + part).astype(BF16)
    made = made_ref[...].astype(F32)
    squares = made * made

    @pl.when(pl.program_id(0) == 0)
    def first_head():
        square_ref[...] = squares

    @pl.when(pl.program_id(0) > 0)
    def later_head():
        square_ref[...] += squares

    for r, out_ref in enumerate(out_refs):
        source = lax.rem(meta_ref[0] + parts - r, parts)
        out_ref[:rows] = made_ref[pl.ds(pl.multiple_of(source * rows, rows), rows)]

    @pl.when(pl.program_id(0) < pl.num_programs(0) - 1)
    def no_sums():
        for out_ref in out_refs:
            out_ref[rows:] = jnp.zeros((EXTRA, HEAD_DIM), BF16)

    @pl.when(pl.program_id(0) == pl.num_programs(0) - 1)
    def last_head():
        rest = jnp.sum(jnp.transpose(square_ref[...]), axis=0, keepdims=True)
        at_row = lax.broadcasted_iota(jnp.int32, (EXTRA, rows), 0)
        tail = jnp.zeros((EXTRA, rows), F32)
        for k in range(2):
            piece = rest.astype(BF16).astype(F32)
            rest = rest - piece
            for part in range(parts):
                row = jnp.broadcast_to(piece[:, part * rows : (part + 1) * rows], (EXTRA, rows))
                tail = jnp.where(at_row == 2 * part + k, row, tail)
        for out_ref in out_refs:
            out_ref[rows:] = tail.astype(BF16)


def heads_forward(meta, a_slots, i_slots, gain, offsets, heads, rows):
    parts = len(a_slots)
    tokens = rows * parts
    packed = a_slots[0].shape[0]
    width = heads * HEAD_DIM
    return pl.pallas_call(
        functools.partial(heads_forward_kernel, parts, rows),
        out_shape=(
            *[jax.ShapeDtypeStruct((rows + EXTRA, width), BF16) for r in range(parts)],
        ),
        grid_spec=pltpu.PrefetchScalarGridSpec(
            num_scalar_prefetch=1,
            grid=(heads,),
            in_specs=[
                *[head_column(packed)] * parts,
                *[head_column(i_slots[0].shape[0])] * parts,
                whole_column(1, heads),
                offset_spec(heads),
            ],
            out_specs=(head_column(rows + EXTRA),) * parts,
            scratch_shapes=[
                pltpu.VMEM((tokens, HEAD_DIM), F32),
                pltpu.VMEM((tokens, HEAD_DIM), BF16),
                pltpu.VMEM((HEAD_DIM, 3 * HEAD_DIM), BF16),
                pltpu.VMEM((tokens, HEAD_DIM), BF16),
                pltpu.VMEM((tokens, HEAD_DIM), F32),
            ],
        ),
        compiler_params=pltpu.CompilerParams(vmem_limit_bytes=VMEM_LIMIT),
        cost_estimate=pl.CostEstimate(
            flops=heads * tokens, bytes_accessed=tokens, transcendentals=0
        ),
        name="heads_forward",
    )(meta, *a_slots, *i_slots, gain, offsets)


def memory_kernel(parts, width, meta_ref, *refs):
    out_refs, other_refs = refs[:parts], refs[parts : 2 * parts - 1]
    gain_ref, *share_refs, memory_ref = refs[2 * parts - 1 :]
    wide = memory_ref.shape[1]
    rows = memory_ref.shape[0] // parts
    total = None
    for ref in (out_refs[0], *other_refs):
        tail = ref[rows:, wide - rows :].astype(F32)
        pieces = [tail[2 * p : 2 * p + 1] + tail[2 * p + 1 : 2 * p + 2] for p in range(parts)]
        row = jnp.concatenate(pieces, axis=1)
        total = row if total is None else total + row
    inverse = lax.rsqrt(total / width + eps_norm)
    gain = gain_ref[:, pl.ds(pl.multiple_of(meta_ref[0] * wide, 128), wide)]
    spread_inverse = jnp.transpose(jnp.broadcast_to(inverse, (128, inverse.shape[1])))
    for r, out_ref in enumerate(out_refs):
        source = lax.rem(meta_ref[0] + parts - r, parts)
        memory_ref[pl.ds(pl.multiple_of(source * rows, rows), rows)] = out_ref[:rows]
    made = memory_ref[...].astype(F32)
    memory_ref[...] = (made * spread_inverse[:, :1] * gain).astype(BF16)
    for k, share_ref in enumerate(share_refs):
        size = share_ref.shape[0]
        share_ref[...] = memory_ref[k * size : (k + 1) * size]


def memory_rows(meta, outs, others, gain, width, shares):
    parts = len(outs)
    rows, wide = outs[0].shape[0] - EXTRA, outs[0].shape[1]
    return pl.pallas_call(
        functools.partial(memory_kernel, parts, width),
        out_shape=[jax.ShapeDtypeStruct((rows * parts // shares, wide), BF16)] * shares,
        in_specs=[SMEM_SPEC] + [VMEM_SPEC] * (2 * parts),
        out_specs=[VMEM_SPEC] * shares,
        scratch_shapes=[pltpu.VMEM((rows * parts, wide), BF16)],
        compiler_params=pltpu.CompilerParams(vmem_limit_bytes=VMEM_LIMIT),
        cost_estimate=pl.CostEstimate(flops=rows, bytes_accessed=rows, transcendentals=0),
        name="memory_rows",
    )(meta, *outs, *others, gain)


def place_kernel(parts, meta_ref, *refs):
    out_ref = refs[parts]
    wide = refs[0].shape[1]
    for r in range(parts):
        source = lax.rem(meta_ref[0] + r, parts)
        out_ref[:, pl.ds(pl.multiple_of(source * wide, 128), wide)] = refs[r][: out_ref.shape[0]]


def place_columns(meta, slots):
    parts = len(slots)
    rows, wide = slots[0].shape[0] - EXTRA, slots[0].shape[1]
    return pl.pallas_call(
        functools.partial(place_kernel, parts),
        out_shape=jax.ShapeDtypeStruct((rows, wide * parts), BF16),
        in_specs=[SMEM_SPEC] + [VMEM_SPEC] * parts,
        out_specs=VMEM_SPEC,
        compiler_params=pltpu.CompilerParams(vmem_limit_bytes=VMEM_LIMIT),
        cost_estimate=pl.CostEstimate(flops=0, bytes_accessed=rows, transcendentals=0),
        name="place_columns",
    )(meta, *slots)


def heads_finish_kernel(parts, meta_ref, *refs):
    g_refs = refs[:parts]
    x_ref, inverse_ref, gain_ref, cot_ref, out_ref, weight_hbm, bias_ref, scaled_ref, weight_ref, sem = refs[parts:]
    rows, width = x_ref.shape
    wide = width // parts
    heads = wide // HEAD_DIM
    depth = HEAD_DIM // parts
    for r in range(parts):
        source = lax.rem(meta_ref[0] + r, parts)
        for h in range(heads):
            for j in range(3):
                weight_ref[j, source * heads + h] = g_refs[r][
                    rows + j * depth : rows + (j + 1) * depth, h * HEAD_DIM : (h + 1) * HEAD_DIM
                ].astype(F32)
    weight_copy = pltpu.make_async_copy(weight_ref, weight_hbm, sem)
    weight_copy.start()
    lane = lax.broadcasted_iota(jnp.int32, (bias_ref.shape[0], HEAD_DIM), 1)
    bias = jnp.zeros(lane.shape, F32)
    for r in range(parts):
        source = lax.rem(meta_ref[0] + r, parts)
        columns = pl.ds(pl.multiple_of(source * wide, 128), wide)
        scaled_ref[:, columns] = g_refs[r][:rows].astype(F32) * gain_ref[:, columns]
        shares = g_refs[r][rows + 3 * depth :].astype(F32)
        for h in range(heads):
            bias = jnp.where(lane == source * heads + h, shares[:, h * HEAD_DIM : (h + 1) * HEAD_DIM], bias)
    bias_ref[...] = bias[:, : bias_ref.shape[1]]
    x = x_ref[...].astype(F32)
    scaled = scaled_ref[...]
    inverse = inverse_ref[:, :1]
    mean = jnp.mean(scaled * x, axis=-1, keepdims=True)
    result = inverse * scaled - x * (inverse * inverse * inverse * mean)
    out_ref[...] = (cot_ref[...].astype(F32) + result).astype(BF16)
    weight_copy.wait()


def heads_finish(meta, g_slots, x, inverse, gain, cotangent, buckets):
    parts = len(g_slots)
    rows, width = x.shape
    heads = width // HEAD_DIM
    weight_shape = (3, heads, HEAD_DIM // parts, HEAD_DIM)
    return pl.pallas_call(
        functools.partial(heads_finish_kernel, parts),
        out_shape=(
            jax.ShapeDtypeStruct((rows, width), BF16),
            jax.ShapeDtypeStruct(weight_shape, F32),
            jax.ShapeDtypeStruct((buckets // parts, heads), F32),
        ),
        in_specs=[SMEM_SPEC] + [VMEM_SPEC] * (parts + 4),
        out_specs=(VMEM_SPEC, pl.BlockSpec(memory_space=pl.ANY), VMEM_SPEC),
        scratch_shapes=[
            pltpu.VMEM((rows, width), F32),
            pltpu.VMEM(weight_shape, F32),
            pltpu.SemaphoreType.DMA,
        ],
        compiler_params=pltpu.CompilerParams(vmem_limit_bytes=VMEM_LIMIT),
        cost_estimate=pl.CostEstimate(flops=12 * rows * width, bytes_accessed=14 * rows * width, transcendentals=0),
        name="heads_finish",
    )(meta, *g_slots, x, inverse, gain, cotangent)


def offset_table(rel_bias):
    onehot = jnp.asarray(bucket_onehot(rel_bias.shape[0]))
    by_offset = jnp.dot(onehot, rel_bias, precision=lax.Precision.HIGHEST).T
    inside = jnp.arange(WINDOW, dtype=jnp.int32) <= 2 * RADIUS
    return jnp.where(inside[None, :], by_offset, masked_score)[:, None, :]


def shifted(value, axis, steps):
    count = lax.axis_size(axis)
    first, last = (max(0, -steps), min(count, count - steps))
    return lax.ppermute(value, axis, [(source, source + steps) for source in range(first, last)])


def spread_memory(shares, section, sections):
    last = sections - 1
    couple = jnp.where(section == last, shares[-1], 0)
    for s, share in enumerate(shares[:-1]):
        couple = couple + lax.ppermute(share, "section", [(last, 2 * s + 1)])
    half = couple.shape[0] // 2
    even = lax.ppermute(couple[:half], "section", [(s + 1, s) for s in range(0, sections, 2)])
    return jnp.where(section % 2 == 0, even, couple[half:])


def heads_body(
    embedded, carried, stash, returned, loss_grad, qkv_weight, rel_bias, norm_gain, final_gain
):
    section = lax.axis_index("section")
    sections = lax.axis_size("section")
    parts = lax.axis_size("seq")
    rows, width = embedded.shape
    heads = width // HEAD_DIM // parts
    buckets = rel_bias.shape[1]
    meta = jnp.stack(
        [lax.axis_index("seq"), section == 0, section == sections - 1]
    ).astype(jnp.int32)

    def exchanged(sends, direction):
        moved = [
            lax.ppermute(sends[r], "seq", [(i, (i + direction * r) % parts) for i in range(parts)])
            for r in range(1, parts)
        ]
        return [sends[0]] + moved

    inverse_b, *a_sends = pack_stash(meta, stash[0], norm_gain, qkv_weight[0], parts)
    a_slots = exchanged(a_sends, 1)
    arrived = shifted(carried[0], "section", 1)
    came_back = shifted(returned[0], "section", -1)
    i_slots = exchanged(pack_rows(meta, embedded, arrived, parts, True), 1)
    *c_sends, cotangent = pack_rows(meta, loss_grad, came_back, parts, False)
    c_slots = exchanged(c_sends, 1)
    c_slots[0] = cotangent

    offsets = offset_table(rel_bias[0])
    onehot = jnp.asarray(bucket_onehot(buckets).T)
    o_sends = heads_forward(meta, a_slots, i_slots, norm_gain, offsets, heads, rows)
    o_sends, c_slots = lax.optimization_barrier((o_sends, c_slots))
    o_slots = exchanged(o_sends, -1)

    *g_sends, gain_grad = heads_backward(
        meta, a_slots, c_slots, norm_gain, offsets, onehot, o_sends[0], heads, 0, heads
    )
    g_sends, o_slots = lax.optimization_barrier((g_sends, o_slots))
    g_slots = exchanged(g_sends, -1)
    output = place_columns(meta, o_slots)
    shares = memory_rows(meta, o_sends, o_slots[1:], final_gain[None], width, sections // 2)
    memory = spread_memory(shares, section, sections)

    input_grad, weight_grad, bias_grad = heads_finish(
        meta, g_slots, stash[0], inverse_b, norm_gain, cotangent, buckets
    )
    return (
        output[None],
        input_grad[None],
        weight_grad[None],
        bias_grad[None],
        gain_grad,
        memory,
    )


def tokens_body(
    embedded, carried, stash, returned, loss_grad, qkv_weight, rel_bias, norm_gain, final_gain
):
    section_index = lax.axis_index("section")
    section_count = lax.axis_size("section")
    seq_index = lax.axis_index("seq")
    seq_count = lax.axis_size("seq")
    rows, width = embedded.shape
    heads = width // HEAD_DIM
    tokens = rows * seq_count
    shard = qkv_weight[0]
    up = [(i, i + 1) for i in range(seq_count - 1)]
    down = [(j, i) for i, j in up]
    group = 4 if heads % 4 == 0 else 1

    own_b, inverse_b = norm_rows(stash[0], norm_gain)
    before_b = lax.ppermute(own_b[rows - RADIUS :], "seq", up)
    after_b = lax.ppermute(own_b[:RADIUS], "seq", down)
    slots = [lax.all_gather(shard, "seq", axis=2, tiled=True)]

    section_up = [(i, (i + 1) % section_count) for i in range(section_count)]
    section_down = [(j, i) for i, j in section_up]
    inbound = lax.ppermute(
        jnp.where(section_index == section_count - 1, embedded, carried[0]), "section", section_up
    )
    cotangent = lax.ppermute(
        jnp.where(section_index == 0, loss_grad, returned[0]), "section", section_down
    )

    onehot = jnp.asarray(bucket_onehot(rel_bias.shape[1]))
    offsets = offset_table(rel_bias[0])
    first_key = RADIUS - seq_index * rows
    meta = jnp.stack([seq_index, first_key, first_key + tokens]).astype(jnp.int32)

    own_a, unused = norm_rows(inbound, norm_gain)
    before_a = lax.ppermute(own_a[rows - RADIUS :], "seq", up)
    after_a = lax.ppermute(own_a[:RADIUS], "seq", down)

    grad_own, lower, upper, offset_grad, *parts = backward_attention(
        meta, before_b, own_b, after_b, cotangent, offsets, slots, group, 0, heads
    )
    from_before = lax.ppermute(upper, "seq", up)
    from_after = lax.ppermute(lower, "seq", down)
    weight_sum = lax.psum_scatter(parts[0], "seq", scatter_dimension=2, tiled=True).astype(F32)

    output = forward_attention(meta, before_a, own_a, after_a, inbound, offsets, slots, group)
    final_normed, unused = norm_rows(output, final_gain[None])
    relaid = lax.all_to_all(final_normed, "seq", split_axis=1, concat_axis=0, tiled=True)
    kept = jnp.where(section_index == section_count - 1, relaid, jnp.zeros_like(relaid))
    memory = lax.psum_scatter(kept, "section", scatter_dimension=0, tiled=True)

    input_grad, gain_part = finish(
        grad_own, from_before, from_after, stash[0], inverse_b, norm_gain, cotangent
    )
    bias_part = jnp.dot(
        offset_grad[:, 0, :], onehot, precision=lax.Precision.HIGHEST
    ).T
    bias_sum = lax.psum_scatter(
        bias_part.astype(BF16), "seq", scatter_dimension=0, tiled=True
    ).astype(F32)
    gain_sum = lax.psum_scatter(
        gain_part.astype(BF16), "seq", scatter_dimension=1, tiled=True
    ).astype(F32)
    return (output[None], input_grad[None], weight_sum[None], bias_sum[None], gain_sum, memory)


def choose_body(embedded, carried, stash, returned, loss_grad, qkv_weight, rel_bias, norm_gain, final_gain):
    parts = lax.axis_size("seq")
    rows, width = embedded.shape
    even = width % (HEAD_DIM * parts) == 0 and HEAD_DIM % (32 * parts) == 0 and rows == 128
    sections = lax.axis_size("section")
    even = even and sections % 2 == 0
    even = even and rel_bias.shape[1] == 8 * parts and width <= 128 * HEAD_DIM and rows * parts % (16 * sections) == 0
    chosen = heads_body if even else tokens_body
    return chosen(
        embedded, carried, stash, returned, loss_grad, qkv_weight, rel_bias, norm_gain, final_gain
    )


def solution(mesh):
    in_specs = (
        P("seq", None),
        P("section", "seq", None),
        P("section", "seq", None),
        P("section", "seq", None),
        P("seq", None),
        P("section", None, None, "seq", None),
        P("section", None, None),
        P("section", None),
        P(),
    )
    out_specs = (
        P("section", "seq", None),
        P("section", "seq", None),
        P("section", None, None, "seq", None),
        P("section", "seq", None),
        P("section", "seq"),
        P("section", "seq"),
    )
    return jax.shard_map(choose_body, mesh=mesh, in_specs=in_specs, out_specs=out_specs, check_vma=False)
```

```python
import functools

import jax
import jax.numpy as jnp
import numpy as np
from jax import lax
from jax.experimental import pallas as pl
from jax.experimental.pallas import tpu as pltpu
from jax.sharding import PartitionSpec as P

RADIUS = 96
HEAD_DIM = 128
ROW_BLOCK = 64
WINDOW = ROW_BLOCK + 2 * RADIUS
eps_norm = 1e-06
bucket_edges = (1, 2, 3, 4, 5, 6, 7, 8, 11, 16, 22, 32, 45, 64, 90)
masked_score = -1e30
F32 = jnp.float32
BF16 = jnp.bfloat16
VMEM_LIMIT = 24 * 1024 * 1024
EXTRA = 8


def bucket_onehot(bucket_count):
    offsets = np.arange(WINDOW) - RADIUS
    magnitude = np.abs(offsets)
    counted = np.zeros(offsets.shape, np.int32)
    for threshold in bucket_edges:
        counted = counted + (magnitude >= threshold)
    counted = counted + 16 * (offsets > 0)
    onehot = (counted[:, None] == np.arange(bucket_count)[None, :]) & (magnitude <= RADIUS)[:, None]
    return onehot.astype(np.float32)


def dot_nn(a, b):
    return lax.dot_general(a, b, (((1,), (0,)), ((), ())), preferred_element_type=F32)


def dot_nt(a, b):
    return lax.dot_general(a, b, (((1,), (1,)), ((), ())), preferred_element_type=F32)


def dot_tn(a, b):
    return lax.dot_general(a, b, (((0,), (0,)), ((), ())), preferred_element_type=F32)


def norm_kernel(x_ref, gain_ref, normed_ref, inverse_ref):
    x = x_ref[...].astype(F32)
    inverse = lax.rsqrt(jnp.mean(x * x, axis=-1, keepdims=True) + eps_norm)
    normed_ref[...] = (x * inverse * gain_ref[...]).astype(BF16)
    inverse_ref[...] = jnp.broadcast_to(inverse, inverse_ref.shape)


def norm_rows(x, gain):
    rows, width = x.shape
    return pl.pallas_call(
        norm_kernel,
        out_shape=(
            jax.ShapeDtypeStruct((rows, width), BF16),
            jax.ShapeDtypeStruct((rows, 128), F32),
        ),
        compiler_params=pltpu.CompilerParams(vmem_limit_bytes=VMEM_LIMIT),
        cost_estimate=pl.CostEstimate(
            flops=6 * rows * width, bytes_accessed=4 * rows * width, transcendentals=rows
        ),
        name="norm_rows",
    )(x, gain)


def load_weight(meta_ref, slot_refs, weight_ref, head, slots):
    depth = HEAD_DIM // slots
    for r, slot_ref in enumerate(slot_refs):
        if slots == 1:
            start = 0
        else:
            start = pl.multiple_of(lax.rem(meta_ref[0] + r, slots) * depth, depth)
        for j in range(3):
            weight_ref[head, pl.ds(start, depth), j * HEAD_DIM : (j + 1) * HEAD_DIM] = slot_ref[j, head]
    return weight_ref[head]


def key_mask(meta_ref, first_key):
    key = lax.broadcasted_iota(jnp.int32, (1, WINDOW), 1) + first_key
    inside = (key >= meta_ref[1]) & (key < meta_ref[2])
    return jnp.where(inside, 0.0, masked_score).astype(F32)


def toeplitz(row):
    return pltpu.roll(
        jnp.broadcast_to(row, (ROW_BLOCK, WINDOW)), 0, 1, stride=1, stride_axis=0
    )


def diagonal_sums(values):
    total = values[:8]
    for a in range(1, ROW_BLOCK // 8):
        total = total + pltpu.roll(values[8 * a : 8 * a + 8], WINDOW - 8 * a, 1)
    row = lax.broadcasted_iota(jnp.int32, total.shape, 0)
    for bit in (1, 2, 4):
        total = jnp.where((row & bit) != 0, pltpu.roll(total, WINDOW - bit, 1), total)
    return jnp.sum(total, axis=0, keepdims=True)


def block_probs(query_rows, key_rows, bias):
    return score_probs(dot_nt(query_rows, key_rows), bias)


def score_probs(products, bias):
    scores = products * (HEAD_DIM ** (-0.5)) + bias
    weights = jnp.exp(scores - jnp.max(scores, axis=-1, keepdims=True))
    return weights * (1.0 / jnp.sum(weights, axis=-1, keepdims=True))


def forward_kernel(slots, group, meta_ref, before_ref, own_ref, after_ref, x_ref, offset_ref, *rest):
    slot_refs = rest[:slots]
    out_ref, weight_ref = rest[slots:]
    rows = own_ref.shape[0]
    blocks = rows // ROW_BLOCK
    masks = [key_mask(meta_ref, b * ROW_BLOCK) for b in range(blocks)]
    for g in range(group):
        columns = slice(g * HEAD_DIM, (g + 1) * HEAD_DIM)
        weight = load_weight(meta_ref, slot_refs, weight_ref, g, slots)
        own = own_ref[:, columns]
        extended = jnp.concatenate([before_ref[:, columns], own, after_ref[:, columns]], axis=0)
        query = dot_nn(own, weight[:, :HEAD_DIM]).astype(BF16)
        key_value = dot_nn(extended, weight[:, HEAD_DIM:]).astype(BF16)
        key, value = key_value[:, :HEAD_DIM], key_value[:, HEAD_DIM:]
        bias = toeplitz(offset_ref[g])
        for b in range(blocks):
            first = b * ROW_BLOCK
            window = slice(first, first + WINDOW)
            probs = block_probs(query[first : first + ROW_BLOCK], key[window], bias + masks[b])
            attended = dot_nn(probs.astype(BF16), value[window])
            kept = x_ref[first : first + ROW_BLOCK, columns].astype(F32)
            out_ref[first : first + ROW_BLOCK, columns] = (kept + attended).astype(BF16)


def column_spec(rows, group, first):
    return pl.BlockSpec((rows, group * HEAD_DIM), lambda i, meta: (0, i + first))


def slot_specs(weight_slots, group):
    return [
        pl.BlockSpec((3, group, slot.shape[2], HEAD_DIM), lambda i, meta: (0, i, 0, 0))
        for slot in weight_slots
    ]


def forward_attention(meta, before, own, after, x, offsets, weight_slots, group):
    rows, width = own.shape
    heads = width // HEAD_DIM
    slots = len(weight_slots)
    return pl.pallas_call(
        functools.partial(forward_kernel, slots, group),
        out_shape=jax.ShapeDtypeStruct((rows, width), BF16),
        grid_spec=pltpu.PrefetchScalarGridSpec(
            num_scalar_prefetch=1,
            grid=(heads // group,),
            in_specs=[
                column_spec(RADIUS, group, 0),
                column_spec(rows, group, 0),
                column_spec(RADIUS, group, 0),
                column_spec(rows, group, 0),
                pl.BlockSpec((group, 1, WINDOW), lambda i, meta: (i, 0, 0)),
                *slot_specs(weight_slots, group),
            ],
            out_specs=column_spec(rows, group, 0),
            scratch_shapes=[pltpu.VMEM((group, HEAD_DIM, 3 * HEAD_DIM), BF16)],
        ),
        compiler_params=pltpu.CompilerParams(vmem_limit_bytes=VMEM_LIMIT),
        cost_estimate=pl.CostEstimate(
            flops=heads * 60_000_000, bytes_accessed=8 * rows * width, transcendentals=heads * 32768
        ),
        name="forward_attention",
    )(meta, before, own, after, x, offsets, *weight_slots)


def backward_kernel(slots, group, meta_ref, before_ref, own_ref, after_ref, cot_ref, offset_ref, *rest):
    slot_refs = rest[:slots]
    rest = rest[slots:]
    grad_ref, lower_ref, upper_ref, offset_grad_ref = rest[:4]
    part_refs = rest[4 : 4 + slots]
    weight_ref, part_ref = rest[4 + slots :]
    rows = own_ref.shape[0]
    blocks = rows // ROW_BLOCK
    scale = HEAD_DIM ** (-0.5)
    masks = [key_mask(meta_ref, b * ROW_BLOCK) for b in range(blocks)]
    for g in range(group):
        columns = slice(g * HEAD_DIM, (g + 1) * HEAD_DIM)
        weight = load_weight(meta_ref, slot_refs, weight_ref, g, slots)
        own = own_ref[:, columns]
        extended = jnp.concatenate([before_ref[:, columns], own, after_ref[:, columns]], axis=0)
        query = dot_nn(own, weight[:, :HEAD_DIM]).astype(BF16)
        key_value = dot_nn(extended, weight[:, HEAD_DIM:]).astype(BF16)
        key, value = key_value[:, :HEAD_DIM], key_value[:, HEAD_DIM:]
        bias = toeplitz(offset_ref[g])
        grad_query, grad_key, grad_value, score_sum = [], [], [], None
        for b in range(blocks):
            first = b * ROW_BLOCK
            window = slice(first, first + WINDOW)
            query_rows = query[first : first + ROW_BLOCK]
            cot_rows = cot_ref[first : first + ROW_BLOCK, columns]
            probs = block_probs(query_rows, key[window], bias + masks[b])
            grad_probs = dot_nt(cot_rows, value[window])
            delta = jnp.sum(probs * grad_probs, axis=-1, keepdims=True)
            grad_scores = probs * (grad_probs - delta)
            score_sum = grad_scores if score_sum is None else score_sum + grad_scores
            grad_packed = grad_scores.astype(BF16)
            grad_query.append(dot_nn(grad_packed, key[window]))
            grad_key.append(dot_tn(grad_packed, query_rows))
            grad_value.append(dot_tn(probs.astype(BF16), cot_rows))

        def joined(parts):
            pieces = []
            for u in range((rows + 2 * RADIUS) // ROW_BLOCK):
                total = None
                for b in range(blocks):
                    if 0 <= u - b < WINDOW // ROW_BLOCK:
                        piece = parts[b][(u - b) * ROW_BLOCK : (u - b + 1) * ROW_BLOCK]
                        total = piece if total is None else total + piece
                pieces.append(total)
            return jnp.concatenate(pieces, axis=0)

        dquery = (jnp.concatenate(grad_query, axis=0) * scale).astype(BF16)
        dkey = (joined(grad_key) * scale).astype(BF16)
        dvalue = joined(grad_value).astype(BF16)
        dkey_value = jnp.concatenate([dkey, dvalue], axis=1)
        grad_extended = dot_nt(dkey_value, weight[:, HEAD_DIM:])
        grad_ref[:, columns] = grad_extended[RADIUS : RADIUS + rows] + dot_nt(dquery, weight[:, :HEAD_DIM])
        lower_ref[:, columns] = grad_extended[:RADIUS].astype(BF16)
        upper_ref[:, columns] = grad_extended[RADIUS + rows :].astype(BF16)
        part_ref[g, :, :HEAD_DIM] = dot_tn(own, dquery)
        part_ref[g, :, HEAD_DIM:] = dot_tn(extended, dkey_value)
        depth = HEAD_DIM // slots
        for r in range(slots):
            if slots == 1:
                start = 0
            else:
                start = pl.multiple_of(lax.rem(meta_ref[0] + r, slots) * depth, depth)
            for j in range(3):
                part_refs[r][j, g] = part_ref[
                    g, pl.ds(start, depth), j * HEAD_DIM : (j + 1) * HEAD_DIM
                ].astype(part_refs[r].dtype)
        offset_grad_ref[g] = diagonal_sums(score_sum)


def backward_attention(meta, before, own, after, cotangent, offsets, weight_slots, group, first_head, heads):
    rows = own.shape[0]
    width = heads * HEAD_DIM
    slots = len(weight_slots)
    first = first_head // group
    slot_shape = weight_slots[0].shape
    part_types = [F32] + [BF16] * (slots - 1) if slots > 1 else [BF16]
    return pl.pallas_call(
        functools.partial(backward_kernel, slots, group),
        out_shape=(
            jax.ShapeDtypeStruct((rows, width), F32),
            jax.ShapeDtypeStruct((RADIUS, width), BF16),
            jax.ShapeDtypeStruct((RADIUS, width), BF16),
            jax.ShapeDtypeStruct((heads, 1, WINDOW), F32),
            *[jax.ShapeDtypeStruct(slot_shape, kind) for kind in part_types],
        ),
        grid_spec=pltpu.PrefetchScalarGridSpec(
            num_scalar_prefetch=1,
            grid=(heads // group,),
            in_specs=[
                column_spec(RADIUS, group, first),
                column_spec(rows, group, first),
                column_spec(RADIUS, group, first),
                column_spec(rows, group, first),
                pl.BlockSpec((group, 1, WINDOW), lambda i, meta: (i + first, 0, 0)),
                *slot_specs(weight_slots, group),
            ],
            out_specs=(
                column_spec(rows, group, 0),
                column_spec(RADIUS, group, 0),
                column_spec(RADIUS, group, 0),
                pl.BlockSpec((group, 1, WINDOW), lambda i, meta: (i, 0, 0)),
                *slot_specs(weight_slots, group),
            ),
            scratch_shapes=[
                pltpu.VMEM((group, HEAD_DIM, 3 * HEAD_DIM), BF16),
                pltpu.VMEM((group, HEAD_DIM, 3 * HEAD_DIM), F32),
            ],
        ),
        compiler_params=pltpu.CompilerParams(vmem_limit_bytes=VMEM_LIMIT),
        cost_estimate=pl.CostEstimate(
            flops=heads * 150_000_000, bytes_accessed=12 * rows * width, transcendentals=heads * 32768
        ),
        name="backward_attention",
    )(meta, before, own, after, cotangent, offsets, *weight_slots)


def finish_kernel(grad_ref, low_ref, high_ref, x_ref, inverse_ref, gain_ref, cot_ref, out_ref, gain_grad_ref):
    rows = x_ref.shape[0]
    grad = grad_ref[...]
    edge = jnp.zeros((rows - RADIUS, grad.shape[1]), F32)
    grad = grad + jnp.concatenate([low_ref[...].astype(F32), edge], axis=0)
    grad = grad + jnp.concatenate([edge, high_ref[...].astype(F32)], axis=0)
    x = x_ref[...].astype(F32)
    inverse = inverse_ref[:, :1]
    gain_grad_ref[...] = jnp.sum(grad * x * inverse, axis=0, keepdims=True)
    scaled = grad * gain_ref[...]
    mean = jnp.mean(scaled * x, axis=-1, keepdims=True)
    result = inverse * scaled - x * (inverse * inverse * inverse * mean)
    out_ref[...] = (cot_ref[...].astype(F32) + result).astype(BF16)


def finish(grad, low, high, x, inverse, gain, cotangent):
    rows, width = x.shape
    return pl.pallas_call(
        finish_kernel,
        out_shape=(
            jax.ShapeDtypeStruct((rows, width), BF16),
            jax.ShapeDtypeStruct((1, width), F32),
        ),
        compiler_params=pltpu.CompilerParams(vmem_limit_bytes=VMEM_LIMIT),
        cost_estimate=pl.CostEstimate(
            flops=16 * rows * width, bytes_accessed=14 * rows * width, transcendentals=0
        ),
        name="finish",
    )(grad, low, high, x, inverse, gain, cotangent)


def column_of(row, rows):
    return jnp.transpose(jnp.broadcast_to(row, (128, rows)))


def split_rows(inverse, pad_rows, width):
    high = inverse.astype(BF16)
    rest = inverse - high.astype(F32)
    middle = rest.astype(BF16)
    low = (rest - middle.astype(F32)).astype(BF16)
    wide = [jnp.transpose(jnp.broadcast_to(v.astype(F32), (v.shape[0], 128)))[:1] for v in (high, middle, low)]
    row = jnp.concatenate(wide + [jnp.zeros((pad_rows - 3, wide[0].shape[1]), F32)], axis=0)
    return row.astype(BF16)


def row_inverse(x):
    x = x.astype(F32)
    return lax.rsqrt(jnp.mean(x * x, axis=-1, keepdims=True) + eps_norm)


def pack_stash_kernel(parts, pieces, meta_ref, x_hbm, gain_hbm, weight_hbm, inverse_ref, *refs):
    out_refs = refs[:parts]
    x_ref, gain_ref, weight_ref, normed_ref, sems = refs[parts:]
    rows, width = x_ref.shape
    depth = weight_ref.shape[2]
    wide = width // parts
    heads = wide // HEAD_DIM
    step = rows // pieces
    gain_copy = pltpu.make_async_copy(gain_hbm, gain_ref, sems.at[0])
    x_copies = [
        pltpu.make_async_copy(x_hbm.at[pl.ds(k * step, step)], x_ref.at[pl.ds(k * step, step)], sems.at[1 + k])
        for k in range(pieces)
    ]
    weight_copies = [
        pltpu.make_async_copy(weight_hbm.at[j], weight_ref.at[j], sems.at[1 + pieces + j]) for j in range(3)
    ]
    for copy in (gain_copy, *x_copies, *weight_copies):
        copy.start()
    gain_copy.wait()
    gain = gain_ref[...]
    for k, copy in enumerate(x_copies):
        copy.wait()
        part = slice(k * step, (k + 1) * step)
        inverse = row_inverse(x_ref[part])
        inverse_ref[part] = jnp.broadcast_to(inverse, (step, 128))
        normed_ref[part] = (x_ref[part].astype(F32) * inverse * gain).astype(BF16)
    for r, out_ref in enumerate(out_refs):
        target = lax.rem(meta_ref[0] + r, parts)
        out_ref[:rows] = normed_ref[:, pl.ds(pl.multiple_of(target * wide, 128), wide)]
    for j, copy in enumerate(weight_copies):
        copy.wait()
        for r, out_ref in enumerate(out_refs):
            target = lax.rem(meta_ref[0] + r, parts)
            for h in range(heads):
                out_ref[rows + j * depth : rows + (j + 1) * depth, h * HEAD_DIM : (h + 1) * HEAD_DIM] = weight_ref[
                    j, target * heads + h
                ]


def pack_rows_kernel(parts, with_inverse, meta_ref, edge_ref, inner_ref, *out_refs):
    rows, width = inner_ref.shape
    wide = width // parts
    edge = 1 if with_inverse else 2
    refs = out_refs[:parts]
    for r, out_ref in enumerate(refs):
        target = lax.rem(meta_ref[0] + r, parts)
        start = pl.multiple_of(target * wide, 128)

        @pl.when(meta_ref[edge] == 1)
        def use_edge():
            out_ref[:rows] = edge_ref[:, pl.ds(start, wide)]

        @pl.when(meta_ref[edge] == 0)
        def use_inner():
            out_ref[:rows] = inner_ref[:, pl.ds(start, wide)]

    def finish_with(source_ref):
        if with_inverse:
            tail = split_rows(row_inverse(source_ref[...]), EXTRA, wide)
            for out_ref in refs:
                out_ref[rows:] = jnp.zeros((EXTRA, wide), BF16)
                out_ref[rows:, :rows] = tail
        else:
            out_refs[parts][...] = source_ref[...]

    @pl.when(meta_ref[edge] == 1)
    def finish_edge():
        finish_with(edge_ref)

    @pl.when(meta_ref[edge] == 0)
    def finish_inner():
        finish_with(inner_ref)


SMEM_SPEC = pl.BlockSpec(memory_space=pltpu.SMEM)
VMEM_SPEC = pl.BlockSpec(memory_space=pltpu.VMEM)


def pack_stash(meta, x, gain, weight, parts):
    rows, width = x.shape
    depth = weight.shape[2]
    shape = (rows + 3 * depth, width // parts)
    return pl.pallas_call(
        functools.partial(pack_stash_kernel, parts, 4),
        out_shape=(
            jax.ShapeDtypeStruct((rows, 128), F32),
            *[jax.ShapeDtypeStruct(shape, BF16) for r in range(parts)],
        ),
        in_specs=[SMEM_SPEC] + [pl.BlockSpec(memory_space=pl.ANY)] * 3,
        out_specs=(VMEM_SPEC,) * (parts + 1),
        scratch_shapes=[
            pltpu.VMEM((rows, width), BF16),
            pltpu.VMEM((1, width), F32),
            pltpu.VMEM(weight.shape, BF16),
            pltpu.VMEM((rows, width), BF16),
            pltpu.SemaphoreType.DMA((8,)),
        ],
        compiler_params=pltpu.CompilerParams(vmem_limit_bytes=58 * 1024 * 1024),
        cost_estimate=pl.CostEstimate(flops=4 * rows * width, bytes_accessed=6 * rows * width, transcendentals=0),
        name="pack_stash",
    )(meta, x, gain, weight)


def pack_rows(meta, edge, inner, parts, with_inverse):
    rows, width = inner.shape
    shape = (rows + (EXTRA if with_inverse else 0), width // parts)
    extra = () if with_inverse else (jax.ShapeDtypeStruct((rows, width), BF16),)
    return pl.pallas_call(
        functools.partial(pack_rows_kernel, parts, with_inverse),
        out_shape=(*[jax.ShapeDtypeStruct(shape, BF16) for r in range(parts)], *extra),
        in_specs=[SMEM_SPEC, VMEM_SPEC, VMEM_SPEC],
        out_specs=(VMEM_SPEC,) * (parts + len(extra)),
        compiler_params=pltpu.CompilerParams(vmem_limit_bytes=VMEM_LIMIT),
        cost_estimate=pl.CostEstimate(flops=4 * rows * width, bytes_accessed=6 * rows * width, transcendentals=0),
        name="pack_inbound" if with_inverse else "pack_cotangent",
    )(meta, edge, inner)


def gather_rows(meta_ref, refs, rows, x_ref):
    parts = len(refs)
    for r, ref in enumerate(refs):
        source = lax.rem(meta_ref[0] + parts - r, parts)
        x_ref[pl.ds(pl.multiple_of(source * rows, rows), rows)] = ref[:rows]


def gather_weight(meta_ref, refs, rows, weight_ref):
    parts = len(refs)
    depth = HEAD_DIM // parts
    for r, ref in enumerate(refs):
        source = lax.rem(meta_ref[0] + parts - r, parts)
        depth_at = pl.ds(pl.multiple_of(source * depth, depth), depth)
        for j in range(3):
            weight_ref[depth_at, j * HEAD_DIM : (j + 1) * HEAD_DIM] = ref[
                rows + j * depth : rows + (j + 1) * depth
            ]


def gather_inverse(meta_ref, refs, rows, inverse_ref):
    parts = len(refs)

    @pl.when(pl.program_id(0) == 0)
    def spread_inverse():
        for r, ref in enumerate(refs):
            source = lax.rem(meta_ref[0] + parts - r, parts)
            tail = ref[rows : rows + EXTRA].astype(F32)
            inverse_ref[pl.ds(pl.multiple_of(source * rows, rows), rows)] = column_of(
                tail[:1] + tail[1:2] + tail[2:3], rows
            )


def block_mask(first_query, tokens):
    key = lax.broadcasted_iota(jnp.int32, (1, WINDOW), 1) + (first_query - RADIUS)
    return jnp.where((key >= 0) & (key < tokens), 0.0, masked_score).astype(F32)


def edge_bias(bias, first, tokens):
    if first < RADIUS or first + ROW_BLOCK + RADIUS > tokens:
        return bias + block_mask(first, tokens)
    return bias


def padded(rows):
    edge = jnp.zeros((RADIUS, rows.shape[1]), rows.dtype)
    return jnp.concatenate([edge, rows, edge], axis=0)


def heads_backward_kernel(parts, rows, meta_ref, *refs):
    a_refs, c_refs = refs[:parts], refs[parts : 2 * parts]
    gain_ref, offset_ref, onehot_ref, after_ref = refs[2 * parts : 2 * parts + 4]
    out_refs = refs[2 * parts + 4 : 3 * parts + 4]
    gain_grad_ref, x_ref, weight_ref, cot_ref, grad_ref, part_ref, bias_ref = refs[3 * parts + 4 :]
    tokens = rows * parts
    depth = HEAD_DIM // parts
    scale = HEAD_DIM ** (-0.5)
    gather_rows(meta_ref, a_refs, rows, x_ref)
    gather_weight(meta_ref, a_refs, rows, weight_ref)
    gather_rows(meta_ref, c_refs, rows, cot_ref)
    weight = weight_ref[...]
    normed = x_ref[...]
    query = dot_nn(normed, weight[:, :HEAD_DIM]).astype(BF16)
    key = padded(dot_nn(normed, weight[:, HEAD_DIM : 2 * HEAD_DIM]).astype(BF16))
    value = padded(dot_nn(normed, weight[:, 2 * HEAD_DIM :]).astype(BF16))
    bias = toeplitz(offset_ref[0])
    blocks = tokens // ROW_BLOCK
    starts = range(0, tokens, ROW_BLOCK)
    cot = cot_ref[...]
    query_rows = [query[f : f + ROW_BLOCK] for f in starts]
    cot_rows = [cot[f : f + ROW_BLOCK] for f in starts]
    products = [dot_nt(rows_q, key[f : f + WINDOW]) for f, rows_q in zip(starts, query_rows)]
    grad_probs = [dot_nt(rows_c, value[f : f + WINDOW]) for f, rows_c in zip(starts, cot_rows)]
    packed, grad_packed, score_sum = [], [], None
    for f, product, grads in zip(starts, products, grad_probs):
        probs = score_probs(product, edge_bias(bias, f, tokens))
        delta = jnp.sum(probs * grads, axis=-1, keepdims=True)
        grad_scores = probs * (grads - delta)
        score_sum = grad_scores if score_sum is None else score_sum + grad_scores
        packed.append(probs.astype(BF16))
        grad_packed.append(grad_scores.astype(BF16))
    grad_query = [dot_nn(part, key[f : f + WINDOW]) for f, part in zip(starts, grad_packed)]
    grad_key = [dot_tn(part, rows_q) for part, rows_q in zip(grad_packed, query_rows)]
    grad_value = [dot_tn(part, rows_c) for part, rows_c in zip(packed, cot_rows)]

    def joined(pieces):
        units = []
        for u in range((tokens + 2 * RADIUS) // ROW_BLOCK):
            total = None
            for b in range(blocks):
                if 0 <= u - b < WINDOW // ROW_BLOCK:
                    piece = pieces[b][(u - b) * ROW_BLOCK : (u - b + 1) * ROW_BLOCK]
                    total = piece if total is None else total + piece
            units.append(total)
        return jnp.concatenate(units, axis=0)[RADIUS : RADIUS + tokens]

    dqkv = jnp.concatenate(
        [
            (jnp.concatenate(grad_query, axis=0) * scale).astype(BF16),
            (joined(grad_key) * scale).astype(BF16),
            joined(grad_value).astype(BF16),
        ],
        axis=1,
    )
    grad_normed = dot_nt(dqkv, weight)
    gain_grad_ref[...] = jnp.sum(grad_normed * normed.astype(F32), axis=0, keepdims=True) / gain_ref[...]
    grad_ref[...] = grad_normed
    part_ref[...] = dot_tn(normed, dqkv)
    bias_grad = jnp.sum(onehot_ref[...] * diagonal_sums(score_sum), axis=1, keepdims=True)
    bias_ref[...] = jnp.broadcast_to(bias_grad, bias_ref.shape)
    buckets = bias_ref.shape[0] // parts
    for r, out_ref in enumerate(out_refs):
        source = lax.rem(meta_ref[0] + parts - r, parts)
        out_ref[:rows] = grad_ref[pl.ds(pl.multiple_of(source * rows, rows), rows)].astype(BF16)
        for j in range(3):
            out_ref[rows + j * depth : rows + (j + 1) * depth] = part_ref[
                pl.ds(pl.multiple_of(source * depth, depth), depth), j * HEAD_DIM : (j + 1) * HEAD_DIM
            ].astype(BF16)
        share = bias_ref[pl.ds(pl.multiple_of(source * buckets, buckets), buckets)]
        out_ref[rows + 3 * depth :] = share.astype(BF16)


def head_column(rows, first=0):
    return pl.BlockSpec((rows, HEAD_DIM), lambda i, meta: (0, i + first))


def whole_column(rows, heads, first=0):
    return pl.BlockSpec((rows, HEAD_DIM), lambda i, meta: (0, meta[0] * heads + first + i))


def offset_spec(heads, first=0):
    return pl.BlockSpec((1, 1, WINDOW), lambda i, meta: (meta[0] * heads + first + i, 0, 0))


def heads_backward(meta, a_slots, c_slots, gain, offsets, onehot, after, heads, first, count):
    parts = len(a_slots)
    rows = c_slots[0].shape[0]
    tokens = rows * parts
    buckets = onehot.shape[0]
    packed = a_slots[0].shape[0]
    made = packed + buckets // parts
    width = count * HEAD_DIM
    return pl.pallas_call(
        functools.partial(heads_backward_kernel, parts, rows),
        out_shape=(
            *[jax.ShapeDtypeStruct((made, width), BF16) for r in range(parts)],
            jax.ShapeDtypeStruct((1, width), F32),
        ),
        grid_spec=pltpu.PrefetchScalarGridSpec(
            num_scalar_prefetch=1,
            grid=(count,),
            in_specs=[
                *[head_column(packed, first)] * parts,
                whole_column(rows, heads, first),
                *[head_column(rows, first)] * (parts - 1),
                whole_column(1, heads, first),
                offset_spec(heads, first),
                pl.BlockSpec((buckets, WINDOW), lambda i, meta: (0, 0)),
                pl.BlockSpec(memory_space=pl.ANY),
            ],
            out_specs=(*[head_column(made)] * parts, head_column(1)),
            scratch_shapes=[
                pltpu.VMEM((tokens, HEAD_DIM), BF16),
                pltpu.VMEM((HEAD_DIM, 3 * HEAD_DIM), BF16),
                pltpu.VMEM((tokens, HEAD_DIM), BF16),
                pltpu.VMEM((tokens, HEAD_DIM), F32),
                pltpu.VMEM((HEAD_DIM, 3 * HEAD_DIM), F32),
                pltpu.VMEM((buckets, HEAD_DIM), F32),
            ],
        ),
        compiler_params=pltpu.CompilerParams(vmem_limit_bytes=VMEM_LIMIT),
        cost_estimate=pl.CostEstimate(
            flops=count * tokens * 400_000, bytes_accessed=tokens * width, transcendentals=0
        ),
        name="heads_backward",
    )(meta, *a_slots, *c_slots, gain, offsets, onehot, after)


def heads_forward_kernel(parts, rows, meta_ref, *refs):
    a_refs, i_refs = refs[:parts], refs[parts : 2 * parts]
    gain_ref, offset_ref = refs[2 * parts : 2 * parts + 2]
    out_refs = refs[2 * parts + 2 : 3 * parts + 2]
    sums_ref, inverse_ref, x_ref, weight_ref, made_ref, square_ref = refs[3 * parts + 2 :]
    tokens = rows * parts
    gather_rows(meta_ref, i_refs, rows, x_ref)
    gather_weight(meta_ref, a_refs, rows, weight_ref)
    gather_inverse(meta_ref, i_refs, rows, inverse_ref)
    weight = weight_ref[...]
    normed = (x_ref[...].astype(F32) * inverse_ref[...] * gain_ref[...]).astype(BF16)
    query = dot_nn(normed, weight[:, :HEAD_DIM]).astype(BF16)
    key = padded(dot_nn(normed, weight[:, HEAD_DIM : 2 * HEAD_DIM]).astype(BF16))
    value = padded(dot_nn(normed, weight[:, 2 * HEAD_DIM :]).astype(BF16))
    bias = toeplitz(offset_ref[0])
    starts = range(0, tokens, ROW_BLOCK)
    products = [dot_nt(query[f : f + ROW_BLOCK], key[f : f + WINDOW]) for f in starts]
    packed = [
        score_probs(product, edge_bias(bias, f, tokens)).astype(BF16) for f, product in zip(starts, products)
    ]
    attended = [dot_nn(part, value[f : f + WINDOW]) for f, part in zip(starts, packed)]
    for f, part in zip(starts, attended):
        made_ref[f : f + ROW_BLOCK] = (x_ref[f : f + ROW_BLOCK].astype(F32) + part).astype(BF16)
    made = made_ref[...].astype(F32)
    squares = made * made

    @pl.when(pl.program_id(0) == 0)
    def first_head():
        square_ref[...] = squares

    @pl.when(pl.program_id(0) > 0)
    def later_head():
        square_ref[...] += squares

    for r, out_ref in enumerate(out_refs):
        source = lax.rem(meta_ref[0] + parts - r, parts)
        out_ref[...] = made_ref[pl.ds(pl.multiple_of(source * rows, rows), rows)]

    @pl.when(pl.program_id(0) == pl.num_programs(0) - 1)
    def last_head():
        total = jnp.sum(jnp.transpose(square_ref[...]), axis=0, keepdims=True)
        sums_ref[...] = jnp.broadcast_to(total, sums_ref.shape)


def heads_forward(meta, a_slots, i_slots, gain, offsets, heads, rows):
    parts = len(a_slots)
    tokens = rows * parts
    packed = a_slots[0].shape[0]
    width = heads * HEAD_DIM
    return pl.pallas_call(
        functools.partial(heads_forward_kernel, parts, rows),
        out_shape=(
            *[jax.ShapeDtypeStruct((rows, width), BF16) for r in range(parts)],
            jax.ShapeDtypeStruct((8, tokens), F32),
        ),
        grid_spec=pltpu.PrefetchScalarGridSpec(
            num_scalar_prefetch=1,
            grid=(heads,),
            in_specs=[
                *[head_column(packed)] * parts,
                *[head_column(i_slots[0].shape[0])] * parts,
                whole_column(1, heads),
                offset_spec(heads),
            ],
            out_specs=(
                *[head_column(rows)] * parts,
                pl.BlockSpec((8, tokens), lambda i, meta: (0, 0)),
            ),
            scratch_shapes=[
                pltpu.VMEM((tokens, HEAD_DIM), F32),
                pltpu.VMEM((tokens, HEAD_DIM), BF16),
                pltpu.VMEM((HEAD_DIM, 3 * HEAD_DIM), BF16),
                pltpu.VMEM((tokens, HEAD_DIM), BF16),
                pltpu.VMEM((tokens, HEAD_DIM), F32),
            ],
        ),
        compiler_params=pltpu.CompilerParams(vmem_limit_bytes=VMEM_LIMIT),
        cost_estimate=pl.CostEstimate(
            flops=heads * tokens, bytes_accessed=tokens, transcendentals=0
        ),
        name="heads_forward",
    )(meta, *a_slots, *i_slots, gain, offsets)


def memory_kernel(parts, width, meta_ref, *refs):
    out_refs, sum_refs = refs[:parts], refs[parts : 2 * parts]
    gain_ref, *share_refs, memory_ref = refs[2 * parts :]
    wide = memory_ref.shape[1]
    rows = memory_ref.shape[0] // parts
    total = sum_refs[0][:1]
    for sum_ref in sum_refs[1:]:
        total = total + sum_ref[:1]
    inverse = lax.rsqrt(total / width + eps_norm)
    gain = gain_ref[:, pl.ds(pl.multiple_of(meta_ref[0] * wide, 128), wide)]
    spread_inverse = jnp.transpose(jnp.broadcast_to(inverse, (128, inverse.shape[1])))
    for r, out_ref in enumerate(out_refs):
        source = lax.rem(meta_ref[0] + parts - r, parts)
        memory_ref[pl.ds(pl.multiple_of(source * rows, rows), rows)] = out_ref[...]
    made = memory_ref[...].astype(F32)
    memory_ref[...] = (made * spread_inverse[:, :1] * gain).astype(BF16)
    for k, share_ref in enumerate(share_refs):
        size = share_ref.shape[0]
        share_ref[...] = memory_ref[k * size : (k + 1) * size]


def memory_rows(meta, outs, sums, gain, width, shares):
    parts = len(outs)
    rows, wide = outs[0].shape
    return pl.pallas_call(
        functools.partial(memory_kernel, parts, width),
        out_shape=[jax.ShapeDtypeStruct((rows * parts // shares, wide), BF16)] * shares,
        in_specs=[SMEM_SPEC] + [VMEM_SPEC] * (2 * parts + 1),
        out_specs=[VMEM_SPEC] * shares,
        scratch_shapes=[pltpu.VMEM((rows * parts, wide), BF16)],
        compiler_params=pltpu.CompilerParams(vmem_limit_bytes=VMEM_LIMIT),
        cost_estimate=pl.CostEstimate(flops=rows, bytes_accessed=rows, transcendentals=0),
        name="memory_rows",
    )(meta, *outs, *sums, gain)


def place_kernel(parts, meta_ref, *refs):
    out_ref = refs[parts + 1]
    wide = refs[0].shape[1]
    for r in range(parts):
        source = lax.rem(meta_ref[0] + r, parts)
        out_ref[:, pl.ds(pl.multiple_of(source * wide, 128), wide)] = refs[r][...]


def place_columns(meta, slots, after):
    parts = len(slots)
    rows, wide = slots[0].shape
    return pl.pallas_call(
        functools.partial(place_kernel, parts),
        out_shape=jax.ShapeDtypeStruct((rows, wide * parts), BF16),
        in_specs=[SMEM_SPEC] + [VMEM_SPEC] * parts + [pl.BlockSpec(memory_space=pl.ANY)],
        out_specs=VMEM_SPEC,
        compiler_params=pltpu.CompilerParams(vmem_limit_bytes=VMEM_LIMIT),
        cost_estimate=pl.CostEstimate(flops=0, bytes_accessed=rows, transcendentals=0),
        name="place_columns",
    )(meta, *slots, after)


def heads_finish_kernel(parts, meta_ref, *refs):
    g_refs = refs[:parts]
    x_ref, inverse_ref, gain_ref, cot_ref, out_ref, weight_hbm, bias_ref, scaled_ref, weight_ref, sem = refs[parts:]
    rows, width = x_ref.shape
    wide = width // parts
    heads = wide // HEAD_DIM
    depth = HEAD_DIM // parts
    for r in range(parts):
        source = lax.rem(meta_ref[0] + r, parts)
        for h in range(heads):
            for j in range(3):
                weight_ref[j, source * heads + h] = g_refs[r][
                    rows + j * depth : rows + (j + 1) * depth, h * HEAD_DIM : (h + 1) * HEAD_DIM
                ].astype(F32)
    weight_copy = pltpu.make_async_copy(weight_ref, weight_hbm, sem)
    weight_copy.start()
    lane = lax.broadcasted_iota(jnp.int32, (bias_ref.shape[0], HEAD_DIM), 1)
    bias = jnp.zeros(lane.shape, F32)
    for r in range(parts):
        source = lax.rem(meta_ref[0] + r, parts)
        columns = pl.ds(pl.multiple_of(source * wide, 128), wide)
        scaled_ref[:, columns] = g_refs[r][:rows].astype(F32) * gain_ref[:, columns]
        shares = g_refs[r][rows + 3 * depth :].astype(F32)
        for h in range(heads):
            bias = jnp.where(lane == source * heads + h, shares[:, h * HEAD_DIM : (h + 1) * HEAD_DIM], bias)
    bias_ref[...] = bias[:, : bias_ref.shape[1]]
    x = x_ref[...].astype(F32)
    scaled = scaled_ref[...]
    inverse = inverse_ref[:, :1]
    mean = jnp.mean(scaled * x, axis=-1, keepdims=True)
    result = inverse * scaled - x * (inverse * inverse * inverse * mean)
    out_ref[...] = (cot_ref[...].astype(F32) + result).astype(BF16)
    weight_copy.wait()


def heads_finish(meta, g_slots, x, inverse, gain, cotangent, buckets):
    parts = len(g_slots)
    rows, width = x.shape
    heads = width // HEAD_DIM
    weight_shape = (3, heads, HEAD_DIM // parts, HEAD_DIM)
    return pl.pallas_call(
        functools.partial(heads_finish_kernel, parts),
        out_shape=(
            jax.ShapeDtypeStruct((rows, width), BF16),
            jax.ShapeDtypeStruct(weight_shape, F32),
            jax.ShapeDtypeStruct((buckets // parts, heads), F32),
        ),
        in_specs=[SMEM_SPEC] + [VMEM_SPEC] * (parts + 4),
        out_specs=(VMEM_SPEC, pl.BlockSpec(memory_space=pl.ANY), VMEM_SPEC),
        scratch_shapes=[
            pltpu.VMEM((rows, width), F32),
            pltpu.VMEM(weight_shape, F32),
            pltpu.SemaphoreType.DMA,
        ],
        compiler_params=pltpu.CompilerParams(vmem_limit_bytes=VMEM_LIMIT),
        cost_estimate=pl.CostEstimate(flops=rows, bytes_accessed=rows, transcendentals=0),
        name="heads_finish",
    )(meta, *g_slots, x, inverse, gain, cotangent)


def offset_table(rel_bias):
    onehot = jnp.asarray(bucket_onehot(rel_bias.shape[0]))
    by_offset = jnp.dot(onehot, rel_bias, precision=lax.Precision.HIGHEST).T
    inside = jnp.arange(WINDOW, dtype=jnp.int32) <= 2 * RADIUS
    return jnp.where(inside[None, :], by_offset, masked_score)[:, None, :]


def shifted(value, axis, steps):
    count = lax.axis_size(axis)
    first, last = (max(0, -steps), min(count, count - steps))
    return lax.ppermute(value, axis, [(source, source + steps) for source in range(first, last)])


def spread_memory(shares, section, sections):
    last = sections - 1
    couple = jnp.where(section == last, shares[-1], 0)
    for s, share in enumerate(shares[:-1]):
        couple = couple + lax.ppermute(share, "section", [(last, 2 * s + 1)])
    half = couple.shape[0] // 2
    even = lax.ppermute(couple[:half], "section", [(s + 1, s) for s in range(0, sections, 2)])
    return jnp.where(section % 2 == 0, even, couple[half:])


def heads_body(
    embedded, carried, stash, returned, loss_grad, qkv_weight, rel_bias, norm_gain, final_gain
):
    section = lax.axis_index("section")
    sections = lax.axis_size("section")
    parts = lax.axis_size("seq")
    rows, width = embedded.shape
    heads = width // HEAD_DIM // parts
    buckets = rel_bias.shape[1]
    meta = jnp.stack(
        [lax.axis_index("seq"), section == 0, section == sections - 1]
    ).astype(jnp.int32)

    def exchanged(sends, direction):
        moved = [
            lax.ppermute(sends[r], "seq", [(i, (i + direction * r) % parts) for i in range(parts)])
            for r in range(1, parts)
        ]
        return [sends[0]] + moved

    inverse_b, *a_sends = pack_stash(meta, stash[0], norm_gain, qkv_weight[0], parts)
    a_slots = exchanged(a_sends, 1)
    arrived = shifted(carried[0], "section", 1)
    came_back = shifted(returned[0], "section", -1)
    *c_sends, cotangent = pack_rows(meta, loss_grad, came_back, parts, False)
    c_slots = exchanged(c_sends, 1)
    c_slots[0] = cotangent
    i_slots = exchanged(pack_rows(meta, embedded, arrived, parts, True), 1)

    offsets = offset_table(rel_bias[0])
    onehot = jnp.asarray(bucket_onehot(buckets).T)
    *g_sends, gain_grad = heads_backward(
        meta, a_slots, c_slots, norm_gain, offsets, onehot, norm_gain, heads, 0, heads
    )
    g_sends, i_slots = lax.optimization_barrier((g_sends, i_slots))
    g_slots = exchanged(g_sends, -1)

    *o_sends, sums = heads_forward(meta, a_slots, i_slots, norm_gain, offsets, heads, rows)
    all_sums = exchanged([sums] * parts, 1)
    o_slots = exchanged(o_sends, -1)
    shares = memory_rows(meta, o_sends, all_sums, final_gain[None], width, sections // 2)
    shares, g_slots = lax.optimization_barrier((shares, g_slots))
    memory = spread_memory(shares, section, sections)
    input_grad, weight_grad, bias_grad = heads_finish(
        meta, g_slots, stash[0], inverse_b, norm_gain, cotangent, buckets
    )
    output = place_columns(meta, o_slots, bias_grad)
    return (
        output[None],
        input_grad[None],
        weight_grad[None],
        bias_grad[None],
        gain_grad,
        memory,
    )


def tokens_body(
    embedded, carried, stash, returned, loss_grad, qkv_weight, rel_bias, norm_gain, final_gain
):
    section_index = lax.axis_index("section")
    section_count = lax.axis_size("section")
    seq_index = lax.axis_index("seq")
    seq_count = lax.axis_size("seq")
    rows, width = embedded.shape
    heads = width // HEAD_DIM
    tokens = rows * seq_count
    shard = qkv_weight[0]
    up = [(i, i + 1) for i in range(seq_count - 1)]
    down = [(j, i) for i, j in up]
    group = 4 if heads % 4 == 0 else 1

    own_b, inverse_b = norm_rows(stash[0], norm_gain)
    before_b = lax.ppermute(own_b[rows - RADIUS :], "seq", up)
    after_b = lax.ppermute(own_b[:RADIUS], "seq", down)
    slots = [lax.all_gather(shard, "seq", axis=2, tiled=True)]

    section_up = [(i, (i + 1) % section_count) for i in range(section_count)]
    section_down = [(j, i) for i, j in section_up]
    inbound = lax.ppermute(
        jnp.where(section_index == section_count - 1, embedded, carried[0]), "section", section_up
    )
    cotangent = lax.ppermute(
        jnp.where(section_index == 0, loss_grad, returned[0]), "section", section_down
    )

    onehot = jnp.asarray(bucket_onehot(rel_bias.shape[1]))
    offsets = offset_table(rel_bias[0])
    first_key = RADIUS - seq_index * rows
    meta = jnp.stack([seq_index, first_key, first_key + tokens]).astype(jnp.int32)

    own_a, unused = norm_rows(inbound, norm_gain)
    before_a = lax.ppermute(own_a[rows - RADIUS :], "seq", up)
    after_a = lax.ppermute(own_a[:RADIUS], "seq", down)

    grad_own, lower, upper, offset_grad, *parts = backward_attention(
        meta, before_b, own_b, after_b, cotangent, offsets, slots, group, 0, heads
    )
    from_before = lax.ppermute(upper, "seq", up)
    from_after = lax.ppermute(lower, "seq", down)
    weight_sum = lax.psum_scatter(parts[0], "seq", scatter_dimension=2, tiled=True).astype(F32)

    output = forward_attention(meta, before_a, own_a, after_a, inbound, offsets, slots, group)
    final_normed, unused = norm_rows(output, final_gain[None])
    relaid = lax.all_to_all(final_normed, "seq", split_axis=1, concat_axis=0, tiled=True)
    kept = jnp.where(section_index == section_count - 1, relaid, jnp.zeros_like(relaid))
    memory = lax.psum_scatter(kept, "section", scatter_dimension=0, tiled=True)

    input_grad, gain_part = finish(
        grad_own, from_before, from_after, stash[0], inverse_b, norm_gain, cotangent
    )
    bias_part = jnp.dot(
        offset_grad[:, 0, :], onehot, precision=lax.Precision.HIGHEST
    ).T
    bias_sum = lax.psum_scatter(
        bias_part.astype(BF16), "seq", scatter_dimension=0, tiled=True
    ).astype(F32)
    gain_sum = lax.psum_scatter(
        gain_part.astype(BF16), "seq", scatter_dimension=1, tiled=True
    ).astype(F32)
    return (output[None], input_grad[None], weight_sum[None], bias_sum[None], gain_sum, memory)


def choose_body(embedded, carried, stash, returned, loss_grad, qkv_weight, rel_bias, norm_gain, final_gain):
    parts = lax.axis_size("seq")
    rows, width = embedded.shape
    even = width % (HEAD_DIM * parts) == 0 and HEAD_DIM % (32 * parts) == 0 and rows == 128
    sections = lax.axis_size("section")
    even = even and sections % 2 == 0
    even = even and rel_bias.shape[1] == 8 * parts and width <= 128 * HEAD_DIM and rows * parts % (16 * sections) == 0
    chosen = heads_body if even else tokens_body
    return chosen(
        embedded, carried, stash, returned, loss_grad, qkv_weight, rel_bias, norm_gain, final_gain
    )


def solution(mesh):
    in_specs = (
        P("seq", None),
        P("section", "seq", None),
        P("section", "seq", None),
        P("section", "seq", None),
        P("seq", None),
        P("section", None, None, "seq", None),
        P("section", None, None),
        P("section", None),
        P(),
    )
    out_specs = (
        P("section", "seq", None),
        P("section", "seq", None),
        P("section", None, None, "seq", None),
        P("section", "seq", None),
        P("section", "seq"),
        P("section", "seq"),
    )
    return jax.shard_map(choose_body, mesh=mesh, in_specs=in_specs, out_specs=out_specs, check_vma=False)
```

```python
import functools

import jax
import jax.numpy as jnp
import numpy as np
from jax import lax
from jax.experimental import pallas as pl
from jax.experimental.pallas import tpu as pltpu
from jax.sharding import PartitionSpec as P

RADIUS = 96
HEAD_DIM = 128
ROW_BLOCK = 64
WINDOW = ROW_BLOCK + 2 * RADIUS
eps_norm = 1e-06
bucket_edges = (1, 2, 3, 4, 5, 6, 7, 8, 11, 16, 22, 32, 45, 64, 90)
masked_score = -1e30
F32 = jnp.float32
BF16 = jnp.bfloat16
VMEM_LIMIT = 24 * 1024 * 1024
EXTRA = 8


def bucket_onehot(bucket_count):
    offsets = np.arange(WINDOW) - RADIUS
    magnitude = np.abs(offsets)
    counted = np.zeros(offsets.shape, np.int32)
    for threshold in bucket_edges:
        counted = counted + (magnitude >= threshold)
    counted = counted + 16 * (offsets > 0)
    onehot = (counted[:, None] == np.arange(bucket_count)[None, :]) & (magnitude <= RADIUS)[:, None]
    return onehot.astype(np.float32)


def dot_nn(a, b):
    return lax.dot_general(a, b, (((1,), (0,)), ((), ())), preferred_element_type=F32)


def dot_nt(a, b):
    return lax.dot_general(a, b, (((1,), (1,)), ((), ())), preferred_element_type=F32)


def dot_tn(a, b):
    return lax.dot_general(a, b, (((0,), (0,)), ((), ())), preferred_element_type=F32)


def norm_kernel(x_ref, gain_ref, normed_ref, inverse_ref):
    x = x_ref[...].astype(F32)
    inverse = lax.rsqrt(jnp.mean(x * x, axis=-1, keepdims=True) + eps_norm)
    normed_ref[...] = (x * inverse * gain_ref[...]).astype(BF16)
    inverse_ref[...] = jnp.broadcast_to(inverse, inverse_ref.shape)


def norm_rows(x, gain):
    rows, width = x.shape
    return pl.pallas_call(
        norm_kernel,
        out_shape=(
            jax.ShapeDtypeStruct((rows, width), BF16),
            jax.ShapeDtypeStruct((rows, 128), F32),
        ),
        compiler_params=pltpu.CompilerParams(vmem_limit_bytes=VMEM_LIMIT),
        cost_estimate=pl.CostEstimate(
            flops=6 * rows * width, bytes_accessed=4 * rows * width, transcendentals=rows
        ),
        name="norm_rows",
    )(x, gain)


def load_weight(meta_ref, slot_refs, weight_ref, head, slots):
    depth = HEAD_DIM // slots
    for r, slot_ref in enumerate(slot_refs):
        if slots == 1:
            start = 0
        else:
            start = pl.multiple_of(lax.rem(meta_ref[0] + r, slots) * depth, depth)
        for j in range(3):
            weight_ref[head, pl.ds(start, depth), j * HEAD_DIM : (j + 1) * HEAD_DIM] = slot_ref[j, head]
    return weight_ref[head]


def key_mask(meta_ref, first_key):
    key = lax.broadcasted_iota(jnp.int32, (1, WINDOW), 1) + first_key
    inside = (key >= meta_ref[1]) & (key < meta_ref[2])
    return jnp.where(inside, 0.0, masked_score).astype(F32)


def toeplitz(row):
    return pltpu.roll(
        jnp.broadcast_to(row, (ROW_BLOCK, WINDOW)), 0, 1, stride=1, stride_axis=0
    )


def diagonal_sums(values):
    total = values[:8]
    for a in range(1, ROW_BLOCK // 8):
        total = total + pltpu.roll(values[8 * a : 8 * a + 8], WINDOW - 8 * a, 1)
    row = lax.broadcasted_iota(jnp.int32, total.shape, 0)
    for bit in (1, 2, 4):
        total = jnp.where((row & bit) != 0, pltpu.roll(total, WINDOW - bit, 1), total)
    return jnp.sum(total, axis=0, keepdims=True)


def block_probs(query_rows, key_rows, bias):
    return score_probs(dot_nt(query_rows, key_rows), bias)


def score_probs(products, bias):
    scores = products * (HEAD_DIM ** (-0.5)) + bias
    weights = jnp.exp(scores - jnp.max(scores, axis=-1, keepdims=True))
    return weights * (1.0 / jnp.sum(weights, axis=-1, keepdims=True))


def forward_kernel(slots, group, meta_ref, before_ref, own_ref, after_ref, x_ref, offset_ref, *rest):
    slot_refs = rest[:slots]
    out_ref, weight_ref = rest[slots:]
    rows = own_ref.shape[0]
    blocks = rows // ROW_BLOCK
    masks = [key_mask(meta_ref, b * ROW_BLOCK) for b in range(blocks)]
    for g in range(group):
        columns = slice(g * HEAD_DIM, (g + 1) * HEAD_DIM)
        weight = load_weight(meta_ref, slot_refs, weight_ref, g, slots)
        own = own_ref[:, columns]
        extended = jnp.concatenate([before_ref[:, columns], own, after_ref[:, columns]], axis=0)
        query = dot_nn(own, weight[:, :HEAD_DIM]).astype(BF16)
        key_value = dot_nn(extended, weight[:, HEAD_DIM:]).astype(BF16)
        key, value = key_value[:, :HEAD_DIM], key_value[:, HEAD_DIM:]
        bias = toeplitz(offset_ref[g])
        for b in range(blocks):
            first = b * ROW_BLOCK
            window = slice(first, first + WINDOW)
            probs = block_probs(query[first : first + ROW_BLOCK], key[window], bias + masks[b])
            attended = dot_nn(probs.astype(BF16), value[window])
            kept = x_ref[first : first + ROW_BLOCK, columns].astype(F32)
            out_ref[first : first + ROW_BLOCK, columns] = (kept + attended).astype(BF16)


def column_spec(rows, group, first):
    return pl.BlockSpec((rows, group * HEAD_DIM), lambda i, meta: (0, i + first))


def slot_specs(weight_slots, group):
    return [
        pl.BlockSpec((3, group, slot.shape[2], HEAD_DIM), lambda i, meta: (0, i, 0, 0))
        for slot in weight_slots
    ]


def forward_attention(meta, before, own, after, x, offsets, weight_slots, group):
    rows, width = own.shape
    heads = width // HEAD_DIM
    slots = len(weight_slots)
    return pl.pallas_call(
        functools.partial(forward_kernel, slots, group),
        out_shape=jax.ShapeDtypeStruct((rows, width), BF16),
        grid_spec=pltpu.PrefetchScalarGridSpec(
            num_scalar_prefetch=1,
            grid=(heads // group,),
            in_specs=[
                column_spec(RADIUS, group, 0),
                column_spec(rows, group, 0),
                column_spec(RADIUS, group, 0),
                column_spec(rows, group, 0),
                pl.BlockSpec((group, 1, WINDOW), lambda i, meta: (i, 0, 0)),
                *slot_specs(weight_slots, group),
            ],
            out_specs=column_spec(rows, group, 0),
            scratch_shapes=[pltpu.VMEM((group, HEAD_DIM, 3 * HEAD_DIM), BF16)],
        ),
        compiler_params=pltpu.CompilerParams(vmem_limit_bytes=VMEM_LIMIT),
        cost_estimate=pl.CostEstimate(
            flops=heads * 60_000_000, bytes_accessed=8 * rows * width, transcendentals=heads * 32768
        ),
        name="forward_attention",
    )(meta, before, own, after, x, offsets, *weight_slots)


def backward_kernel(slots, group, meta_ref, before_ref, own_ref, after_ref, cot_ref, offset_ref, *rest):
    slot_refs = rest[:slots]
    rest = rest[slots:]
    grad_ref, lower_ref, upper_ref, offset_grad_ref = rest[:4]
    part_refs = rest[4 : 4 + slots]
    weight_ref, part_ref = rest[4 + slots :]
    rows = own_ref.shape[0]
    blocks = rows // ROW_BLOCK
    scale = HEAD_DIM ** (-0.5)
    masks = [key_mask(meta_ref, b * ROW_BLOCK) for b in range(blocks)]
    for g in range(group):
        columns = slice(g * HEAD_DIM, (g + 1) * HEAD_DIM)
        weight = load_weight(meta_ref, slot_refs, weight_ref, g, slots)
        own = own_ref[:, columns]
        extended = jnp.concatenate([before_ref[:, columns], own, after_ref[:, columns]], axis=0)
        query = dot_nn(own, weight[:, :HEAD_DIM]).astype(BF16)
        key_value = dot_nn(extended, weight[:, HEAD_DIM:]).astype(BF16)
        key, value = key_value[:, :HEAD_DIM], key_value[:, HEAD_DIM:]
        bias = toeplitz(offset_ref[g])
        grad_query, grad_key, grad_value, score_sum = [], [], [], None
        for b in range(blocks):
            first = b * ROW_BLOCK
            window = slice(first, first + WINDOW)
            query_rows = query[first : first + ROW_BLOCK]
            cot_rows = cot_ref[first : first + ROW_BLOCK, columns]
            probs = block_probs(query_rows, key[window], bias + masks[b])
            grad_probs = dot_nt(cot_rows, value[window])
            delta = jnp.sum(probs * grad_probs, axis=-1, keepdims=True)
            grad_scores = probs * (grad_probs - delta)
            score_sum = grad_scores if score_sum is None else score_sum + grad_scores
            grad_packed = grad_scores.astype(BF16)
            grad_query.append(dot_nn(grad_packed, key[window]))
            grad_key.append(dot_tn(grad_packed, query_rows))
            grad_value.append(dot_tn(probs.astype(BF16), cot_rows))

        def joined(parts):
            pieces = []
            for u in range((rows + 2 * RADIUS) // ROW_BLOCK):
                total = None
                for b in range(blocks):
                    if 0 <= u - b < WINDOW // ROW_BLOCK:
                        piece = parts[b][(u - b) * ROW_BLOCK : (u - b + 1) * ROW_BLOCK]
                        total = piece if total is None else total + piece
                pieces.append(total)
            return jnp.concatenate(pieces, axis=0)

        dquery = (jnp.concatenate(grad_query, axis=0) * scale).astype(BF16)
        dkey = (joined(grad_key) * scale).astype(BF16)
        dvalue = joined(grad_value).astype(BF16)
        dkey_value = jnp.concatenate([dkey, dvalue], axis=1)
        grad_extended = dot_nt(dkey_value, weight[:, HEAD_DIM:])
        grad_ref[:, columns] = grad_extended[RADIUS : RADIUS + rows] + dot_nt(dquery, weight[:, :HEAD_DIM])
        lower_ref[:, columns] = grad_extended[:RADIUS].astype(BF16)
        upper_ref[:, columns] = grad_extended[RADIUS + rows :].astype(BF16)
        part_ref[g, :, :HEAD_DIM] = dot_tn(own, dquery)
        part_ref[g, :, HEAD_DIM:] = dot_tn(extended, dkey_value)
        depth = HEAD_DIM // slots
        for r in range(slots):
            if slots == 1:
                start = 0
            else:
                start = pl.multiple_of(lax.rem(meta_ref[0] + r, slots) * depth, depth)
            for j in range(3):
                part_refs[r][j, g] = part_ref[
                    g, pl.ds(start, depth), j * HEAD_DIM : (j + 1) * HEAD_DIM
                ].astype(part_refs[r].dtype)
        offset_grad_ref[g] = diagonal_sums(score_sum)


def backward_attention(meta, before, own, after, cotangent, offsets, weight_slots, group, first_head, heads):
    rows = own.shape[0]
    width = heads * HEAD_DIM
    slots = len(weight_slots)
    first = first_head // group
    slot_shape = weight_slots[0].shape
    part_types = [F32] + [BF16] * (slots - 1) if slots > 1 else [BF16]
    return pl.pallas_call(
        functools.partial(backward_kernel, slots, group),
        out_shape=(
            jax.ShapeDtypeStruct((rows, width), F32),
            jax.ShapeDtypeStruct((RADIUS, width), BF16),
            jax.ShapeDtypeStruct((RADIUS, width), BF16),
            jax.ShapeDtypeStruct((heads, 1, WINDOW), F32),
            *[jax.ShapeDtypeStruct(slot_shape, kind) for kind in part_types],
        ),
        grid_spec=pltpu.PrefetchScalarGridSpec(
            num_scalar_prefetch=1,
            grid=(heads // group,),
            in_specs=[
                column_spec(RADIUS, group, first),
                column_spec(rows, group, first),
                column_spec(RADIUS, group, first),
                column_spec(rows, group, first),
                pl.BlockSpec((group, 1, WINDOW), lambda i, meta: (i + first, 0, 0)),
                *slot_specs(weight_slots, group),
            ],
            out_specs=(
                column_spec(rows, group, 0),
                column_spec(RADIUS, group, 0),
                column_spec(RADIUS, group, 0),
                pl.BlockSpec((group, 1, WINDOW), lambda i, meta: (i, 0, 0)),
                *slot_specs(weight_slots, group),
            ),
            scratch_shapes=[
                pltpu.VMEM((group, HEAD_DIM, 3 * HEAD_DIM), BF16),
                pltpu.VMEM((group, HEAD_DIM, 3 * HEAD_DIM), F32),
            ],
        ),
        compiler_params=pltpu.CompilerParams(vmem_limit_bytes=VMEM_LIMIT),
        cost_estimate=pl.CostEstimate(
            flops=heads * 150_000_000, bytes_accessed=12 * rows * width, transcendentals=heads * 32768
        ),
        name="backward_attention",
    )(meta, before, own, after, cotangent, offsets, *weight_slots)


def finish_kernel(grad_ref, low_ref, high_ref, x_ref, inverse_ref, gain_ref, cot_ref, out_ref, gain_grad_ref):
    rows = x_ref.shape[0]
    grad = grad_ref[...]
    edge = jnp.zeros((rows - RADIUS, grad.shape[1]), F32)
    grad = grad + jnp.concatenate([low_ref[...].astype(F32), edge], axis=0)
    grad = grad + jnp.concatenate([edge, high_ref[...].astype(F32)], axis=0)
    x = x_ref[...].astype(F32)
    inverse = inverse_ref[:, :1]
    gain_grad_ref[...] = jnp.sum(grad * x * inverse, axis=0, keepdims=True)
    scaled = grad * gain_ref[...]
    mean = jnp.mean(scaled * x, axis=-1, keepdims=True)
    result = inverse * scaled - x * (inverse * inverse * inverse * mean)
    out_ref[...] = (cot_ref[...].astype(F32) + result).astype(BF16)


def finish(grad, low, high, x, inverse, gain, cotangent):
    rows, width = x.shape
    return pl.pallas_call(
        finish_kernel,
        out_shape=(
            jax.ShapeDtypeStruct((rows, width), BF16),
            jax.ShapeDtypeStruct((1, width), F32),
        ),
        compiler_params=pltpu.CompilerParams(vmem_limit_bytes=VMEM_LIMIT),
        cost_estimate=pl.CostEstimate(
            flops=16 * rows * width, bytes_accessed=14 * rows * width, transcendentals=0
        ),
        name="finish",
    )(grad, low, high, x, inverse, gain, cotangent)


def column_of(row, rows):
    return jnp.transpose(jnp.broadcast_to(row, (128, rows)))


def split_rows(inverse, pad_rows, width):
    high = inverse.astype(BF16)
    rest = inverse - high.astype(F32)
    middle = rest.astype(BF16)
    low = (rest - middle.astype(F32)).astype(BF16)
    wide = [jnp.transpose(jnp.broadcast_to(v.astype(F32), (v.shape[0], 128)))[:1] for v in (high, middle, low)]
    row = jnp.concatenate(wide + [jnp.zeros((pad_rows - 3, wide[0].shape[1]), F32)], axis=0)
    return row.astype(BF16)


def row_inverse(x):
    x = x.astype(F32)
    return lax.rsqrt(jnp.mean(x * x, axis=-1, keepdims=True) + eps_norm)


def pack_stash_kernel(parts, pieces, x_hbm, gain_hbm, weight_hbm, inverse_ref, *refs):
    out_refs = refs[:parts]
    x_ref, gain_ref, weight_ref, normed_ref, sems = refs[parts:]
    rows, width = x_ref.shape
    depth = weight_ref.shape[2]
    wide = width // parts
    heads = wide // HEAD_DIM
    step = rows // pieces
    gain_copy = pltpu.make_async_copy(gain_hbm, gain_ref, sems.at[0])
    x_copies = [
        pltpu.make_async_copy(x_hbm.at[pl.ds(k * step, step)], x_ref.at[pl.ds(k * step, step)], sems.at[1 + k])
        for k in range(pieces)
    ]
    weight_copies = [
        pltpu.make_async_copy(weight_hbm.at[j], weight_ref.at[j], sems.at[1 + pieces + j]) for j in range(3)
    ]
    for copy in (gain_copy, *x_copies, *weight_copies):
        copy.start()
    gain_copy.wait()
    gain = gain_ref[...]
    for k, copy in enumerate(x_copies):
        copy.wait()
        part = slice(k * step, (k + 1) * step)
        inverse = row_inverse(x_ref[part])
        inverse_ref[part] = jnp.broadcast_to(inverse, (step, 128))
        normed_ref[part] = (x_ref[part].astype(F32) * inverse * gain).astype(BF16)
    for r, out_ref in enumerate(out_refs):
        target = lax.rem(lax.axis_index("seq") + r, parts)
        out_ref[:rows] = normed_ref[:, pl.ds(pl.multiple_of(target * wide, 128), wide)]
    for j, copy in enumerate(weight_copies):
        copy.wait()
        for r, out_ref in enumerate(out_refs):
            target = lax.rem(lax.axis_index("seq") + r, parts)
            for h in range(heads):
                out_ref[rows + j * depth : rows + (j + 1) * depth, h * HEAD_DIM : (h + 1) * HEAD_DIM] = weight_ref[
                    j, target * heads + h
                ]


def pack_rows_kernel(parts, with_inverse, meta_ref, edge_ref, inner_ref, *out_refs):
    rows, width = inner_ref.shape
    wide = width // parts
    edge = 1 if with_inverse else 2
    refs = out_refs[:parts]
    for r, out_ref in enumerate(refs):
        target = lax.rem(meta_ref[0] + r, parts)
        start = pl.multiple_of(target * wide, 128)

        @pl.when(meta_ref[edge] == 1)
        def use_edge():
            out_ref[:rows] = edge_ref[:, pl.ds(start, wide)]

        @pl.when(meta_ref[edge] == 0)
        def use_inner():
            out_ref[:rows] = inner_ref[:, pl.ds(start, wide)]

    def finish_with(source_ref):
        if with_inverse:
            tail = split_rows(row_inverse(source_ref[...]), EXTRA, wide)
            for out_ref in refs:
                out_ref[rows:] = jnp.zeros((EXTRA, wide), BF16)
                out_ref[rows:, :rows] = tail
        else:
            out_refs[parts][...] = source_ref[...]

    @pl.when(meta_ref[edge] == 1)
    def finish_edge():
        finish_with(edge_ref)

    @pl.when(meta_ref[edge] == 0)
    def finish_inner():
        finish_with(inner_ref)


SMEM_SPEC = pl.BlockSpec(memory_space=pltpu.SMEM)
VMEM_SPEC = pl.BlockSpec(memory_space=pltpu.VMEM)


def pack_stash(x, gain, weight, parts):
    rows, width = x.shape
    depth = weight.shape[2]
    shape = (rows + 3 * depth, width // parts)
    return pl.pallas_call(
        functools.partial(pack_stash_kernel, parts, 4),
        out_shape=(
            jax.ShapeDtypeStruct((rows, 128), F32),
            *[jax.ShapeDtypeStruct(shape, BF16) for r in range(parts)],
        ),
        in_specs=[pl.BlockSpec(memory_space=pl.ANY)] * 3,
        out_specs=(VMEM_SPEC,) * (parts + 1),
        scratch_shapes=[
            pltpu.VMEM((rows, width), BF16),
            pltpu.VMEM((1, width), F32),
            pltpu.VMEM(weight.shape, BF16),
            pltpu.VMEM((rows, width), BF16),
            pltpu.SemaphoreType.DMA((8,)),
        ],
        compiler_params=pltpu.CompilerParams(vmem_limit_bytes=58 * 1024 * 1024),
        cost_estimate=pl.CostEstimate(flops=4 * rows * width, bytes_accessed=6 * rows * width, transcendentals=0),
        name="pack_stash",
    )(x, gain, weight)


def pack_rows(meta, edge, inner, parts, with_inverse):
    rows, width = inner.shape
    shape = (rows + (EXTRA if with_inverse else 0), width // parts)
    extra = () if with_inverse else (jax.ShapeDtypeStruct((rows, width), BF16),)
    return pl.pallas_call(
        functools.partial(pack_rows_kernel, parts, with_inverse),
        out_shape=(*[jax.ShapeDtypeStruct(shape, BF16) for r in range(parts)], *extra),
        in_specs=[SMEM_SPEC, VMEM_SPEC, VMEM_SPEC],
        out_specs=(VMEM_SPEC,) * (parts + len(extra)),
        compiler_params=pltpu.CompilerParams(vmem_limit_bytes=VMEM_LIMIT),
        cost_estimate=pl.CostEstimate(flops=4 * rows * width, bytes_accessed=6 * rows * width, transcendentals=0),
        name="pack_inbound" if with_inverse else "pack_cotangent",
    )(meta, edge, inner)


def gather_rows(meta_ref, refs, rows, x_ref):
    parts = len(refs)
    for r, ref in enumerate(refs):
        source = lax.rem(meta_ref[0] + parts - r, parts)
        x_ref[pl.ds(pl.multiple_of(source * rows, rows), rows)] = ref[:rows]


def gather_weight(meta_ref, refs, rows, weight_ref):
    parts = len(refs)
    depth = HEAD_DIM // parts
    for r, ref in enumerate(refs):
        source = lax.rem(meta_ref[0] + parts - r, parts)
        depth_at = pl.ds(pl.multiple_of(source * depth, depth), depth)
        for j in range(3):
            weight_ref[depth_at, j * HEAD_DIM : (j + 1) * HEAD_DIM] = ref[
                rows + j * depth : rows + (j + 1) * depth
            ]


def gather_inverse(meta_ref, refs, rows, inverse_ref):
    parts = len(refs)

    @pl.when(pl.program_id(0) == 0)
    def spread_inverse():
        for r, ref in enumerate(refs):
            source = lax.rem(meta_ref[0] + parts - r, parts)
            tail = ref[rows : rows + EXTRA].astype(F32)
            inverse_ref[pl.ds(pl.multiple_of(source * rows, rows), rows)] = column_of(
                tail[:1] + tail[1:2] + tail[2:3], rows
            )


def block_mask(first_query, tokens):
    key = lax.broadcasted_iota(jnp.int32, (1, WINDOW), 1) + (first_query - RADIUS)
    return jnp.where((key >= 0) & (key < tokens), 0.0, masked_score).astype(F32)


def edge_bias(bias, first, tokens):
    if first < RADIUS or first + ROW_BLOCK + RADIUS > tokens:
        return bias + block_mask(first, tokens)
    return bias


def padded(rows):
    edge = jnp.zeros((RADIUS, rows.shape[1]), rows.dtype)
    return jnp.concatenate([edge, rows, edge], axis=0)


def heads_backward_kernel(parts, rows, meta_ref, *refs):
    a_refs, c_refs = refs[:parts], refs[parts : 2 * parts]
    gain_ref, offset_ref, onehot_ref, after_ref = refs[2 * parts : 2 * parts + 4]
    out_refs = refs[2 * parts + 4 : 3 * parts + 4]
    gain_grad_ref, x_ref, weight_ref, cot_ref, grad_ref, part_ref, bias_ref = refs[3 * parts + 4 :]
    tokens = rows * parts
    depth = HEAD_DIM // parts
    scale = HEAD_DIM ** (-0.5)
    gather_rows(meta_ref, a_refs, rows, x_ref)
    gather_weight(meta_ref, a_refs, rows, weight_ref)
    gather_rows(meta_ref, c_refs, rows, cot_ref)
    weight = weight_ref[...]
    normed = x_ref[...]
    query = dot_nn(normed, weight[:, :HEAD_DIM]).astype(BF16)
    key = padded(dot_nn(normed, weight[:, HEAD_DIM : 2 * HEAD_DIM]).astype(BF16))
    value = padded(dot_nn(normed, weight[:, 2 * HEAD_DIM :]).astype(BF16))
    bias = toeplitz(offset_ref[0])
    blocks = tokens // ROW_BLOCK
    starts = range(0, tokens, ROW_BLOCK)
    cot = cot_ref[...]
    query_rows = [query[f : f + ROW_BLOCK] for f in starts]
    cot_rows = [cot[f : f + ROW_BLOCK] for f in starts]
    products = [dot_nt(rows_q, key[f : f + WINDOW]) for f, rows_q in zip(starts, query_rows)]
    grad_probs = [dot_nt(rows_c, value[f : f + WINDOW]) for f, rows_c in zip(starts, cot_rows)]
    packed, grad_packed, score_sum = [], [], None
    for f, product, grads in zip(starts, products, grad_probs):
        probs = score_probs(product, edge_bias(bias, f, tokens))
        delta = jnp.sum(probs * grads, axis=-1, keepdims=True)
        grad_scores = probs * (grads - delta)
        score_sum = grad_scores if score_sum is None else score_sum + grad_scores
        packed.append(probs.astype(BF16))
        grad_packed.append(grad_scores.astype(BF16))
    grad_query = [dot_nn(part, key[f : f + WINDOW]) for f, part in zip(starts, grad_packed)]
    grad_key = [dot_tn(part, rows_q) for part, rows_q in zip(grad_packed, query_rows)]
    grad_value = [dot_tn(part, rows_c) for part, rows_c in zip(packed, cot_rows)]

    def joined(pieces):
        units = []
        for u in range((tokens + 2 * RADIUS) // ROW_BLOCK):
            total = None
            for b in range(blocks):
                if 0 <= u - b < WINDOW // ROW_BLOCK:
                    piece = pieces[b][(u - b) * ROW_BLOCK : (u - b + 1) * ROW_BLOCK]
                    total = piece if total is None else total + piece
            units.append(total)
        return jnp.concatenate(units, axis=0)[RADIUS : RADIUS + tokens]

    dqkv = jnp.concatenate(
        [
            (jnp.concatenate(grad_query, axis=0) * scale).astype(BF16),
            (joined(grad_key) * scale).astype(BF16),
            joined(grad_value).astype(BF16),
        ],
        axis=1,
    )
    grad_normed = dot_nt(dqkv, weight)
    gain_grad_ref[...] = jnp.sum(grad_normed * normed.astype(F32), axis=0, keepdims=True) / gain_ref[...]
    grad_ref[...] = grad_normed
    part_ref[...] = dot_tn(normed, dqkv)
    bias_grad = jnp.sum(onehot_ref[...] * diagonal_sums(score_sum), axis=1, keepdims=True)
    bias_ref[...] = jnp.broadcast_to(bias_grad, bias_ref.shape)
    buckets = bias_ref.shape[0] // parts
    for r, out_ref in enumerate(out_refs):
        source = lax.rem(meta_ref[0] + parts - r, parts)
        out_ref[:rows] = grad_ref[pl.ds(pl.multiple_of(source * rows, rows), rows)].astype(BF16)
        for j in range(3):
            out_ref[rows + j * depth : rows + (j + 1) * depth] = part_ref[
                pl.ds(pl.multiple_of(source * depth, depth), depth), j * HEAD_DIM : (j + 1) * HEAD_DIM
            ].astype(BF16)
        share = bias_ref[pl.ds(pl.multiple_of(source * buckets, buckets), buckets)]
        out_ref[rows + 3 * depth :] = share.astype(BF16)


def head_column(rows, first=0):
    return pl.BlockSpec((rows, HEAD_DIM), lambda i, meta: (0, i + first))


def whole_column(rows, heads, first=0):
    return pl.BlockSpec((rows, HEAD_DIM), lambda i, meta: (0, meta[0] * heads + first + i))


def offset_spec(heads, first=0):
    return pl.BlockSpec((1, 1, WINDOW), lambda i, meta: (meta[0] * heads + first + i, 0, 0))


def heads_backward(meta, a_slots, c_slots, gain, offsets, onehot, after, heads, first, count):
    parts = len(a_slots)
    rows = c_slots[0].shape[0]
    tokens = rows * parts
    buckets = onehot.shape[0]
    packed = a_slots[0].shape[0]
    made = packed + buckets // parts
    width = count * HEAD_DIM
    return pl.pallas_call(
        functools.partial(heads_backward_kernel, parts, rows),
        out_shape=(
            *[jax.ShapeDtypeStruct((made, width), BF16) for r in range(parts)],
            jax.ShapeDtypeStruct((1, width), F32),
        ),
        grid_spec=pltpu.PrefetchScalarGridSpec(
            num_scalar_prefetch=1,
            grid=(count,),
            in_specs=[
                *[head_column(packed, first)] * parts,
                whole_column(rows, heads, first),
                *[head_column(rows, first)] * (parts - 1),
                whole_column(1, heads, first),
                offset_spec(heads, first),
                pl.BlockSpec((buckets, WINDOW), lambda i, meta: (0, 0)),
                pl.BlockSpec(memory_space=pl.ANY),
            ],
            out_specs=(*[head_column(made)] * parts, head_column(1)),
            scratch_shapes=[
                pltpu.VMEM((tokens, HEAD_DIM), BF16),
                pltpu.VMEM((HEAD_DIM, 3 * HEAD_DIM), BF16),
                pltpu.VMEM((tokens, HEAD_DIM), BF16),
                pltpu.VMEM((tokens, HEAD_DIM), F32),
                pltpu.VMEM((HEAD_DIM, 3 * HEAD_DIM), F32),
                pltpu.VMEM((buckets, HEAD_DIM), F32),
            ],
        ),
        compiler_params=pltpu.CompilerParams(vmem_limit_bytes=VMEM_LIMIT),
        cost_estimate=pl.CostEstimate(
            flops=count * tokens * 400_000, bytes_accessed=tokens * width, transcendentals=0
        ),
        name="heads_backward",
    )(meta, *a_slots, *c_slots, gain, offsets, onehot, after)


def heads_forward_kernel(parts, rows, meta_ref, *refs):
    a_refs, i_refs = refs[:parts], refs[parts : 2 * parts]
    gain_ref, offset_ref = refs[2 * parts : 2 * parts + 2]
    out_refs = refs[2 * parts + 2 : 3 * parts + 2]
    inverse_ref, x_ref, weight_ref, made_ref, square_ref = refs[3 * parts + 2 :]
    tokens = rows * parts
    gather_rows(meta_ref, i_refs, rows, x_ref)
    gather_weight(meta_ref, a_refs, rows, weight_ref)
    gather_inverse(meta_ref, i_refs, rows, inverse_ref)
    weight = weight_ref[...]
    normed = (x_ref[...].astype(F32) * inverse_ref[...] * gain_ref[...]).astype(BF16)
    query = dot_nn(normed, weight[:, :HEAD_DIM]).astype(BF16)
    key = padded(dot_nn(normed, weight[:, HEAD_DIM : 2 * HEAD_DIM]).astype(BF16))
    value = padded(dot_nn(normed, weight[:, 2 * HEAD_DIM :]).astype(BF16))
    bias = toeplitz(offset_ref[0])
    starts = range(0, tokens, ROW_BLOCK)
    products = [dot_nt(query[f : f + ROW_BLOCK], key[f : f + WINDOW]) for f in starts]
    packed = [
        score_probs(product, edge_bias(bias, f, tokens)).astype(BF16) for f, product in zip(starts, products)
    ]
    attended = [dot_nn(part, value[f : f + WINDOW]) for f, part in zip(starts, packed)]
    for f, part in zip(starts, attended):
        made_ref[f : f + ROW_BLOCK] = (x_ref[f : f + ROW_BLOCK].astype(F32) + part).astype(BF16)
    made = made_ref[...].astype(F32)
    squares = made * made

    @pl.when(pl.program_id(0) == 0)
    def first_head():
        square_ref[...] = squares

    @pl.when(pl.program_id(0) > 0)
    def later_head():
        square_ref[...] += squares

    for r, out_ref in enumerate(out_refs):
        source = lax.rem(meta_ref[0] + parts - r, parts)
        out_ref[:rows] = made_ref[pl.ds(pl.multiple_of(source * rows, rows), rows)]

    @pl.when(pl.program_id(0) < pl.num_programs(0) - 1)
    def no_sums():
        for out_ref in out_refs:
            out_ref[rows:] = jnp.zeros((EXTRA, HEAD_DIM), BF16)

    @pl.when(pl.program_id(0) == pl.num_programs(0) - 1)
    def last_head():
        rest = jnp.sum(jnp.transpose(square_ref[...]), axis=0, keepdims=True)
        at_row = lax.broadcasted_iota(jnp.int32, (EXTRA, rows), 0)
        tail = jnp.zeros((EXTRA, rows), F32)
        for k in range(2):
            piece = rest.astype(BF16).astype(F32)
            rest = rest - piece
            for part in range(parts):
                row = jnp.broadcast_to(piece[:, part * rows : (part + 1) * rows], (EXTRA, rows))
                tail = jnp.where(at_row == 2 * part + k, row, tail)
        for out_ref in out_refs:
            out_ref[rows:] = tail.astype(BF16)


def heads_forward(meta, a_slots, i_slots, gain, offsets, heads, rows):
    parts = len(a_slots)
    tokens = rows * parts
    packed = a_slots[0].shape[0]
    width = heads * HEAD_DIM
    return pl.pallas_call(
        functools.partial(heads_forward_kernel, parts, rows),
        out_shape=(
            *[jax.ShapeDtypeStruct((rows + EXTRA, width), BF16) for r in range(parts)],
        ),
        grid_spec=pltpu.PrefetchScalarGridSpec(
            num_scalar_prefetch=1,
            grid=(heads,),
            in_specs=[
                *[head_column(packed)] * parts,
                *[head_column(i_slots[0].shape[0])] * parts,
                whole_column(1, heads),
                offset_spec(heads),
            ],
            out_specs=(head_column(rows + EXTRA),) * parts,
            scratch_shapes=[
                pltpu.VMEM((tokens, HEAD_DIM), F32),
                pltpu.VMEM((tokens, HEAD_DIM), BF16),
                pltpu.VMEM((HEAD_DIM, 3 * HEAD_DIM), BF16),
                pltpu.VMEM((tokens, HEAD_DIM), BF16),
                pltpu.VMEM((tokens, HEAD_DIM), F32),
            ],
        ),
        compiler_params=pltpu.CompilerParams(vmem_limit_bytes=VMEM_LIMIT),
        cost_estimate=pl.CostEstimate(
            flops=heads * tokens, bytes_accessed=tokens, transcendentals=0
        ),
        name="heads_forward",
    )(meta, *a_slots, *i_slots, gain, offsets)


def memory_kernel(parts, width, meta_ref, *refs):
    out_refs, other_refs = refs[:parts], refs[parts : 2 * parts - 1]
    gain_ref, *share_refs, memory_ref = refs[2 * parts - 1 :]
    wide = memory_ref.shape[1]
    rows = memory_ref.shape[0] // parts
    total = None
    for ref in (out_refs[0], *other_refs):
        tail = ref[rows:, wide - rows :].astype(F32)
        pieces = [tail[2 * p : 2 * p + 1] + tail[2 * p + 1 : 2 * p + 2] for p in range(parts)]
        row = jnp.concatenate(pieces, axis=1)
        total = row if total is None else total + row
    inverse = lax.rsqrt(total / width + eps_norm)
    gain = gain_ref[:, pl.ds(pl.multiple_of(meta_ref[0] * wide, 128), wide)]
    spread_inverse = jnp.transpose(jnp.broadcast_to(inverse, (128, inverse.shape[1])))
    for r, out_ref in enumerate(out_refs):
        source = lax.rem(meta_ref[0] + parts - r, parts)
        memory_ref[pl.ds(pl.multiple_of(source * rows, rows), rows)] = out_ref[:rows]
    made = memory_ref[...].astype(F32)
    memory_ref[...] = (made * spread_inverse[:, :1] * gain).astype(BF16)
    for k, share_ref in enumerate(share_refs):
        size = share_ref.shape[0]
        share_ref[...] = memory_ref[k * size : (k + 1) * size]


def memory_rows(meta, outs, others, gain, width, shares):
    parts = len(outs)
    rows, wide = outs[0].shape[0] - EXTRA, outs[0].shape[1]
    return pl.pallas_call(
        functools.partial(memory_kernel, parts, width),
        out_shape=[jax.ShapeDtypeStruct((rows * parts // shares, wide), BF16)] * shares,
        in_specs=[SMEM_SPEC] + [VMEM_SPEC] * (2 * parts),
        out_specs=[VMEM_SPEC] * shares,
        scratch_shapes=[pltpu.VMEM((rows * parts, wide), BF16)],
        compiler_params=pltpu.CompilerParams(vmem_limit_bytes=VMEM_LIMIT),
        cost_estimate=pl.CostEstimate(flops=rows, bytes_accessed=rows, transcendentals=0),
        name="memory_rows",
    )(meta, *outs, *others, gain)


def place_kernel(parts, meta_ref, *refs):
    out_ref = refs[parts]
    wide = refs[0].shape[1]
    for r in range(parts):
        source = lax.rem(meta_ref[0] + r, parts)
        out_ref[:, pl.ds(pl.multiple_of(source * wide, 128), wide)] = refs[r][: out_ref.shape[0]]


def place_columns(meta, slots):
    parts = len(slots)
    rows, wide = slots[0].shape[0] - EXTRA, slots[0].shape[1]
    return pl.pallas_call(
        functools.partial(place_kernel, parts),
        out_shape=jax.ShapeDtypeStruct((rows, wide * parts), BF16),
        in_specs=[SMEM_SPEC] + [VMEM_SPEC] * parts,
        out_specs=VMEM_SPEC,
        compiler_params=pltpu.CompilerParams(vmem_limit_bytes=VMEM_LIMIT),
        cost_estimate=pl.CostEstimate(flops=0, bytes_accessed=rows, transcendentals=0),
        name="place_columns",
    )(meta, *slots)


def heads_finish_kernel(parts, meta_ref, *refs):
    g_refs = refs[:parts]
    x_ref, inverse_ref, gain_ref, cot_ref, out_ref, weight_hbm, bias_ref, scaled_ref, weight_ref, sem = refs[parts:]
    rows, width = x_ref.shape
    wide = width // parts
    heads = wide // HEAD_DIM
    depth = HEAD_DIM // parts
    for r in range(parts):
        source = lax.rem(meta_ref[0] + r, parts)
        for h in range(heads):
            for j in range(3):
                weight_ref[j, source * heads + h] = g_refs[r][
                    rows + j * depth : rows + (j + 1) * depth, h * HEAD_DIM : (h + 1) * HEAD_DIM
                ].astype(F32)
    weight_copy = pltpu.make_async_copy(weight_ref, weight_hbm, sem)
    weight_copy.start()
    lane = lax.broadcasted_iota(jnp.int32, (bias_ref.shape[0], HEAD_DIM), 1)
    bias = jnp.zeros(lane.shape, F32)
    for r in range(parts):
        source = lax.rem(meta_ref[0] + r, parts)
        columns = pl.ds(pl.multiple_of(source * wide, 128), wide)
        scaled_ref[:, columns] = g_refs[r][:rows].astype(F32) * gain_ref[:, columns]
        shares = g_refs[r][rows + 3 * depth :].astype(F32)
        for h in range(heads):
            bias = jnp.where(lane == source * heads + h, shares[:, h * HEAD_DIM : (h + 1) * HEAD_DIM], bias)
    bias_ref[...] = bias[:, : bias_ref.shape[1]]
    x = x_ref[...].astype(F32)
    scaled = scaled_ref[...]
    inverse = inverse_ref[:, :1]
    mean = jnp.mean(scaled * x, axis=-1, keepdims=True)
    result = inverse * scaled - x * (inverse * inverse * inverse * mean)
    out_ref[...] = (cot_ref[...].astype(F32) + result).astype(BF16)
    weight_copy.wait()


def heads_finish(meta, g_slots, x, inverse, gain, cotangent, buckets):
    parts = len(g_slots)
    rows, width = x.shape
    heads = width // HEAD_DIM
    weight_shape = (3, heads, HEAD_DIM // parts, HEAD_DIM)
    return pl.pallas_call(
        functools.partial(heads_finish_kernel, parts),
        out_shape=(
            jax.ShapeDtypeStruct((rows, width), BF16),
            jax.ShapeDtypeStruct(weight_shape, F32),
            jax.ShapeDtypeStruct((buckets // parts, heads), F32),
        ),
        in_specs=[SMEM_SPEC] + [VMEM_SPEC] * (parts + 4),
        out_specs=(VMEM_SPEC, pl.BlockSpec(memory_space=pl.ANY), VMEM_SPEC),
        scratch_shapes=[
            pltpu.VMEM((rows, width), F32),
            pltpu.VMEM(weight_shape, F32),
            pltpu.SemaphoreType.DMA,
        ],
        compiler_params=pltpu.CompilerParams(vmem_limit_bytes=VMEM_LIMIT),
        cost_estimate=pl.CostEstimate(flops=12 * rows * width, bytes_accessed=14 * rows * width, transcendentals=0),
        name="heads_finish",
    )(meta, *g_slots, x, inverse, gain, cotangent)


def offset_table(rel_bias):
    onehot = jnp.asarray(bucket_onehot(rel_bias.shape[0]))
    by_offset = jnp.dot(onehot, rel_bias, precision=lax.Precision.HIGHEST).T
    inside = jnp.arange(WINDOW, dtype=jnp.int32) <= 2 * RADIUS
    return jnp.where(inside[None, :], by_offset, masked_score)[:, None, :]


def shifted(value, axis, steps):
    count = lax.axis_size(axis)
    first, last = (max(0, -steps), min(count, count - steps))
    return lax.ppermute(value, axis, [(source, source + steps) for source in range(first, last)])


def spread_memory(shares, section, sections):
    last = sections - 1
    couple = jnp.where(section == last, shares[-1], 0)
    for s, share in enumerate(shares[:-1]):
        couple = couple + lax.ppermute(share, "section", [(last, 2 * s + 1)])
    half = couple.shape[0] // 2
    even = lax.ppermute(couple[:half], "section", [(s + 1, s) for s in range(0, sections, 2)])
    return jnp.where(section % 2 == 0, even, couple[half:])


def heads_body(
    embedded, carried, stash, returned, loss_grad, qkv_weight, rel_bias, norm_gain, final_gain
):
    section = lax.axis_index("section")
    sections = lax.axis_size("section")
    parts = lax.axis_size("seq")
    rows, width = embedded.shape
    heads = width // HEAD_DIM // parts
    buckets = rel_bias.shape[1]
    meta = jnp.stack(
        [lax.axis_index("seq"), section == 0, section == sections - 1]
    ).astype(jnp.int32)

    def exchanged(sends, direction):
        moved = [
            lax.ppermute(sends[r], "seq", [(i, (i + direction * r) % parts) for i in range(parts)])
            for r in range(1, parts)
        ]
        return [sends[0]] + moved

    inverse_b, *a_sends = pack_stash(stash[0], norm_gain, qkv_weight[0], parts)
    a_slots = exchanged(a_sends, 1)
    arrived = shifted(carried[0], "section", 1)
    came_back = shifted(returned[0], "section", -1)
    i_slots = exchanged(pack_rows(meta, embedded, arrived, parts, True), 1)
    *c_sends, cotangent = pack_rows(meta, loss_grad, came_back, parts, False)
    c_slots = exchanged(c_sends, 1)
    c_slots[0] = cotangent

    offsets = offset_table(rel_bias[0])
    onehot = jnp.asarray(bucket_onehot(buckets).T)
    o_sends = heads_forward(meta, a_slots, i_slots, norm_gain, offsets, heads, rows)
    o_slots = exchanged(o_sends, -1)

    *g_sends, gain_grad = heads_backward(
        meta, a_slots, c_slots, norm_gain, offsets, onehot, o_sends[0], heads, 0, heads
    )
    g_sends, o_slots = lax.optimization_barrier((g_sends, o_slots))
    g_slots = exchanged(g_sends, -1)
    output = place_columns(meta, o_slots)
    shares = memory_rows(meta, o_sends, o_slots[1:], final_gain[None], width, sections // 2)
    memory = spread_memory(shares, section, sections)

    input_grad, weight_grad, bias_grad = heads_finish(
        meta, g_slots, stash[0], inverse_b, norm_gain, cotangent, buckets
    )
    return (
        output[None],
        input_grad[None],
        weight_grad[None],
        bias_grad[None],
        gain_grad,
        memory,
    )


def tokens_body(
    embedded, carried, stash, returned, loss_grad, qkv_weight, rel_bias, norm_gain, final_gain
):
    section_index = lax.axis_index("section")
    section_count = lax.axis_size("section")
    seq_index = lax.axis_index("seq")
    seq_count = lax.axis_size("seq")
    rows, width = embedded.shape
    heads = width // HEAD_DIM
    tokens = rows * seq_count
    shard = qkv_weight[0]
    up = [(i, i + 1) for i in range(seq_count - 1)]
    down = [(j, i) for i, j in up]
    group = 4 if heads % 4 == 0 else 1

    own_b, inverse_b = norm_rows(stash[0], norm_gain)
    before_b = lax.ppermute(own_b[rows - RADIUS :], "seq", up)
    after_b = lax.ppermute(own_b[:RADIUS], "seq", down)
    slots = [lax.all_gather(shard, "seq", axis=2, tiled=True)]

    section_up = [(i, (i + 1) % section_count) for i in range(section_count)]
    section_down = [(j, i) for i, j in section_up]
    inbound = lax.ppermute(
        jnp.where(section_index == section_count - 1, embedded, carried[0]), "section", section_up
    )
    cotangent = lax.ppermute(
        jnp.where(section_index == 0, loss_grad, returned[0]), "section", section_down
    )

    onehot = jnp.asarray(bucket_onehot(rel_bias.shape[1]))
    offsets = offset_table(rel_bias[0])
    first_key = RADIUS - seq_index * rows
    meta = jnp.stack([seq_index, first_key, first_key + tokens]).astype(jnp.int32)

    own_a, unused = norm_rows(inbound, norm_gain)
    before_a = lax.ppermute(own_a[rows - RADIUS :], "seq", up)
    after_a = lax.ppermute(own_a[:RADIUS], "seq", down)

    grad_own, lower, upper, offset_grad, *parts = backward_attention(
        meta, before_b, own_b, after_b, cotangent, offsets, slots, group, 0, heads
    )
    from_before = lax.ppermute(upper, "seq", up)
    from_after = lax.ppermute(lower, "seq", down)
    weight_sum = lax.psum_scatter(parts[0], "seq", scatter_dimension=2, tiled=True).astype(F32)

    output = forward_attention(meta, before_a, own_a, after_a, inbound, offsets, slots, group)
    final_normed, unused = norm_rows(output, final_gain[None])
    relaid = lax.all_to_all(final_normed, "seq", split_axis=1, concat_axis=0, tiled=True)
    kept = jnp.where(section_index == section_count - 1, relaid, jnp.zeros_like(relaid))
    memory = lax.psum_scatter(kept, "section", scatter_dimension=0, tiled=True)

    input_grad, gain_part = finish(
        grad_own, from_before, from_after, stash[0], inverse_b, norm_gain, cotangent
    )
    bias_part = jnp.dot(
        offset_grad[:, 0, :], onehot, precision=lax.Precision.HIGHEST
    ).T
    bias_sum = lax.psum_scatter(
        bias_part.astype(BF16), "seq", scatter_dimension=0, tiled=True
    ).astype(F32)
    gain_sum = lax.psum_scatter(
        gain_part.astype(BF16), "seq", scatter_dimension=1, tiled=True
    ).astype(F32)
    return (output[None], input_grad[None], weight_sum[None], bias_sum[None], gain_sum, memory)


def choose_body(embedded, carried, stash, returned, loss_grad, qkv_weight, rel_bias, norm_gain, final_gain):
    parts = lax.axis_size("seq")
    rows, width = embedded.shape
    even = width % (HEAD_DIM * parts) == 0 and HEAD_DIM % (32 * parts) == 0 and rows == 128
    sections = lax.axis_size("section")
    even = even and sections % 2 == 0
    even = even and rel_bias.shape[1] == 8 * parts and width <= 128 * HEAD_DIM and rows * parts % (16 * sections) == 0
    chosen = heads_body if even else tokens_body
    return chosen(
        embedded, carried, stash, returned, loss_grad, qkv_weight, rel_bias, norm_gain, final_gain
    )


def solution(mesh):
    in_specs = (
        P("seq", None),
        P("section", "seq", None),
        P("section", "seq", None),
        P("section", "seq", None),
        P("seq", None),
        P("section", None, None, "seq", None),
        P("section", None, None),
        P("section", None),
        P(),
    )
    out_specs = (
        P("section", "seq", None),
        P("section", "seq", None),
        P("section", None, None, "seq", None),
        P("section", "seq", None),
        P("section", "seq"),
        P("section", "seq"),
    )
    return jax.shard_map(choose_body, mesh=mesh, in_specs=in_specs, out_specs=out_specs, check_vma=False)
```

```python
import functools

import jax
import jax.numpy as jnp
import numpy as np
from jax import lax
from jax.experimental import pallas as pl
from jax.experimental.pallas import tpu as pltpu
from jax.sharding import PartitionSpec as P

RADIUS = 96
HEAD_DIM = 128
ROW_BLOCK = 64
WINDOW = ROW_BLOCK + 2 * RADIUS
eps_norm = 1e-06
bucket_edges = (1, 2, 3, 4, 5, 6, 7, 8, 11, 16, 22, 32, 45, 64, 90)
masked_score = -1e30
F32 = jnp.float32
BF16 = jnp.bfloat16
VMEM_LIMIT = 24 * 1024 * 1024
EXTRA = 8


def bucket_onehot(bucket_count):
    offsets = np.arange(WINDOW) - RADIUS
    magnitude = np.abs(offsets)
    counted = np.zeros(offsets.shape, np.int32)
    for threshold in bucket_edges:
        counted = counted + (magnitude >= threshold)
    counted = counted + 16 * (offsets > 0)
    onehot = (counted[:, None] == np.arange(bucket_count)[None, :]) & (magnitude <= RADIUS)[:, None]
    return onehot.astype(np.float32)


def dot_nn(a, b):
    return lax.dot_general(a, b, (((1,), (0,)), ((), ())), preferred_element_type=F32)


def dot_nt(a, b):
    return lax.dot_general(a, b, (((1,), (1,)), ((), ())), preferred_element_type=F32)


def dot_tn(a, b):
    return lax.dot_general(a, b, (((0,), (0,)), ((), ())), preferred_element_type=F32)


def norm_kernel(x_ref, gain_ref, normed_ref, inverse_ref):
    x = x_ref[...].astype(F32)
    inverse = lax.rsqrt(jnp.mean(x * x, axis=-1, keepdims=True) + eps_norm)
    normed_ref[...] = (x * inverse * gain_ref[...]).astype(BF16)
    inverse_ref[...] = jnp.broadcast_to(inverse, inverse_ref.shape)


def norm_rows(x, gain):
    rows, width = x.shape
    return pl.pallas_call(
        norm_kernel,
        out_shape=(
            jax.ShapeDtypeStruct((rows, width), BF16),
            jax.ShapeDtypeStruct((rows, 128), F32),
        ),
        compiler_params=pltpu.CompilerParams(vmem_limit_bytes=VMEM_LIMIT),
        cost_estimate=pl.CostEstimate(
            flops=6 * rows * width, bytes_accessed=4 * rows * width, transcendentals=rows
        ),
        name="norm_rows",
    )(x, gain)


def load_weight(meta_ref, slot_refs, weight_ref, head, slots):
    depth = HEAD_DIM // slots
    for r, slot_ref in enumerate(slot_refs):
        if slots == 1:
            start = 0
        else:
            start = pl.multiple_of(lax.rem(meta_ref[0] + r, slots) * depth, depth)
        for j in range(3):
            weight_ref[head, pl.ds(start, depth), j * HEAD_DIM : (j + 1) * HEAD_DIM] = slot_ref[j, head]
    return weight_ref[head]


def key_mask(meta_ref, first_key):
    key = lax.broadcasted_iota(jnp.int32, (1, WINDOW), 1) + first_key
    inside = (key >= meta_ref[1]) & (key < meta_ref[2])
    return jnp.where(inside, 0.0, masked_score).astype(F32)


def toeplitz(row):
    return pltpu.roll(
        jnp.broadcast_to(row, (ROW_BLOCK, WINDOW)), 0, 1, stride=1, stride_axis=0
    )


def diagonal_sums(values):
    total = values[:8]
    for a in range(1, ROW_BLOCK // 8):
        total = total + pltpu.roll(values[8 * a : 8 * a + 8], WINDOW - 8 * a, 1)
    row = lax.broadcasted_iota(jnp.int32, total.shape, 0)
    for bit in (1, 2, 4):
        total = jnp.where((row & bit) != 0, pltpu.roll(total, WINDOW - bit, 1), total)
    return jnp.sum(total, axis=0, keepdims=True)


def block_probs(query_rows, key_rows, bias):
    return score_probs(dot_nt(query_rows, key_rows), bias)


def score_probs(products, bias):
    scores = products * (HEAD_DIM ** (-0.5)) + bias
    weights = jnp.exp(scores - jnp.max(scores, axis=-1, keepdims=True))
    return weights * (1.0 / jnp.sum(weights, axis=-1, keepdims=True))


def forward_kernel(slots, group, meta_ref, before_ref, own_ref, after_ref, x_ref, offset_ref, *rest):
    slot_refs = rest[:slots]
    out_ref, weight_ref = rest[slots:]
    rows = own_ref.shape[0]
    blocks = rows // ROW_BLOCK
    masks = [key_mask(meta_ref, b * ROW_BLOCK) for b in range(blocks)]
    for g in range(group):
        columns = slice(g * HEAD_DIM, (g + 1) * HEAD_DIM)
        weight = load_weight(meta_ref, slot_refs, weight_ref, g, slots)
        own = own_ref[:, columns]
        extended = jnp.concatenate([before_ref[:, columns], own, after_ref[:, columns]], axis=0)
        query = dot_nn(own, weight[:, :HEAD_DIM]).astype(BF16)
        key_value = dot_nn(extended, weight[:, HEAD_DIM:]).astype(BF16)
        key, value = key_value[:, :HEAD_DIM], key_value[:, HEAD_DIM:]
        bias = toeplitz(offset_ref[g])
        for b in range(blocks):
            first = b * ROW_BLOCK
            window = slice(first, first + WINDOW)
            probs = block_probs(query[first : first + ROW_BLOCK], key[window], bias + masks[b])
            attended = dot_nn(probs.astype(BF16), value[window])
            kept = x_ref[first : first + ROW_BLOCK, columns].astype(F32)
            out_ref[first : first + ROW_BLOCK, columns] = (kept + attended).astype(BF16)


def column_spec(rows, group, first):
    return pl.BlockSpec((rows, group * HEAD_DIM), lambda i, meta: (0, i + first))


def slot_specs(weight_slots, group):
    return [
        pl.BlockSpec((3, group, slot.shape[2], HEAD_DIM), lambda i, meta: (0, i, 0, 0))
        for slot in weight_slots
    ]


def forward_attention(meta, before, own, after, x, offsets, weight_slots, group):
    rows, width = own.shape
    heads = width // HEAD_DIM
    slots = len(weight_slots)
    return pl.pallas_call(
        functools.partial(forward_kernel, slots, group),
        out_shape=jax.ShapeDtypeStruct((rows, width), BF16),
        grid_spec=pltpu.PrefetchScalarGridSpec(
            num_scalar_prefetch=1,
            grid=(heads // group,),
            in_specs=[
                column_spec(RADIUS, group, 0),
                column_spec(rows, group, 0),
                column_spec(RADIUS, group, 0),
                column_spec(rows, group, 0),
                pl.BlockSpec((group, 1, WINDOW), lambda i, meta: (i, 0, 0)),
                *slot_specs(weight_slots, group),
            ],
            out_specs=column_spec(rows, group, 0),
            scratch_shapes=[pltpu.VMEM((group, HEAD_DIM, 3 * HEAD_DIM), BF16)],
        ),
        compiler_params=pltpu.CompilerParams(vmem_limit_bytes=VMEM_LIMIT),
        cost_estimate=pl.CostEstimate(
            flops=heads * 60_000_000, bytes_accessed=8 * rows * width, transcendentals=heads * 32768
        ),
        name="forward_attention",
    )(meta, before, own, after, x, offsets, *weight_slots)


def backward_kernel(slots, group, meta_ref, before_ref, own_ref, after_ref, cot_ref, offset_ref, *rest):
    slot_refs = rest[:slots]
    rest = rest[slots:]
    grad_ref, lower_ref, upper_ref, offset_grad_ref = rest[:4]
    part_refs = rest[4 : 4 + slots]
    weight_ref, part_ref = rest[4 + slots :]
    rows = own_ref.shape[0]
    blocks = rows // ROW_BLOCK
    scale = HEAD_DIM ** (-0.5)
    masks = [key_mask(meta_ref, b * ROW_BLOCK) for b in range(blocks)]
    for g in range(group):
        columns = slice(g * HEAD_DIM, (g + 1) * HEAD_DIM)
        weight = load_weight(meta_ref, slot_refs, weight_ref, g, slots)
        own = own_ref[:, columns]
        extended = jnp.concatenate([before_ref[:, columns], own, after_ref[:, columns]], axis=0)
        query = dot_nn(own, weight[:, :HEAD_DIM]).astype(BF16)
        key_value = dot_nn(extended, weight[:, HEAD_DIM:]).astype(BF16)
        key, value = key_value[:, :HEAD_DIM], key_value[:, HEAD_DIM:]
        bias = toeplitz(offset_ref[g])
        grad_query, grad_key, grad_value, score_sum = [], [], [], None
        for b in range(blocks):
            first = b * ROW_BLOCK
            window = slice(first, first + WINDOW)
            query_rows = query[first : first + ROW_BLOCK]
            cot_rows = cot_ref[first : first + ROW_BLOCK, columns]
            probs = block_probs(query_rows, key[window], bias + masks[b])
            grad_probs = dot_nt(cot_rows, value[window])
            delta = jnp.sum(probs * grad_probs, axis=-1, keepdims=True)
            grad_scores = probs * (grad_probs - delta)
            score_sum = grad_scores if score_sum is None else score_sum + grad_scores
            grad_packed = grad_scores.astype(BF16)
            grad_query.append(dot_nn(grad_packed, key[window]))
            grad_key.append(dot_tn(grad_packed, query_rows))
            grad_value.append(dot_tn(probs.astype(BF16), cot_rows))

        def joined(parts):
            pieces = []
            for u in range((rows + 2 * RADIUS) // ROW_BLOCK):
                total = None
                for b in range(blocks):
                    if 0 <= u - b < WINDOW // ROW_BLOCK:
                        piece = parts[b][(u - b) * ROW_BLOCK : (u - b + 1) * ROW_BLOCK]
                        total = piece if total is None else total + piece
                pieces.append(total)
            return jnp.concatenate(pieces, axis=0)

        dquery = (jnp.concatenate(grad_query, axis=0) * scale).astype(BF16)
        dkey = (joined(grad_key) * scale).astype(BF16)
        dvalue = joined(grad_value).astype(BF16)
        dkey_value = jnp.concatenate([dkey, dvalue], axis=1)
        grad_extended = dot_nt(dkey_value, weight[:, HEAD_DIM:])
        grad_ref[:, columns] = grad_extended[RADIUS : RADIUS + rows] + dot_nt(dquery, weight[:, :HEAD_DIM])
        lower_ref[:, columns] = grad_extended[:RADIUS].astype(BF16)
        upper_ref[:, columns] = grad_extended[RADIUS + rows :].astype(BF16)
        part_ref[g, :, :HEAD_DIM] = dot_tn(own, dquery)
        part_ref[g, :, HEAD_DIM:] = dot_tn(extended, dkey_value)
        depth = HEAD_DIM // slots
        for r in range(slots):
            if slots == 1:
                start = 0
            else:
                start = pl.multiple_of(lax.rem(meta_ref[0] + r, slots) * depth, depth)
            for j in range(3):
                part_refs[r][j, g] = part_ref[
                    g, pl.ds(start, depth), j * HEAD_DIM : (j + 1) * HEAD_DIM
                ].astype(part_refs[r].dtype)
        offset_grad_ref[g] = diagonal_sums(score_sum)


def backward_attention(meta, before, own, after, cotangent, offsets, weight_slots, group, first_head, heads):
    rows = own.shape[0]
    width = heads * HEAD_DIM
    slots = len(weight_slots)
    first = first_head // group
    slot_shape = weight_slots[0].shape
    part_types = [F32] + [BF16] * (slots - 1) if slots > 1 else [BF16]
    return pl.pallas_call(
        functools.partial(backward_kernel, slots, group),
        out_shape=(
            jax.ShapeDtypeStruct((rows, width), F32),
            jax.ShapeDtypeStruct((RADIUS, width), BF16),
            jax.ShapeDtypeStruct((RADIUS, width), BF16),
            jax.ShapeDtypeStruct((heads, 1, WINDOW), F32),
            *[jax.ShapeDtypeStruct(slot_shape, kind) for kind in part_types],
        ),
        grid_spec=pltpu.PrefetchScalarGridSpec(
            num_scalar_prefetch=1,
            grid=(heads // group,),
            in_specs=[
                column_spec(RADIUS, group, first),
                column_spec(rows, group, first),
                column_spec(RADIUS, group, first),
                column_spec(rows, group, first),
                pl.BlockSpec((group, 1, WINDOW), lambda i, meta: (i + first, 0, 0)),
                *slot_specs(weight_slots, group),
            ],
            out_specs=(
                column_spec(rows, group, 0),
                column_spec(RADIUS, group, 0),
                column_spec(RADIUS, group, 0),
                pl.BlockSpec((group, 1, WINDOW), lambda i, meta: (i, 0, 0)),
                *slot_specs(weight_slots, group),
            ),
            scratch_shapes=[
                pltpu.VMEM((group, HEAD_DIM, 3 * HEAD_DIM), BF16),
                pltpu.VMEM((group, HEAD_DIM, 3 * HEAD_DIM), F32),
            ],
        ),
        compiler_params=pltpu.CompilerParams(vmem_limit_bytes=VMEM_LIMIT),
        cost_estimate=pl.CostEstimate(
            flops=heads * 150_000_000, bytes_accessed=12 * rows * width, transcendentals=heads * 32768
        ),
        name="backward_attention",
    )(meta, before, own, after, cotangent, offsets, *weight_slots)


def finish_kernel(grad_ref, low_ref, high_ref, x_ref, inverse_ref, gain_ref, cot_ref, out_ref, gain_grad_ref):
    rows = x_ref.shape[0]
    grad = grad_ref[...]
    edge = jnp.zeros((rows - RADIUS, grad.shape[1]), F32)
    grad = grad + jnp.concatenate([low_ref[...].astype(F32), edge], axis=0)
    grad = grad + jnp.concatenate([edge, high_ref[...].astype(F32)], axis=0)
    x = x_ref[...].astype(F32)
    inverse = inverse_ref[:, :1]
    gain_grad_ref[...] = jnp.sum(grad * x * inverse, axis=0, keepdims=True)
    scaled = grad * gain_ref[...]
    mean = jnp.mean(scaled * x, axis=-1, keepdims=True)
    result = inverse * scaled - x * (inverse * inverse * inverse * mean)
    out_ref[...] = (cot_ref[...].astype(F32) + result).astype(BF16)


def finish(grad, low, high, x, inverse, gain, cotangent):
    rows, width = x.shape
    return pl.pallas_call(
        finish_kernel,
        out_shape=(
            jax.ShapeDtypeStruct((rows, width), BF16),
            jax.ShapeDtypeStruct((1, width), F32),
        ),
        compiler_params=pltpu.CompilerParams(vmem_limit_bytes=VMEM_LIMIT),
        cost_estimate=pl.CostEstimate(
            flops=16 * rows * width, bytes_accessed=14 * rows * width, transcendentals=0
        ),
        name="finish",
    )(grad, low, high, x, inverse, gain, cotangent)


def column_of(row, rows):
    return jnp.transpose(jnp.broadcast_to(row, (128, rows)))


def split_rows(inverse, pad_rows, width):
    high = inverse.astype(BF16)
    rest = inverse - high.astype(F32)
    middle = rest.astype(BF16)
    low = (rest - middle.astype(F32)).astype(BF16)
    wide = [jnp.transpose(jnp.broadcast_to(v.astype(F32), (v.shape[0], 128)))[:1] for v in (high, middle, low)]
    row = jnp.concatenate(wide + [jnp.zeros((pad_rows - 3, wide[0].shape[1]), F32)], axis=0)
    return row.astype(BF16)


def row_inverse(x):
    x = x.astype(F32)
    return lax.rsqrt(jnp.mean(x * x, axis=-1, keepdims=True) + eps_norm)


def pack_stash_kernel(parts, pieces, x_hbm, gain_hbm, weight_hbm, inverse_ref, *refs):
    out_refs = refs[:parts]
    x_ref, gain_ref, weight_ref, normed_ref, sems = refs[parts:]
    rows, width = x_ref.shape
    depth = weight_ref.shape[2]
    wide = width // parts
    heads = wide // HEAD_DIM
    step = rows // pieces
    gain_copy = pltpu.make_async_copy(gain_hbm, gain_ref, sems.at[0])
    x_copies = [
        pltpu.make_async_copy(x_hbm.at[pl.ds(k * step, step)], x_ref.at[pl.ds(k * step, step)], sems.at[1 + k])
        for k in range(pieces)
    ]
    weight_copies = [
        pltpu.make_async_copy(weight_hbm.at[j], weight_ref.at[j], sems.at[1 + pieces + j]) for j in range(3)
    ]
    for copy in (gain_copy, *x_copies, *weight_copies):
        copy.start()
    gain_copy.wait()
    gain = gain_ref[...]
    for k, copy in enumerate(x_copies):
        copy.wait()
        part = slice(k * step, (k + 1) * step)
        inverse = row_inverse(x_ref[part])
        inverse_ref[part] = jnp.broadcast_to(inverse, (step, 128))
        normed_ref[part] = (x_ref[part].astype(F32) * inverse * gain).astype(BF16)
    for r, out_ref in enumerate(out_refs):
        target = lax.rem(lax.axis_index("seq") + r, parts)
        out_ref[:rows] = normed_ref[:, pl.ds(pl.multiple_of(target * wide, 128), wide)]
    for j, copy in enumerate(weight_copies):
        copy.wait()
        for r, out_ref in enumerate(out_refs):
            target = lax.rem(lax.axis_index("seq") + r, parts)
            for h in range(heads):
                out_ref[rows + j * depth : rows + (j + 1) * depth, h * HEAD_DIM : (h + 1) * HEAD_DIM] = weight_ref[
                    j, target * heads + h
                ]


def pack_rows_kernel(parts, with_inverse, meta_ref, edge_ref, inner_ref, *out_refs):
    rows, width = inner_ref.shape
    wide = width // parts
    edge = 1 if with_inverse else 2
    refs = out_refs[:parts]
    for r, out_ref in enumerate(refs):
        target = lax.rem(meta_ref[0] + r, parts)
        start = pl.multiple_of(target * wide, 128)

        @pl.when(meta_ref[edge] == 1)
        def use_edge():
            out_ref[:rows] = edge_ref[:, pl.ds(start, wide)]

        @pl.when(meta_ref[edge] == 0)
        def use_inner():
            out_ref[:rows] = inner_ref[:, pl.ds(start, wide)]

    def finish_with(source_ref):
        if with_inverse:
            tail = split_rows(row_inverse(source_ref[...]), EXTRA, wide)
            for out_ref in refs:
                out_ref[rows:] = jnp.zeros((EXTRA, wide), BF16)
                out_ref[rows:, :rows] = tail
        else:
            out_refs[parts][...] = source_ref[...]

    @pl.when(meta_ref[edge] == 1)
    def finish_edge():
        finish_with(edge_ref)

    @pl.when(meta_ref[edge] == 0)
    def finish_inner():
        finish_with(inner_ref)


SMEM_SPEC = pl.BlockSpec(memory_space=pltpu.SMEM)
VMEM_SPEC = pl.BlockSpec(memory_space=pltpu.VMEM)


def pack_stash(x, gain, weight, parts):
    rows, width = x.shape
    depth = weight.shape[2]
    shape = (rows + 3 * depth, width // parts)
    return pl.pallas_call(
        functools.partial(pack_stash_kernel, parts, 4),
        out_shape=(
            jax.ShapeDtypeStruct((rows, 128), F32),
            *[jax.ShapeDtypeStruct(shape, BF16) for r in range(parts)],
        ),
        in_specs=[pl.BlockSpec(memory_space=pl.ANY)] * 3,
        out_specs=(VMEM_SPEC,) * (parts + 1),
        scratch_shapes=[
            pltpu.VMEM((rows, width), BF16),
            pltpu.VMEM((1, width), F32),
            pltpu.VMEM(weight.shape, BF16),
            pltpu.VMEM((rows, width), BF16),
            pltpu.SemaphoreType.DMA((8,)),
        ],
        compiler_params=pltpu.CompilerParams(vmem_limit_bytes=58 * 1024 * 1024),
        cost_estimate=pl.CostEstimate(flops=4 * rows * width, bytes_accessed=6 * rows * width, transcendentals=0),
        name="pack_stash",
    )(x, gain, weight)


def pack_rows(meta, edge, inner, parts, with_inverse):
    rows, width = inner.shape
    shape = (rows + (EXTRA if with_inverse else 0), width // parts)
    extra = () if with_inverse else (jax.ShapeDtypeStruct((rows, width), BF16),)
    return pl.pallas_call(
        functools.partial(pack_rows_kernel, parts, with_inverse),
        out_shape=(*[jax.ShapeDtypeStruct(shape, BF16) for r in range(parts)], *extra),
        in_specs=[SMEM_SPEC, VMEM_SPEC, VMEM_SPEC],
        out_specs=(VMEM_SPEC,) * (parts + len(extra)),
        compiler_params=pltpu.CompilerParams(vmem_limit_bytes=VMEM_LIMIT),
        cost_estimate=pl.CostEstimate(flops=4 * rows * width, bytes_accessed=6 * rows * width, transcendentals=0),
        name="pack_inbound" if with_inverse else "pack_cotangent",
    )(meta, edge, inner)


def slot_order(parts):
    return sorted(range(parts), key=lambda r: min(r, parts - r))


def gather_rows(meta_ref, refs, rows, x_ref):
    parts = len(refs)
    for r, ref in zip(slot_order(parts), refs):
        source = lax.rem(meta_ref[0] + parts - r, parts)
        x_ref[pl.ds(pl.multiple_of(source * rows, rows), rows)] = ref[:rows]


def gather_weight(meta_ref, refs, rows, weight_ref):
    parts = len(refs)
    depth = HEAD_DIM // parts
    for r, ref in zip(slot_order(parts), refs):
        source = lax.rem(meta_ref[0] + parts - r, parts)
        depth_at = pl.ds(pl.multiple_of(source * depth, depth), depth)
        for j in range(3):
            weight_ref[depth_at, j * HEAD_DIM : (j + 1) * HEAD_DIM] = ref[
                rows + j * depth : rows + (j + 1) * depth
            ]


def gather_inverse(meta_ref, refs, rows, inverse_ref):
    parts = len(refs)

    @pl.when(pl.program_id(0) == 0)
    def spread_inverse():
        for r, ref in zip(slot_order(parts), refs):
            source = lax.rem(meta_ref[0] + parts - r, parts)
            tail = ref[rows : rows + EXTRA].astype(F32)
            inverse_ref[pl.ds(pl.multiple_of(source * rows, rows), rows)] = column_of(
                tail[:1] + tail[1:2] + tail[2:3], rows
            )


def block_mask(first_query, tokens):
    key = lax.broadcasted_iota(jnp.int32, (1, WINDOW), 1) + (first_query - RADIUS)
    return jnp.where((key >= 0) & (key < tokens), 0.0, masked_score).astype(F32)


def edge_bias(bias, first, tokens):
    if first < RADIUS or first + ROW_BLOCK + RADIUS > tokens:
        return bias + block_mask(first, tokens)
    return bias


def padded(rows):
    edge = jnp.zeros((RADIUS, rows.shape[1]), rows.dtype)
    return jnp.concatenate([edge, rows, edge], axis=0)


def heads_backward_kernel(parts, rows, meta_ref, *refs):
    a_refs, c_refs = refs[:parts], refs[parts : 2 * parts]
    gain_ref, offset_ref, onehot_ref, after_ref = refs[2 * parts : 2 * parts + 4]
    out_refs = refs[2 * parts + 4 : 3 * parts + 4]
    gain_grad_ref, x_ref, weight_ref, cot_ref, grad_ref, part_ref, bias_ref = refs[3 * parts + 4 :]
    tokens = rows * parts
    depth = HEAD_DIM // parts
    scale = HEAD_DIM ** (-0.5)
    gather_rows(meta_ref, a_refs, rows, x_ref)
    gather_weight(meta_ref, a_refs, rows, weight_ref)
    gather_rows(meta_ref, c_refs, rows, cot_ref)
    weight = weight_ref[...]
    normed = x_ref[...]
    query = dot_nn(normed, weight[:, :HEAD_DIM]).astype(BF16)
    key = padded(dot_nn(normed, weight[:, HEAD_DIM : 2 * HEAD_DIM]).astype(BF16))
    value = padded(dot_nn(normed, weight[:, 2 * HEAD_DIM :]).astype(BF16))
    bias = toeplitz(offset_ref[0])
    blocks = tokens // ROW_BLOCK
    starts = range(0, tokens, ROW_BLOCK)
    cot = cot_ref[...]
    query_rows = [query[f : f + ROW_BLOCK] for f in starts]
    cot_rows = [cot[f : f + ROW_BLOCK] for f in starts]
    products = [dot_nt(rows_q, key[f : f + WINDOW]) for f, rows_q in zip(starts, query_rows)]
    grad_probs = [dot_nt(rows_c, value[f : f + WINDOW]) for f, rows_c in zip(starts, cot_rows)]
    packed, grad_packed, score_sum = [], [], None
    for f, product, grads in zip(starts, products, grad_probs):
        probs = score_probs(product, edge_bias(bias, f, tokens))
        delta = jnp.sum(probs * grads, axis=-1, keepdims=True)
        grad_scores = probs * (grads - delta)
        score_sum = grad_scores if score_sum is None else score_sum + grad_scores
        packed.append(probs.astype(BF16))
        grad_packed.append(grad_scores.astype(BF16))
    grad_query = [dot_nn(part, key[f : f + WINDOW]) for f, part in zip(starts, grad_packed)]
    grad_key = [dot_tn(part, rows_q) for part, rows_q in zip(grad_packed, query_rows)]
    grad_value = [dot_tn(part, rows_c) for part, rows_c in zip(packed, cot_rows)]

    def joined(pieces):
        units = []
        for u in range((tokens + 2 * RADIUS) // ROW_BLOCK):
            total = None
            for b in range(blocks):
                if 0 <= u - b < WINDOW // ROW_BLOCK:
                    piece = pieces[b][(u - b) * ROW_BLOCK : (u - b + 1) * ROW_BLOCK]
                    total = piece if total is None else total + piece
            units.append(total)
        return jnp.concatenate(units, axis=0)[RADIUS : RADIUS + tokens]

    dqkv = jnp.concatenate(
        [
            (jnp.concatenate(grad_query, axis=0) * scale).astype(BF16),
            (joined(grad_key) * scale).astype(BF16),
            joined(grad_value).astype(BF16),
        ],
        axis=1,
    )
    grad_normed = dot_nt(dqkv, weight)
    gain_grad_ref[...] = jnp.sum(grad_normed * normed.astype(F32), axis=0, keepdims=True) / gain_ref[...]
    grad_ref[...] = grad_normed
    part_ref[...] = dot_tn(normed, dqkv)
    bias_grad = jnp.sum(onehot_ref[...] * diagonal_sums(score_sum), axis=1, keepdims=True)
    bias_ref[...] = jnp.broadcast_to(bias_grad, bias_ref.shape)
    buckets = bias_ref.shape[0] // parts
    for r, out_ref in enumerate(out_refs):
        source = lax.rem(meta_ref[0] + parts - r, parts)
        out_ref[:rows] = grad_ref[pl.ds(pl.multiple_of(source * rows, rows), rows)].astype(BF16)
        for j in range(3):
            out_ref[rows + j * depth : rows + (j + 1) * depth] = part_ref[
                pl.ds(pl.multiple_of(source * depth, depth), depth), j * HEAD_DIM : (j + 1) * HEAD_DIM
            ].astype(BF16)
        share = bias_ref[pl.ds(pl.multiple_of(source * buckets, buckets), buckets)]
        out_ref[rows + 3 * depth :] = share.astype(BF16)


def head_column(rows, first=0):
    return pl.BlockSpec((rows, HEAD_DIM), lambda i, meta: (0, i + first))


def whole_column(rows, heads, first=0):
    return pl.BlockSpec((rows, HEAD_DIM), lambda i, meta: (0, meta[0] * heads + first + i))


def offset_spec(heads, first=0):
    return pl.BlockSpec((1, 1, WINDOW), lambda i, meta: (meta[0] * heads + first + i, 0, 0))


def heads_backward(meta, a_slots, c_slots, gain, offsets, onehot, after, heads, first, count):
    parts = len(a_slots)
    rows = c_slots[0].shape[0]
    tokens = rows * parts
    buckets = onehot.shape[0]
    packed = a_slots[0].shape[0]
    made = packed + buckets // parts
    width = count * HEAD_DIM
    return pl.pallas_call(
        functools.partial(heads_backward_kernel, parts, rows),
        out_shape=(
            *[jax.ShapeDtypeStruct((made, width), BF16) for r in range(parts)],
            jax.ShapeDtypeStruct((1, width), F32),
        ),
        grid_spec=pltpu.PrefetchScalarGridSpec(
            num_scalar_prefetch=1,
            grid=(count,),
            in_specs=[
                *[head_column(packed, first)] * parts,
                whole_column(rows, heads, first),
                *[head_column(rows, first)] * (parts - 1),
                whole_column(1, heads, first),
                offset_spec(heads, first),
                pl.BlockSpec((buckets, WINDOW), lambda i, meta: (0, 0)),
                pl.BlockSpec(memory_space=pl.ANY),
            ],
            out_specs=(*[head_column(made)] * parts, head_column(1)),
            scratch_shapes=[
                pltpu.VMEM((tokens, HEAD_DIM), BF16),
                pltpu.VMEM((HEAD_DIM, 3 * HEAD_DIM), BF16),
                pltpu.VMEM((tokens, HEAD_DIM), BF16),
                pltpu.VMEM((tokens, HEAD_DIM), F32),
                pltpu.VMEM((HEAD_DIM, 3 * HEAD_DIM), F32),
                pltpu.VMEM((buckets, HEAD_DIM), F32),
            ],
        ),
        compiler_params=pltpu.CompilerParams(vmem_limit_bytes=VMEM_LIMIT),
        cost_estimate=pl.CostEstimate(
            flops=count * tokens * 400_000, bytes_accessed=tokens * width, transcendentals=0
        ),
        name="heads_backward",
    )(meta, *a_slots, *c_slots, gain, offsets, onehot, after)


def heads_forward_kernel(parts, rows, meta_ref, *refs):
    a_refs, i_refs = refs[:parts], refs[parts : 2 * parts]
    gain_ref, offset_ref = refs[2 * parts : 2 * parts + 2]
    out_refs = refs[2 * parts + 2 : 3 * parts + 2]
    inverse_ref, x_ref, weight_ref, made_ref, square_ref = refs[3 * parts + 2 :]
    tokens = rows * parts
    gather_rows(meta_ref, i_refs, rows, x_ref)
    gather_weight(meta_ref, a_refs, rows, weight_ref)
    gather_inverse(meta_ref, i_refs, rows, inverse_ref)
    weight = weight_ref[...]
    normed = (x_ref[...].astype(F32) * inverse_ref[...] * gain_ref[...]).astype(BF16)
    query = dot_nn(normed, weight[:, :HEAD_DIM]).astype(BF16)
    key = padded(dot_nn(normed, weight[:, HEAD_DIM : 2 * HEAD_DIM]).astype(BF16))
    value = padded(dot_nn(normed, weight[:, 2 * HEAD_DIM :]).astype(BF16))
    bias = toeplitz(offset_ref[0])
    starts = range(0, tokens, ROW_BLOCK)
    products = [dot_nt(query[f : f + ROW_BLOCK], key[f : f + WINDOW]) for f in starts]
    packed = [
        score_probs(product, edge_bias(bias, f, tokens)).astype(BF16) for f, product in zip(starts, products)
    ]
    attended = [dot_nn(part, value[f : f + WINDOW]) for f, part in zip(starts, packed)]
    for f, part in zip(starts, attended):
        made_ref[f : f + ROW_BLOCK] = (x_ref[f : f + ROW_BLOCK].astype(F32) + part).astype(BF16)
    made = made_ref[...].astype(F32)
    squares = made * made

    @pl.when(pl.program_id(0) == 0)
    def first_head():
        square_ref[...] = squares

    @pl.when(pl.program_id(0) > 0)
    def later_head():
        square_ref[...] += squares

    for r, out_ref in enumerate(out_refs):
        source = lax.rem(meta_ref[0] + parts - r, parts)
        out_ref[:rows] = made_ref[pl.ds(pl.multiple_of(source * rows, rows), rows)]

    @pl.when(pl.program_id(0) < pl.num_programs(0) - 1)
    def no_sums():
        for out_ref in out_refs:
            out_ref[rows:] = jnp.zeros((EXTRA, HEAD_DIM), BF16)

    @pl.when(pl.program_id(0) == pl.num_programs(0) - 1)
    def last_head():
        rest = jnp.sum(jnp.transpose(square_ref[...]), axis=0, keepdims=True)
        at_row = lax.broadcasted_iota(jnp.int32, (EXTRA, rows), 0)
        tail = jnp.zeros((EXTRA, rows), F32)
        for k in range(2):
            piece = rest.astype(BF16).astype(F32)
            rest = rest - piece
            for part in range(parts):
                row = jnp.broadcast_to(piece[:, part * rows : (part + 1) * rows], (EXTRA, rows))
                tail = jnp.where(at_row == 2 * part + k, row, tail)
        for out_ref in out_refs:
            out_ref[rows:] = tail.astype(BF16)


def heads_forward(meta, a_slots, i_slots, gain, offsets, heads, rows):
    parts = len(a_slots)
    tokens = rows * parts
    packed = a_slots[0].shape[0]
    width = heads * HEAD_DIM
    return pl.pallas_call(
        functools.partial(heads_forward_kernel, parts, rows),
        out_shape=(
            *[jax.ShapeDtypeStruct((rows + EXTRA, width), BF16) for r in range(parts)],
        ),
        grid_spec=pltpu.PrefetchScalarGridSpec(
            num_scalar_prefetch=1,
            grid=(heads,),
            in_specs=[
                *[head_column(packed)] * parts,
                *[head_column(i_slots[0].shape[0])] * parts,
                whole_column(1, heads),
                offset_spec(heads),
            ],
            out_specs=(head_column(rows + EXTRA),) * parts,
            scratch_shapes=[
                pltpu.VMEM((tokens, HEAD_DIM), F32),
                pltpu.VMEM((tokens, HEAD_DIM), BF16),
                pltpu.VMEM((HEAD_DIM, 3 * HEAD_DIM), BF16),
                pltpu.VMEM((tokens, HEAD_DIM), BF16),
                pltpu.VMEM((tokens, HEAD_DIM), F32),
            ],
        ),
        compiler_params=pltpu.CompilerParams(vmem_limit_bytes=VMEM_LIMIT),
        cost_estimate=pl.CostEstimate(
            flops=heads * tokens, bytes_accessed=tokens, transcendentals=0
        ),
        name="heads_forward",
    )(meta, *a_slots, *i_slots, gain, offsets)


def memory_kernel(parts, width, meta_ref, *refs):
    out_refs, other_refs = refs[:parts], refs[parts : 2 * parts - 1]
    gain_ref, *share_refs, memory_ref = refs[2 * parts - 1 :]
    wide = memory_ref.shape[1]
    rows = memory_ref.shape[0] // parts
    total = None
    for ref in (out_refs[0], *other_refs):
        tail = ref[rows:, wide - rows :].astype(F32)
        pieces = [tail[2 * p : 2 * p + 1] + tail[2 * p + 1 : 2 * p + 2] for p in range(parts)]
        row = jnp.concatenate(pieces, axis=1)
        total = row if total is None else total + row
    inverse = lax.rsqrt(total / width + eps_norm)
    gain = gain_ref[:, pl.ds(pl.multiple_of(meta_ref[0] * wide, 128), wide)]
    spread_inverse = jnp.transpose(jnp.broadcast_to(inverse, (128, inverse.shape[1])))
    for r, out_ref in enumerate(out_refs):
        source = lax.rem(meta_ref[0] + parts - r, parts)
        memory_ref[pl.ds(pl.multiple_of(source * rows, rows), rows)] = out_ref[:rows]
    made = memory_ref[...].astype(F32)
    memory_ref[...] = (made * spread_inverse[:, :1] * gain).astype(BF16)
    for k, share_ref in enumerate(share_refs):
        size = share_ref.shape[0]
        share_ref[...] = memory_ref[k * size : (k + 1) * size]


def memory_rows(meta, outs, others, gain, width, shares):
    parts = len(outs)
    rows, wide = outs[0].shape[0] - EXTRA, outs[0].shape[1]
    return pl.pallas_call(
        functools.partial(memory_kernel, parts, width),
        out_shape=[jax.ShapeDtypeStruct((rows * parts // shares, wide), BF16)] * shares,
        in_specs=[SMEM_SPEC] + [VMEM_SPEC] * (2 * parts),
        out_specs=[VMEM_SPEC] * shares,
        scratch_shapes=[pltpu.VMEM((rows * parts, wide), BF16)],
        compiler_params=pltpu.CompilerParams(vmem_limit_bytes=VMEM_LIMIT),
        cost_estimate=pl.CostEstimate(flops=rows, bytes_accessed=rows, transcendentals=0),
        name="memory_rows",
    )(meta, *outs, *others, gain)


def place_kernel(parts, meta_ref, *refs):
    out_ref = refs[parts]
    wide = refs[0].shape[1]
    for r, ref in zip(slot_order(parts), refs):
        source = lax.rem(meta_ref[0] + r, parts)
        out_ref[:, pl.ds(pl.multiple_of(source * wide, 128), wide)] = ref[: out_ref.shape[0]]


def place_columns(meta, slots):
    parts = len(slots)
    rows, wide = slots[0].shape[0] - EXTRA, slots[0].shape[1]
    return pl.pallas_call(
        functools.partial(place_kernel, parts),
        out_shape=jax.ShapeDtypeStruct((rows, wide * parts), BF16),
        in_specs=[SMEM_SPEC] + [VMEM_SPEC] * parts,
        out_specs=VMEM_SPEC,
        compiler_params=pltpu.CompilerParams(vmem_limit_bytes=VMEM_LIMIT),
        cost_estimate=pl.CostEstimate(flops=0, bytes_accessed=rows, transcendentals=0),
        name="place_columns",
    )(meta, *slots)


def heads_finish_kernel(parts, meta_ref, *refs):
    g_refs = refs[:parts]
    x_ref, inverse_ref, gain_ref, cot_ref, out_ref, weight_hbm, bias_ref, scaled_ref, weight_ref, sem = refs[parts:]
    rows, width = x_ref.shape
    wide = width // parts
    heads = wide // HEAD_DIM
    depth = HEAD_DIM // parts
    for r, g_ref in zip(slot_order(parts), g_refs):
        source = lax.rem(meta_ref[0] + r, parts)
        for h in range(heads):
            for j in range(3):
                weight_ref[j, source * heads + h] = g_ref[
                    rows + j * depth : rows + (j + 1) * depth, h * HEAD_DIM : (h + 1) * HEAD_DIM
                ].astype(F32)
    weight_copy = pltpu.make_async_copy(weight_ref, weight_hbm, sem)
    weight_copy.start()
    lane = lax.broadcasted_iota(jnp.int32, (bias_ref.shape[0], HEAD_DIM), 1)
    bias = jnp.zeros(lane.shape, F32)
    for r, g_ref in zip(slot_order(parts), g_refs):
        source = lax.rem(meta_ref[0] + r, parts)
        columns = pl.ds(pl.multiple_of(source * wide, 128), wide)
        scaled_ref[:, columns] = g_ref[:rows].astype(F32) * gain_ref[:, columns]
        shares = g_ref[rows + 3 * depth :].astype(F32)
        for h in range(heads):
            bias = jnp.where(lane == source * heads + h, shares[:, h * HEAD_DIM : (h + 1) * HEAD_DIM], bias)
    bias_ref[...] = bias[:, : bias_ref.shape[1]]
    x = x_ref[...].astype(F32)
    scaled = scaled_ref[...]
    inverse = inverse_ref[:, :1]
    mean = jnp.mean(scaled * x, axis=-1, keepdims=True)
    result = inverse * scaled - x * (inverse * inverse * inverse * mean)
    out_ref[...] = (cot_ref[...].astype(F32) + result).astype(BF16)
    weight_copy.wait()


def heads_finish(meta, g_slots, x, inverse, gain, cotangent, buckets):
    parts = len(g_slots)
    rows, width = x.shape
    heads = width // HEAD_DIM
    weight_shape = (3, heads, HEAD_DIM // parts, HEAD_DIM)
    return pl.pallas_call(
        functools.partial(heads_finish_kernel, parts),
        out_shape=(
            jax.ShapeDtypeStruct((rows, width), BF16),
            jax.ShapeDtypeStruct(weight_shape, F32),
            jax.ShapeDtypeStruct((buckets // parts, heads), F32),
        ),
        in_specs=[SMEM_SPEC] + [VMEM_SPEC] * (parts + 4),
        out_specs=(VMEM_SPEC, pl.BlockSpec(memory_space=pl.ANY), VMEM_SPEC),
        scratch_shapes=[
            pltpu.VMEM((rows, width), F32),
            pltpu.VMEM(weight_shape, F32),
            pltpu.SemaphoreType.DMA,
        ],
        compiler_params=pltpu.CompilerParams(vmem_limit_bytes=VMEM_LIMIT),
        cost_estimate=pl.CostEstimate(flops=12 * rows * width, bytes_accessed=14 * rows * width, transcendentals=0),
        name="heads_finish",
    )(meta, *g_slots, x, inverse, gain, cotangent)


def offset_table(rel_bias):
    onehot = jnp.asarray(bucket_onehot(rel_bias.shape[0]))
    by_offset = jnp.dot(onehot, rel_bias, precision=lax.Precision.HIGHEST).T
    inside = jnp.arange(WINDOW, dtype=jnp.int32) <= 2 * RADIUS
    return jnp.where(inside[None, :], by_offset, masked_score)[:, None, :]


def shifted(value, axis, steps):
    count = lax.axis_size(axis)
    first, last = (max(0, -steps), min(count, count - steps))
    return lax.ppermute(value, axis, [(source, source + steps) for source in range(first, last)])


def spread_memory(shares, section, sections):
    last = sections - 1
    couple = jnp.where(section == last, shares[-1], 0)
    for s, share in enumerate(shares[:-1]):
        couple = couple + lax.ppermute(share, "section", [(last, 2 * s + 1)])
    half = couple.shape[0] // 2
    even = lax.ppermute(couple[:half], "section", [(s + 1, s) for s in range(0, sections, 2)])
    return jnp.where(section % 2 == 0, even, couple[half:])


def heads_body(
    embedded, carried, stash, returned, loss_grad, qkv_weight, rel_bias, norm_gain, final_gain
):
    section = lax.axis_index("section")
    sections = lax.axis_size("section")
    parts = lax.axis_size("seq")
    rows, width = embedded.shape
    heads = width // HEAD_DIM // parts
    buckets = rel_bias.shape[1]
    meta = jnp.stack(
        [lax.axis_index("seq"), section == 0, section == sections - 1]
    ).astype(jnp.int32)

    def exchanged(sends, direction):
        return [
            lax.ppermute(sends[r], "seq", [(i, (i + direction * r) % parts) for i in range(parts)]) if r else sends[0]
            for r in slot_order(parts)
        ]

    inverse_b, *a_sends = pack_stash(stash[0], norm_gain, qkv_weight[0], parts)
    a_slots = exchanged(a_sends, 1)
    arrived = shifted(carried[0], "section", 1)
    came_back = shifted(returned[0], "section", -1)
    i_slots = exchanged(pack_rows(meta, embedded, arrived, parts, True), 1)
    *c_sends, cotangent = pack_rows(meta, loss_grad, came_back, parts, False)
    c_slots = exchanged(c_sends, 1)
    c_slots[0] = cotangent

    offsets = offset_table(rel_bias[0])
    onehot = jnp.asarray(bucket_onehot(buckets).T)
    o_sends = heads_forward(meta, a_slots, i_slots, norm_gain, offsets, heads, rows)
    o_slots = exchanged(o_sends, -1)

    *g_sends, gain_grad = heads_backward(
        meta, a_slots, c_slots, norm_gain, offsets, onehot, o_sends[0], heads, 0, heads
    )
    g_sends, o_slots = lax.optimization_barrier((g_sends, o_slots))
    g_slots = exchanged(g_sends, -1)
    output = place_columns(meta, o_slots)
    shares = memory_rows(meta, o_sends, o_slots[1:], final_gain[None], width, sections // 2)
    memory = spread_memory(shares, section, sections)

    input_grad, weight_grad, bias_grad = heads_finish(
        meta, g_slots, stash[0], inverse_b, norm_gain, cotangent, buckets
    )
    return (
        output[None],
        input_grad[None],
        weight_grad[None],
        bias_grad[None],
        gain_grad,
        memory,
    )


def tokens_body(
    embedded, carried, stash, returned, loss_grad, qkv_weight, rel_bias, norm_gain, final_gain
):
    section_index = lax.axis_index("section")
    section_count = lax.axis_size("section")
    seq_index = lax.axis_index("seq")
    seq_count = lax.axis_size("seq")
    rows, width = embedded.shape
    heads = width // HEAD_DIM
    tokens = rows * seq_count
    shard = qkv_weight[0]
    up = [(i, i + 1) for i in range(seq_count - 1)]
    down = [(j, i) for i, j in up]
    group = 4 if heads % 4 == 0 else 1

    own_b, inverse_b = norm_rows(stash[0], norm_gain)
    before_b = lax.ppermute(own_b[rows - RADIUS :], "seq", up)
    after_b = lax.ppermute(own_b[:RADIUS], "seq", down)
    slots = [lax.all_gather(shard, "seq", axis=2, tiled=True)]

    section_up = [(i, (i + 1) % section_count) for i in range(section_count)]
    section_down = [(j, i) for i, j in section_up]
    inbound = lax.ppermute(
        jnp.where(section_index == section_count - 1, embedded, carried[0]), "section", section_up
    )
    cotangent = lax.ppermute(
        jnp.where(section_index == 0, loss_grad, returned[0]), "section", section_down
    )

    onehot = jnp.asarray(bucket_onehot(rel_bias.shape[1]))
    offsets = offset_table(rel_bias[0])
    first_key = RADIUS - seq_index * rows
    meta = jnp.stack([seq_index, first_key, first_key + tokens]).astype(jnp.int32)

    own_a, unused = norm_rows(inbound, norm_gain)
    before_a = lax.ppermute(own_a[rows - RADIUS :], "seq", up)
    after_a = lax.ppermute(own_a[:RADIUS], "seq", down)

    grad_own, lower, upper, offset_grad, *parts = backward_attention(
        meta, before_b, own_b, after_b, cotangent, offsets, slots, group, 0, heads
    )
    from_before = lax.ppermute(upper, "seq", up)
    from_after = lax.ppermute(lower, "seq", down)
    weight_sum = lax.psum_scatter(parts[0], "seq", scatter_dimension=2, tiled=True).astype(F32)

    output = forward_attention(meta, before_a, own_a, after_a, inbound, offsets, slots, group)
    final_normed, unused = norm_rows(output, final_gain[None])
    relaid = lax.all_to_all(final_normed, "seq", split_axis=1, concat_axis=0, tiled=True)
    kept = jnp.where(section_index == section_count - 1, relaid, jnp.zeros_like(relaid))
    memory = lax.psum_scatter(kept, "section", scatter_dimension=0, tiled=True)

    input_grad, gain_part = finish(
        grad_own, from_before, from_after, stash[0], inverse_b, norm_gain, cotangent
    )
    bias_part = jnp.dot(
        offset_grad[:, 0, :], onehot, precision=lax.Precision.HIGHEST
    ).T
    bias_sum = lax.psum_scatter(
        bias_part.astype(BF16), "seq", scatter_dimension=0, tiled=True
    ).astype(F32)
    gain_sum = lax.psum_scatter(
        gain_part.astype(BF16), "seq", scatter_dimension=1, tiled=True
    ).astype(F32)
    return (output[None], input_grad[None], weight_sum[None], bias_sum[None], gain_sum, memory)


def choose_body(embedded, carried, stash, returned, loss_grad, qkv_weight, rel_bias, norm_gain, final_gain):
    parts = lax.axis_size("seq")
    rows, width = embedded.shape
    even = width % (HEAD_DIM * parts) == 0 and HEAD_DIM % (32 * parts) == 0 and rows == 128
    sections = lax.axis_size("section")
    even = even and sections % 2 == 0
    even = even and rel_bias.shape[1] == 8 * parts and width <= 128 * HEAD_DIM and rows * parts % (16 * sections) == 0
    chosen = heads_body if even else tokens_body
    return chosen(
        embedded, carried, stash, returned, loss_grad, qkv_weight, rel_bias, norm_gain, final_gain
    )


def solution(mesh):
    in_specs = (
        P("seq", None),
        P("section", "seq", None),
        P("section", "seq", None),
        P("section", "seq", None),
        P("seq", None),
        P("section", None, None, "seq", None),
        P("section", None, None),
        P("section", None),
        P(),
    )
    out_specs = (
        P("section", "seq", None),
        P("section", "seq", None),
        P("section", None, None, "seq", None),
        P("section", "seq", None),
        P("section", "seq"),
        P("section", "seq"),
    )
    return jax.shard_map(choose_body, mesh=mesh, in_specs=in_specs, out_specs=out_specs, check_vma=False)
```

```python
import functools

import jax
import jax.numpy as jnp
import numpy as np
from jax import lax
from jax.experimental import pallas as pl
from jax.experimental.pallas import tpu as pltpu
from jax.sharding import PartitionSpec as P

RADIUS = 96
HEAD_DIM = 128
ROW_BLOCK = 64
WINDOW = ROW_BLOCK + 2 * RADIUS
eps_norm = 1e-06
bucket_edges = (1, 2, 3, 4, 5, 6, 7, 8, 11, 16, 22, 32, 45, 64, 90)
masked_score = -1e30
F32 = jnp.float32
BF16 = jnp.bfloat16
VMEM_LIMIT = 24 * 1024 * 1024
EXTRA = 8


def bucket_onehot(bucket_count):
    offsets = np.arange(WINDOW) - RADIUS
    magnitude = np.abs(offsets)
    counted = np.zeros(offsets.shape, np.int32)
    for threshold in bucket_edges:
        counted = counted + (magnitude >= threshold)
    counted = counted + 16 * (offsets > 0)
    onehot = (counted[:, None] == np.arange(bucket_count)[None, :]) & (magnitude <= RADIUS)[:, None]
    return onehot.astype(np.float32)


def dot_nn(a, b):
    return lax.dot_general(a, b, (((1,), (0,)), ((), ())), preferred_element_type=F32)


def dot_nt(a, b):
    return lax.dot_general(a, b, (((1,), (1,)), ((), ())), preferred_element_type=F32)


def dot_tn(a, b):
    return lax.dot_general(a, b, (((0,), (0,)), ((), ())), preferred_element_type=F32)


def norm_kernel(x_ref, gain_ref, normed_ref, inverse_ref):
    x = x_ref[...].astype(F32)
    inverse = lax.rsqrt(jnp.mean(x * x, axis=-1, keepdims=True) + eps_norm)
    normed_ref[...] = (x * inverse * gain_ref[...]).astype(BF16)
    inverse_ref[...] = jnp.broadcast_to(inverse, inverse_ref.shape)


def norm_rows(x, gain):
    rows, width = x.shape
    return pl.pallas_call(
        norm_kernel,
        out_shape=(
            jax.ShapeDtypeStruct((rows, width), BF16),
            jax.ShapeDtypeStruct((rows, 128), F32),
        ),
        compiler_params=pltpu.CompilerParams(vmem_limit_bytes=VMEM_LIMIT),
        cost_estimate=pl.CostEstimate(
            flops=6 * rows * width, bytes_accessed=4 * rows * width, transcendentals=rows
        ),
        name="norm_rows",
    )(x, gain)


def load_weight(meta_ref, slot_refs, weight_ref, head, slots):
    depth = HEAD_DIM // slots
    for r, slot_ref in enumerate(slot_refs):
        if slots == 1:
            start = 0
        else:
            start = pl.multiple_of(lax.rem(meta_ref[0] + r, slots) * depth, depth)
        for j in range(3):
            weight_ref[head, pl.ds(start, depth), j * HEAD_DIM : (j + 1) * HEAD_DIM] = slot_ref[j, head]
    return weight_ref[head]


def key_mask(meta_ref, first_key):
    key = lax.broadcasted_iota(jnp.int32, (1, WINDOW), 1) + first_key
    inside = (key >= meta_ref[1]) & (key < meta_ref[2])
    return jnp.where(inside, 0.0, masked_score).astype(F32)


def toeplitz(row):
    return pltpu.roll(
        jnp.broadcast_to(row, (ROW_BLOCK, WINDOW)), 0, 1, stride=1, stride_axis=0
    )


def diagonal_sums(values):
    total = values[:8]
    for a in range(1, ROW_BLOCK // 8):
        total = total + pltpu.roll(values[8 * a : 8 * a + 8], WINDOW - 8 * a, 1)
    row = lax.broadcasted_iota(jnp.int32, total.shape, 0)
    for bit in (1, 2, 4):
        total = jnp.where((row & bit) != 0, pltpu.roll(total, WINDOW - bit, 1), total)
    return jnp.sum(total, axis=0, keepdims=True)


def block_probs(query_rows, key_rows, bias):
    return score_probs(dot_nt(query_rows, key_rows), bias)


def score_probs(products, bias):
    scores = products * (HEAD_DIM ** (-0.5)) + bias
    weights = jnp.exp(scores - jnp.max(scores, axis=-1, keepdims=True))
    return weights * (1.0 / jnp.sum(weights, axis=-1, keepdims=True))


def forward_kernel(slots, group, meta_ref, before_ref, own_ref, after_ref, x_ref, offset_ref, *rest):
    slot_refs = rest[:slots]
    out_ref, weight_ref = rest[slots:]
    rows = own_ref.shape[0]
    blocks = rows // ROW_BLOCK
    masks = [key_mask(meta_ref, b * ROW_BLOCK) for b in range(blocks)]
    for g in range(group):
        columns = slice(g * HEAD_DIM, (g + 1) * HEAD_DIM)
        weight = load_weight(meta_ref, slot_refs, weight_ref, g, slots)
        own = own_ref[:, columns]
        extended = jnp.concatenate([before_ref[:, columns], own, after_ref[:, columns]], axis=0)
        query = dot_nn(own, weight[:, :HEAD_DIM]).astype(BF16)
        key_value = dot_nn(extended, weight[:, HEAD_DIM:]).astype(BF16)
        key, value = key_value[:, :HEAD_DIM], key_value[:, HEAD_DIM:]
        bias = toeplitz(offset_ref[g])
        for b in range(blocks):
            first = b * ROW_BLOCK
            window = slice(first, first + WINDOW)
            probs = block_probs(query[first : first + ROW_BLOCK], key[window], bias + masks[b])
            attended = dot_nn(probs.astype(BF16), value[window])
            kept = x_ref[first : first + ROW_BLOCK, columns].astype(F32)
            out_ref[first : first + ROW_BLOCK, columns] = (kept + attended).astype(BF16)


def column_spec(rows, group, first):
    return pl.BlockSpec((rows, group * HEAD_DIM), lambda i, meta: (0, i + first))


def slot_specs(weight_slots, group):
    return [
        pl.BlockSpec((3, group, slot.shape[2], HEAD_DIM), lambda i, meta: (0, i, 0, 0))
        for slot in weight_slots
    ]


def forward_attention(meta, before, own, after, x, offsets, weight_slots, group):
    rows, width = own.shape
    heads = width // HEAD_DIM
    slots = len(weight_slots)
    return pl.pallas_call(
        functools.partial(forward_kernel, slots, group),
        out_shape=jax.ShapeDtypeStruct((rows, width), BF16),
        grid_spec=pltpu.PrefetchScalarGridSpec(
            num_scalar_prefetch=1,
            grid=(heads // group,),
            in_specs=[
                column_spec(RADIUS, group, 0),
                column_spec(rows, group, 0),
                column_spec(RADIUS, group, 0),
                column_spec(rows, group, 0),
                pl.BlockSpec((group, 1, WINDOW), lambda i, meta: (i, 0, 0)),
                *slot_specs(weight_slots, group),
            ],
            out_specs=column_spec(rows, group, 0),
            scratch_shapes=[pltpu.VMEM((group, HEAD_DIM, 3 * HEAD_DIM), BF16)],
        ),
        compiler_params=pltpu.CompilerParams(vmem_limit_bytes=VMEM_LIMIT),
        cost_estimate=pl.CostEstimate(
            flops=heads * 60_000_000, bytes_accessed=8 * rows * width, transcendentals=heads * 32768
        ),
        name="forward_attention",
    )(meta, before, own, after, x, offsets, *weight_slots)


def backward_kernel(slots, group, meta_ref, before_ref, own_ref, after_ref, cot_ref, offset_ref, *rest):
    slot_refs = rest[:slots]
    rest = rest[slots:]
    grad_ref, lower_ref, upper_ref, offset_grad_ref = rest[:4]
    part_refs = rest[4 : 4 + slots]
    weight_ref, part_ref = rest[4 + slots :]
    rows = own_ref.shape[0]
    blocks = rows // ROW_BLOCK
    scale = HEAD_DIM ** (-0.5)
    masks = [key_mask(meta_ref, b * ROW_BLOCK) for b in range(blocks)]
    for g in range(group):
        columns = slice(g * HEAD_DIM, (g + 1) * HEAD_DIM)
        weight = load_weight(meta_ref, slot_refs, weight_ref, g, slots)
        own = own_ref[:, columns]
        extended = jnp.concatenate([before_ref[:, columns], own, after_ref[:, columns]], axis=0)
        query = dot_nn(own, weight[:, :HEAD_DIM]).astype(BF16)
        key_value = dot_nn(extended, weight[:, HEAD_DIM:]).astype(BF16)
        key, value = key_value[:, :HEAD_DIM], key_value[:, HEAD_DIM:]
        bias = toeplitz(offset_ref[g])
        grad_query, grad_key, grad_value, score_sum = [], [], [], None
        for b in range(blocks):
            first = b * ROW_BLOCK
            window = slice(first, first + WINDOW)
            query_rows = query[first : first + ROW_BLOCK]
            cot_rows = cot_ref[first : first + ROW_BLOCK, columns]
            probs = block_probs(query_rows, key[window], bias + masks[b])
            grad_probs = dot_nt(cot_rows, value[window])
            delta = jnp.sum(probs * grad_probs, axis=-1, keepdims=True)
            grad_scores = probs * (grad_probs - delta)
            score_sum = grad_scores if score_sum is None else score_sum + grad_scores
            grad_packed = grad_scores.astype(BF16)
            grad_query.append(dot_nn(grad_packed, key[window]))
            grad_key.append(dot_tn(grad_packed, query_rows))
            grad_value.append(dot_tn(probs.astype(BF16), cot_rows))

        def joined(parts):
            pieces = []
            for u in range((rows + 2 * RADIUS) // ROW_BLOCK):
                total = None
                for b in range(blocks):
                    if 0 <= u - b < WINDOW // ROW_BLOCK:
                        piece = parts[b][(u - b) * ROW_BLOCK : (u - b + 1) * ROW_BLOCK]
                        total = piece if total is None else total + piece
                pieces.append(total)
            return jnp.concatenate(pieces, axis=0)

        dquery = (jnp.concatenate(grad_query, axis=0) * scale).astype(BF16)
        dkey = (joined(grad_key) * scale).astype(BF16)
        dvalue = joined(grad_value).astype(BF16)
        dkey_value = jnp.concatenate([dkey, dvalue], axis=1)
        grad_extended = dot_nt(dkey_value, weight[:, HEAD_DIM:])
        grad_ref[:, columns] = grad_extended[RADIUS : RADIUS + rows] + dot_nt(dquery, weight[:, :HEAD_DIM])
        lower_ref[:, columns] = grad_extended[:RADIUS].astype(BF16)
        upper_ref[:, columns] = grad_extended[RADIUS + rows :].astype(BF16)
        part_ref[g, :, :HEAD_DIM] = dot_tn(own, dquery)
        part_ref[g, :, HEAD_DIM:] = dot_tn(extended, dkey_value)
        depth = HEAD_DIM // slots
        for r in range(slots):
            if slots == 1:
                start = 0
            else:
                start = pl.multiple_of(lax.rem(meta_ref[0] + r, slots) * depth, depth)
            for j in range(3):
                part_refs[r][j, g] = part_ref[
                    g, pl.ds(start, depth), j * HEAD_DIM : (j + 1) * HEAD_DIM
                ].astype(part_refs[r].dtype)
        offset_grad_ref[g] = diagonal_sums(score_sum)


def backward_attention(meta, before, own, after, cotangent, offsets, weight_slots, group, first_head, heads):
    rows = own.shape[0]
    width = heads * HEAD_DIM
    slots = len(weight_slots)
    first = first_head // group
    slot_shape = weight_slots[0].shape
    part_types = [F32] + [BF16] * (slots - 1) if slots > 1 else [BF16]
    return pl.pallas_call(
        functools.partial(backward_kernel, slots, group),
        out_shape=(
            jax.ShapeDtypeStruct((rows, width), F32),
            jax.ShapeDtypeStruct((RADIUS, width), BF16),
            jax.ShapeDtypeStruct((RADIUS, width), BF16),
            jax.ShapeDtypeStruct((heads, 1, WINDOW), F32),
            *[jax.ShapeDtypeStruct(slot_shape, kind) for kind in part_types],
        ),
        grid_spec=pltpu.PrefetchScalarGridSpec(
            num_scalar_prefetch=1,
            grid=(heads // group,),
            in_specs=[
                column_spec(RADIUS, group, first),
                column_spec(rows, group, first),
                column_spec(RADIUS, group, first),
                column_spec(rows, group, first),
                pl.BlockSpec((group, 1, WINDOW), lambda i, meta: (i + first, 0, 0)),
                *slot_specs(weight_slots, group),
            ],
            out_specs=(
                column_spec(rows, group, 0),
                column_spec(RADIUS, group, 0),
                column_spec(RADIUS, group, 0),
                pl.BlockSpec((group, 1, WINDOW), lambda i, meta: (i, 0, 0)),
                *slot_specs(weight_slots, group),
            ),
            scratch_shapes=[
                pltpu.VMEM((group, HEAD_DIM, 3 * HEAD_DIM), BF16),
                pltpu.VMEM((group, HEAD_DIM, 3 * HEAD_DIM), F32),
            ],
        ),
        compiler_params=pltpu.CompilerParams(vmem_limit_bytes=VMEM_LIMIT),
        cost_estimate=pl.CostEstimate(
            flops=heads * 150_000_000, bytes_accessed=12 * rows * width, transcendentals=heads * 32768
        ),
        name="backward_attention",
    )(meta, before, own, after, cotangent, offsets, *weight_slots)


def finish_kernel(grad_ref, low_ref, high_ref, x_ref, inverse_ref, gain_ref, cot_ref, out_ref, gain_grad_ref):
    rows = x_ref.shape[0]
    grad = grad_ref[...]
    edge = jnp.zeros((rows - RADIUS, grad.shape[1]), F32)
    grad = grad + jnp.concatenate([low_ref[...].astype(F32), edge], axis=0)
    grad = grad + jnp.concatenate([edge, high_ref[...].astype(F32)], axis=0)
    x = x_ref[...].astype(F32)
    inverse = inverse_ref[:, :1]
    gain_grad_ref[...] = jnp.sum(grad * x * inverse, axis=0, keepdims=True)
    scaled = grad * gain_ref[...]
    mean = jnp.mean(scaled * x, axis=-1, keepdims=True)
    result = inverse * scaled - x * (inverse * inverse * inverse * mean)
    out_ref[...] = (cot_ref[...].astype(F32) + result).astype(BF16)


def finish(grad, low, high, x, inverse, gain, cotangent):
    rows, width = x.shape
    return pl.pallas_call(
        finish_kernel,
        out_shape=(
            jax.ShapeDtypeStruct((rows, width), BF16),
            jax.ShapeDtypeStruct((1, width), F32),
        ),
        compiler_params=pltpu.CompilerParams(vmem_limit_bytes=VMEM_LIMIT),
        cost_estimate=pl.CostEstimate(
            flops=16 * rows * width, bytes_accessed=14 * rows * width, transcendentals=0
        ),
        name="finish",
    )(grad, low, high, x, inverse, gain, cotangent)


def column_of(row, rows):
    return jnp.transpose(jnp.broadcast_to(row, (128, rows)))


def split_rows(inverse, pad_rows, width):
    high = inverse.astype(BF16)
    rest = inverse - high.astype(F32)
    middle = rest.astype(BF16)
    low = (rest - middle.astype(F32)).astype(BF16)
    wide = [jnp.transpose(jnp.broadcast_to(v.astype(F32), (v.shape[0], 128)))[:1] for v in (high, middle, low)]
    row = jnp.concatenate(wide + [jnp.zeros((pad_rows - 3, wide[0].shape[1]), F32)], axis=0)
    return row.astype(BF16)


def row_inverse(x):
    x = x.astype(F32)
    return lax.rsqrt(jnp.mean(x * x, axis=-1, keepdims=True) + eps_norm)


def pack_stash_kernel(parts, pieces, x_hbm, gain_hbm, weight_hbm, inverse_ref, *refs):
    out_refs = refs[:parts]
    x_ref, gain_ref, weight_ref, normed_ref, sems = refs[parts:]
    rows, width = x_ref.shape
    depth = weight_ref.shape[2]
    wide = width // parts
    heads = wide // HEAD_DIM
    step = rows // pieces
    gain_copy = pltpu.make_async_copy(gain_hbm, gain_ref, sems.at[0])
    x_copies = [
        pltpu.make_async_copy(x_hbm.at[pl.ds(k * step, step)], x_ref.at[pl.ds(k * step, step)], sems.at[1 + k])
        for k in range(pieces)
    ]
    weight_copies = [
        pltpu.make_async_copy(weight_hbm.at[j], weight_ref.at[j], sems.at[1 + pieces + j]) for j in range(3)
    ]
    for copy in (gain_copy, *x_copies, *weight_copies):
        copy.start()
    gain_copy.wait()
    gain = gain_ref[...]
    for k, copy in enumerate(x_copies):
        copy.wait()
        part = slice(k * step, (k + 1) * step)
        inverse = row_inverse(x_ref[part])
        inverse_ref[part] = jnp.broadcast_to(inverse, (step, 128))
        normed_ref[part] = (x_ref[part].astype(F32) * inverse * gain).astype(BF16)
    for r, out_ref in enumerate(out_refs):
        target = lax.rem(lax.axis_index("seq") + r, parts)
        out_ref[:rows] = normed_ref[:, pl.ds(pl.multiple_of(target * wide, 128), wide)]
    for j, copy in enumerate(weight_copies):
        copy.wait()
        for r, out_ref in enumerate(out_refs):
            target = lax.rem(lax.axis_index("seq") + r, parts)
            for h in range(heads):
                out_ref[rows + j * depth : rows + (j + 1) * depth, h * HEAD_DIM : (h + 1) * HEAD_DIM] = weight_ref[
                    j, target * heads + h
                ]


def pack_rows_kernel(parts, with_inverse, meta_ref, edge_ref, inner_ref, *out_refs):
    rows, width = inner_ref.shape
    wide = width // parts
    edge = 1 if with_inverse else 2
    refs = out_refs[:parts]
    for r, out_ref in enumerate(refs):
        target = lax.rem(meta_ref[0] + r, parts)
        start = pl.multiple_of(target * wide, 128)

        @pl.when(meta_ref[edge] == 1)
        def use_edge():
            out_ref[:rows] = edge_ref[:, pl.ds(start, wide)]

        @pl.when(meta_ref[edge] == 0)
        def use_inner():
            out_ref[:rows] = inner_ref[:, pl.ds(start, wide)]

    def finish_with(source_ref):
        if with_inverse:
            tail = split_rows(row_inverse(source_ref[...]), EXTRA, wide)
            for out_ref in refs:
                out_ref[rows:] = jnp.zeros((EXTRA, wide), BF16)
                out_ref[rows:, :rows] = tail
        else:
            out_refs[parts][...] = source_ref[...]

    @pl.when(meta_ref[edge] == 1)
    def finish_edge():
        finish_with(edge_ref)

    @pl.when(meta_ref[edge] == 0)
    def finish_inner():
        finish_with(inner_ref)


SMEM_SPEC = pl.BlockSpec(memory_space=pltpu.SMEM)
VMEM_SPEC = pl.BlockSpec(memory_space=pltpu.VMEM)


def pack_stash(x, gain, weight, parts):
    rows, width = x.shape
    depth = weight.shape[2]
    shape = (rows + 3 * depth, width // parts)
    return pl.pallas_call(
        functools.partial(pack_stash_kernel, parts, 4),
        out_shape=(
            jax.ShapeDtypeStruct((rows, 128), F32),
            *[jax.ShapeDtypeStruct(shape, BF16) for r in range(parts)],
        ),
        in_specs=[pl.BlockSpec(memory_space=pl.ANY)] * 3,
        out_specs=(VMEM_SPEC,) * (parts + 1),
        scratch_shapes=[
            pltpu.VMEM((rows, width), BF16),
            pltpu.VMEM((1, width), F32),
            pltpu.VMEM(weight.shape, BF16),
            pltpu.VMEM((rows, width), BF16),
            pltpu.SemaphoreType.DMA((8,)),
        ],
        compiler_params=pltpu.CompilerParams(vmem_limit_bytes=58 * 1024 * 1024),
        cost_estimate=pl.CostEstimate(flops=4 * rows * width, bytes_accessed=6 * rows * width, transcendentals=0),
        name="pack_stash",
    )(x, gain, weight)


def pack_rows(meta, edge, inner, parts, with_inverse):
    rows, width = inner.shape
    shape = (rows + (EXTRA if with_inverse else 0), width // parts)
    extra = () if with_inverse else (jax.ShapeDtypeStruct((rows, width), BF16),)
    return pl.pallas_call(
        functools.partial(pack_rows_kernel, parts, with_inverse),
        out_shape=(*[jax.ShapeDtypeStruct(shape, BF16) for r in range(parts)], *extra),
        in_specs=[SMEM_SPEC, VMEM_SPEC, VMEM_SPEC],
        out_specs=(VMEM_SPEC,) * (parts + len(extra)),
        compiler_params=pltpu.CompilerParams(vmem_limit_bytes=VMEM_LIMIT),
        cost_estimate=pl.CostEstimate(flops=4 * rows * width, bytes_accessed=6 * rows * width, transcendentals=0),
        name="pack_inbound" if with_inverse else "pack_cotangent",
    )(meta, edge, inner)


def slot_order(parts):
    return sorted(range(parts), key=lambda r: min(r, parts - r))


def gather_rows(meta_ref, refs, rows, x_ref):
    parts = len(refs)
    for r, ref in zip(slot_order(parts), refs):
        source = lax.rem(meta_ref[0] + parts - r, parts)
        x_ref[pl.ds(pl.multiple_of(source * rows, rows), rows)] = ref[:rows]


def gather_weight(meta_ref, refs, rows, weight_ref):
    parts = len(refs)
    depth = HEAD_DIM // parts
    for r, ref in zip(slot_order(parts), refs):
        source = lax.rem(meta_ref[0] + parts - r, parts)
        depth_at = pl.ds(pl.multiple_of(source * depth, depth), depth)
        for j in range(3):
            weight_ref[depth_at, j * HEAD_DIM : (j + 1) * HEAD_DIM] = ref[
                rows + j * depth : rows + (j + 1) * depth
            ]


def gather_inverse(meta_ref, refs, rows, inverse_ref):
    parts = len(refs)

    @pl.when(pl.program_id(0) == 0)
    def spread_inverse():
        for r, ref in zip(slot_order(parts), refs):
            source = lax.rem(meta_ref[0] + parts - r, parts)
            tail = ref[rows : rows + EXTRA].astype(F32)
            inverse_ref[pl.ds(pl.multiple_of(source * rows, rows), rows)] = column_of(
                tail[:1] + tail[1:2] + tail[2:3], rows
            )


def block_mask(first_query, tokens):
    key = lax.broadcasted_iota(jnp.int32, (1, WINDOW), 1) + (first_query - RADIUS)
    return jnp.where((key >= 0) & (key < tokens), 0.0, masked_score).astype(F32)


def edge_bias(bias, first, tokens):
    if first < RADIUS or first + ROW_BLOCK + RADIUS > tokens:
        return bias + block_mask(first, tokens)
    return bias


def padded(rows):
    edge = jnp.zeros((RADIUS, rows.shape[1]), rows.dtype)
    return jnp.concatenate([edge, rows, edge], axis=0)


def heads_backward_kernel(parts, rows, meta_ref, *refs):
    a_refs, c_refs = refs[:parts], refs[parts : 2 * parts]
    gain_ref, offset_ref, onehot_ref, after_ref = refs[2 * parts : 2 * parts + 4]
    out_refs = refs[2 * parts + 4 : 3 * parts + 4]
    gain_grad_ref, x_ref, weight_ref, cot_ref, grad_ref, part_ref, bias_ref = refs[3 * parts + 4 :]
    tokens = rows * parts
    depth = HEAD_DIM // parts
    scale = HEAD_DIM ** (-0.5)
    gather_rows(meta_ref, a_refs, rows, x_ref)
    gather_weight(meta_ref, a_refs, rows, weight_ref)
    gather_rows(meta_ref, c_refs, rows, cot_ref)
    weight = weight_ref[...]
    normed = x_ref[...]
    query = dot_nn(normed, weight[:, :HEAD_DIM]).astype(BF16)
    key = padded(dot_nn(normed, weight[:, HEAD_DIM : 2 * HEAD_DIM]).astype(BF16))
    value = padded(dot_nn(normed, weight[:, 2 * HEAD_DIM :]).astype(BF16))
    bias = toeplitz(offset_ref[0])
    blocks = tokens // ROW_BLOCK
    starts = range(0, tokens, ROW_BLOCK)
    cot = cot_ref[...]
    query_rows = [query[f : f + ROW_BLOCK] for f in starts]
    cot_rows = [cot[f : f + ROW_BLOCK] for f in starts]
    products = [dot_nt(rows_q, key[f : f + WINDOW]) for f, rows_q in zip(starts, query_rows)]
    grad_probs = [dot_nt(rows_c, value[f : f + WINDOW]) for f, rows_c in zip(starts, cot_rows)]
    packed, grad_packed, score_sum = [], [], None
    for f, product, grads in zip(starts, products, grad_probs):
        probs = score_probs(product, edge_bias(bias, f, tokens))
        delta = jnp.sum(probs * grads, axis=-1, keepdims=True)
        grad_scores = probs * (grads - delta)
        score_sum = grad_scores if score_sum is None else score_sum + grad_scores
        packed.append(probs.astype(BF16))
        grad_packed.append(grad_scores.astype(BF16))
    grad_query = [dot_nn(part, key[f : f + WINDOW]) for f, part in zip(starts, grad_packed)]
    grad_key = [dot_tn(part, rows_q) for part, rows_q in zip(grad_packed, query_rows)]
    grad_value = [dot_tn(part, rows_c) for part, rows_c in zip(packed, cot_rows)]

    def joined(pieces):
        units = []
        for u in range((tokens + 2 * RADIUS) // ROW_BLOCK):
            total = None
            for b in range(blocks):
                if 0 <= u - b < WINDOW // ROW_BLOCK:
                    piece = pieces[b][(u - b) * ROW_BLOCK : (u - b + 1) * ROW_BLOCK]
                    total = piece if total is None else total + piece
            units.append(total)
        return jnp.concatenate(units, axis=0)[RADIUS : RADIUS + tokens]

    dqkv = jnp.concatenate(
        [
            (jnp.concatenate(grad_query, axis=0) * scale).astype(BF16),
            (joined(grad_key) * scale).astype(BF16),
            joined(grad_value).astype(BF16),
        ],
        axis=1,
    )
    grad_normed = dot_nt(dqkv, weight)
    gain_grad_ref[...] = jnp.sum(grad_normed * normed.astype(F32), axis=0, keepdims=True) / gain_ref[...]
    grad_ref[...] = grad_normed
    part_ref[...] = dot_tn(normed, dqkv)
    bias_grad = jnp.sum(onehot_ref[...] * diagonal_sums(score_sum), axis=1, keepdims=True)
    bias_ref[...] = jnp.broadcast_to(bias_grad, bias_ref.shape)
    buckets = bias_ref.shape[0] // parts
    for r, out_ref in enumerate(out_refs):
        source = lax.rem(meta_ref[0] + parts - r, parts)
        out_ref[:rows] = grad_ref[pl.ds(pl.multiple_of(source * rows, rows), rows)].astype(BF16)
        for j in range(3):
            out_ref[rows + j * depth : rows + (j + 1) * depth] = part_ref[
                pl.ds(pl.multiple_of(source * depth, depth), depth), j * HEAD_DIM : (j + 1) * HEAD_DIM
            ].astype(BF16)
        share = bias_ref[pl.ds(pl.multiple_of(source * buckets, buckets), buckets)]
        out_ref[rows + 3 * depth :] = share.astype(BF16)


def head_column(rows, first=0):
    return pl.BlockSpec((rows, HEAD_DIM), lambda i, meta: (0, i + first))


def whole_column(rows, heads, first=0):
    return pl.BlockSpec((rows, HEAD_DIM), lambda i, meta: (0, meta[0] * heads + first + i))


def offset_spec(heads, first=0):
    return pl.BlockSpec((1, 1, WINDOW), lambda i, meta: (meta[0] * heads + first + i, 0, 0))


def heads_backward(meta, a_slots, c_slots, gain, offsets, onehot, after, heads, first, count):
    parts = len(a_slots)
    rows = c_slots[0].shape[0]
    tokens = rows * parts
    buckets = onehot.shape[0]
    packed = a_slots[0].shape[0]
    made = packed + buckets // parts
    width = count * HEAD_DIM
    return pl.pallas_call(
        functools.partial(heads_backward_kernel, parts, rows),
        out_shape=(
            *[jax.ShapeDtypeStruct((made, width), BF16) for r in range(parts)],
            jax.ShapeDtypeStruct((1, width), F32),
        ),
        grid_spec=pltpu.PrefetchScalarGridSpec(
            num_scalar_prefetch=1,
            grid=(count,),
            in_specs=[
                *[head_column(packed, first)] * parts,
                whole_column(rows, heads, first),
                *[head_column(rows, first)] * (parts - 1),
                whole_column(1, heads, first),
                offset_spec(heads, first),
                pl.BlockSpec((buckets, WINDOW), lambda i, meta: (0, 0)),
                pl.BlockSpec(memory_space=pl.ANY),
            ],
            out_specs=(*[head_column(made)] * parts, head_column(1)),
            scratch_shapes=[
                pltpu.VMEM((tokens, HEAD_DIM), BF16),
                pltpu.VMEM((HEAD_DIM, 3 * HEAD_DIM), BF16),
                pltpu.VMEM((tokens, HEAD_DIM), BF16),
                pltpu.VMEM((tokens, HEAD_DIM), F32),
                pltpu.VMEM((HEAD_DIM, 3 * HEAD_DIM), F32),
                pltpu.VMEM((buckets, HEAD_DIM), F32),
            ],
        ),
        compiler_params=pltpu.CompilerParams(vmem_limit_bytes=VMEM_LIMIT),
        cost_estimate=pl.CostEstimate(
            flops=count * tokens * 400_000, bytes_accessed=tokens * width, transcendentals=0
        ),
        name="heads_backward",
    )(meta, *a_slots, *c_slots, gain, offsets, onehot, after)


def heads_forward_kernel(parts, rows, meta_ref, *refs):
    a_refs, i_refs = refs[:parts], refs[parts : 2 * parts]
    gain_ref, offset_ref = refs[2 * parts : 2 * parts + 2]
    out_refs = refs[2 * parts + 2 : 3 * parts + 2]
    inverse_ref, x_ref, weight_ref, made_ref, square_ref = refs[3 * parts + 2 :]
    tokens = rows * parts
    gather_rows(meta_ref, i_refs, rows, x_ref)
    gather_weight(meta_ref, a_refs, rows, weight_ref)
    gather_inverse(meta_ref, i_refs, rows, inverse_ref)
    weight = weight_ref[...]
    normed = (x_ref[...].astype(F32) * inverse_ref[...] * gain_ref[...]).astype(BF16)
    query = dot_nn(normed, weight[:, :HEAD_DIM]).astype(BF16)
    key = padded(dot_nn(normed, weight[:, HEAD_DIM : 2 * HEAD_DIM]).astype(BF16))
    value = padded(dot_nn(normed, weight[:, 2 * HEAD_DIM :]).astype(BF16))
    bias = toeplitz(offset_ref[0])
    starts = range(0, tokens, ROW_BLOCK)
    products = [dot_nt(query[f : f + ROW_BLOCK], key[f : f + WINDOW]) for f in starts]
    packed = [
        score_probs(product, edge_bias(bias, f, tokens)).astype(BF16) for f, product in zip(starts, products)
    ]
    attended = [dot_nn(part, value[f : f + WINDOW]) for f, part in zip(starts, packed)]
    for f, part in zip(starts, attended):
        made_ref[f : f + ROW_BLOCK] = (x_ref[f : f + ROW_BLOCK].astype(F32) + part).astype(BF16)
    made = made_ref[...].astype(F32)
    squares = made * made

    @pl.when(pl.program_id(0) == 0)
    def first_head():
        square_ref[...] = squares

    @pl.when(pl.program_id(0) > 0)
    def later_head():
        square_ref[...] += squares

    for r, out_ref in enumerate(out_refs):
        source = lax.rem(meta_ref[0] + parts - r, parts)
        out_ref[:rows] = made_ref[pl.ds(pl.multiple_of(source * rows, rows), rows)]

    @pl.when(pl.program_id(0) < pl.num_programs(0) - 1)
    def no_sums():
        for out_ref in out_refs:
            out_ref[rows:] = jnp.zeros((EXTRA, HEAD_DIM), BF16)

    @pl.when(pl.program_id(0) == pl.num_programs(0) - 1)
    def last_head():
        rest = jnp.sum(jnp.transpose(square_ref[...]), axis=0, keepdims=True)
        at_row = lax.broadcasted_iota(jnp.int32, (EXTRA, rows), 0)
        tail = jnp.zeros((EXTRA, rows), F32)
        for k in range(2):
            piece = rest.astype(BF16).astype(F32)
            rest = rest - piece
            for part in range(parts):
                row = jnp.broadcast_to(piece[:, part * rows : (part + 1) * rows], (EXTRA, rows))
                tail = jnp.where(at_row == 2 * part + k, row, tail)
        for out_ref in out_refs:
            out_ref[rows:] = tail.astype(BF16)


def heads_forward(meta, a_slots, i_slots, gain, offsets, heads, rows):
    parts = len(a_slots)
    tokens = rows * parts
    packed = a_slots[0].shape[0]
    width = heads * HEAD_DIM
    return pl.pallas_call(
        functools.partial(heads_forward_kernel, parts, rows),
        out_shape=(
            *[jax.ShapeDtypeStruct((rows + EXTRA, width), BF16) for r in range(parts)],
        ),
        grid_spec=pltpu.PrefetchScalarGridSpec(
            num_scalar_prefetch=1,
            grid=(heads,),
            in_specs=[
                *[head_column(packed)] * parts,
                *[head_column(i_slots[0].shape[0])] * parts,
                whole_column(1, heads),
                offset_spec(heads),
            ],
            out_specs=(head_column(rows + EXTRA),) * parts,
            scratch_shapes=[
                pltpu.VMEM((tokens, HEAD_DIM), F32),
                pltpu.VMEM((tokens, HEAD_DIM), BF16),
                pltpu.VMEM((HEAD_DIM, 3 * HEAD_DIM), BF16),
                pltpu.VMEM((tokens, HEAD_DIM), BF16),
                pltpu.VMEM((tokens, HEAD_DIM), F32),
            ],
        ),
        compiler_params=pltpu.CompilerParams(vmem_limit_bytes=VMEM_LIMIT),
        cost_estimate=pl.CostEstimate(
            flops=heads * tokens, bytes_accessed=tokens, transcendentals=0
        ),
        name="heads_forward",
    )(meta, *a_slots, *i_slots, gain, offsets)


def memory_kernel(parts, width, meta_ref, *refs):
    out_refs, other_refs = refs[:parts], refs[parts : 2 * parts - 1]
    gain_ref, *share_refs, memory_ref = refs[2 * parts - 1 :]
    wide = memory_ref.shape[1]
    rows = memory_ref.shape[0] // parts
    total = None
    for ref in (out_refs[0], *other_refs):
        tail = ref[rows:, wide - rows :].astype(F32)
        pieces = [tail[2 * p : 2 * p + 1] + tail[2 * p + 1 : 2 * p + 2] for p in range(parts)]
        row = jnp.concatenate(pieces, axis=1)
        total = row if total is None else total + row
    inverse = lax.rsqrt(total / width + eps_norm)
    gain = gain_ref[:, pl.ds(pl.multiple_of(meta_ref[0] * wide, 128), wide)]
    spread_inverse = jnp.transpose(jnp.broadcast_to(inverse, (128, inverse.shape[1])))
    for r, out_ref in enumerate(out_refs):
        source = lax.rem(meta_ref[0] + parts - r, parts)
        memory_ref[pl.ds(pl.multiple_of(source * rows, rows), rows)] = out_ref[:rows]
    made = memory_ref[...].astype(F32)
    memory_ref[...] = (made * spread_inverse[:, :1] * gain).astype(BF16)
    for k, share_ref in enumerate(share_refs):
        size = share_ref.shape[0]
        share_ref[...] = memory_ref[k * size : (k + 1) * size]


def memory_rows(meta, outs, others, gain, width, shares):
    parts = len(outs)
    rows, wide = outs[0].shape[0] - EXTRA, outs[0].shape[1]
    return pl.pallas_call(
        functools.partial(memory_kernel, parts, width),
        out_shape=[jax.ShapeDtypeStruct((rows * parts // shares, wide), BF16)] * shares,
        in_specs=[SMEM_SPEC] + [VMEM_SPEC] * (2 * parts),
        out_specs=[VMEM_SPEC] * shares,
        scratch_shapes=[pltpu.VMEM((rows * parts, wide), BF16)],
        compiler_params=pltpu.CompilerParams(vmem_limit_bytes=VMEM_LIMIT),
        cost_estimate=pl.CostEstimate(flops=rows, bytes_accessed=rows, transcendentals=0),
        name="memory_rows",
    )(meta, *outs, *others, gain)


def place_kernel(parts, meta_ref, *refs):
    out_ref = refs[parts]
    wide = refs[0].shape[1]
    for r, ref in zip(slot_order(parts), refs):
        source = lax.rem(meta_ref[0] + r, parts)
        out_ref[:, pl.ds(pl.multiple_of(source * wide, 128), wide)] = ref[: out_ref.shape[0]]


def place_columns(meta, slots):
    parts = len(slots)
    rows, wide = slots[0].shape[0] - EXTRA, slots[0].shape[1]
    return pl.pallas_call(
        functools.partial(place_kernel, parts),
        out_shape=jax.ShapeDtypeStruct((rows, wide * parts), BF16),
        in_specs=[SMEM_SPEC] + [VMEM_SPEC] * parts,
        out_specs=VMEM_SPEC,
        compiler_params=pltpu.CompilerParams(vmem_limit_bytes=VMEM_LIMIT),
        cost_estimate=pl.CostEstimate(flops=0, bytes_accessed=rows, transcendentals=0),
        name="place_columns",
    )(meta, *slots)


def store_weights(g_ref, weight_ref, rows, depth, heads):
    for h in range(heads):
        for j in range(3):
            weight_ref[j, h] = g_ref[
                rows + j * depth : rows + (j + 1) * depth, h * HEAD_DIM : (h + 1) * HEAD_DIM
            ].astype(F32)


def weight_copies(weight_ref, weight_hbm, first_head, heads, sems):
    return [
        pltpu.make_async_copy(weight_ref.at[j], weight_hbm.at[j, pl.ds(first_head, heads)], sems.at[j])
        for j in range(3)
    ]


def add_bias(bias, g_ref, first_row, first_head, heads):
    lane = lax.broadcasted_iota(jnp.int32, bias.shape, 1)
    shares = g_ref[first_row:].astype(F32)
    for h in range(heads):
        bias = jnp.where(lane == first_head + h, shares[:, h * HEAD_DIM : (h + 1) * HEAD_DIM], bias)
    return bias


def early_finish_kernel(parts, meta_ref, *refs):
    g_refs = refs[: parts - 1]
    x_ref, inverse_ref, gain_ref, cot_ref = refs[parts - 1 : parts + 3]
    base_ref, row_ref, weight_hbm, bias_ref, weight_ref, sems = refs[parts + 3 :]
    rows, width = x_ref.shape
    wide = width // parts
    heads = wide // HEAD_DIM
    depth = HEAD_DIM // parts
    order = slot_order(parts)
    inverse = inverse_ref[:, :1]
    bias = jnp.zeros(bias_ref.shape, F32)
    total = jnp.zeros((rows, 1), F32)
    copies = []
    for k, g_ref in enumerate(g_refs):
        source = lax.rem(meta_ref[0] + order[k], parts)
        store_weights(g_ref, weight_ref.at[k], rows, depth, heads)
        for copy in weight_copies(weight_ref.at[k], weight_hbm, source * heads, heads, sems.at[k]):
            copy.start()
            copies.append(copy)
        bias = add_bias(bias, g_ref, rows + 3 * depth, source * heads, heads)
        columns = pl.ds(pl.multiple_of(source * wide, 128), wide)
        scaled = g_ref[:rows].astype(F32) * gain_ref[:, columns]
        total = total + jnp.sum(scaled * x_ref[:, columns].astype(F32), axis=-1, keepdims=True)
        base_ref[:, columns] = cot_ref[:, columns].astype(F32) + inverse * scaled
    last = pl.ds(pl.multiple_of(lax.rem(meta_ref[0] + order[-1], parts) * wide, 128), wide)
    base_ref[:, last] = cot_ref[:, last].astype(F32)
    row_ref[...] = jnp.broadcast_to(total, row_ref.shape)
    bias_ref[...] = bias
    for copy in copies:
        copy.wait()


def late_finish_kernel(parts, meta_ref, *refs):
    base_ref, row_ref, early_bias_ref, g_ref, x_ref, inverse_ref, gain_ref, early_hbm = refs[:8]
    out_ref, weight_hbm, bias_ref, weight_ref, sems = refs[8:]
    rows, width = x_ref.shape
    wide = width // parts
    heads = wide // HEAD_DIM
    depth = HEAD_DIM // parts
    source = lax.rem(meta_ref[0] + slot_order(parts)[-1], parts)
    store_weights(g_ref, weight_ref, rows, depth, heads)
    copies = weight_copies(weight_ref, weight_hbm, source * heads, heads, sems)
    for copy in copies:
        copy.start()
    bias = add_bias(early_bias_ref[...], g_ref, rows + 3 * depth, source * heads, heads)
    bias_ref[...] = bias[:, : bias_ref.shape[1]]
    columns = pl.ds(pl.multiple_of(source * wide, 128), wide)
    inverse = inverse_ref[:, :1]
    scaled = g_ref[:rows].astype(F32) * gain_ref[:, columns]
    total = row_ref[:, :1] + jnp.sum(scaled * x_ref[:, columns].astype(F32), axis=-1, keepdims=True)
    factor = inverse * inverse * inverse * (total / width)
    out_ref[...] = (base_ref[...] - x_ref[...].astype(F32) * factor).astype(BF16)
    out_ref[:, columns] = (
        base_ref[:, columns] + (inverse * scaled - x_ref[:, columns].astype(F32) * factor)
    ).astype(BF16)
    for copy in copies:
        copy.wait()


def heads_finish(meta, g_slots, x, inverse, gain, cotangent, buckets):
    parts = len(g_slots)
    rows, width = x.shape
    heads = width // HEAD_DIM
    depth = HEAD_DIM // parts
    any_spec = pl.BlockSpec(memory_space=pl.ANY)
    weight = jax.ShapeDtypeStruct((3, heads, depth, HEAD_DIM), F32)
    piece = (3, heads // parts, depth, HEAD_DIM)
    cost = pl.CostEstimate(flops=rows * width, bytes_accessed=rows * width, transcendentals=0)
    params = pltpu.CompilerParams(vmem_limit_bytes=VMEM_LIMIT)
    base, row, early, bias = pl.pallas_call(
        functools.partial(early_finish_kernel, parts),
        out_shape=(
            jax.ShapeDtypeStruct((rows, width), F32),
            jax.ShapeDtypeStruct((rows, 128), F32),
            weight,
            jax.ShapeDtypeStruct((buckets // parts, HEAD_DIM), F32),
        ),
        in_specs=[SMEM_SPEC] + [VMEM_SPEC] * (parts + 3),
        out_specs=(VMEM_SPEC, VMEM_SPEC, any_spec, VMEM_SPEC),
        scratch_shapes=[pltpu.VMEM((parts - 1, *piece), F32), pltpu.SemaphoreType.DMA((parts - 1, 3))],
        compiler_params=params,
        cost_estimate=cost,
        name="early_finish",
    )(meta, *g_slots[:-1], x, inverse, gain, cotangent)
    return pl.pallas_call(
        functools.partial(late_finish_kernel, parts),
        out_shape=(
            jax.ShapeDtypeStruct((rows, width), BF16),
            weight,
            jax.ShapeDtypeStruct((buckets // parts, heads), F32),
        ),
        in_specs=[SMEM_SPEC] + [VMEM_SPEC] * 7 + [any_spec],
        out_specs=(VMEM_SPEC, any_spec, VMEM_SPEC),
        input_output_aliases={8: 1},
        scratch_shapes=[pltpu.VMEM(piece, F32), pltpu.SemaphoreType.DMA((3,))],
        compiler_params=params,
        cost_estimate=cost,
        name="late_finish",
    )(meta, base, row, bias, g_slots[-1], x, inverse, gain, early)


def offset_table(rel_bias):
    onehot = jnp.asarray(bucket_onehot(rel_bias.shape[0]))
    by_offset = jnp.dot(onehot, rel_bias, precision=lax.Precision.HIGHEST).T
    inside = jnp.arange(WINDOW, dtype=jnp.int32) <= 2 * RADIUS
    return jnp.where(inside[None, :], by_offset, masked_score)[:, None, :]


def shifted(value, axis, steps):
    count = lax.axis_size(axis)
    first, last = (max(0, -steps), min(count, count - steps))
    return lax.ppermute(value, axis, [(source, source + steps) for source in range(first, last)])


def spread_memory(shares, section, sections):
    last = sections - 1
    couple = jnp.where(section == last, shares[-1], 0)
    for s, share in enumerate(shares[:-1]):
        couple = couple + lax.ppermute(share, "section", [(last, 2 * s + 1)])
    half = couple.shape[0] // 2
    even = lax.ppermute(couple[:half], "section", [(s + 1, s) for s in range(0, sections, 2)])
    return jnp.where(section % 2 == 0, even, couple[half:])


def heads_body(
    embedded, carried, stash, returned, loss_grad, qkv_weight, rel_bias, norm_gain, final_gain
):
    section = lax.axis_index("section")
    sections = lax.axis_size("section")
    parts = lax.axis_size("seq")
    rows, width = embedded.shape
    heads = width // HEAD_DIM // parts
    buckets = rel_bias.shape[1]
    meta = jnp.stack(
        [lax.axis_index("seq"), section == 0, section == sections - 1]
    ).astype(jnp.int32)

    def exchanged(sends, direction):
        return [
            lax.ppermute(sends[r], "seq", [(i, (i + direction * r) % parts) for i in range(parts)]) if r else sends[0]
            for r in slot_order(parts)
        ]

    inverse_b, *a_sends = pack_stash(stash[0], norm_gain, qkv_weight[0], parts)
    a_slots = exchanged(a_sends, 1)
    arrived = shifted(carried[0], "section", 1)
    came_back = shifted(returned[0], "section", -1)
    i_slots = exchanged(pack_rows(meta, embedded, arrived, parts, True), 1)
    *c_sends, cotangent = pack_rows(meta, loss_grad, came_back, parts, False)
    c_slots = exchanged(c_sends, 1)
    c_slots[0] = cotangent

    offsets = offset_table(rel_bias[0])
    onehot = jnp.asarray(bucket_onehot(buckets).T)
    o_sends = heads_forward(meta, a_slots, i_slots, norm_gain, offsets, heads, rows)
    o_slots = exchanged(o_sends, -1)

    *g_sends, gain_grad = heads_backward(
        meta, a_slots, c_slots, norm_gain, offsets, onehot, o_sends[0], heads, 0, heads
    )
    g_sends, o_slots = lax.optimization_barrier((g_sends, o_slots))
    g_slots = exchanged(g_sends, -1)
    output = place_columns(meta, o_slots)
    shares = memory_rows(meta, o_sends, o_slots[1:], final_gain[None], width, sections // 2)
    memory = spread_memory(shares, section, sections)

    input_grad, weight_grad, bias_grad = heads_finish(
        meta, g_slots, stash[0], inverse_b, norm_gain, cotangent, buckets
    )
    return (
        output[None],
        input_grad[None],
        weight_grad[None],
        bias_grad[None],
        gain_grad,
        memory,
    )


def tokens_body(
    embedded, carried, stash, returned, loss_grad, qkv_weight, rel_bias, norm_gain, final_gain
):
    section_index = lax.axis_index("section")
    section_count = lax.axis_size("section")
    seq_index = lax.axis_index("seq")
    seq_count = lax.axis_size("seq")
    rows, width = embedded.shape
    heads = width // HEAD_DIM
    tokens = rows * seq_count
    shard = qkv_weight[0]
    up = [(i, i + 1) for i in range(seq_count - 1)]
    down = [(j, i) for i, j in up]
    group = 4 if heads % 4 == 0 else 1

    own_b, inverse_b = norm_rows(stash[0], norm_gain)
    before_b = lax.ppermute(own_b[rows - RADIUS :], "seq", up)
    after_b = lax.ppermute(own_b[:RADIUS], "seq", down)
    slots = [lax.all_gather(shard, "seq", axis=2, tiled=True)]

    section_up = [(i, (i + 1) % section_count) for i in range(section_count)]
    section_down = [(j, i) for i, j in section_up]
    inbound = lax.ppermute(
        jnp.where(section_index == section_count - 1, embedded, carried[0]), "section", section_up
    )
    cotangent = lax.ppermute(
        jnp.where(section_index == 0, loss_grad, returned[0]), "section", section_down
    )

    onehot = jnp.asarray(bucket_onehot(rel_bias.shape[1]))
    offsets = offset_table(rel_bias[0])
    first_key = RADIUS - seq_index * rows
    meta = jnp.stack([seq_index, first_key, first_key + tokens]).astype(jnp.int32)

    own_a, unused = norm_rows(inbound, norm_gain)
    before_a = lax.ppermute(own_a[rows - RADIUS :], "seq", up)
    after_a = lax.ppermute(own_a[:RADIUS], "seq", down)

    grad_own, lower, upper, offset_grad, *parts = backward_attention(
        meta, before_b, own_b, after_b, cotangent, offsets, slots, group, 0, heads
    )
    from_before = lax.ppermute(upper, "seq", up)
    from_after = lax.ppermute(lower, "seq", down)
    weight_sum = lax.psum_scatter(parts[0], "seq", scatter_dimension=2, tiled=True).astype(F32)

    output = forward_attention(meta, before_a, own_a, after_a, inbound, offsets, slots, group)
    final_normed, unused = norm_rows(output, final_gain[None])
    relaid = lax.all_to_all(final_normed, "seq", split_axis=1, concat_axis=0, tiled=True)
    kept = jnp.where(section_index == section_count - 1, relaid, jnp.zeros_like(relaid))
    memory = lax.psum_scatter(kept, "section", scatter_dimension=0, tiled=True)

    input_grad, gain_part = finish(
        grad_own, from_before, from_after, stash[0], inverse_b, norm_gain, cotangent
    )
    bias_part = jnp.dot(
        offset_grad[:, 0, :], onehot, precision=lax.Precision.HIGHEST
    ).T
    bias_sum = lax.psum_scatter(
        bias_part.astype(BF16), "seq", scatter_dimension=0, tiled=True
    ).astype(F32)
    gain_sum = lax.psum_scatter(
        gain_part.astype(BF16), "seq", scatter_dimension=1, tiled=True
    ).astype(F32)
    return (output[None], input_grad[None], weight_sum[None], bias_sum[None], gain_sum, memory)


def choose_body(embedded, carried, stash, returned, loss_grad, qkv_weight, rel_bias, norm_gain, final_gain):
    parts = lax.axis_size("seq")
    rows, width = embedded.shape
    even = parts > 1 and width % (HEAD_DIM * parts) == 0 and HEAD_DIM % (32 * parts) == 0 and rows == 128
    sections = lax.axis_size("section")
    even = even and sections % 2 == 0
    even = even and rel_bias.shape[1] == 8 * parts and width <= 128 * HEAD_DIM and rows * parts % (16 * sections) == 0
    chosen = heads_body if even else tokens_body
    return chosen(
        embedded, carried, stash, returned, loss_grad, qkv_weight, rel_bias, norm_gain, final_gain
    )


def solution(mesh):
    in_specs = (
        P("seq", None),
        P("section", "seq", None),
        P("section", "seq", None),
        P("section", "seq", None),
        P("seq", None),
        P("section", None, None, "seq", None),
        P("section", None, None),
        P("section", None),
        P(),
    )
    out_specs = (
        P("section", "seq", None),
        P("section", "seq", None),
        P("section", None, None, "seq", None),
        P("section", "seq", None),
        P("section", "seq"),
        P("section", "seq"),
    )
    return jax.shard_map(choose_body, mesh=mesh, in_specs=in_specs, out_specs=out_specs, check_vma=False)
```

```python
import functools

import jax
import jax.numpy as jnp
import numpy as np
from jax import lax
from jax.experimental import pallas as pl
from jax.experimental.pallas import tpu as pltpu
from jax.sharding import PartitionSpec as P

RADIUS = 96
HEAD_DIM = 128
ROW_BLOCK = 64
WINDOW = ROW_BLOCK + 2 * RADIUS
eps_norm = 1e-06
bucket_edges = (1, 2, 3, 4, 5, 6, 7, 8, 11, 16, 22, 32, 45, 64, 90)
masked_score = -1e30
F32 = jnp.float32
BF16 = jnp.bfloat16
VMEM_LIMIT = 24 * 1024 * 1024
EXTRA = 8


def bucket_onehot(bucket_count):
    offsets = np.arange(WINDOW) - RADIUS
    magnitude = np.abs(offsets)
    counted = np.zeros(offsets.shape, np.int32)
    for threshold in bucket_edges:
        counted = counted + (magnitude >= threshold)
    counted = counted + 16 * (offsets > 0)
    onehot = (counted[:, None] == np.arange(bucket_count)[None, :]) & (magnitude <= RADIUS)[:, None]
    return onehot.astype(np.float32)


def dot_nn(a, b):
    return lax.dot_general(a, b, (((1,), (0,)), ((), ())), preferred_element_type=F32)


def dot_nt(a, b):
    return lax.dot_general(a, b, (((1,), (1,)), ((), ())), preferred_element_type=F32)


def dot_tn(a, b):
    return lax.dot_general(a, b, (((0,), (0,)), ((), ())), preferred_element_type=F32)


def norm_kernel(x_ref, gain_ref, normed_ref, inverse_ref):
    x = x_ref[...].astype(F32)
    inverse = lax.rsqrt(jnp.mean(x * x, axis=-1, keepdims=True) + eps_norm)
    normed_ref[...] = (x * inverse * gain_ref[...]).astype(BF16)
    inverse_ref[...] = jnp.broadcast_to(inverse, inverse_ref.shape)


def norm_rows(x, gain):
    rows, width = x.shape
    return pl.pallas_call(
        norm_kernel,
        out_shape=(
            jax.ShapeDtypeStruct((rows, width), BF16),
            jax.ShapeDtypeStruct((rows, 128), F32),
        ),
        compiler_params=pltpu.CompilerParams(vmem_limit_bytes=VMEM_LIMIT),
        cost_estimate=pl.CostEstimate(
            flops=6 * rows * width, bytes_accessed=4 * rows * width, transcendentals=rows
        ),
        name="norm_rows",
    )(x, gain)


def load_weight(meta_ref, slot_refs, weight_ref, head, slots):
    depth = HEAD_DIM // slots
    for r, slot_ref in enumerate(slot_refs):
        if slots == 1:
            start = 0
        else:
            start = pl.multiple_of(lax.rem(meta_ref[0] + r, slots) * depth, depth)
        for j in range(3):
            weight_ref[head, pl.ds(start, depth), j * HEAD_DIM : (j + 1) * HEAD_DIM] = slot_ref[j, head]
    return weight_ref[head]


def key_mask(meta_ref, first_key):
    key = lax.broadcasted_iota(jnp.int32, (1, WINDOW), 1) + first_key
    inside = (key >= meta_ref[1]) & (key < meta_ref[2])
    return jnp.where(inside, 0.0, masked_score).astype(F32)


def toeplitz(row):
    return pltpu.roll(
        jnp.broadcast_to(row, (ROW_BLOCK, WINDOW)), 0, 1, stride=1, stride_axis=0
    )


def diagonal_sums(values):
    total = values[:8]
    for a in range(1, ROW_BLOCK // 8):
        total = total + pltpu.roll(values[8 * a : 8 * a + 8], WINDOW - 8 * a, 1)
    row = lax.broadcasted_iota(jnp.int32, total.shape, 0)
    for bit in (1, 2, 4):
        total = jnp.where((row & bit) != 0, pltpu.roll(total, WINDOW - bit, 1), total)
    return jnp.sum(total, axis=0, keepdims=True)


def block_probs(query_rows, key_rows, bias):
    return score_probs(dot_nt(query_rows, key_rows), bias)


def score_probs(products, bias):
    scores = products * (HEAD_DIM ** (-0.5)) + bias
    weights = jnp.exp(scores - jnp.max(scores, axis=-1, keepdims=True))
    return weights * (1.0 / jnp.sum(weights, axis=-1, keepdims=True))


def forward_kernel(slots, group, meta_ref, before_ref, own_ref, after_ref, x_ref, offset_ref, *rest):
    slot_refs = rest[:slots]
    out_ref, weight_ref = rest[slots:]
    rows = own_ref.shape[0]
    blocks = rows // ROW_BLOCK
    masks = [key_mask(meta_ref, b * ROW_BLOCK) for b in range(blocks)]
    for g in range(group):
        columns = slice(g * HEAD_DIM, (g + 1) * HEAD_DIM)
        weight = load_weight(meta_ref, slot_refs, weight_ref, g, slots)
        own = own_ref[:, columns]
        extended = jnp.concatenate([before_ref[:, columns], own, after_ref[:, columns]], axis=0)
        query = dot_nn(own, weight[:, :HEAD_DIM]).astype(BF16)
        key_value = dot_nn(extended, weight[:, HEAD_DIM:]).astype(BF16)
        key, value = key_value[:, :HEAD_DIM], key_value[:, HEAD_DIM:]
        bias = toeplitz(offset_ref[g])
        for b in range(blocks):
            first = b * ROW_BLOCK
            window = slice(first, first + WINDOW)
            probs = block_probs(query[first : first + ROW_BLOCK], key[window], bias + masks[b])
            attended = dot_nn(probs.astype(BF16), value[window])
            kept = x_ref[first : first + ROW_BLOCK, columns].astype(F32)
            out_ref[first : first + ROW_BLOCK, columns] = (kept + attended).astype(BF16)


def column_spec(rows, group, first):
    return pl.BlockSpec((rows, group * HEAD_DIM), lambda i, meta: (0, i + first))


def slot_specs(weight_slots, group):
    return [
        pl.BlockSpec((3, group, slot.shape[2], HEAD_DIM), lambda i, meta: (0, i, 0, 0))
        for slot in weight_slots
    ]


def forward_attention(meta, before, own, after, x, offsets, weight_slots, group):
    rows, width = own.shape
    heads = width // HEAD_DIM
    slots = len(weight_slots)
    return pl.pallas_call(
        functools.partial(forward_kernel, slots, group),
        out_shape=jax.ShapeDtypeStruct((rows, width), BF16),
        grid_spec=pltpu.PrefetchScalarGridSpec(
            num_scalar_prefetch=1,
            grid=(heads // group,),
            in_specs=[
                column_spec(RADIUS, group, 0),
                column_spec(rows, group, 0),
                column_spec(RADIUS, group, 0),
                column_spec(rows, group, 0),
                pl.BlockSpec((group, 1, WINDOW), lambda i, meta: (i, 0, 0)),
                *slot_specs(weight_slots, group),
            ],
            out_specs=column_spec(rows, group, 0),
            scratch_shapes=[pltpu.VMEM((group, HEAD_DIM, 3 * HEAD_DIM), BF16)],
        ),
        compiler_params=pltpu.CompilerParams(vmem_limit_bytes=VMEM_LIMIT),
        cost_estimate=pl.CostEstimate(
            flops=heads * 60_000_000, bytes_accessed=8 * rows * width, transcendentals=heads * 32768
        ),
        name="forward_attention",
    )(meta, before, own, after, x, offsets, *weight_slots)


def backward_kernel(slots, group, meta_ref, before_ref, own_ref, after_ref, cot_ref, offset_ref, *rest):
    slot_refs = rest[:slots]
    rest = rest[slots:]
    grad_ref, lower_ref, upper_ref, offset_grad_ref = rest[:4]
    part_refs = rest[4 : 4 + slots]
    weight_ref, part_ref = rest[4 + slots :]
    rows = own_ref.shape[0]
    blocks = rows // ROW_BLOCK
    scale = HEAD_DIM ** (-0.5)
    masks = [key_mask(meta_ref, b * ROW_BLOCK) for b in range(blocks)]
    for g in range(group):
        columns = slice(g * HEAD_DIM, (g + 1) * HEAD_DIM)
        weight = load_weight(meta_ref, slot_refs, weight_ref, g, slots)
        own = own_ref[:, columns]
        extended = jnp.concatenate([before_ref[:, columns], own, after_ref[:, columns]], axis=0)
        query = dot_nn(own, weight[:, :HEAD_DIM]).astype(BF16)
        key_value = dot_nn(extended, weight[:, HEAD_DIM:]).astype(BF16)
        key, value = key_value[:, :HEAD_DIM], key_value[:, HEAD_DIM:]
        bias = toeplitz(offset_ref[g])
        grad_query, grad_key, grad_value, score_sum = [], [], [], None
        for b in range(blocks):
            first = b * ROW_BLOCK
            window = slice(first, first + WINDOW)
            query_rows = query[first : first + ROW_BLOCK]
            cot_rows = cot_ref[first : first + ROW_BLOCK, columns]
            probs = block_probs(query_rows, key[window], bias + masks[b])
            grad_probs = dot_nt(cot_rows, value[window])
            delta = jnp.sum(probs * grad_probs, axis=-1, keepdims=True)
            grad_scores = probs * (grad_probs - delta)
            score_sum = grad_scores if score_sum is None else score_sum + grad_scores
            grad_packed = grad_scores.astype(BF16)
            grad_query.append(dot_nn(grad_packed, key[window]))
            grad_key.append(dot_tn(grad_packed, query_rows))
            grad_value.append(dot_tn(probs.astype(BF16), cot_rows))

        def joined(parts):
            pieces = []
            for u in range((rows + 2 * RADIUS) // ROW_BLOCK):
                total = None
                for b in range(blocks):
                    if 0 <= u - b < WINDOW // ROW_BLOCK:
                        piece = parts[b][(u - b) * ROW_BLOCK : (u - b + 1) * ROW_BLOCK]
                        total = piece if total is None else total + piece
                pieces.append(total)
            return jnp.concatenate(pieces, axis=0)

        dquery = (jnp.concatenate(grad_query, axis=0) * scale).astype(BF16)
        dkey = (joined(grad_key) * scale).astype(BF16)
        dvalue = joined(grad_value).astype(BF16)
        dkey_value = jnp.concatenate([dkey, dvalue], axis=1)
        grad_extended = dot_nt(dkey_value, weight[:, HEAD_DIM:])
        grad_ref[:, columns] = grad_extended[RADIUS : RADIUS + rows] + dot_nt(dquery, weight[:, :HEAD_DIM])
        lower_ref[:, columns] = grad_extended[:RADIUS].astype(BF16)
        upper_ref[:, columns] = grad_extended[RADIUS + rows :].astype(BF16)
        part_ref[g, :, :HEAD_DIM] = dot_tn(own, dquery)
        part_ref[g, :, HEAD_DIM:] = dot_tn(extended, dkey_value)
        depth = HEAD_DIM // slots
        for r in range(slots):
            if slots == 1:
                start = 0
            else:
                start = pl.multiple_of(lax.rem(meta_ref[0] + r, slots) * depth, depth)
            for j in range(3):
                part_refs[r][j, g] = part_ref[
                    g, pl.ds(start, depth), j * HEAD_DIM : (j + 1) * HEAD_DIM
                ].astype(part_refs[r].dtype)
        offset_grad_ref[g] = diagonal_sums(score_sum)


def backward_attention(meta, before, own, after, cotangent, offsets, weight_slots, group, first_head, heads):
    rows = own.shape[0]
    width = heads * HEAD_DIM
    slots = len(weight_slots)
    first = first_head // group
    slot_shape = weight_slots[0].shape
    part_types = [F32] + [BF16] * (slots - 1) if slots > 1 else [BF16]
    return pl.pallas_call(
        functools.partial(backward_kernel, slots, group),
        out_shape=(
            jax.ShapeDtypeStruct((rows, width), F32),
            jax.ShapeDtypeStruct((RADIUS, width), BF16),
            jax.ShapeDtypeStruct((RADIUS, width), BF16),
            jax.ShapeDtypeStruct((heads, 1, WINDOW), F32),
            *[jax.ShapeDtypeStruct(slot_shape, kind) for kind in part_types],
        ),
        grid_spec=pltpu.PrefetchScalarGridSpec(
            num_scalar_prefetch=1,
            grid=(heads // group,),
            in_specs=[
                column_spec(RADIUS, group, first),
                column_spec(rows, group, first),
                column_spec(RADIUS, group, first),
                column_spec(rows, group, first),
                pl.BlockSpec((group, 1, WINDOW), lambda i, meta: (i + first, 0, 0)),
                *slot_specs(weight_slots, group),
            ],
            out_specs=(
                column_spec(rows, group, 0),
                column_spec(RADIUS, group, 0),
                column_spec(RADIUS, group, 0),
                pl.BlockSpec((group, 1, WINDOW), lambda i, meta: (i, 0, 0)),
                *slot_specs(weight_slots, group),
            ),
            scratch_shapes=[
                pltpu.VMEM((group, HEAD_DIM, 3 * HEAD_DIM), BF16),
                pltpu.VMEM((group, HEAD_DIM, 3 * HEAD_DIM), F32),
            ],
        ),
        compiler_params=pltpu.CompilerParams(vmem_limit_bytes=VMEM_LIMIT),
        cost_estimate=pl.CostEstimate(
            flops=heads * 150_000_000, bytes_accessed=12 * rows * width, transcendentals=heads * 32768
        ),
        name="backward_attention",
    )(meta, before, own, after, cotangent, offsets, *weight_slots)


def finish_kernel(grad_ref, low_ref, high_ref, x_ref, inverse_ref, gain_ref, cot_ref, out_ref, gain_grad_ref):
    rows = x_ref.shape[0]
    grad = grad_ref[...]
    edge = jnp.zeros((rows - RADIUS, grad.shape[1]), F32)
    grad = grad + jnp.concatenate([low_ref[...].astype(F32), edge], axis=0)
    grad = grad + jnp.concatenate([edge, high_ref[...].astype(F32)], axis=0)
    x = x_ref[...].astype(F32)
    inverse = inverse_ref[:, :1]
    gain_grad_ref[...] = jnp.sum(grad * x * inverse, axis=0, keepdims=True)
    scaled = grad * gain_ref[...]
    mean = jnp.mean(scaled * x, axis=-1, keepdims=True)
    result = inverse * scaled - x * (inverse * inverse * inverse * mean)
    out_ref[...] = (cot_ref[...].astype(F32) + result).astype(BF16)


def finish(grad, low, high, x, inverse, gain, cotangent):
    rows, width = x.shape
    return pl.pallas_call(
        finish_kernel,
        out_shape=(
            jax.ShapeDtypeStruct((rows, width), BF16),
            jax.ShapeDtypeStruct((1, width), F32),
        ),
        compiler_params=pltpu.CompilerParams(vmem_limit_bytes=VMEM_LIMIT),
        cost_estimate=pl.CostEstimate(
            flops=16 * rows * width, bytes_accessed=14 * rows * width, transcendentals=0
        ),
        name="finish",
    )(grad, low, high, x, inverse, gain, cotangent)


def column_of(row, rows):
    return jnp.transpose(jnp.broadcast_to(row, (128, rows)))


def split_rows(inverse, pad_rows, width):
    high = inverse.astype(BF16)
    rest = inverse - high.astype(F32)
    middle = rest.astype(BF16)
    low = (rest - middle.astype(F32)).astype(BF16)
    wide = [jnp.transpose(jnp.broadcast_to(v.astype(F32), (v.shape[0], 128)))[:1] for v in (high, middle, low)]
    row = jnp.concatenate(wide + [jnp.zeros((pad_rows - 3, wide[0].shape[1]), F32)], axis=0)
    return row.astype(BF16)


def row_inverse(x):
    x = x.astype(F32)
    return lax.rsqrt(jnp.mean(x * x, axis=-1, keepdims=True) + eps_norm)


def pack_stash_kernel(parts, pieces, x_hbm, gain_hbm, weight_hbm, inverse_ref, *refs):
    out_refs = refs[:parts]
    x_ref, gain_ref, weight_ref, normed_ref, sems = refs[parts:]
    rows, width = x_ref.shape
    depth = weight_ref.shape[2]
    wide = width // parts
    heads = wide // HEAD_DIM
    step = rows // pieces
    gain_copy = pltpu.make_async_copy(gain_hbm, gain_ref, sems.at[0])
    x_copies = [
        pltpu.make_async_copy(x_hbm.at[pl.ds(k * step, step)], x_ref.at[pl.ds(k * step, step)], sems.at[1 + k])
        for k in range(pieces)
    ]
    weight_copies = [
        pltpu.make_async_copy(weight_hbm.at[j], weight_ref.at[j], sems.at[1 + pieces + j]) for j in range(3)
    ]
    for copy in (gain_copy, *x_copies, *weight_copies):
        copy.start()
    gain_copy.wait()
    gain = gain_ref[...]
    for k, copy in enumerate(x_copies):
        copy.wait()
        part = slice(k * step, (k + 1) * step)
        inverse = row_inverse(x_ref[part])
        inverse_ref[part] = jnp.broadcast_to(inverse, (step, 128))
        normed_ref[part] = (x_ref[part].astype(F32) * inverse * gain).astype(BF16)
    for r, out_ref in enumerate(out_refs):
        target = lax.rem(lax.axis_index("seq") + r, parts)
        out_ref[:rows] = normed_ref[:, pl.ds(pl.multiple_of(target * wide, 128), wide)]
    for j, copy in enumerate(weight_copies):
        copy.wait()
        for r, out_ref in enumerate(out_refs):
            target = lax.rem(lax.axis_index("seq") + r, parts)
            for h in range(heads):
                out_ref[rows + j * depth : rows + (j + 1) * depth, h * HEAD_DIM : (h + 1) * HEAD_DIM] = weight_ref[
                    j, target * heads + h
                ]


def pack_rows_kernel(parts, with_inverse, meta_ref, edge_ref, inner_ref, *out_refs):
    rows, width = inner_ref.shape
    wide = width // parts
    edge = 1 if with_inverse else 2
    refs = out_refs[:parts]
    for r, out_ref in enumerate(refs):
        target = lax.rem(meta_ref[0] + r, parts)
        start = pl.multiple_of(target * wide, 128)

        @pl.when(meta_ref[edge] == 1)
        def use_edge():
            out_ref[:rows] = edge_ref[:, pl.ds(start, wide)]

        @pl.when(meta_ref[edge] == 0)
        def use_inner():
            out_ref[:rows] = inner_ref[:, pl.ds(start, wide)]

    def finish_with(source_ref):
        if with_inverse:
            tail = split_rows(row_inverse(source_ref[...]), EXTRA, wide)
            for out_ref in refs:
                out_ref[rows:] = jnp.zeros((EXTRA, wide), BF16)
                out_ref[rows:, :rows] = tail
        else:
            out_refs[parts][...] = source_ref[...]

    @pl.when(meta_ref[edge] == 1)
    def finish_edge():
        finish_with(edge_ref)

    @pl.when(meta_ref[edge] == 0)
    def finish_inner():
        finish_with(inner_ref)


SMEM_SPEC = pl.BlockSpec(memory_space=pltpu.SMEM)
VMEM_SPEC = pl.BlockSpec(memory_space=pltpu.VMEM)


def pack_stash(x, gain, weight, parts):
    rows, width = x.shape
    depth = weight.shape[2]
    shape = (rows + 3 * depth, width // parts)
    return pl.pallas_call(
        functools.partial(pack_stash_kernel, parts, 4),
        out_shape=(
            jax.ShapeDtypeStruct((rows, 128), F32),
            *[jax.ShapeDtypeStruct(shape, BF16) for r in range(parts)],
        ),
        in_specs=[pl.BlockSpec(memory_space=pl.ANY)] * 3,
        out_specs=(VMEM_SPEC,) * (parts + 1),
        scratch_shapes=[
            pltpu.VMEM((rows, width), BF16),
            pltpu.VMEM((1, width), F32),
            pltpu.VMEM(weight.shape, BF16),
            pltpu.VMEM((rows, width), BF16),
            pltpu.SemaphoreType.DMA((8,)),
        ],
        compiler_params=pltpu.CompilerParams(vmem_limit_bytes=58 * 1024 * 1024),
        cost_estimate=pl.CostEstimate(flops=4 * rows * width, bytes_accessed=6 * rows * width, transcendentals=0),
        name="pack_stash",
    )(x, gain, weight)


def pack_rows(meta, edge, inner, parts, with_inverse):
    rows, width = inner.shape
    shape = (rows + (EXTRA if with_inverse else 0), width // parts)
    extra = () if with_inverse else (jax.ShapeDtypeStruct((rows, width), BF16),)
    return pl.pallas_call(
        functools.partial(pack_rows_kernel, parts, with_inverse),
        out_shape=(*[jax.ShapeDtypeStruct(shape, BF16) for r in range(parts)], *extra),
        in_specs=[SMEM_SPEC, VMEM_SPEC, VMEM_SPEC],
        out_specs=(VMEM_SPEC,) * (parts + len(extra)),
        compiler_params=pltpu.CompilerParams(vmem_limit_bytes=VMEM_LIMIT),
        cost_estimate=pl.CostEstimate(flops=4 * rows * width, bytes_accessed=6 * rows * width, transcendentals=0),
        name="pack_inbound" if with_inverse else "pack_cotangent",
    )(meta, edge, inner)


def slot_order(parts):
    return sorted(range(parts), key=lambda r: min(r, parts - r))


def gather_rows(meta_ref, refs, rows, x_ref):
    parts = len(refs)
    for r, ref in zip(slot_order(parts), refs):
        source = lax.rem(meta_ref[0] + parts - r, parts)
        x_ref[pl.ds(pl.multiple_of(source * rows, rows), rows)] = ref[:rows]


def gather_weight(meta_ref, refs, rows, weight_ref):
    parts = len(refs)
    depth = HEAD_DIM // parts
    for r, ref in zip(slot_order(parts), refs):
        source = lax.rem(meta_ref[0] + parts - r, parts)
        depth_at = pl.ds(pl.multiple_of(source * depth, depth), depth)
        for j in range(3):
            weight_ref[depth_at, j * HEAD_DIM : (j + 1) * HEAD_DIM] = ref[
                rows + j * depth : rows + (j + 1) * depth
            ]


def gather_inverse(meta_ref, refs, rows, inverse_ref):
    parts = len(refs)

    @pl.when(pl.program_id(0) == 0)
    def spread_inverse():
        for r, ref in zip(slot_order(parts), refs):
            source = lax.rem(meta_ref[0] + parts - r, parts)
            tail = ref[rows : rows + EXTRA].astype(F32)
            inverse_ref[pl.ds(pl.multiple_of(source * rows, rows), rows)] = column_of(
                tail[:1] + tail[1:2] + tail[2:3], rows
            )


def block_mask(first_query, tokens):
    key = lax.broadcasted_iota(jnp.int32, (1, WINDOW), 1) + (first_query - RADIUS)
    return jnp.where((key >= 0) & (key < tokens), 0.0, masked_score).astype(F32)


def edge_bias(bias, first, tokens):
    if first < RADIUS or first + ROW_BLOCK + RADIUS > tokens:
        return bias + block_mask(first, tokens)
    return bias


def padded(rows):
    edge = jnp.zeros((RADIUS, rows.shape[1]), rows.dtype)
    return jnp.concatenate([edge, rows, edge], axis=0)


def heads_backward_kernel(parts, rows, meta_ref, *refs):
    a_refs, c_refs = refs[:parts], refs[parts : 2 * parts]
    gain_ref, offset_ref, onehot_ref, after_ref = refs[2 * parts : 2 * parts + 4]
    out_refs = refs[2 * parts + 4 : 3 * parts + 4]
    gain_grad_ref, x_ref, weight_ref, cot_ref, grad_ref, part_ref, bias_ref = refs[3 * parts + 4 :]
    tokens = rows * parts
    depth = HEAD_DIM // parts
    scale = HEAD_DIM ** (-0.5)
    gather_rows(meta_ref, a_refs, rows, x_ref)
    gather_weight(meta_ref, a_refs, rows, weight_ref)
    gather_rows(meta_ref, c_refs, rows, cot_ref)
    weight = weight_ref[...]
    normed = x_ref[...]
    query = dot_nn(normed, weight[:, :HEAD_DIM]).astype(BF16)
    key = padded(dot_nn(normed, weight[:, HEAD_DIM : 2 * HEAD_DIM]).astype(BF16))
    value = padded(dot_nn(normed, weight[:, 2 * HEAD_DIM :]).astype(BF16))
    bias = toeplitz(offset_ref[0])
    blocks = tokens // ROW_BLOCK
    starts = range(0, tokens, ROW_BLOCK)
    cot = cot_ref[...]
    query_rows = [query[f : f + ROW_BLOCK] for f in starts]
    cot_rows = [cot[f : f + ROW_BLOCK] for f in starts]
    products = [dot_nt(rows_q, key[f : f + WINDOW]) for f, rows_q in zip(starts, query_rows)]
    grad_probs = [dot_nt(rows_c, value[f : f + WINDOW]) for f, rows_c in zip(starts, cot_rows)]
    packed, grad_packed, score_sum = [], [], None
    for f, product, grads in zip(starts, products, grad_probs):
        probs = score_probs(product, edge_bias(bias, f, tokens))
        delta = jnp.sum(probs * grads, axis=-1, keepdims=True)
        grad_scores = probs * (grads - delta)
        score_sum = grad_scores if score_sum is None else score_sum + grad_scores
        packed.append(probs.astype(BF16))
        grad_packed.append(grad_scores.astype(BF16))
    grad_query = [dot_nn(part, key[f : f + WINDOW]) for f, part in zip(starts, grad_packed)]
    grad_key = [dot_tn(part, rows_q) for part, rows_q in zip(grad_packed, query_rows)]
    grad_value = [dot_tn(part, rows_c) for part, rows_c in zip(packed, cot_rows)]

    def joined(pieces):
        units = []
        for u in range((tokens + 2 * RADIUS) // ROW_BLOCK):
            total = None
            for b in range(blocks):
                if 0 <= u - b < WINDOW // ROW_BLOCK:
                    piece = pieces[b][(u - b) * ROW_BLOCK : (u - b + 1) * ROW_BLOCK]
                    total = piece if total is None else total + piece
            units.append(total)
        return jnp.concatenate(units, axis=0)[RADIUS : RADIUS + tokens]

    dqkv = jnp.concatenate(
        [
            (jnp.concatenate(grad_query, axis=0) * scale).astype(BF16),
            (joined(grad_key) * scale).astype(BF16),
            joined(grad_value).astype(BF16),
        ],
        axis=1,
    )
    grad_normed = dot_nt(dqkv, weight)
    gain_grad_ref[...] = jnp.sum(grad_normed * normed.astype(F32), axis=0, keepdims=True) / gain_ref[...]
    grad_ref[...] = grad_normed
    part_ref[...] = dot_tn(normed, dqkv)
    bias_grad = jnp.sum(onehot_ref[...] * diagonal_sums(score_sum), axis=1, keepdims=True)
    bias_ref[...] = jnp.broadcast_to(bias_grad, bias_ref.shape)
    buckets = bias_ref.shape[0] // parts
    for r, out_ref in enumerate(out_refs):
        source = lax.rem(meta_ref[0] + parts - r, parts)
        out_ref[:rows] = grad_ref[pl.ds(pl.multiple_of(source * rows, rows), rows)].astype(BF16)
        for j in range(3):
            out_ref[rows + j * depth : rows + (j + 1) * depth] = part_ref[
                pl.ds(pl.multiple_of(source * depth, depth), depth), j * HEAD_DIM : (j + 1) * HEAD_DIM
            ].astype(BF16)
        share = bias_ref[pl.ds(pl.multiple_of(source * buckets, buckets), buckets)]
        out_ref[rows + 3 * depth :] = share.astype(BF16)


def head_column(rows, first=0):
    return pl.BlockSpec((rows, HEAD_DIM), lambda i, meta: (0, i + first))


def whole_column(rows, heads, first=0):
    return pl.BlockSpec((rows, HEAD_DIM), lambda i, meta: (0, meta[0] * heads + first + i))


def offset_spec(heads, first=0):
    return pl.BlockSpec((1, 1, WINDOW), lambda i, meta: (meta[0] * heads + first + i, 0, 0))


def heads_backward(meta, a_slots, c_slots, gain, offsets, onehot, after, heads, first, count):
    parts = len(a_slots)
    rows = c_slots[0].shape[0]
    tokens = rows * parts
    buckets = onehot.shape[0]
    packed = a_slots[0].shape[0]
    made = packed + buckets // parts
    width = count * HEAD_DIM
    return pl.pallas_call(
        functools.partial(heads_backward_kernel, parts, rows),
        out_shape=(
            *[jax.ShapeDtypeStruct((made, width), BF16) for r in range(parts)],
            jax.ShapeDtypeStruct((1, width), F32),
        ),
        grid_spec=pltpu.PrefetchScalarGridSpec(
            num_scalar_prefetch=1,
            grid=(count,),
            in_specs=[
                *[head_column(packed, first)] * parts,
                whole_column(rows, heads, first),
                *[head_column(rows, first)] * (parts - 1),
                whole_column(1, heads, first),
                offset_spec(heads, first),
                pl.BlockSpec((buckets, WINDOW), lambda i, meta: (0, 0)),
                pl.BlockSpec(memory_space=pl.ANY),
            ],
            out_specs=(*[head_column(made)] * parts, head_column(1)),
            scratch_shapes=[
                pltpu.VMEM((tokens, HEAD_DIM), BF16),
                pltpu.VMEM((HEAD_DIM, 3 * HEAD_DIM), BF16),
                pltpu.VMEM((tokens, HEAD_DIM), BF16),
                pltpu.VMEM((tokens, HEAD_DIM), F32),
                pltpu.VMEM((HEAD_DIM, 3 * HEAD_DIM), F32),
                pltpu.VMEM((buckets, HEAD_DIM), F32),
            ],
        ),
        compiler_params=pltpu.CompilerParams(vmem_limit_bytes=VMEM_LIMIT),
        cost_estimate=pl.CostEstimate(
            flops=count * tokens * 400_000, bytes_accessed=tokens * width, transcendentals=0
        ),
        name="heads_backward",
    )(meta, *a_slots, *c_slots, gain, offsets, onehot, after)


def heads_forward_kernel(parts, rows, meta_ref, *refs):
    a_refs, i_refs = refs[:parts], refs[parts : 2 * parts]
    gain_ref, offset_ref = refs[2 * parts : 2 * parts + 2]
    out_refs = refs[2 * parts + 2 : 3 * parts + 2]
    inverse_ref, x_ref, weight_ref, made_ref, square_ref = refs[3 * parts + 2 :]
    tokens = rows * parts
    gather_rows(meta_ref, i_refs, rows, x_ref)
    gather_weight(meta_ref, a_refs, rows, weight_ref)
    gather_inverse(meta_ref, i_refs, rows, inverse_ref)
    weight = weight_ref[...]
    normed = (x_ref[...].astype(F32) * inverse_ref[...] * gain_ref[...]).astype(BF16)
    query = dot_nn(normed, weight[:, :HEAD_DIM]).astype(BF16)
    key = padded(dot_nn(normed, weight[:, HEAD_DIM : 2 * HEAD_DIM]).astype(BF16))
    value = padded(dot_nn(normed, weight[:, 2 * HEAD_DIM :]).astype(BF16))
    bias = toeplitz(offset_ref[0])
    starts = range(0, tokens, ROW_BLOCK)
    products = [dot_nt(query[f : f + ROW_BLOCK], key[f : f + WINDOW]) for f in starts]
    packed = [
        score_probs(product, edge_bias(bias, f, tokens)).astype(BF16) for f, product in zip(starts, products)
    ]
    attended = [dot_nn(part, value[f : f + WINDOW]) for f, part in zip(starts, packed)]
    for f, part in zip(starts, attended):
        made_ref[f : f + ROW_BLOCK] = (x_ref[f : f + ROW_BLOCK].astype(F32) + part).astype(BF16)
    made = made_ref[...].astype(F32)
    squares = made * made

    @pl.when(pl.program_id(0) == 0)
    def first_head():
        square_ref[...] = squares

    @pl.when(pl.program_id(0) > 0)
    def later_head():
        square_ref[...] += squares

    for r, out_ref in enumerate(out_refs):
        source = lax.rem(meta_ref[0] + parts - r, parts)
        out_ref[:rows] = made_ref[pl.ds(pl.multiple_of(source * rows, rows), rows)]

    @pl.when(pl.program_id(0) < pl.num_programs(0) - 1)
    def no_sums():
        for out_ref in out_refs:
            out_ref[rows:] = jnp.zeros((EXTRA, HEAD_DIM), BF16)

    @pl.when(pl.program_id(0) == pl.num_programs(0) - 1)
    def last_head():
        rest = jnp.sum(jnp.transpose(square_ref[...]), axis=0, keepdims=True)
        at_row = lax.broadcasted_iota(jnp.int32, (EXTRA, rows), 0)
        tail = jnp.zeros((EXTRA, rows), F32)
        for k in range(2):
            piece = rest.astype(BF16).astype(F32)
            rest = rest - piece
            for part in range(parts):
                row = jnp.broadcast_to(piece[:, part * rows : (part + 1) * rows], (EXTRA, rows))
                tail = jnp.where(at_row == 2 * part + k, row, tail)
        for out_ref in out_refs:
            out_ref[rows:] = tail.astype(BF16)


def heads_forward(meta, a_slots, i_slots, gain, offsets, heads, rows):
    parts = len(a_slots)
    tokens = rows * parts
    packed = a_slots[0].shape[0]
    width = heads * HEAD_DIM
    return pl.pallas_call(
        functools.partial(heads_forward_kernel, parts, rows),
        out_shape=(
            *[jax.ShapeDtypeStruct((rows + EXTRA, width), BF16) for r in range(parts)],
        ),
        grid_spec=pltpu.PrefetchScalarGridSpec(
            num_scalar_prefetch=1,
            grid=(heads,),
            in_specs=[
                *[head_column(packed)] * parts,
                *[head_column(i_slots[0].shape[0])] * parts,
                whole_column(1, heads),
                offset_spec(heads),
            ],
            out_specs=(head_column(rows + EXTRA),) * parts,
            scratch_shapes=[
                pltpu.VMEM((tokens, HEAD_DIM), F32),
                pltpu.VMEM((tokens, HEAD_DIM), BF16),
                pltpu.VMEM((HEAD_DIM, 3 * HEAD_DIM), BF16),
                pltpu.VMEM((tokens, HEAD_DIM), BF16),
                pltpu.VMEM((tokens, HEAD_DIM), F32),
            ],
        ),
        compiler_params=pltpu.CompilerParams(vmem_limit_bytes=VMEM_LIMIT),
        cost_estimate=pl.CostEstimate(
            flops=heads * tokens, bytes_accessed=tokens, transcendentals=0
        ),
        name="heads_forward",
    )(meta, *a_slots, *i_slots, gain, offsets)


def memory_kernel(parts, width, sections, meta_ref, *refs):
    out_refs, other_refs = refs[:parts], refs[parts : 2 * parts - 1]
    gain_ref, *share_refs, memory_ref = refs[2 * parts - 1 :]
    wide = memory_ref.shape[1]
    rows = memory_ref.shape[0] // parts
    total = None
    for ref in (out_refs[0], *other_refs):
        tail = ref[rows:, wide - rows :].astype(F32)
        pieces = [tail[2 * p : 2 * p + 1] + tail[2 * p + 1 : 2 * p + 2] for p in range(parts)]
        row = jnp.concatenate(pieces, axis=1)
        total = row if total is None else total + row
    inverse = lax.rsqrt(total / width + eps_norm)
    gain = gain_ref[:, pl.ds(pl.multiple_of(meta_ref[0] * wide, 128), wide)]
    spread_inverse = jnp.transpose(jnp.broadcast_to(inverse, (128, inverse.shape[1])))
    for r, out_ref in enumerate(out_refs):
        source = lax.rem(meta_ref[0] + parts - r, parts)
        memory_ref[pl.ds(pl.multiple_of(source * rows, rows), rows)] = out_ref[:rows]
    made = memory_ref[...].astype(F32)
    memory_ref[...] = (made * spread_inverse[:, :1] * gain).astype(BF16)
    for k, share_ref in enumerate(share_refs):
        size = 2 * share_ref.shape[0] // sections
        for i in range(sections // 2):
            share_ref[i * size : (i + 1) * size] = memory_ref[(2 * i + k) * size : (2 * i + k + 1) * size]


def memory_rows(meta, outs, others, gain, width, sections):
    parts = len(outs)
    rows, wide = outs[0].shape[0] - EXTRA, outs[0].shape[1]
    return pl.pallas_call(
        functools.partial(memory_kernel, parts, width, sections),
        out_shape=[jax.ShapeDtypeStruct((rows * parts // 2, wide), BF16)] * 2,
        in_specs=[SMEM_SPEC] + [VMEM_SPEC] * (2 * parts),
        out_specs=[VMEM_SPEC] * 2,
        scratch_shapes=[pltpu.VMEM((rows * parts, wide), BF16)],
        compiler_params=pltpu.CompilerParams(vmem_limit_bytes=VMEM_LIMIT),
        cost_estimate=pl.CostEstimate(flops=rows, bytes_accessed=rows, transcendentals=0),
        name="memory_rows",
    )(meta, *outs, *others, gain)


def place_kernel(parts, meta_ref, *refs):
    out_ref = refs[parts]
    wide = refs[0].shape[1]
    for r, ref in zip(slot_order(parts), refs):
        source = lax.rem(meta_ref[0] + r, parts)
        out_ref[:, pl.ds(pl.multiple_of(source * wide, 128), wide)] = ref[: out_ref.shape[0]]


def place_columns(meta, slots):
    parts = len(slots)
    rows, wide = slots[0].shape[0] - EXTRA, slots[0].shape[1]
    return pl.pallas_call(
        functools.partial(place_kernel, parts),
        out_shape=jax.ShapeDtypeStruct((rows, wide * parts), BF16),
        in_specs=[SMEM_SPEC] + [VMEM_SPEC] * parts,
        out_specs=VMEM_SPEC,
        compiler_params=pltpu.CompilerParams(vmem_limit_bytes=VMEM_LIMIT),
        cost_estimate=pl.CostEstimate(flops=0, bytes_accessed=rows, transcendentals=0),
        name="place_columns",
    )(meta, *slots)


def store_weights(g_ref, weight_ref, rows, depth, heads):
    for h in range(heads):
        for j in range(3):
            weight_ref[j, h] = g_ref[
                rows + j * depth : rows + (j + 1) * depth, h * HEAD_DIM : (h + 1) * HEAD_DIM
            ].astype(F32)


def weight_copies(weight_ref, weight_hbm, first_head, heads, sems):
    return [
        pltpu.make_async_copy(weight_ref.at[j], weight_hbm.at[j, pl.ds(first_head, heads)], sems.at[j])
        for j in range(3)
    ]


def add_bias(bias, g_ref, first_row, first_head, heads):
    lane = lax.broadcasted_iota(jnp.int32, bias.shape, 1)
    shares = g_ref[first_row:].astype(F32)
    for h in range(heads):
        bias = jnp.where(lane == first_head + h, shares[:, h * HEAD_DIM : (h + 1) * HEAD_DIM], bias)
    return bias


def early_finish_kernel(parts, meta_ref, *refs):
    g_refs = refs[: parts - 1]
    x_ref, inverse_ref, gain_ref, cot_ref = refs[parts - 1 : parts + 3]
    base_ref, row_ref, weight_hbm, bias_ref, weight_ref, sems = refs[parts + 3 :]
    rows, width = x_ref.shape
    wide = width // parts
    heads = wide // HEAD_DIM
    depth = HEAD_DIM // parts
    order = slot_order(parts)
    inverse = inverse_ref[:, :1]
    bias = jnp.zeros(bias_ref.shape, F32)
    total = jnp.zeros((rows, 1), F32)
    copies = []
    for k, g_ref in enumerate(g_refs):
        source = lax.rem(meta_ref[0] + order[k], parts)
        store_weights(g_ref, weight_ref.at[k], rows, depth, heads)
        for copy in weight_copies(weight_ref.at[k], weight_hbm, source * heads, heads, sems.at[k]):
            copy.start()
            copies.append(copy)
        bias = add_bias(bias, g_ref, rows + 3 * depth, source * heads, heads)
        columns = pl.ds(pl.multiple_of(source * wide, 128), wide)
        scaled = g_ref[:rows].astype(F32) * gain_ref[:, columns]
        total = total + jnp.sum(scaled * x_ref[:, columns].astype(F32), axis=-1, keepdims=True)
        base_ref[:, columns] = cot_ref[:, columns].astype(F32) + inverse * scaled
    last = pl.ds(pl.multiple_of(lax.rem(meta_ref[0] + order[-1], parts) * wide, 128), wide)
    base_ref[:, last] = cot_ref[:, last].astype(F32)
    row_ref[...] = jnp.broadcast_to(total, row_ref.shape)
    bias_ref[...] = bias
    for copy in copies:
        copy.wait()


def late_finish_kernel(parts, meta_ref, *refs):
    base_ref, row_ref, early_bias_ref, g_ref, x_ref, inverse_ref, gain_ref, early_hbm, after_hbm = refs[:9]
    out_ref, weight_hbm, bias_ref, weight_ref, sems = refs[9:]
    rows, width = x_ref.shape
    wide = width // parts
    heads = wide // HEAD_DIM
    depth = HEAD_DIM // parts
    source = lax.rem(meta_ref[0] + slot_order(parts)[-1], parts)
    store_weights(g_ref, weight_ref, rows, depth, heads)
    copies = weight_copies(weight_ref, weight_hbm, source * heads, heads, sems)
    for copy in copies:
        copy.start()
    bias = add_bias(early_bias_ref[...], g_ref, rows + 3 * depth, source * heads, heads)
    bias_ref[...] = bias[:, : bias_ref.shape[1]]
    columns = pl.ds(pl.multiple_of(source * wide, 128), wide)
    inverse = inverse_ref[:, :1]
    scaled = g_ref[:rows].astype(F32) * gain_ref[:, columns]
    total = row_ref[:, :1] + jnp.sum(scaled * x_ref[:, columns].astype(F32), axis=-1, keepdims=True)
    factor = inverse * inverse * inverse * (total / width)
    out_ref[...] = (base_ref[...] - x_ref[...].astype(F32) * factor).astype(BF16)
    out_ref[:, columns] = (
        base_ref[:, columns] + (inverse * scaled - x_ref[:, columns].astype(F32) * factor)
    ).astype(BF16)
    for copy in copies:
        copy.wait()


def heads_finish(meta, g_slots, x, inverse, gain, cotangent, after, buckets):
    parts = len(g_slots)
    rows, width = x.shape
    heads = width // HEAD_DIM
    depth = HEAD_DIM // parts
    any_spec = pl.BlockSpec(memory_space=pl.ANY)
    weight = jax.ShapeDtypeStruct((3, heads, depth, HEAD_DIM), F32)
    piece = (3, heads // parts, depth, HEAD_DIM)
    cost = pl.CostEstimate(flops=rows * width, bytes_accessed=rows * width, transcendentals=0)
    params = pltpu.CompilerParams(vmem_limit_bytes=VMEM_LIMIT)
    base, row, early, bias = pl.pallas_call(
        functools.partial(early_finish_kernel, parts),
        out_shape=(
            jax.ShapeDtypeStruct((rows, width), F32),
            jax.ShapeDtypeStruct((rows, 128), F32),
            weight,
            jax.ShapeDtypeStruct((buckets // parts, HEAD_DIM), F32),
        ),
        in_specs=[SMEM_SPEC] + [VMEM_SPEC] * (parts + 3),
        out_specs=(VMEM_SPEC, VMEM_SPEC, any_spec, VMEM_SPEC),
        scratch_shapes=[pltpu.VMEM((parts - 1, *piece), F32), pltpu.SemaphoreType.DMA((parts - 1, 3))],
        compiler_params=params,
        cost_estimate=cost,
        name="early_finish",
    )(meta, *g_slots[:-1], x, inverse, gain, cotangent)
    return pl.pallas_call(
        functools.partial(late_finish_kernel, parts),
        out_shape=(
            jax.ShapeDtypeStruct((rows, width), BF16),
            weight,
            jax.ShapeDtypeStruct((buckets // parts, heads), F32),
        ),
        in_specs=[SMEM_SPEC] + [VMEM_SPEC] * 7 + [any_spec] * 2,
        out_specs=(VMEM_SPEC, any_spec, VMEM_SPEC),
        input_output_aliases={8: 1},
        scratch_shapes=[pltpu.VMEM(piece, F32), pltpu.SemaphoreType.DMA((3,))],
        compiler_params=params,
        cost_estimate=cost,
        name="late_finish",
    )(meta, base, row, bias, g_slots[-1], x, inverse, gain, early, after)


def offset_table(rel_bias):
    onehot = jnp.asarray(bucket_onehot(rel_bias.shape[0]))
    by_offset = jnp.dot(onehot, rel_bias, precision=lax.Precision.HIGHEST).T
    inside = jnp.arange(WINDOW, dtype=jnp.int32) <= 2 * RADIUS
    return jnp.where(inside[None, :], by_offset, masked_score)[:, None, :]


def shifted(value, axis, steps):
    count = lax.axis_size(axis)
    first, last = (max(0, -steps), min(count, count - steps))
    return lax.ppermute(value, axis, [(source, source + steps) for source in range(first, last)])


def spread_memory(even, odd, section, sections):
    last = sections - 1
    share = 2 * even.shape[0] // sections
    held = jnp.where(section == last - 1, lax.ppermute(even, "section", [(last, last - 1)]), odd)
    memory = jnp.where(section >= last - 1, held[even.shape[0] - share :], 0)
    for i in range(sections // 2 - 1):
        memory = memory + lax.ppermute(
            held[i * share : (i + 1) * share], "section", [(last, 2 * i + 1), (last - 1, 2 * i)]
        )
    return memory


def heads_body(
    embedded, carried, stash, returned, loss_grad, qkv_weight, rel_bias, norm_gain, final_gain
):
    section = lax.axis_index("section")
    sections = lax.axis_size("section")
    parts = lax.axis_size("seq")
    rows, width = embedded.shape
    heads = width // HEAD_DIM // parts
    buckets = rel_bias.shape[1]
    meta = jnp.stack(
        [lax.axis_index("seq"), section == 0, section == sections - 1]
    ).astype(jnp.int32)

    def exchanged(sends, direction):
        return [
            lax.ppermute(sends[r], "seq", [(i, (i + direction * r) % parts) for i in range(parts)]) if r else sends[0]
            for r in slot_order(parts)
        ]

    inverse_b, *a_sends = pack_stash(stash[0], norm_gain, qkv_weight[0], parts)
    a_slots = exchanged(a_sends, 1)
    arrived = shifted(carried[0], "section", 1)
    came_back = shifted(returned[0], "section", -1)
    i_slots = exchanged(pack_rows(meta, embedded, arrived, parts, True), 1)
    *c_sends, cotangent = pack_rows(meta, loss_grad, came_back, parts, False)
    c_slots = exchanged(c_sends, 1)
    c_slots[0] = cotangent

    offsets = offset_table(rel_bias[0])
    onehot = jnp.asarray(bucket_onehot(buckets).T)
    o_sends = heads_forward(meta, a_slots, i_slots, norm_gain, offsets, heads, rows)
    o_slots = exchanged(o_sends, -1)

    *g_sends, gain_grad = heads_backward(
        meta, a_slots, c_slots, norm_gain, offsets, onehot, o_sends[0], heads, 0, heads
    )
    g_sends, o_slots = lax.optimization_barrier((g_sends, o_slots))
    g_slots = exchanged(g_sends, -1)
    output = place_columns(meta, o_slots)
    shares = memory_rows(meta, o_sends, o_slots[1:], final_gain[None], width, sections)
    memory = spread_memory(*shares, section, sections)

    input_grad, weight_grad, bias_grad = heads_finish(
        meta, g_slots, stash[0], inverse_b, norm_gain, cotangent, memory, buckets
    )
    return (
        output[None],
        input_grad[None],
        weight_grad[None],
        bias_grad[None],
        gain_grad,
        memory,
    )


def tokens_body(
    embedded, carried, stash, returned, loss_grad, qkv_weight, rel_bias, norm_gain, final_gain
):
    section_index = lax.axis_index("section")
    section_count = lax.axis_size("section")
    seq_index = lax.axis_index("seq")
    seq_count = lax.axis_size("seq")
    rows, width = embedded.shape
    heads = width // HEAD_DIM
    tokens = rows * seq_count
    shard = qkv_weight[0]
    up = [(i, i + 1) for i in range(seq_count - 1)]
    down = [(j, i) for i, j in up]
    group = 4 if heads % 4 == 0 else 1

    own_b, inverse_b = norm_rows(stash[0], norm_gain)
    before_b = lax.ppermute(own_b[rows - RADIUS :], "seq", up)
    after_b = lax.ppermute(own_b[:RADIUS], "seq", down)
    slots = [lax.all_gather(shard, "seq", axis=2, tiled=True)]

    section_up = [(i, (i + 1) % section_count) for i in range(section_count)]
    section_down = [(j, i) for i, j in section_up]
    inbound = lax.ppermute(
        jnp.where(section_index == section_count - 1, embedded, carried[0]), "section", section_up
    )
    cotangent = lax.ppermute(
        jnp.where(section_index == 0, loss_grad, returned[0]), "section", section_down
    )

    onehot = jnp.asarray(bucket_onehot(rel_bias.shape[1]))
    offsets = offset_table(rel_bias[0])
    first_key = RADIUS - seq_index * rows
    meta = jnp.stack([seq_index, first_key, first_key + tokens]).astype(jnp.int32)

    own_a, unused = norm_rows(inbound, norm_gain)
    before_a = lax.ppermute(own_a[rows - RADIUS :], "seq", up)
    after_a = lax.ppermute(own_a[:RADIUS], "seq", down)

    grad_own, lower, upper, offset_grad, *parts = backward_attention(
        meta, before_b, own_b, after_b, cotangent, offsets, slots, group, 0, heads
    )
    from_before = lax.ppermute(upper, "seq", up)
    from_after = lax.ppermute(lower, "seq", down)
    weight_sum = lax.psum_scatter(parts[0], "seq", scatter_dimension=2, tiled=True).astype(F32)

    output = forward_attention(meta, before_a, own_a, after_a, inbound, offsets, slots, group)
    final_normed, unused = norm_rows(output, final_gain[None])
    relaid = lax.all_to_all(final_normed, "seq", split_axis=1, concat_axis=0, tiled=True)
    kept = jnp.where(section_index == section_count - 1, relaid, jnp.zeros_like(relaid))
    memory = lax.psum_scatter(kept, "section", scatter_dimension=0, tiled=True)

    input_grad, gain_part = finish(
        grad_own, from_before, from_after, stash[0], inverse_b, norm_gain, cotangent
    )
    bias_part = jnp.dot(
        offset_grad[:, 0, :], onehot, precision=lax.Precision.HIGHEST
    ).T
    bias_sum = lax.psum_scatter(
        bias_part.astype(BF16), "seq", scatter_dimension=0, tiled=True
    ).astype(F32)
    gain_sum = lax.psum_scatter(
        gain_part.astype(BF16), "seq", scatter_dimension=1, tiled=True
    ).astype(F32)
    return (output[None], input_grad[None], weight_sum[None], bias_sum[None], gain_sum, memory)


def choose_body(embedded, carried, stash, returned, loss_grad, qkv_weight, rel_bias, norm_gain, final_gain):
    parts = lax.axis_size("seq")
    rows, width = embedded.shape
    even = parts > 1 and width % (HEAD_DIM * parts) == 0 and HEAD_DIM % (32 * parts) == 0 and rows == 128
    sections = lax.axis_size("section")
    even = even and sections % 2 == 0
    even = even and rel_bias.shape[1] == 8 * parts and width <= 128 * HEAD_DIM and rows * parts % (16 * sections) == 0
    chosen = heads_body if even else tokens_body
    return chosen(
        embedded, carried, stash, returned, loss_grad, qkv_weight, rel_bias, norm_gain, final_gain
    )


def solution(mesh):
    in_specs = (
        P("seq", None),
        P("section", "seq", None),
        P("section", "seq", None),
        P("section", "seq", None),
        P("seq", None),
        P("section", None, None, "seq", None),
        P("section", None, None),
        P("section", None),
        P(),
    )
    out_specs = (
        P("section", "seq", None),
        P("section", "seq", None),
        P("section", None, None, "seq", None),
        P("section", "seq", None),
        P("section", "seq"),
        P("section", "seq"),
    )
    return jax.shard_map(choose_body, mesh=mesh, in_specs=in_specs, out_specs=out_specs, check_vma=False)
```

```python
import functools

import jax
import jax.numpy as jnp
import numpy as np
from jax import lax
from jax.experimental import pallas as pl
from jax.experimental.pallas import tpu as pltpu
from jax.sharding import PartitionSpec as P

RADIUS = 96
HEAD_DIM = 128
ROW_BLOCK = 64
WINDOW = ROW_BLOCK + 2 * RADIUS
eps_norm = 1e-06
bucket_edges = (1, 2, 3, 4, 5, 6, 7, 8, 11, 16, 22, 32, 45, 64, 90)
masked_score = -1e30
F32 = jnp.float32
BF16 = jnp.bfloat16
VMEM_LIMIT = 14 * 1024 * 1024
EXTRA = 8


def bucket_onehot(bucket_count):
    offsets = np.arange(WINDOW) - RADIUS
    magnitude = np.abs(offsets)
    counted = np.zeros(offsets.shape, np.int32)
    for threshold in bucket_edges:
        counted = counted + (magnitude >= threshold)
    counted = counted + 16 * (offsets > 0)
    onehot = (counted[:, None] == np.arange(bucket_count)[None, :]) & (magnitude <= RADIUS)[:, None]
    return onehot.astype(np.float32)


def dot_nn(a, b):
    return lax.dot_general(a, b, (((1,), (0,)), ((), ())), preferred_element_type=F32)


def dot_nt(a, b):
    return lax.dot_general(a, b, (((1,), (1,)), ((), ())), preferred_element_type=F32)


def dot_tn(a, b):
    return lax.dot_general(a, b, (((0,), (0,)), ((), ())), preferred_element_type=F32)


def norm_kernel(x_ref, gain_ref, normed_ref, inverse_ref):
    x = x_ref[...].astype(F32)
    inverse = lax.rsqrt(jnp.mean(x * x, axis=-1, keepdims=True) + eps_norm)
    normed_ref[...] = (x * inverse * gain_ref[...]).astype(BF16)
    inverse_ref[...] = jnp.broadcast_to(inverse, inverse_ref.shape)


def norm_rows(x, gain):
    rows, width = x.shape
    return pl.pallas_call(
        norm_kernel,
        out_shape=(
            jax.ShapeDtypeStruct((rows, width), BF16),
            jax.ShapeDtypeStruct((rows, 128), F32),
        ),
        compiler_params=pltpu.CompilerParams(vmem_limit_bytes=VMEM_LIMIT),
        cost_estimate=pl.CostEstimate(
            flops=6 * rows * width, bytes_accessed=4 * rows * width, transcendentals=rows
        ),
        name="norm_rows",
    )(x, gain)


def load_weight(meta_ref, slot_refs, weight_ref, head, slots):
    depth = HEAD_DIM // slots
    for r, slot_ref in enumerate(slot_refs):
        if slots == 1:
            start = 0
        else:
            start = pl.multiple_of(lax.rem(meta_ref[0] + r, slots) * depth, depth)
        for j in range(3):
            weight_ref[head, pl.ds(start, depth), j * HEAD_DIM : (j + 1) * HEAD_DIM] = slot_ref[j, head]
    return weight_ref[head]


def key_mask(meta_ref, first_key):
    key = lax.broadcasted_iota(jnp.int32, (1, WINDOW), 1) + first_key
    inside = (key >= meta_ref[1]) & (key < meta_ref[2])
    return jnp.where(inside, 0.0, masked_score).astype(F32)


def toeplitz(row):
    return pltpu.roll(
        jnp.broadcast_to(row, (ROW_BLOCK, WINDOW)), 0, 1, stride=1, stride_axis=0
    )


def diagonal_sums(values):
    total = values[:8]
    for a in range(1, ROW_BLOCK // 8):
        total = total + pltpu.roll(values[8 * a : 8 * a + 8], WINDOW - 8 * a, 1)
    row = lax.broadcasted_iota(jnp.int32, total.shape, 0)
    for bit in (1, 2, 4):
        total = jnp.where((row & bit) != 0, pltpu.roll(total, WINDOW - bit, 1), total)
    return jnp.sum(total, axis=0, keepdims=True)


def block_probs(query_rows, key_rows, bias):
    return score_probs(dot_nt(query_rows, key_rows), bias)


def score_probs(products, bias):
    scores = products * (HEAD_DIM ** (-0.5)) + bias
    weights = jnp.exp(scores - jnp.max(scores, axis=-1, keepdims=True))
    return weights * (1.0 / jnp.sum(weights, axis=-1, keepdims=True))


def forward_kernel(slots, group, meta_ref, before_ref, own_ref, after_ref, x_ref, offset_ref, *rest):
    slot_refs = rest[:slots]
    out_ref, weight_ref = rest[slots:]
    rows = own_ref.shape[0]
    blocks = rows // ROW_BLOCK
    masks = [key_mask(meta_ref, b * ROW_BLOCK) for b in range(blocks)]
    for g in range(group):
        columns = slice(g * HEAD_DIM, (g + 1) * HEAD_DIM)
        weight = load_weight(meta_ref, slot_refs, weight_ref, g, slots)
        own = own_ref[:, columns]
        extended = jnp.concatenate([before_ref[:, columns], own, after_ref[:, columns]], axis=0)
        query = dot_nn(own, weight[:, :HEAD_DIM]).astype(BF16)
        key_value = dot_nn(extended, weight[:, HEAD_DIM:]).astype(BF16)
        key, value = key_value[:, :HEAD_DIM], key_value[:, HEAD_DIM:]
        bias = toeplitz(offset_ref[g])
        for b in range(blocks):
            first = b * ROW_BLOCK
            window = slice(first, first + WINDOW)
            probs = block_probs(query[first : first + ROW_BLOCK], key[window], bias + masks[b])
            attended = dot_nn(probs.astype(BF16), value[window])
            kept = x_ref[first : first + ROW_BLOCK, columns].astype(F32)
            out_ref[first : first + ROW_BLOCK, columns] = (kept + attended).astype(BF16)


def column_spec(rows, group, first):
    return pl.BlockSpec((rows, group * HEAD_DIM), lambda i, meta: (0, i + first))


def slot_specs(weight_slots, group):
    return [
        pl.BlockSpec((3, group, slot.shape[2], HEAD_DIM), lambda i, meta: (0, i, 0, 0))
        for slot in weight_slots
    ]


def forward_attention(meta, before, own, after, x, offsets, weight_slots, group):
    rows, width = own.shape
    heads = width // HEAD_DIM
    slots = len(weight_slots)
    return pl.pallas_call(
        functools.partial(forward_kernel, slots, group),
        out_shape=jax.ShapeDtypeStruct((rows, width), BF16),
        grid_spec=pltpu.PrefetchScalarGridSpec(
            num_scalar_prefetch=1,
            grid=(heads // group,),
            in_specs=[
                column_spec(RADIUS, group, 0),
                column_spec(rows, group, 0),
                column_spec(RADIUS, group, 0),
                column_spec(rows, group, 0),
                pl.BlockSpec((group, 1, WINDOW), lambda i, meta: (i, 0, 0)),
                *slot_specs(weight_slots, group),
            ],
            out_specs=column_spec(rows, group, 0),
            scratch_shapes=[pltpu.VMEM((group, HEAD_DIM, 3 * HEAD_DIM), BF16)],
        ),
        compiler_params=pltpu.CompilerParams(vmem_limit_bytes=VMEM_LIMIT),
        cost_estimate=pl.CostEstimate(
            flops=heads * 60_000_000, bytes_accessed=8 * rows * width, transcendentals=heads * 32768
        ),
        name="forward_attention",
    )(meta, before, own, after, x, offsets, *weight_slots)


def backward_kernel(slots, group, meta_ref, before_ref, own_ref, after_ref, cot_ref, offset_ref, *rest):
    slot_refs = rest[:slots]
    rest = rest[slots:]
    grad_ref, lower_ref, upper_ref, offset_grad_ref = rest[:4]
    part_refs = rest[4 : 4 + slots]
    weight_ref, part_ref = rest[4 + slots :]
    rows = own_ref.shape[0]
    blocks = rows // ROW_BLOCK
    scale = HEAD_DIM ** (-0.5)
    masks = [key_mask(meta_ref, b * ROW_BLOCK) for b in range(blocks)]
    for g in range(group):
        columns = slice(g * HEAD_DIM, (g + 1) * HEAD_DIM)
        weight = load_weight(meta_ref, slot_refs, weight_ref, g, slots)
        own = own_ref[:, columns]
        extended = jnp.concatenate([before_ref[:, columns], own, after_ref[:, columns]], axis=0)
        query = dot_nn(own, weight[:, :HEAD_DIM]).astype(BF16)
        key_value = dot_nn(extended, weight[:, HEAD_DIM:]).astype(BF16)
        key, value = key_value[:, :HEAD_DIM], key_value[:, HEAD_DIM:]
        bias = toeplitz(offset_ref[g])
        grad_query, grad_key, grad_value, score_sum = [], [], [], None
        for b in range(blocks):
            first = b * ROW_BLOCK
            window = slice(first, first + WINDOW)
            query_rows = query[first : first + ROW_BLOCK]
            cot_rows = cot_ref[first : first + ROW_BLOCK, columns]
            probs = block_probs(query_rows, key[window], bias + masks[b])
            grad_probs = dot_nt(cot_rows, value[window])
            delta = jnp.sum(probs * grad_probs, axis=-1, keepdims=True)
            grad_scores = probs * (grad_probs - delta)
            score_sum = grad_scores if score_sum is None else score_sum + grad_scores
            grad_packed = grad_scores.astype(BF16)
            grad_query.append(dot_nn(grad_packed, key[window]))
            grad_key.append(dot_tn(grad_packed, query_rows))
            grad_value.append(dot_tn(probs.astype(BF16), cot_rows))

        def joined(parts):
            pieces = []
            for u in range((rows + 2 * RADIUS) // ROW_BLOCK):
                total = None
                for b in range(blocks):
                    if 0 <= u - b < WINDOW // ROW_BLOCK:
                        piece = parts[b][(u - b) * ROW_BLOCK : (u - b + 1) * ROW_BLOCK]
                        total = piece if total is None else total + piece
                pieces.append(total)
            return jnp.concatenate(pieces, axis=0)

        dquery = (jnp.concatenate(grad_query, axis=0) * scale).astype(BF16)
        dkey = (joined(grad_key) * scale).astype(BF16)
        dvalue = joined(grad_value).astype(BF16)
        dkey_value = jnp.concatenate([dkey, dvalue], axis=1)
        grad_extended = dot_nt(dkey_value, weight[:, HEAD_DIM:])
        grad_ref[:, columns] = grad_extended[RADIUS : RADIUS + rows] + dot_nt(dquery, weight[:, :HEAD_DIM])
        lower_ref[:, columns] = grad_extended[:RADIUS].astype(BF16)
        upper_ref[:, columns] = grad_extended[RADIUS + rows :].astype(BF16)
        part_ref[g, :, :HEAD_DIM] = dot_tn(own, dquery)
        part_ref[g, :, HEAD_DIM:] = dot_tn(extended, dkey_value)
        depth = HEAD_DIM // slots
        for r in range(slots):
            if slots == 1:
                start = 0
            else:
                start = pl.multiple_of(lax.rem(meta_ref[0] + r, slots) * depth, depth)
            for j in range(3):
                part_refs[r][j, g] = part_ref[
                    g, pl.ds(start, depth), j * HEAD_DIM : (j + 1) * HEAD_DIM
                ].astype(part_refs[r].dtype)
        offset_grad_ref[g] = diagonal_sums(score_sum)


def backward_attention(meta, before, own, after, cotangent, offsets, weight_slots, group, first_head, heads):
    rows = own.shape[0]
    width = heads * HEAD_DIM
    slots = len(weight_slots)
    first = first_head // group
    slot_shape = weight_slots[0].shape
    part_types = [F32] + [BF16] * (slots - 1) if slots > 1 else [BF16]
    return pl.pallas_call(
        functools.partial(backward_kernel, slots, group),
        out_shape=(
            jax.ShapeDtypeStruct((rows, width), F32),
            jax.ShapeDtypeStruct((RADIUS, width), BF16),
            jax.ShapeDtypeStruct((RADIUS, width), BF16),
            jax.ShapeDtypeStruct((heads, 1, WINDOW), F32),
            *[jax.ShapeDtypeStruct(slot_shape, kind) for kind in part_types],
        ),
        grid_spec=pltpu.PrefetchScalarGridSpec(
            num_scalar_prefetch=1,
            grid=(heads // group,),
            in_specs=[
                column_spec(RADIUS, group, first),
                column_spec(rows, group, first),
                column_spec(RADIUS, group, first),
                column_spec(rows, group, first),
                pl.BlockSpec((group, 1, WINDOW), lambda i, meta: (i + first, 0, 0)),
                *slot_specs(weight_slots, group),
            ],
            out_specs=(
                column_spec(rows, group, 0),
                column_spec(RADIUS, group, 0),
                column_spec(RADIUS, group, 0),
                pl.BlockSpec((group, 1, WINDOW), lambda i, meta: (i, 0, 0)),
                *slot_specs(weight_slots, group),
            ),
            scratch_shapes=[
                pltpu.VMEM((group, HEAD_DIM, 3 * HEAD_DIM), BF16),
                pltpu.VMEM((group, HEAD_DIM, 3 * HEAD_DIM), F32),
            ],
        ),
        compiler_params=pltpu.CompilerParams(vmem_limit_bytes=VMEM_LIMIT),
        cost_estimate=pl.CostEstimate(
            flops=heads * 150_000_000, bytes_accessed=12 * rows * width, transcendentals=heads * 32768
        ),
        name="backward_attention",
    )(meta, before, own, after, cotangent, offsets, *weight_slots)


def finish_kernel(grad_ref, low_ref, high_ref, x_ref, inverse_ref, gain_ref, cot_ref, out_ref, gain_grad_ref):
    rows = x_ref.shape[0]
    grad = grad_ref[...]
    edge = jnp.zeros((rows - RADIUS, grad.shape[1]), F32)
    grad = grad + jnp.concatenate([low_ref[...].astype(F32), edge], axis=0)
    grad = grad + jnp.concatenate([edge, high_ref[...].astype(F32)], axis=0)
    x = x_ref[...].astype(F32)
    inverse = inverse_ref[:, :1]
    gain_grad_ref[...] = jnp.sum(grad * x * inverse, axis=0, keepdims=True)
    scaled = grad * gain_ref[...]
    mean = jnp.mean(scaled * x, axis=-1, keepdims=True)
    result = inverse * scaled - x * (inverse * inverse * inverse * mean)
    out_ref[...] = (cot_ref[...].astype(F32) + result).astype(BF16)


def finish(grad, low, high, x, inverse, gain, cotangent):
    rows, width = x.shape
    return pl.pallas_call(
        finish_kernel,
        out_shape=(
            jax.ShapeDtypeStruct((rows, width), BF16),
            jax.ShapeDtypeStruct((1, width), F32),
        ),
        compiler_params=pltpu.CompilerParams(vmem_limit_bytes=VMEM_LIMIT),
        cost_estimate=pl.CostEstimate(
            flops=16 * rows * width, bytes_accessed=14 * rows * width, transcendentals=0
        ),
        name="finish",
    )(grad, low, high, x, inverse, gain, cotangent)


def column_of(row, rows):
    return jnp.transpose(jnp.broadcast_to(row, (128, rows)))


def split_rows(inverse, pad_rows, width):
    high = inverse.astype(BF16)
    rest = inverse - high.astype(F32)
    middle = rest.astype(BF16)
    low = (rest - middle.astype(F32)).astype(BF16)
    wide = [jnp.transpose(jnp.broadcast_to(v.astype(F32), (v.shape[0], 128)))[:1] for v in (high, middle, low)]
    row = jnp.concatenate(wide + [jnp.zeros((pad_rows - 3, wide[0].shape[1]), F32)], axis=0)
    return row.astype(BF16)


def row_inverse(x):
    x = x.astype(F32)
    return lax.rsqrt(jnp.mean(x * x, axis=-1, keepdims=True) + eps_norm)


def pack_stash_kernel(parts, pieces, x_hbm, gain_hbm, weight_hbm, inverse_ref, *refs):
    out_refs = refs[:parts]
    x_ref, gain_ref, weight_ref, normed_ref, sems = refs[parts:]
    rows, width = x_ref.shape
    depth = weight_ref.shape[2]
    wide = width // parts
    heads = wide // HEAD_DIM
    step = rows // pieces
    gain_copy = pltpu.make_async_copy(gain_hbm, gain_ref, sems.at[0])
    x_copies = [
        pltpu.make_async_copy(x_hbm.at[pl.ds(k * step, step)], x_ref.at[pl.ds(k * step, step)], sems.at[1 + k])
        for k in range(pieces)
    ]
    weight_copies = [
        pltpu.make_async_copy(weight_hbm.at[j], weight_ref.at[j], sems.at[1 + pieces + j]) for j in range(3)
    ]
    for copy in (gain_copy, *x_copies, *weight_copies):
        copy.start()
    gain_copy.wait()
    gain = gain_ref[...]
    for k, copy in enumerate(x_copies):
        copy.wait()
        part = slice(k * step, (k + 1) * step)
        inverse = row_inverse(x_ref[part])
        inverse_ref[part] = jnp.broadcast_to(inverse, (step, 128))
        normed_ref[part] = (x_ref[part].astype(F32) * inverse * gain).astype(BF16)
    for r, out_ref in enumerate(out_refs):
        target = lax.rem(lax.axis_index("seq") + r, parts)
        out_ref[:rows] = normed_ref[:, pl.ds(pl.multiple_of(target * wide, 128), wide)]
    for j, copy in enumerate(weight_copies):
        copy.wait()
        for r, out_ref in enumerate(out_refs):
            target = lax.rem(lax.axis_index("seq") + r, parts)
            for h in range(heads):
                out_ref[rows + j * depth : rows + (j + 1) * depth, h * HEAD_DIM : (h + 1) * HEAD_DIM] = weight_ref[
                    j, target * heads + h
                ]


def pack_rows_kernel(parts, with_inverse, meta_ref, edge_ref, inner_ref, *out_refs):
    rows, width = inner_ref.shape
    wide = width // parts
    edge = 1 if with_inverse else 2
    refs = out_refs[:parts]
    for r, out_ref in enumerate(refs):
        target = lax.rem(meta_ref[0] + r, parts)
        start = pl.multiple_of(target * wide, 128)

        @pl.when(meta_ref[edge] == 1)
        def use_edge():
            out_ref[:rows] = edge_ref[:, pl.ds(start, wide)]

        @pl.when(meta_ref[edge] == 0)
        def use_inner():
            out_ref[:rows] = inner_ref[:, pl.ds(start, wide)]

    def finish_with(source_ref):
        if with_inverse:
            tail = split_rows(row_inverse(source_ref[...]), EXTRA, wide)
            for out_ref in refs:
                out_ref[rows:] = jnp.zeros((EXTRA, wide), BF16)
                out_ref[rows:, :rows] = tail
        else:
            out_refs[parts][...] = source_ref[...]

    @pl.when(meta_ref[edge] == 1)
    def finish_edge():
        finish_with(edge_ref)

    @pl.when(meta_ref[edge] == 0)
    def finish_inner():
        finish_with(inner_ref)


SMEM_SPEC = pl.BlockSpec(memory_space=pltpu.SMEM)
VMEM_SPEC = pl.BlockSpec(memory_space=pltpu.VMEM)


def pack_stash(x, gain, weight, parts):
    rows, width = x.shape
    depth = weight.shape[2]
    shape = (rows + 3 * depth, width // parts)
    return pl.pallas_call(
        functools.partial(pack_stash_kernel, parts, 4),
        out_shape=(
            jax.ShapeDtypeStruct((rows, 128), F32),
            *[jax.ShapeDtypeStruct(shape, BF16) for r in range(parts)],
        ),
        in_specs=[pl.BlockSpec(memory_space=pl.ANY)] * 3,
        out_specs=(VMEM_SPEC,) * (parts + 1),
        scratch_shapes=[
            pltpu.VMEM((rows, width), BF16),
            pltpu.VMEM((1, width), F32),
            pltpu.VMEM(weight.shape, BF16),
            pltpu.VMEM((rows, width), BF16),
            pltpu.SemaphoreType.DMA((8,)),
        ],
        compiler_params=pltpu.CompilerParams(vmem_limit_bytes=58 * 1024 * 1024),
        cost_estimate=pl.CostEstimate(flops=4 * rows * width, bytes_accessed=6 * rows * width, transcendentals=0),
        name="pack_stash",
    )(x, gain, weight)


def pack_rows(meta, edge, inner, parts, with_inverse):
    rows, width = inner.shape
    shape = (rows + (EXTRA if with_inverse else 0), width // parts)
    extra = () if with_inverse else (jax.ShapeDtypeStruct((rows, width), BF16),)
    return pl.pallas_call(
        functools.partial(pack_rows_kernel, parts, with_inverse),
        out_shape=(*[jax.ShapeDtypeStruct(shape, BF16) for r in range(parts)], *extra),
        in_specs=[SMEM_SPEC, VMEM_SPEC, VMEM_SPEC],
        out_specs=(VMEM_SPEC,) * (parts + len(extra)),
        compiler_params=pltpu.CompilerParams(vmem_limit_bytes=VMEM_LIMIT),
        cost_estimate=pl.CostEstimate(flops=4 * rows * width, bytes_accessed=6 * rows * width, transcendentals=0),
        name="pack_inbound" if with_inverse else "pack_cotangent",
    )(meta, edge, inner)


def slot_order(parts):
    return sorted(range(parts), key=lambda r: min(r, parts - r))


def gather_rows(meta_ref, refs, rows, x_ref):
    parts = len(refs)
    for r, ref in zip(slot_order(parts), refs):
        source = lax.rem(meta_ref[0] + parts - r, parts)
        x_ref[pl.ds(pl.multiple_of(source * rows, rows), rows)] = ref[:rows]


def gather_weight(meta_ref, refs, rows, weight_ref):
    parts = len(refs)
    depth = HEAD_DIM // parts
    for r, ref in zip(slot_order(parts), refs):
        source = lax.rem(meta_ref[0] + parts - r, parts)
        depth_at = pl.ds(pl.multiple_of(source * depth, depth), depth)
        for j in range(3):
            weight_ref[depth_at, j * HEAD_DIM : (j + 1) * HEAD_DIM] = ref[
                rows + j * depth : rows + (j + 1) * depth
            ]


def gather_inverse(meta_ref, refs, rows, inverse_ref):
    parts = len(refs)

    @pl.when(pl.program_id(0) == 0)
    def spread_inverse():
        for r, ref in zip(slot_order(parts), refs):
            source = lax.rem(meta_ref[0] + parts - r, parts)
            tail = ref[rows : rows + EXTRA].astype(F32)
            inverse_ref[pl.ds(pl.multiple_of(source * rows, rows), rows)] = column_of(
                tail[:1] + tail[1:2] + tail[2:3], rows
            )


def block_mask(first_query, tokens):
    key = lax.broadcasted_iota(jnp.int32, (1, WINDOW), 1) + (first_query - RADIUS)
    return jnp.where((key >= 0) & (key < tokens), 0.0, masked_score).astype(F32)


def edge_bias(bias, first, tokens):
    if first < RADIUS or first + ROW_BLOCK + RADIUS > tokens:
        return bias + block_mask(first, tokens)
    return bias


def padded(rows):
    edge = jnp.zeros((RADIUS, rows.shape[1]), rows.dtype)
    return jnp.concatenate([edge, rows, edge], axis=0)


def heads_backward_kernel(parts, rows, meta_ref, *refs):
    a_refs, c_refs = refs[:parts], refs[parts : 2 * parts]
    gain_ref, offset_ref, onehot_ref, after_ref = refs[2 * parts : 2 * parts + 4]
    out_refs = refs[2 * parts + 4 : 3 * parts + 4]
    gain_grad_ref, x_ref, weight_ref, cot_ref, grad_ref, part_ref, bias_ref = refs[3 * parts + 4 :]
    tokens = rows * parts
    depth = HEAD_DIM // parts
    scale = HEAD_DIM ** (-0.5)
    gather_rows(meta_ref, a_refs, rows, x_ref)
    gather_weight(meta_ref, a_refs, rows, weight_ref)
    gather_rows(meta_ref, c_refs, rows, cot_ref)
    weight = weight_ref[...]
    normed = x_ref[...]
    query = dot_nn(normed, weight[:, :HEAD_DIM]).astype(BF16)
    key = padded(dot_nn(normed, weight[:, HEAD_DIM : 2 * HEAD_DIM]).astype(BF16))
    value = padded(dot_nn(normed, weight[:, 2 * HEAD_DIM :]).astype(BF16))
    bias = toeplitz(offset_ref[0])
    blocks = tokens // ROW_BLOCK
    starts = range(0, tokens, ROW_BLOCK)
    cot = cot_ref[...]
    query_rows = [query[f : f + ROW_BLOCK] for f in starts]
    cot_rows = [cot[f : f + ROW_BLOCK] for f in starts]
    products = [dot_nt(rows_q, key[f : f + WINDOW]) for f, rows_q in zip(starts, query_rows)]
    grad_probs = [dot_nt(rows_c, value[f : f + WINDOW]) for f, rows_c in zip(starts, cot_rows)]
    packed, grad_packed, score_sum = [], [], None
    for f, product, grads in zip(starts, products, grad_probs):
        probs = score_probs(product, edge_bias(bias, f, tokens))
        delta = jnp.sum(probs * grads, axis=-1, keepdims=True)
        grad_scores = probs * (grads - delta)
        score_sum = grad_scores if score_sum is None else score_sum + grad_scores
        packed.append(probs.astype(BF16))
        grad_packed.append(grad_scores.astype(BF16))
    grad_query = [dot_nn(part, key[f : f + WINDOW]) for f, part in zip(starts, grad_packed)]
    grad_key = [dot_tn(part, rows_q) for part, rows_q in zip(grad_packed, query_rows)]
    grad_value = [dot_tn(part, rows_c) for part, rows_c in zip(packed, cot_rows)]

    def joined(pieces):
        units = []
        for u in range((tokens + 2 * RADIUS) // ROW_BLOCK):
            total = None
            for b in range(blocks):
                if 0 <= u - b < WINDOW // ROW_BLOCK:
                    piece = pieces[b][(u - b) * ROW_BLOCK : (u - b + 1) * ROW_BLOCK]
                    total = piece if total is None else total + piece
            units.append(total)
        return jnp.concatenate(units, axis=0)[RADIUS : RADIUS + tokens]

    dqkv = jnp.concatenate(
        [
            (jnp.concatenate(grad_query, axis=0) * scale).astype(BF16),
            (joined(grad_key) * scale).astype(BF16),
            joined(grad_value).astype(BF16),
        ],
        axis=1,
    )
    grad_normed = dot_nt(dqkv, weight)
    gain_grad_ref[...] = jnp.sum(grad_normed * normed.astype(F32), axis=0, keepdims=True) / gain_ref[...]
    grad_ref[...] = grad_normed
    part_ref[...] = dot_tn(normed, dqkv)
    bias_grad = jnp.sum(onehot_ref[...] * diagonal_sums(score_sum), axis=1, keepdims=True)
    bias_ref[...] = jnp.broadcast_to(bias_grad, bias_ref.shape)
    buckets = bias_ref.shape[0] // parts
    for r, out_ref in enumerate(out_refs):
        source = lax.rem(meta_ref[0] + parts - r, parts)
        out_ref[:rows] = grad_ref[pl.ds(pl.multiple_of(source * rows, rows), rows)].astype(BF16)
        for j in range(3):
            out_ref[rows + j * depth : rows + (j + 1) * depth] = part_ref[
                pl.ds(pl.multiple_of(source * depth, depth), depth), j * HEAD_DIM : (j + 1) * HEAD_DIM
            ].astype(BF16)
        share = bias_ref[pl.ds(pl.multiple_of(source * buckets, buckets), buckets)]
        out_ref[rows + 3 * depth :] = share.astype(BF16)


def head_column(rows, first=0):
    return pl.BlockSpec((rows, HEAD_DIM), lambda i, meta: (0, i + first))


def whole_column(rows, heads, first=0):
    return pl.BlockSpec((rows, HEAD_DIM), lambda i, meta: (0, meta[0] * heads + first + i))


def offset_spec(heads, first=0):
    return pl.BlockSpec((1, 1, WINDOW), lambda i, meta: (meta[0] * heads + first + i, 0, 0))


def heads_backward(meta, a_slots, c_slots, gain, offsets, onehot, after, heads, first, count):
    parts = len(a_slots)
    rows = c_slots[0].shape[0]
    tokens = rows * parts
    buckets = onehot.shape[0]
    packed = a_slots[0].shape[0]
    made = packed + buckets // parts
    width = count * HEAD_DIM
    return pl.pallas_call(
        functools.partial(heads_backward_kernel, parts, rows),
        out_shape=(
            *[jax.ShapeDtypeStruct((made, width), BF16) for r in range(parts)],
            jax.ShapeDtypeStruct((1, width), F32),
        ),
        grid_spec=pltpu.PrefetchScalarGridSpec(
            num_scalar_prefetch=1,
            grid=(count,),
            in_specs=[
                *[head_column(packed, first)] * parts,
                whole_column(rows, heads, first),
                *[head_column(rows, first)] * (parts - 1),
                whole_column(1, heads, first),
                offset_spec(heads, first),
                pl.BlockSpec((buckets, WINDOW), lambda i, meta: (0, 0)),
                pl.BlockSpec(memory_space=pl.ANY),
            ],
            out_specs=(*[head_column(made)] * parts, head_column(1)),
            scratch_shapes=[
                pltpu.VMEM((tokens, HEAD_DIM), BF16),
                pltpu.VMEM((HEAD_DIM, 3 * HEAD_DIM), BF16),
                pltpu.VMEM((tokens, HEAD_DIM), BF16),
                pltpu.VMEM((tokens, HEAD_DIM), F32),
                pltpu.VMEM((HEAD_DIM, 3 * HEAD_DIM), F32),
                pltpu.VMEM((buckets, HEAD_DIM), F32),
            ],
        ),
        compiler_params=pltpu.CompilerParams(vmem_limit_bytes=VMEM_LIMIT),
        cost_estimate=pl.CostEstimate(
            flops=count * tokens * 400_000, bytes_accessed=tokens * width, transcendentals=0
        ),
        name="heads_backward",
    )(meta, *a_slots, *c_slots, gain, offsets, onehot, after)


def heads_forward_kernel(parts, rows, meta_ref, *refs):
    a_refs, i_refs = refs[:parts], refs[parts : 2 * parts]
    gain_ref, offset_ref = refs[2 * parts : 2 * parts + 2]
    out_refs = refs[2 * parts + 2 : 3 * parts + 2]
    inverse_ref, x_ref, weight_ref, made_ref, square_ref = refs[3 * parts + 2 :]
    tokens = rows * parts
    gather_rows(meta_ref, i_refs, rows, x_ref)
    gather_weight(meta_ref, a_refs, rows, weight_ref)
    gather_inverse(meta_ref, i_refs, rows, inverse_ref)
    weight = weight_ref[...]
    normed = (x_ref[...].astype(F32) * inverse_ref[...] * gain_ref[...]).astype(BF16)
    query = dot_nn(normed, weight[:, :HEAD_DIM]).astype(BF16)
    key = padded(dot_nn(normed, weight[:, HEAD_DIM : 2 * HEAD_DIM]).astype(BF16))
    value = padded(dot_nn(normed, weight[:, 2 * HEAD_DIM :]).astype(BF16))
    bias = toeplitz(offset_ref[0])
    starts = range(0, tokens, ROW_BLOCK)
    products = [dot_nt(query[f : f + ROW_BLOCK], key[f : f + WINDOW]) for f in starts]
    packed = [
        score_probs(product, edge_bias(bias, f, tokens)).astype(BF16) for f, product in zip(starts, products)
    ]
    attended = [dot_nn(part, value[f : f + WINDOW]) for f, part in zip(starts, packed)]
    for f, part in zip(starts, attended):
        made_ref[f : f + ROW_BLOCK] = (x_ref[f : f + ROW_BLOCK].astype(F32) + part).astype(BF16)
    made = made_ref[...].astype(F32)
    squares = made * made

    @pl.when(pl.program_id(0) == 0)
    def first_head():
        square_ref[...] = squares

    @pl.when(pl.program_id(0) > 0)
    def later_head():
        square_ref[...] += squares

    for r, out_ref in enumerate(out_refs):
        source = lax.rem(meta_ref[0] + parts - r, parts)
        out_ref[:rows] = made_ref[pl.ds(pl.multiple_of(source * rows, rows), rows)]

    @pl.when(pl.program_id(0) < pl.num_programs(0) - 1)
    def no_sums():
        for out_ref in out_refs:
            out_ref[rows:] = jnp.zeros((EXTRA, HEAD_DIM), BF16)

    @pl.when(pl.program_id(0) == pl.num_programs(0) - 1)
    def last_head():
        rest = jnp.sum(jnp.transpose(square_ref[...]), axis=0, keepdims=True)
        at_row = lax.broadcasted_iota(jnp.int32, (EXTRA, rows), 0)
        tail = jnp.zeros((EXTRA, rows), F32)
        for k in range(2):
            piece = rest.astype(BF16).astype(F32)
            rest = rest - piece
            for part in range(parts):
                row = jnp.broadcast_to(piece[:, part * rows : (part + 1) * rows], (EXTRA, rows))
                tail = jnp.where(at_row == 2 * part + k, row, tail)
        for out_ref in out_refs:
            out_ref[rows:] = tail.astype(BF16)


def heads_forward(meta, a_slots, i_slots, gain, offsets, heads, rows):
    parts = len(a_slots)
    tokens = rows * parts
    packed = a_slots[0].shape[0]
    width = heads * HEAD_DIM
    return pl.pallas_call(
        functools.partial(heads_forward_kernel, parts, rows),
        out_shape=(
            *[jax.ShapeDtypeStruct((rows + EXTRA, width), BF16) for r in range(parts)],
        ),
        grid_spec=pltpu.PrefetchScalarGridSpec(
            num_scalar_prefetch=1,
            grid=(heads,),
            in_specs=[
                *[head_column(packed)] * parts,
                *[head_column(i_slots[0].shape[0])] * parts,
                whole_column(1, heads),
                offset_spec(heads),
            ],
            out_specs=(head_column(rows + EXTRA),) * parts,
            scratch_shapes=[
                pltpu.VMEM((tokens, HEAD_DIM), F32),
                pltpu.VMEM((tokens, HEAD_DIM), BF16),
                pltpu.VMEM((HEAD_DIM, 3 * HEAD_DIM), BF16),
                pltpu.VMEM((tokens, HEAD_DIM), BF16),
                pltpu.VMEM((tokens, HEAD_DIM), F32),
            ],
        ),
        compiler_params=pltpu.CompilerParams(vmem_limit_bytes=VMEM_LIMIT),
        cost_estimate=pl.CostEstimate(
            flops=heads * tokens, bytes_accessed=tokens, transcendentals=0
        ),
        name="heads_forward",
    )(meta, *a_slots, *i_slots, gain, offsets)


def memory_kernel(parts, width, sections, meta_ref, *refs):
    out_refs, other_refs = refs[:parts], refs[parts : 2 * parts - 1]
    gain_ref, *share_refs, memory_ref = refs[2 * parts - 1 :]
    wide = memory_ref.shape[1]
    rows = memory_ref.shape[0] // parts
    total = None
    for ref in (out_refs[0], *other_refs):
        tail = ref[rows:, wide - rows :].astype(F32)
        pieces = [tail[2 * p : 2 * p + 1] + tail[2 * p + 1 : 2 * p + 2] for p in range(parts)]
        row = jnp.concatenate(pieces, axis=1)
        total = row if total is None else total + row
    inverse = lax.rsqrt(total / width + eps_norm)
    gain = gain_ref[:, pl.ds(pl.multiple_of(meta_ref[0] * wide, 128), wide)]
    spread_inverse = jnp.transpose(jnp.broadcast_to(inverse, (128, inverse.shape[1])))
    for r, out_ref in enumerate(out_refs):
        source = lax.rem(meta_ref[0] + parts - r, parts)
        memory_ref[pl.ds(pl.multiple_of(source * rows, rows), rows)] = out_ref[:rows]
    made = memory_ref[...].astype(F32)
    memory_ref[...] = (made * spread_inverse[:, :1] * gain).astype(BF16)
    for k, share_ref in enumerate(share_refs):
        size = 2 * share_ref.shape[0] // sections
        for i in range(sections // 2):
            share_ref[i * size : (i + 1) * size] = memory_ref[(2 * i + k) * size : (2 * i + k + 1) * size]


def memory_rows(meta, outs, others, gain, width, sections):
    parts = len(outs)
    rows, wide = outs[0].shape[0] - EXTRA, outs[0].shape[1]
    return pl.pallas_call(
        functools.partial(memory_kernel, parts, width, sections),
        out_shape=[jax.ShapeDtypeStruct((rows * parts // 2, wide), BF16)] * 2,
        in_specs=[SMEM_SPEC] + [VMEM_SPEC] * (2 * parts),
        out_specs=[VMEM_SPEC] * 2,
        scratch_shapes=[pltpu.VMEM((rows * parts, wide), BF16)],
        compiler_params=pltpu.CompilerParams(vmem_limit_bytes=VMEM_LIMIT),
        cost_estimate=pl.CostEstimate(flops=rows, bytes_accessed=rows, transcendentals=0),
        name="memory_rows",
    )(meta, *outs, *others, gain)


def place_kernel(parts, meta_ref, *refs):
    out_ref = refs[parts]
    wide = refs[0].shape[1]
    for r, ref in zip(slot_order(parts), refs):
        source = lax.rem(meta_ref[0] + r, parts)
        out_ref[:, pl.ds(pl.multiple_of(source * wide, 128), wide)] = ref[: out_ref.shape[0]]


def place_columns(meta, slots):
    parts = len(slots)
    rows, wide = slots[0].shape[0] - EXTRA, slots[0].shape[1]
    return pl.pallas_call(
        functools.partial(place_kernel, parts),
        out_shape=jax.ShapeDtypeStruct((rows, wide * parts), BF16),
        in_specs=[SMEM_SPEC] + [VMEM_SPEC] * parts,
        out_specs=VMEM_SPEC,
        compiler_params=pltpu.CompilerParams(vmem_limit_bytes=VMEM_LIMIT),
        cost_estimate=pl.CostEstimate(flops=0, bytes_accessed=rows, transcendentals=0),
        name="place_columns",
    )(meta, *slots)


def store_weights(g_ref, weight_ref, rows, depth, heads):
    for h in range(heads):
        for j in range(3):
            weight_ref[j, h] = g_ref[
                rows + j * depth : rows + (j + 1) * depth, h * HEAD_DIM : (h + 1) * HEAD_DIM
            ].astype(F32)


def weight_copies(weight_ref, weight_hbm, first_head, heads, sems):
    return [
        pltpu.make_async_copy(weight_ref.at[j], weight_hbm.at[j, pl.ds(first_head, heads)], sems.at[j])
        for j in range(3)
    ]


def add_bias(bias, g_ref, first_row, first_head, heads):
    lane = lax.broadcasted_iota(jnp.int32, bias.shape, 1)
    shares = g_ref[first_row:].astype(F32)
    for h in range(heads):
        bias = jnp.where(lane == first_head + h, shares[:, h * HEAD_DIM : (h + 1) * HEAD_DIM], bias)
    return bias


def early_finish_kernel(parts, meta_ref, *refs):
    g_refs = refs[: parts - 1]
    x_ref, inverse_ref, gain_ref, cot_ref = refs[parts - 1 : parts + 3]
    base_ref, row_ref, weight_hbm, bias_ref, weight_ref, sems = refs[parts + 3 :]
    rows, width = x_ref.shape
    wide = width // parts
    heads = wide // HEAD_DIM
    depth = HEAD_DIM // parts
    order = slot_order(parts)
    inverse = inverse_ref[:, :1]
    bias = jnp.zeros(bias_ref.shape, F32)
    total = jnp.zeros((rows, 1), F32)
    copies = []
    for k, g_ref in enumerate(g_refs):
        source = lax.rem(meta_ref[0] + order[k], parts)
        store_weights(g_ref, weight_ref.at[k], rows, depth, heads)
        for copy in weight_copies(weight_ref.at[k], weight_hbm, source * heads, heads, sems.at[k]):
            copy.start()
            copies.append(copy)
        bias = add_bias(bias, g_ref, rows + 3 * depth, source * heads, heads)
        columns = pl.ds(pl.multiple_of(source * wide, 128), wide)
        scaled = g_ref[:rows].astype(F32) * gain_ref[:, columns]
        total = total + jnp.sum(scaled * x_ref[:, columns].astype(F32), axis=-1, keepdims=True)
        base_ref[:, columns] = cot_ref[:, columns].astype(F32) + inverse * scaled
    last = pl.ds(pl.multiple_of(lax.rem(meta_ref[0] + order[-1], parts) * wide, 128), wide)
    base_ref[:, last] = cot_ref[:, last].astype(F32)
    row_ref[...] = jnp.broadcast_to(total, row_ref.shape)
    bias_ref[...] = bias
    for copy in copies:
        copy.wait()


def late_finish_kernel(parts, meta_ref, *refs):
    base_ref, row_ref, early_bias_ref, g_ref, x_ref, inverse_ref, gain_ref, early_hbm, after_hbm = refs[:9]
    out_ref, weight_hbm, bias_ref, weight_ref, sems = refs[9:]
    rows, width = x_ref.shape
    wide = width // parts
    heads = wide // HEAD_DIM
    depth = HEAD_DIM // parts
    source = lax.rem(meta_ref[0] + slot_order(parts)[-1], parts)
    store_weights(g_ref, weight_ref, rows, depth, heads)
    copies = weight_copies(weight_ref, weight_hbm, source * heads, heads, sems)
    for copy in copies:
        copy.start()
    bias = add_bias(early_bias_ref[...], g_ref, rows + 3 * depth, source * heads, heads)
    bias_ref[...] = bias[:, : bias_ref.shape[1]]
    columns = pl.ds(pl.multiple_of(source * wide, 128), wide)
    inverse = inverse_ref[:, :1]
    scaled = g_ref[:rows].astype(F32) * gain_ref[:, columns]
    total = row_ref[:, :1] + jnp.sum(scaled * x_ref[:, columns].astype(F32), axis=-1, keepdims=True)
    factor = inverse * inverse * inverse * (total / width)
    out_ref[...] = (base_ref[...] - x_ref[...].astype(F32) * factor).astype(BF16)
    out_ref[:, columns] = (
        base_ref[:, columns] + (inverse * scaled - x_ref[:, columns].astype(F32) * factor)
    ).astype(BF16)
    for copy in copies:
        copy.wait()


def heads_finish(meta, g_slots, x, inverse, gain, cotangent, after, buckets):
    parts = len(g_slots)
    rows, width = x.shape
    heads = width // HEAD_DIM
    depth = HEAD_DIM // parts
    any_spec = pl.BlockSpec(memory_space=pl.ANY)
    weight = jax.ShapeDtypeStruct((3, heads, depth, HEAD_DIM), F32)
    piece = (3, heads // parts, depth, HEAD_DIM)
    cost = pl.CostEstimate(flops=rows * width, bytes_accessed=rows * width, transcendentals=0)
    params = pltpu.CompilerParams(vmem_limit_bytes=VMEM_LIMIT)
    base, row, early, bias = pl.pallas_call(
        functools.partial(early_finish_kernel, parts),
        out_shape=(
            jax.ShapeDtypeStruct((rows, width), F32),
            jax.ShapeDtypeStruct((rows, 128), F32),
            weight,
            jax.ShapeDtypeStruct((buckets // parts, HEAD_DIM), F32),
        ),
        in_specs=[SMEM_SPEC] + [VMEM_SPEC] * (parts + 3),
        out_specs=(VMEM_SPEC, VMEM_SPEC, any_spec, VMEM_SPEC),
        scratch_shapes=[pltpu.VMEM((parts - 1, *piece), F32), pltpu.SemaphoreType.DMA((parts - 1, 3))],
        compiler_params=params,
        cost_estimate=cost,
        name="early_finish",
    )(meta, *g_slots[:-1], x, inverse, gain, cotangent)
    return pl.pallas_call(
        functools.partial(late_finish_kernel, parts),
        out_shape=(
            jax.ShapeDtypeStruct((rows, width), BF16),
            weight,
            jax.ShapeDtypeStruct((buckets // parts, heads), F32),
        ),
        in_specs=[SMEM_SPEC] + [VMEM_SPEC] * 7 + [any_spec] * 2,
        out_specs=(VMEM_SPEC, any_spec, VMEM_SPEC),
        input_output_aliases={8: 1},
        scratch_shapes=[pltpu.VMEM(piece, F32), pltpu.SemaphoreType.DMA((3,))],
        compiler_params=params,
        cost_estimate=cost,
        name="late_finish",
    )(meta, base, row, bias, g_slots[-1], x, inverse, gain, early, after)


def offset_table(rel_bias):
    onehot = jnp.asarray(bucket_onehot(rel_bias.shape[0]))
    by_offset = jnp.dot(onehot, rel_bias, precision=lax.Precision.HIGHEST).T
    inside = jnp.arange(WINDOW, dtype=jnp.int32) <= 2 * RADIUS
    return jnp.where(inside[None, :], by_offset, masked_score)[:, None, :]


def shifted(value, axis, steps):
    count = lax.axis_size(axis)
    first, last = (max(0, -steps), min(count, count - steps))
    return lax.ppermute(value, axis, [(source, source + steps) for source in range(first, last)])


def spread_memory(even, odd, section, sections):
    last = sections - 1
    share = 2 * even.shape[0] // sections
    held = jnp.where(section == last - 1, lax.ppermute(even, "section", [(last, last - 1)]), odd)
    memory = jnp.where(section >= last - 1, held[even.shape[0] - share :], 0)
    for i in range(sections // 2 - 1):
        memory = memory + lax.ppermute(
            held[i * share : (i + 1) * share], "section", [(last, 2 * i + 1), (last - 1, 2 * i)]
        )
    return memory


def heads_body(
    embedded, carried, stash, returned, loss_grad, qkv_weight, rel_bias, norm_gain, final_gain
):
    section = lax.axis_index("section")
    sections = lax.axis_size("section")
    parts = lax.axis_size("seq")
    rows, width = embedded.shape
    heads = width // HEAD_DIM // parts
    buckets = rel_bias.shape[1]
    meta = jnp.stack(
        [lax.axis_index("seq"), section == 0, section == sections - 1]
    ).astype(jnp.int32)

    def exchanged(sends, direction):
        return [
            lax.ppermute(sends[r], "seq", [(i, (i + direction * r) % parts) for i in range(parts)]) if r else sends[0]
            for r in slot_order(parts)
        ]

    inverse_b, *a_sends = pack_stash(stash[0], norm_gain, qkv_weight[0], parts)
    a_slots = exchanged(a_sends, 1)
    arrived = shifted(carried[0], "section", 1)
    came_back = shifted(returned[0], "section", -1)
    i_slots = exchanged(pack_rows(meta, embedded, arrived, parts, True), 1)
    *c_sends, cotangent = pack_rows(meta, loss_grad, came_back, parts, False)
    c_slots = exchanged(c_sends, 1)
    c_slots[0] = cotangent

    offsets = offset_table(rel_bias[0])
    onehot = jnp.asarray(bucket_onehot(buckets).T)
    o_sends = heads_forward(meta, a_slots, i_slots, norm_gain, offsets, heads, rows)
    o_slots = exchanged(o_sends, -1)

    *g_sends, gain_grad = heads_backward(
        meta, a_slots, c_slots, norm_gain, offsets, onehot, o_sends[0], heads, 0, heads
    )
    g_sends, o_slots = lax.optimization_barrier((g_sends, o_slots))
    g_slots = exchanged(g_sends, -1)
    output = place_columns(meta, o_slots)
    shares = memory_rows(meta, o_sends, o_slots[1:], final_gain[None], width, sections)
    memory = spread_memory(*shares, section, sections)

    input_grad, weight_grad, bias_grad = heads_finish(
        meta, g_slots, stash[0], inverse_b, norm_gain, cotangent, memory, buckets
    )
    return (
        output[None],
        input_grad[None],
        weight_grad[None],
        bias_grad[None],
        gain_grad,
        memory,
    )


def tokens_body(
    embedded, carried, stash, returned, loss_grad, qkv_weight, rel_bias, norm_gain, final_gain
):
    section_index = lax.axis_index("section")
    section_count = lax.axis_size("section")
    seq_index = lax.axis_index("seq")
    seq_count = lax.axis_size("seq")
    rows, width = embedded.shape
    heads = width // HEAD_DIM
    tokens = rows * seq_count
    shard = qkv_weight[0]
    up = [(i, i + 1) for i in range(seq_count - 1)]
    down = [(j, i) for i, j in up]
    group = 4 if heads % 4 == 0 else 1

    own_b, inverse_b = norm_rows(stash[0], norm_gain)
    before_b = lax.ppermute(own_b[rows - RADIUS :], "seq", up)
    after_b = lax.ppermute(own_b[:RADIUS], "seq", down)
    slots = [lax.all_gather(shard, "seq", axis=2, tiled=True)]

    section_up = [(i, (i + 1) % section_count) for i in range(section_count)]
    section_down = [(j, i) for i, j in section_up]
    inbound = lax.ppermute(
        jnp.where(section_index == section_count - 1, embedded, carried[0]), "section", section_up
    )
    cotangent = lax.ppermute(
        jnp.where(section_index == 0, loss_grad, returned[0]), "section", section_down
    )

    onehot = jnp.asarray(bucket_onehot(rel_bias.shape[1]))
    offsets = offset_table(rel_bias[0])
    first_key = RADIUS - seq_index * rows
    meta = jnp.stack([seq_index, first_key, first_key + tokens]).astype(jnp.int32)

    own_a, unused = norm_rows(inbound, norm_gain)
    before_a = lax.ppermute(own_a[rows - RADIUS :], "seq", up)
    after_a = lax.ppermute(own_a[:RADIUS], "seq", down)

    grad_own, lower, upper, offset_grad, *parts = backward_attention(
        meta, before_b, own_b, after_b, cotangent, offsets, slots, group, 0, heads
    )
    from_before = lax.ppermute(upper, "seq", up)
    from_after = lax.ppermute(lower, "seq", down)
    weight_sum = lax.psum_scatter(parts[0], "seq", scatter_dimension=2, tiled=True).astype(F32)

    output = forward_attention(meta, before_a, own_a, after_a, inbound, offsets, slots, group)
    final_normed, unused = norm_rows(output, final_gain[None])
    relaid = lax.all_to_all(final_normed, "seq", split_axis=1, concat_axis=0, tiled=True)
    kept = jnp.where(section_index == section_count - 1, relaid, jnp.zeros_like(relaid))
    memory = lax.psum_scatter(kept, "section", scatter_dimension=0, tiled=True)

    input_grad, gain_part = finish(
        grad_own, from_before, from_after, stash[0], inverse_b, norm_gain, cotangent
    )
    bias_part = jnp.dot(
        offset_grad[:, 0, :], onehot, precision=lax.Precision.HIGHEST
    ).T
    bias_sum = lax.psum_scatter(
        bias_part.astype(BF16), "seq", scatter_dimension=0, tiled=True
    ).astype(F32)
    gain_sum = lax.psum_scatter(
        gain_part.astype(BF16), "seq", scatter_dimension=1, tiled=True
    ).astype(F32)
    return (output[None], input_grad[None], weight_sum[None], bias_sum[None], gain_sum, memory)


def choose_body(embedded, carried, stash, returned, loss_grad, qkv_weight, rel_bias, norm_gain, final_gain):
    parts = lax.axis_size("seq")
    rows, width = embedded.shape
    even = parts > 1 and width % (HEAD_DIM * parts) == 0 and HEAD_DIM % (32 * parts) == 0 and rows == 128
    sections = lax.axis_size("section")
    even = even and sections % 2 == 0
    even = even and rel_bias.shape[1] == 8 * parts and width <= 128 * HEAD_DIM and rows * parts % (16 * sections) == 0
    chosen = heads_body if even else tokens_body
    return chosen(
        embedded, carried, stash, returned, loss_grad, qkv_weight, rel_bias, norm_gain, final_gain
    )


def solution(mesh):
    in_specs = (
        P("seq", None),
        P("section", "seq", None),
        P("section", "seq", None),
        P("section", "seq", None),
        P("seq", None),
        P("section", None, None, "seq", None),
        P("section", None, None),
        P("section", None),
        P(),
    )
    out_specs = (
        P("section", "seq", None),
        P("section", "seq", None),
        P("section", None, None, "seq", None),
        P("section", "seq", None),
        P("section", "seq"),
        P("section", "seq"),
    )
    return jax.shard_map(choose_body, mesh=mesh, in_specs=in_specs, out_specs=out_specs, check_vma=False)
```
